128 devices in a mesh: row: 32 (over z, y, core), col: 4 (over x).
Axes of the slice: x: 4, y: 4, z: 4, core: 2. Of those that a mesh axis runs over, the one named last changes fastest.
Arguments:
- tokens: bfloat16 [16384, 2048], P('row', 'col'), may hold values from -6 to 6
- cotangent: bfloat16 [16384, 2048], P('row', 'col'), may hold values from -6 to 6
- destination: int32 [16384], P('row'), may hold values from 0 to 16383, as said below
- segment_ids: int32 [16384], P('row'), may hold values from 0 to 7, as said below
- attn_gain: float32 [2048], replicated, may hold values from 0.5 to 1.5
- w_query: bfloat16 [2048, 2048], P('row', 'col'), may hold values from -0.125 to 0.125
- w_key: bfloat16 [2048, 256], P('row', 'col'), may hold values from -0.125 to 0.125
- w_value: bfloat16 [2048, 256], P('row', 'col'), may hold values from -0.125 to 0.125
- w_output: bfloat16 [2048, 2048], P('row', 'col'), may hold values from -0.5 to 0.5
- ffn_gain: float32 [2048], replicated, may hold values from 0.5 to 1.5
- w_gate: bfloat16 [2048, 5632], P('row', 'col'), may hold values from -0.125 to 0.125
- w_up: bfloat16 [2048, 5632], P('row', 'col'), may hold values from -0.125 to 0.125
- w_down: bfloat16 [2048, 5632], P('row', 'col'), may hold values from -0.078125 to 0.078125
Outputs:
- output: bfloat16 [16384, 2048], P('row', 'col')
- input_grad: bfloat16 [16384, 2048], P('row', 'col')
- attn_gain_grad: float32 [2048], P('row')
- w_query_grad: float32 [2048, 2048], P('row', 'col')
- w_key_grad: float32 [2048, 256], P('row', 'col')
- w_value_grad: float32 [2048, 256], P('row', 'col')
- w_output_grad: float32 [2048, 2048], P('row', 'col')
- ffn_gain_grad: float32 [2048], P('row')
- w_gate_grad: float32 [2048, 5632], P('row', 'col')
- w_up_grad: float32 [2048, 5632], P('row', 'col')
- w_down_grad: float32 [2048, 5632], P('row', 'col')
The draws below stay inside these ranges and needn't reach their ends.
Inputs may be any that keep to these rules, and one draw needn't show every extreme that they name: `destination`: A permutation; the tokens of each aligned block of 512 arriving tokens go to exactly 16 places in each aligned block of 512 balanced places. `segment_ids`: within each aligned block of 512 places the ids start at 0 and rise by one where a new sequence begins, so a block holds at most 8 sequences; in every draw some block holds a single sequence of 512 tokens and some block holds 8 sequences.
All inputs are finite; a program needn't handle non-finite values.
Results may differ from the reference program's by a relative error of at most 0.028.
Values may be sent and summed in bfloat16 or wider, within the bound.
No kernel may reach another device: no remote copies, remote signals or barrier semaphores. Data moves between devices by JAX's collectives and lax.ppermute only.
A program may use at most 128 MiB of HBM per device.

```python
import jax
import jax.numpy as jnp
from jax import lax

D = 2048
HEADS = 32
KV = 4
HD = 64
FF = 5632
TOK_ROW = 512
TOKENS = 16384


def draw_destination(key, part):
    group_count = TOKENS // TOK_ROW
    pair_rows = TOK_ROW // group_count
    all_keys = jax.random.split(jax.random.fold_in(key, 11), 2 * group_count)
    order_out = jax.vmap(lambda sub_key: jax.random.permutation(sub_key, TOK_ROW))(all_keys[:group_count])
    order_in = jax.vmap(lambda sub_key: jax.random.permutation(sub_key, TOK_ROW))(all_keys[group_count:])
    source_ids = jnp.arange(group_count, dtype=jnp.int32)[:, None]
    target_group = order_out // pair_rows
    slot_index = source_ids * pair_rows + order_out % pair_rows
    target_pos = target_group * TOK_ROW + order_in[target_group, slot_index]
    return target_pos.reshape(-1).astype(jnp.int32)


def draw_segment_ids(key, part):
    group_count = TOKENS // TOK_ROW
    first_key, second_key = jax.random.split(jax.random.fold_in(key, 23))
    scores = jax.random.randint(first_key, (group_count, TOK_ROW), 0, TOK_ROW)
    starts = (scores < 4).astype(jnp.int32)
    single = jax.random.randint(second_key, (), 0, group_count)
    fuller = (single + 1) % group_count
    block_ids = jnp.arange(group_count, dtype=jnp.int32)[:, None]
    place_ids = jnp.arange(TOK_ROW, dtype=jnp.int32)[None, :]
    regular = (place_ids % (TOK_ROW // 8) == 0).astype(jnp.int32)
    starts = jnp.where(block_ids == fuller, regular, starts)
    starts = jnp.where(block_ids == single, 0, starts)
    starts = starts.at[:, 0].set(1)
    counted = jnp.minimum(jnp.cumsum(starts, axis=1) - 1, 7)
    return counted.reshape(-1).astype(jnp.int32)


def strengthened(array, key, source, target, blocks, factor):
    owner, partner = [(jnp.arange(array.shape[axis_at]) // (array.shape[axis_at] // blocks)).reshape([-1 if axis == axis_at else 1 for axis in range(array.ndim)]) for axis_at in (source, target)]
    chosen = jax.random.permutation(key, blocks)[partner]
    strong = (owner == chosen) | (owner == (partner + blocks // 2) % blocks)
    return jnp.where(strong, factor * array, array)


def block_scale(key, extent, cuts, smallest, high):
    level = 1.0
    for axis_at, parts in cuts:
        heights = jax.random.uniform(jax.random.fold_in(jax.random.fold_in(key, 6), axis_at), (parts,), jnp.float32, smallest / len(cuts), high / len(cuts))
        level = level * jnp.repeat(jnp.exp(heights), extent[axis_at] // parts).reshape((-1,) + (1,) * (len(extent) - 1 - axis_at))
    return level


def noise(stream_key, shape, deviation, most, pieces=(), kind=jnp.bfloat16):
    drawn = jax.random.normal(stream_key, shape, jnp.float32) * deviation
    if len(pieces) > 0:
        drawn = block_scale(stream_key, shape, pieces, -0.22, 0.18) * drawn
    return jnp.clip(drawn, min=-most, max=most).astype(kind)


def noise_with(stream_key, extent, spread, most, cuts, heavy, kind=jnp.bfloat16):
    entries = spread * jax.random.normal(stream_key, extent, jnp.float32)
    if cuts:
        entries = entries * block_scale(stream_key, extent, cuts, -0.22, 0.18)
    return jnp.clip(strengthened(entries, jax.random.fold_in(stream_key, 3), *heavy), -most, most).astype(kind)


def setup_inputs(seed: int = 0) -> dict:
    arg_keys = jax.random.split(jax.random.key(seed), 14)
    return {
        "tokens": noise(arg_keys[0], (TOKENS, D), 1.0, 6.0, ((0, 32), (1, 4))),
        "cotangent": noise_with(arg_keys[1], (TOKENS, D), 1.0, 6.0, ((0, 32), (1, 4)), (0, 1, 32, 2.75)),
        "destination": draw_destination(jax.random.fold_in(arg_keys[13], 71), 0),
        "segment_ids": draw_segment_ids(jax.random.fold_in(arg_keys[13], 71), 0),
        "attn_gain": jnp.clip(1.0 + 0.1 * jax.random.normal(arg_keys[4], (D,), jnp.float32), 0.5, 1.5),
        "w_query": noise(arg_keys[5], (D, HEADS * HD), D ** -0.5, 0.125, ((0, 32), (1, 4))),
        "w_key": noise(arg_keys[6], (D, KV * HD), D ** -0.5, 0.125, ((0, 32), (1, 4))),
        "w_value": noise(arg_keys[7], (D, KV * HD), D ** -0.5, 0.125, ((0, 32), (1, 4))),
        "w_output": noise(arg_keys[8], (D, HEADS * HD), (D // 16) ** -0.5, 0.5, ((0, 32), (1, 4))),
        "ffn_gain": jnp.clip(1.0 + 0.1 * jax.random.normal(arg_keys[9], (D,), jnp.float32), 0.5, 1.5),
        "w_gate": noise(arg_keys[10], (D, FF), D ** -0.5, 0.125, ((0, 32), (1, 4))),
        "w_up": noise(arg_keys[11], (D, FF), D ** -0.5, 0.125, ((0, 32), (1, 4))),
        "w_down": noise(arg_keys[12], (D, FF), FF ** -0.5, 0.078125, ((0, 32), (1, 4))),
    }


EPS = 1e-05
ROPE_BASE = 10000.0

@jax.custom_vjp
def low(v):
    return lax.optimization_barrier(v.astype(jnp.bfloat16)).astype(jnp.float32)

@jax.custom_vjp
def low_back(v):
    return v

def low_keep(v):
    return (low(v), None)

def low_pass(kept, grad):
    return (grad,)

def back_keep(v):
    return (v, None)

def back_low(kept, grad):
    return (low(grad),)
low.defvjp(low_keep, low_pass)
low_back.defvjp(back_keep, back_low)

def rope_tables(positions):
    half_width = HD // 2
    freqs = ROPE_BASE ** (-(jnp.arange(half_width, dtype=jnp.float32) * 2.0 / HD))
    angles = positions.astype(jnp.float32)[:, None] * freqs[None, :]
    return (jnp.cos(angles)[:, None, :], jnp.sin(angles)[:, None, :])

def rotate(values, cosine, sine):
    half_width = values.shape[-1] // 2
    first = values[..., :half_width]
    second = values[..., half_width:]
    return jnp.concatenate([first * cosine - second * sine, second * cosine + first * sine], axis=-1)

def positions_of(segment_ids):
    index = jnp.arange(segment_ids.shape[0], dtype=jnp.int32)
    change = jnp.concatenate([jnp.ones((1,), dtype=jnp.bool_), segment_ids[1:] != segment_ids[:-1]])
    starts = jnp.where(change, index, jnp.zeros_like(index))
    return index - lax.cummax(starts, axis=0)

def allowed_pairs(segment_ids):
    index = jnp.arange(segment_ids.shape[0], dtype=jnp.int32)
    return (segment_ids[:, None] == segment_ids[None, :]) & (index[None, :] <= index[:, None])

def rms_scale(values):
    return lax.rsqrt(lax.optimization_barrier(jnp.mean(values * values, axis=-1, keepdims=True)) + EPS)

def group_layer(params, rows, segment_ids):
    attn_gain, w_query, w_key, w_value, w_output, ffn_gain, w_gate, w_up, w_down = params
    highest = lax.Precision.HIGHEST
    row_count = rows.shape[0]
    group_size = HEADS // KV
    normed_one = low(rows * rms_scale(rows) * attn_gain)
    query = low_back(jnp.dot(normed_one, w_query, precision=highest))
    key_raw = low_back(jnp.dot(normed_one, w_key, precision=highest))
    values = low(low_back(jnp.dot(normed_one, w_value, precision=highest)))
    cosine, sine = rope_tables(positions_of(segment_ids))
    query_rot = low(rotate(query.reshape(row_count, HEADS, HD), cosine, sine))
    key_rot = low(rotate(key_raw.reshape(row_count, KV, HD), cosine, sine))
    grouped = query_rot.reshape(row_count, KV, group_size, HD)
    scores = low_back(jnp.einsum('qkgd,skd->kgqs', grouped, key_rot, precision=highest) * HD ** (-0.5))
    scores = jnp.where(allowed_pairs(segment_ids), scores, -1e+30)
    peak = lax.optimization_barrier(jnp.max(scores, axis=-1, keepdims=True))
    expo = jnp.exp(scores - peak)
    probs = low(expo / lax.optimization_barrier(jnp.sum(expo, axis=-1, keepdims=True)))
    mixed = jnp.einsum('kgqs,skd->qkgd', probs, values.reshape(row_count, KV, HD), precision=highest)
    mixed = low(low_back(mixed.reshape(row_count, HEADS * HD)))
    attn = low_back(jnp.dot(mixed, w_output.T, precision=highest))
    resid = rows + attn
    normed_two = low(resid * rms_scale(resid) * ffn_gain)
    gate = low_back(jnp.dot(normed_two, w_gate, precision=highest))
    upper = low_back(jnp.dot(normed_two, w_up, precision=highest))
    activ = low(gate * jax.nn.sigmoid(gate) * upper)
    return resid + jnp.dot(activ, w_down.T, precision=highest)

def reference(tokens, cotangent, destination, segment_ids, attn_gain, w_query, w_key, w_value, w_output, ffn_gain, w_gate, w_up, w_down):
    group_count = TOKENS // TOK_ROW
    source = jnp.argsort(destination).astype(jnp.int32)
    rows_all = tokens.astype(jnp.float32)[source].reshape(group_count, TOK_ROW, D)
    grads_all = cotangent.astype(jnp.float32)[source].reshape(group_count, TOK_ROW, D)
    segments = segment_ids.reshape(group_count, TOK_ROW)
    params = (attn_gain.astype(jnp.float32), w_query.astype(jnp.float32), w_key.astype(jnp.float32), w_value.astype(jnp.float32), w_output.astype(jnp.float32), ffn_gain.astype(jnp.float32), w_gate.astype(jnp.float32), w_up.astype(jnp.float32), w_down.astype(jnp.float32))
    layer = jax.checkpoint(group_layer)

    def forward(weights, inputs):

        def map_body(entry_pair):
            return layer(weights, entry_pair[0], entry_pair[1])
        return lax.map(map_body, (inputs, segments))
    outputs, pullback = jax.vjp(forward, params, rows_all)
    weight_grads, input_grads = pullback(grads_all)
    output = outputs.reshape(TOKENS, D)[destination].astype(jnp.bfloat16)
    input_grad = input_grads.reshape(TOKENS, D)[destination].astype(jnp.bfloat16)
    return (output, input_grad, weight_grads[0], weight_grads[1], weight_grads[2], weight_grads[3], weight_grads[4], weight_grads[5], weight_grads[6], weight_grads[7], weight_grads[8])
```

```python
from functools import partial

import jax
import jax.numpy as jnp
from jax import lax
from jax.sharding import PartitionSpec as P

HEADS = 32
KV = 4
HD = 64


EPS = 1e-05
ROPE_BASE = 10000.0


def rope_tables(positions):
    half_width = HD // 2
    freqs = ROPE_BASE ** (-(jnp.arange(half_width, dtype=jnp.float32) * 2.0 / HD))
    angles = positions.astype(jnp.float32)[:, None] * freqs[None, :]
    return (jnp.cos(angles)[:, None, :], jnp.sin(angles)[:, None, :])


def rotate(values, cosine, sine):
    half_width = values.shape[-1] // 2
    first = values[..., :half_width]
    second = values[..., half_width:]
    return jnp.concatenate(
        [first * cosine - second * sine, second * cosine + first * sine], axis=-1
    )


def rotate_back(grads, cosine, sine):
    half_width = grads.shape[-1] // 2
    first = grads[..., :half_width]
    second = grads[..., half_width:]
    return jnp.concatenate(
        [first * cosine + second * sine, second * cosine - first * sine], axis=-1
    )


def positions_of(segment_ids):
    index = jnp.arange(segment_ids.shape[0], dtype=jnp.int32)
    change = jnp.concatenate([jnp.ones((1,), dtype=jnp.bool_), segment_ids[1:] != segment_ids[:-1]])
    starts = jnp.where(change, index, jnp.zeros_like(index))
    return index - lax.cummax(starts, axis=0)


def allowed_pairs(segment_ids):
    index = jnp.arange(segment_ids.shape[0], dtype=jnp.int32)
    return (segment_ids[:, None] == segment_ids[None, :]) & (index[None, :] <= index[:, None])


def rms_scale(values):
    return lax.rsqrt(jnp.mean(values * values, axis=-1, keepdims=True) + EPS)


def norm_back(values, inv_root, gain, grads):
    normed = values * inv_root
    scaled = grads * gain
    result = inv_root * (scaled - normed * jnp.mean(scaled * normed, axis=-1, keepdims=True))
    return (result, jnp.sum(grads * normed, axis=0))


def matmul(left, right):
    return jnp.dot(left, right, preferred_element_type=jnp.float32)


def head_scores(query_head, key_head, allowed, scale_factor):
    scores = matmul(query_head, key_head.T) * scale_factor
    return jnp.where(allowed, scores, -1e30)


def head_forward(inputs, key_heads, value_heads, allowed, scale_factor):
    query_head, kv_slot = inputs
    scores = head_scores(query_head, key_heads[kv_slot], allowed, scale_factor)
    peak = jnp.max(scores, axis=-1, keepdims=True)
    expo = jnp.exp(scores - peak)
    total = jnp.sum(expo, axis=-1, keepdims=True)
    probs = expo / total
    mixed = matmul(probs.astype(jnp.bfloat16), value_heads[kv_slot])
    return (mixed, (peak + jnp.log(total))[:, 0])


def head_backward(inputs, key_heads, value_heads, allowed, scale_factor):
    query_head, kv_slot, grad_head, log_total = inputs
    key_head = key_heads[kv_slot]
    value_head = value_heads[kv_slot]
    scores = head_scores(query_head, key_head, allowed, scale_factor)
    probs = jnp.exp(scores - log_total[:, None])
    prob_grad = matmul(grad_head, value_head.T)
    value_grad = matmul(probs.astype(jnp.bfloat16).T, grad_head)
    inner = jnp.sum(probs * prob_grad, axis=-1, keepdims=True)
    score_grad = (probs * (prob_grad - inner)).astype(jnp.bfloat16)
    query_grad = matmul(score_grad, key_head) * scale_factor
    key_grad = matmul(score_grad.T, query_head) * scale_factor
    return (query_grad, key_grad, value_grad)


def gather_rows(parts):
    widths = [part.shape[1] for part in parts]
    packed = lax.all_gather(jnp.concatenate(parts, axis=1), "row", axis=0, tiled=True)
    pieces = []
    offset = 0
    for width in widths:
        pieces.append(packed[:, offset : offset + width])
        offset += width
    return pieces


def scatter_rows(parts):
    columns = [part.reshape(part.shape[0], -1).astype(jnp.bfloat16) for part in parts]
    widths = [column.shape[1] for column in columns]
    packed = lax.psum_scatter(
        jnp.concatenate(columns, axis=1), "row", scatter_dimension=0, tiled=True
    ).astype(jnp.float32)
    pieces = []
    offset = 0
    for part, width in zip(parts, widths):
        piece = packed[:, offset : offset + width]
        pieces.append(piece.reshape(-1) if part.ndim == 1 else piece)
        offset += width
    return pieces


def body(
    tokens,
    cotangent,
    destination,
    segment_ids,
    attn_gain,
    w_query,
    w_key,
    w_value,
    w_output,
    ffn_gain,
    w_gate,
    w_up,
    w_down,
):
    row_count = tokens.shape[0]
    quarter = tokens.shape[1]
    col_start = lax.axis_index("col") * quarter
    group_size = HEADS // KV
    send_order = jnp.argsort(destination)
    slot_ids = destination[send_order] % row_count
    arrived_rows, arrived_grads, arrived_slots = (
        lax.all_to_all(tokens[send_order], "row", split_axis=0, concat_axis=0, tiled=True),
        lax.all_to_all(cotangent[send_order], "row", split_axis=0, concat_axis=0, tiled=True),
        lax.all_to_all(slot_ids, "row", split_axis=0, concat_axis=0, tiled=True),
    )
    placing = jnp.argsort(arrived_slots)
    full_rows, full_grads = (
        lax.all_gather(arrived_rows[placing], "col", axis=1, tiled=True),
        lax.all_gather(arrived_grads[placing], "col", axis=1, tiled=True),
    )
    query_w, key_w, value_w, output_w = gather_rows([w_query, w_key, w_value, w_output])
    cosine, sine = rope_tables(positions_of(segment_ids))
    allowed = allowed_pairs(segment_ids)
    rows_wide = full_rows.astype(jnp.float32)
    inv_one = rms_scale(rows_wide)
    normed_one = (rows_wide * inv_one * attn_gain).astype(jnp.bfloat16)
    query = matmul(normed_one, query_w)
    key_raw = matmul(normed_one, key_w)
    value_raw = matmul(normed_one, value_w)
    query_heads_count = query.shape[1] // HD
    kv_count = key_raw.shape[1] // HD
    query_rot = (
        rotate(query.reshape(row_count, query_heads_count, HD), cosine, sine)
        .astype(jnp.bfloat16)
        .transpose(1, 0, 2)
    )
    key_rot = (
        rotate(key_raw.reshape(row_count, kv_count, HD), cosine, sine)
        .astype(jnp.bfloat16)
        .transpose(1, 0, 2)
    )
    value_heads = value_raw.astype(jnp.bfloat16).reshape(row_count, kv_count, HD).transpose(1, 0, 2)
    kv_slots = jnp.arange(query_heads_count, dtype=jnp.int32) // group_size
    scale_factor = HD ** (-0.5)
    mixed_heads, log_totals = lax.map(
        partial(
            head_forward,
            key_heads=key_rot,
            value_heads=value_heads,
            allowed=allowed,
            scale_factor=scale_factor,
        ),
        (query_rot, kv_slots),
    )
    mixed = (
        mixed_heads.transpose(1, 0, 2)
        .reshape(row_count, query_heads_count * HD)
        .astype(jnp.bfloat16)
    )
    attn_terms = matmul(mixed, output_w.T)
    attn_full = lax.psum(attn_terms, "col")
    resid = rows_wide + attn_full
    inv_two = rms_scale(resid)
    normed_two = (resid * inv_two * ffn_gain).astype(jnp.bfloat16)
    resid_part = lax.dynamic_slice_in_dim(resid, col_start, quarter, 1)
    gate_w, up_w, down_w = gather_rows([w_gate, w_up, w_down])
    gate = matmul(normed_two, gate_w)
    upper = matmul(normed_two, up_w)
    sigmoid_gate = jax.nn.sigmoid(gate)
    activ = (gate * sigmoid_gate * upper).astype(jnp.bfloat16)
    ffn_share = lax.psum_scatter(
        matmul(activ, down_w.T).astype(jnp.bfloat16), "col", scatter_dimension=1, tiled=True
    ).astype(jnp.float32)
    output_share = (resid_part + ffn_share).astype(jnp.bfloat16)
    down_weight_grad = matmul(full_grads.T, activ)
    act_grad = matmul(full_grads, down_w)
    gate_grad = (act_grad * upper * sigmoid_gate * (1.0 + gate * (1.0 - sigmoid_gate))).astype(
        jnp.bfloat16
    )
    up_grad = (act_grad * gate * sigmoid_gate).astype(jnp.bfloat16)
    gate_weight_grad = matmul(normed_two.T, gate_grad)
    up_weight_grad = matmul(normed_two.T, up_grad)
    normed_terms_two = matmul(gate_grad, gate_w.T) + matmul(up_grad, up_w.T)
    normed_grad_two = lax.psum(normed_terms_two, "col")
    resid_norm_grad, ffn_gain_grad = norm_back(resid, inv_two, ffn_gain, normed_grad_two)
    resid_grad = full_grads.astype(jnp.float32) + resid_norm_grad
    attn_grad_low = resid_grad.astype(jnp.bfloat16)
    output_weight_grad = matmul(attn_grad_low.T, mixed)
    mixed_grad = matmul(attn_grad_low, output_w).astype(jnp.bfloat16)
    mixed_grad_heads = mixed_grad.reshape(row_count, query_heads_count, HD).transpose(1, 0, 2)
    query_grads, key_grads, value_grads = lax.map(
        partial(
            head_backward,
            key_heads=key_rot,
            value_heads=value_heads,
            allowed=allowed,
            scale_factor=scale_factor,
        ),
        (query_rot, kv_slots, mixed_grad_heads, log_totals),
    )
    query_grad = (
        rotate_back(query_grads.transpose(1, 0, 2), cosine, sine)
        .reshape(row_count, query_heads_count * HD)
        .astype(jnp.bfloat16)
    )
    key_sum = key_grads.reshape(kv_count, group_size, row_count, HD).sum(axis=1).transpose(1, 0, 2)
    key_grad = (
        rotate_back(key_sum, cosine, sine).reshape(row_count, kv_count * HD).astype(jnp.bfloat16)
    )
    value_sum = (
        value_grads.reshape(kv_count, group_size, row_count, HD).sum(axis=1).transpose(1, 0, 2)
    )
    value_grad = value_sum.reshape(row_count, kv_count * HD).astype(jnp.bfloat16)
    query_weight_grad = matmul(normed_one.T, query_grad)
    key_weight_grad = matmul(normed_one.T, key_grad)
    value_weight_grad = matmul(normed_one.T, value_grad)
    normed_terms_one = (
        matmul(query_grad, query_w.T) + matmul(key_grad, key_w.T) + matmul(value_grad, value_w.T)
    )
    normed_grad_one = lax.psum(normed_terms_one.astype(jnp.bfloat16), "col").astype(jnp.float32)
    rows_norm_grad, attn_gain_grad = norm_back(rows_wide, inv_one, attn_gain, normed_grad_one)
    rows_grad = resid_grad + rows_norm_grad
    input_share = lax.dynamic_slice_in_dim(rows_grad, col_start, quarter, 1).astype(jnp.bfloat16)
    (
        query_result,
        key_result,
        value_result,
        output_result,
        gate_result,
        up_result,
        down_result,
        attn_gain_result,
        ffn_gain_result,
    ) = scatter_rows(
        [
            query_weight_grad,
            key_weight_grad,
            value_weight_grad,
            output_weight_grad,
            gate_weight_grad,
            up_weight_grad,
            down_weight_grad,
            attn_gain_grad,
            ffn_gain_grad,
        ]
    )
    back_rows, back_grads = (
        lax.all_to_all(output_share[arrived_slots], "row", split_axis=0, concat_axis=0, tiled=True),
        lax.all_to_all(input_share[arrived_slots], "row", split_axis=0, concat_axis=0, tiled=True),
    )
    restore = jnp.argsort(send_order)
    return (
        back_rows[restore],
        back_grads[restore],
        attn_gain_result,
        query_result,
        key_result,
        value_result,
        output_result,
        ffn_gain_result,
        gate_result,
        up_result,
        down_result,
    )

def solution(mesh):
    placed = (
        P("row", "col"),
        P("row", "col"),
        P("row"),
        P("row"),
        P(),
        P("row", "col"),
        P("row", "col"),
        P("row", "col"),
        P("row", "col"),
        P(),
        P("row", "col"),
        P("row", "col"),
        P("row", "col"),
    )
    return jax.shard_map(
        body,
        mesh=mesh,
        in_specs=placed,
        out_specs=(
            P("row", "col"),
            P("row", "col"),
            P("row"),
            P("row", "col"),
            P("row", "col"),
            P("row", "col"),
            P("row", "col"),
            P("row"),
            P("row", "col"),
            P("row", "col"),
            P("row", "col"),
        ),
        check_vma=False,
    )
```

```python
from functools import partial

import jax
import jax.numpy as jnp
from jax import lax
from jax.experimental import pallas as pl
from jax.experimental.pallas import tpu as pltpu
from jax.sharding import PartitionSpec as P

HEADS = 32
KV = 4
HD = 64


EPS = 1e-05
ROPE_BASE = 10000.0


def rope_tables(positions):
    half_width = HD // 2
    freqs = ROPE_BASE ** (-(jnp.arange(half_width, dtype=jnp.float32) * 2.0 / HD))
    angles = positions.astype(jnp.float32)[:, None] * freqs[None, :]
    return (jnp.cos(angles)[:, None, :], jnp.sin(angles)[:, None, :])


def rotate(values, cosine, sine):
    half_width = values.shape[-1] // 2
    first = values[..., :half_width]
    second = values[..., half_width:]
    return jnp.concatenate(
        [first * cosine - second * sine, second * cosine + first * sine], axis=-1
    )


def rotate_back(grads, cosine, sine):
    half_width = grads.shape[-1] // 2
    first = grads[..., :half_width]
    second = grads[..., half_width:]
    return jnp.concatenate(
        [first * cosine + second * sine, second * cosine - first * sine], axis=-1
    )


def positions_of(segment_ids):
    index = jnp.arange(segment_ids.shape[0], dtype=jnp.int32)
    change = jnp.concatenate([jnp.ones((1,), dtype=jnp.bool_), segment_ids[1:] != segment_ids[:-1]])
    starts = jnp.where(change, index, jnp.zeros_like(index))
    return index - lax.cummax(starts, axis=0)


def allowed_pairs(segment_ids):
    index = jnp.arange(segment_ids.shape[0], dtype=jnp.int32)
    return (segment_ids[:, None] == segment_ids[None, :]) & (index[None, :] <= index[:, None])


def rms_scale(values):
    return lax.rsqrt(jnp.mean(values * values, axis=-1, keepdims=True) + EPS)


def norm_back(values, inv_root, gain, grads):
    normed = values * inv_root
    scaled = grads * gain
    result = inv_root * (scaled - normed * jnp.mean(scaled * normed, axis=-1, keepdims=True))
    return (result, jnp.sum(grads * normed, axis=0))


def matmul(left, right):
    return jnp.dot(left, right, preferred_element_type=jnp.float32)


def head_scores(query_head, key_head, allowed, scale_factor):
    scores = matmul(query_head, key_head.T) * scale_factor
    return jnp.where(allowed, scores, -1e30)


def head_forward(inputs, key_heads, value_heads, allowed, scale_factor):
    query_head, kv_slot = inputs
    scores = head_scores(query_head, key_heads[kv_slot], allowed, scale_factor)
    peak = jnp.max(scores, axis=-1, keepdims=True)
    expo = jnp.exp(scores - peak)
    total = jnp.sum(expo, axis=-1, keepdims=True)
    probs = expo / total
    mixed = matmul(probs.astype(jnp.bfloat16), value_heads[kv_slot])
    return (mixed, (peak + jnp.log(total))[:, 0])


def head_backward(inputs, key_heads, value_heads, allowed, scale_factor):
    query_head, kv_slot, grad_head, log_total = inputs
    key_head = key_heads[kv_slot]
    value_head = value_heads[kv_slot]
    scores = head_scores(query_head, key_head, allowed, scale_factor)
    probs = jnp.exp(scores - log_total[:, None])
    prob_grad = matmul(grad_head, value_head.T)
    value_grad = matmul(probs.astype(jnp.bfloat16).T, grad_head)
    inner = jnp.sum(probs * prob_grad, axis=-1, keepdims=True)
    score_grad = (probs * (prob_grad - inner)).astype(jnp.bfloat16)
    query_grad = matmul(score_grad, key_head) * scale_factor
    key_grad = matmul(score_grad.T, query_head) * scale_factor
    return (query_grad, key_grad, value_grad)


GRAD_BLOCK = 128


def split_columns(packed, widths):
    pieces = []
    offset = 0
    for width in widths:
        pieces.append(packed[:, offset : offset + width])
        offset += width
    return pieces


def gather_rows(parts):
    return lax.all_gather(jnp.concatenate(parts, axis=1), "row", axis=0, tiled=True)


def grad_block_kernel(select_ref, left_ref, right_ref, tail_ref, out_ref):
    step = pl.program_id(0)
    last = pl.num_programs(0) - 1

    @pl.when(step < last)
    def _():
        out_ref[...] = jnp.dot(
            left_ref[0], right_ref[...], preferred_element_type=jnp.float32
        ).astype(out_ref.dtype)

    @pl.when(step == last)
    def _():
        out_ref[...] = tail_ref[...]


def packed_weight_grads(lefts, segments, tail):
    left_stack = jnp.stack([left.T for left in lefts])
    right = jnp.concatenate([seg for _, seg in segments], axis=1)
    column_owner = []
    for index, seg in segments:
        column_owner += [index] * seg.shape[1]
    assert len(column_owner) % GRAD_BLOCK == 0
    select = column_owner[::GRAD_BLOCK]
    assert column_owner == [owner for owner in select for _ in range(GRAD_BLOCK)]
    right_blocks = len(select)
    select.append(select[-1])
    features, tokens = left_stack.shape[1], left_stack.shape[2]
    total = right.shape[1] + GRAD_BLOCK
    return pl.pallas_call(
        grad_block_kernel,
        out_shape=jax.ShapeDtypeStruct((features, total), jnp.bfloat16),
        grid_spec=pltpu.PrefetchScalarGridSpec(
            num_scalar_prefetch=1,
            grid=(len(select),),
            in_specs=[
                pl.BlockSpec((1, features, tokens), lambda j, sel: (sel[j], 0, 0)),
                pl.BlockSpec(
                    (tokens, GRAD_BLOCK), lambda j, sel: (0, jnp.minimum(j, right_blocks - 1))
                ),
                pl.BlockSpec((features, GRAD_BLOCK), lambda j, sel: (0, 0)),
            ],
            out_specs=pl.BlockSpec((features, GRAD_BLOCK), lambda j, sel: (0, j)),
        ),
    )(jnp.asarray(select, dtype=jnp.int32), left_stack, right, tail)


def body(
    tokens,
    cotangent,
    destination,
    segment_ids,
    attn_gain,
    w_query,
    w_key,
    w_value,
    w_output,
    ffn_gain,
    w_gate,
    w_up,
    w_down,
):
    row_count = tokens.shape[0]
    quarter = tokens.shape[1]
    col_start = lax.axis_index("col") * quarter
    group_size = HEADS // KV
    send_order = jnp.argsort(destination)
    slot_ids = destination[send_order] % row_count
    arrived_pair, arrived_slots = (
        lax.all_to_all(
            jnp.stack([tokens, cotangent])[:, send_order], "row", split_axis=1, concat_axis=1, tiled=True
        ),
        lax.all_to_all(slot_ids, "row", split_axis=0, concat_axis=0, tiled=True),
    )
    placing = jnp.argsort(arrived_slots)
    full_pair = lax.all_gather(arrived_pair[:, placing], "col", axis=2, tiled=True)
    full_rows, full_grads = full_pair[0], full_pair[1]
    attn_widths = [w_query.shape[1], w_key.shape[1], w_value.shape[1], w_output.shape[1]]
    ffn_widths = [w_gate.shape[1], w_up.shape[1], w_down.shape[1]]
    attn_packed = gather_rows([w_query, w_key, w_value, w_output])
    ffn_packed = gather_rows([w_gate, w_up, w_down])
    query_w, key_w, value_w, output_w = split_columns(attn_packed, attn_widths)
    cosine, sine = rope_tables(positions_of(segment_ids))
    allowed = allowed_pairs(segment_ids)
    rows_wide = full_rows.astype(jnp.float32)
    inv_one = rms_scale(rows_wide)
    normed_one = (rows_wide * inv_one * attn_gain).astype(jnp.bfloat16)
    query = matmul(normed_one, query_w)
    key_raw = matmul(normed_one, key_w)
    value_raw = matmul(normed_one, value_w)
    query_heads_count = query.shape[1] // HD
    kv_count = key_raw.shape[1] // HD
    query_rot = (
        rotate(query.reshape(row_count, query_heads_count, HD), cosine, sine)
        .astype(jnp.bfloat16)
        .transpose(1, 0, 2)
    )
    key_rot = (
        rotate(key_raw.reshape(row_count, kv_count, HD), cosine, sine)
        .astype(jnp.bfloat16)
        .transpose(1, 0, 2)
    )
    value_heads = value_raw.astype(jnp.bfloat16).reshape(row_count, kv_count, HD).transpose(1, 0, 2)
    kv_slots = jnp.arange(query_heads_count, dtype=jnp.int32) // group_size
    scale_factor = HD ** (-0.5)
    mixed_heads, log_totals = lax.map(
        partial(
            head_forward,
            key_heads=key_rot,
            value_heads=value_heads,
            allowed=allowed,
            scale_factor=scale_factor,
        ),
        (query_rot, kv_slots),
    )
    mixed = (
        mixed_heads.transpose(1, 0, 2)
        .reshape(row_count, query_heads_count * HD)
        .astype(jnp.bfloat16)
    )
    attn_terms = matmul(mixed, output_w.T)
    attn_terms, ffn_packed = lax.optimization_barrier((attn_terms, ffn_packed))
    attn_full = lax.psum(attn_terms, "col")
    resid = rows_wide + attn_full
    inv_two = rms_scale(resid)
    normed_two = (resid * inv_two * ffn_gain).astype(jnp.bfloat16)
    resid_part = lax.dynamic_slice_in_dim(resid, col_start, quarter, 1)
    gate_w, up_w, down_w = split_columns(ffn_packed, ffn_widths)
    gate = matmul(normed_two, gate_w)
    upper = matmul(normed_two, up_w)
    sigmoid_gate = jax.nn.sigmoid(gate)
    activ = (gate * sigmoid_gate * upper).astype(jnp.bfloat16)
    ffn_share = lax.psum_scatter(
        matmul(activ, down_w.T).astype(jnp.bfloat16), "col", scatter_dimension=1, tiled=True
    ).astype(jnp.float32)
    output_share = (resid_part + ffn_share).astype(jnp.bfloat16)
    act_grad = matmul(full_grads, down_w)
    gate_grad = (act_grad * upper * sigmoid_gate * (1.0 + gate * (1.0 - sigmoid_gate))).astype(
        jnp.bfloat16
    )
    up_grad = (act_grad * gate * sigmoid_gate).astype(jnp.bfloat16)
    normed_terms_two = matmul(gate_grad, gate_w.T) + matmul(up_grad, up_w.T)
    normed_grad_two = lax.psum(normed_terms_two, "col")
    resid_norm_grad, ffn_gain_grad = norm_back(resid, inv_two, ffn_gain, normed_grad_two)
    resid_grad = full_grads.astype(jnp.float32) + resid_norm_grad
    attn_grad_low = resid_grad.astype(jnp.bfloat16)
    mixed_grad = matmul(attn_grad_low, output_w).astype(jnp.bfloat16)
    mixed_grad_heads = mixed_grad.reshape(row_count, query_heads_count, HD).transpose(1, 0, 2)
    query_grads, key_grads, value_grads = lax.map(
        partial(
            head_backward,
            key_heads=key_rot,
            value_heads=value_heads,
            allowed=allowed,
            scale_factor=scale_factor,
        ),
        (query_rot, kv_slots, mixed_grad_heads, log_totals),
    )
    query_grad = (
        rotate_back(query_grads.transpose(1, 0, 2), cosine, sine)
        .reshape(row_count, query_heads_count * HD)
        .astype(jnp.bfloat16)
    )
    key_sum = key_grads.reshape(kv_count, group_size, row_count, HD).sum(axis=1).transpose(1, 0, 2)
    key_grad = (
        rotate_back(key_sum, cosine, sine).reshape(row_count, kv_count * HD).astype(jnp.bfloat16)
    )
    value_sum = (
        value_grads.reshape(kv_count, group_size, row_count, HD).sum(axis=1).transpose(1, 0, 2)
    )
    value_grad = value_sum.reshape(row_count, kv_count * HD).astype(jnp.bfloat16)
    normed_terms_one = (
        matmul(query_grad, query_w.T) + matmul(key_grad, key_w.T) + matmul(value_grad, value_w.T)
    )
    normed_grad_one = lax.psum(normed_terms_one.astype(jnp.bfloat16), "col").astype(jnp.float32)
    rows_norm_grad, attn_gain_grad = norm_back(rows_wide, inv_one, attn_gain, normed_grad_one)
    rows_grad = resid_grad + rows_norm_grad
    input_share = lax.dynamic_slice_in_dim(rows_grad, col_start, quarter, 1).astype(jnp.bfloat16)
    gain_tail = jnp.concatenate(
        [
            attn_gain_grad[:, None],
            ffn_gain_grad[:, None],
            jnp.zeros((attn_gain_grad.shape[0], GRAD_BLOCK - 2), jnp.float32),
        ],
        axis=1,
    ).astype(jnp.bfloat16)
    grads_packed = packed_weight_grads(
        [normed_one, attn_grad_low, normed_two, full_grads],
        [
            (0, query_grad),
            (0, key_grad),
            (0, value_grad),
            (1, mixed),
            (2, gate_grad),
            (2, up_grad),
            (3, activ),
        ],
        gain_tail,
    )
    grads_local = lax.psum_scatter(grads_packed, "row", scatter_dimension=0, tiled=True).astype(
        jnp.float32
    )
    (
        query_result,
        key_result,
        value_result,
        output_result,
        gate_result,
        up_result,
        down_result,
        attn_gain_result,
        ffn_gain_result,
    ) = split_columns(grads_local, attn_widths + ffn_widths + [1, 1])
    attn_gain_result = attn_gain_result.reshape(-1)
    ffn_gain_result = ffn_gain_result.reshape(-1)
    back_pair = lax.all_to_all(
        jnp.stack([output_share, input_share])[:, arrived_slots],
        "row",
        split_axis=1,
        concat_axis=1,
        tiled=True,
    )
    back_rows, back_grads = back_pair[0], back_pair[1]
    restore = jnp.argsort(send_order)
    return (
        back_rows[restore],
        back_grads[restore],
        attn_gain_result,
        query_result,
        key_result,
        value_result,
        output_result,
        ffn_gain_result,
        gate_result,
        up_result,
        down_result,
    )

def solution(mesh):
    placed = (
        P("row", "col"),
        P("row", "col"),
        P("row"),
        P("row"),
        P(),
        P("row", "col"),
        P("row", "col"),
        P("row", "col"),
        P("row", "col"),
        P(),
        P("row", "col"),
        P("row", "col"),
        P("row", "col"),
    )
    return jax.shard_map(
        body,
        mesh=mesh,
        in_specs=placed,
        out_specs=(
            P("row", "col"),
            P("row", "col"),
            P("row"),
            P("row", "col"),
            P("row", "col"),
            P("row", "col"),
            P("row", "col"),
            P("row"),
            P("row", "col"),
            P("row", "col"),
            P("row", "col"),
        ),
        check_vma=False,
    )
```

```python
from functools import partial

import jax
import jax.numpy as jnp
from jax import lax
from jax.experimental import pallas as pl
from jax.experimental.pallas import tpu as pltpu
from jax.sharding import PartitionSpec as P

HEADS = 32
KV = 4
HD = 64


EPS = 1e-05
ROPE_BASE = 10000.0


def rope_tables(positions):
    half_width = HD // 2
    freqs = ROPE_BASE ** (-(jnp.arange(half_width, dtype=jnp.float32) * 2.0 / HD))
    angles = positions.astype(jnp.float32)[:, None] * freqs[None, :]
    return (jnp.cos(angles)[:, None, :], jnp.sin(angles)[:, None, :])


def rotate(values, cosine, sine):
    half_width = values.shape[-1] // 2
    first = values[..., :half_width]
    second = values[..., half_width:]
    return jnp.concatenate(
        [first * cosine - second * sine, second * cosine + first * sine], axis=-1
    )


def rotate_back(grads, cosine, sine):
    half_width = grads.shape[-1] // 2
    first = grads[..., :half_width]
    second = grads[..., half_width:]
    return jnp.concatenate(
        [first * cosine + second * sine, second * cosine - first * sine], axis=-1
    )


def positions_of(segment_ids):
    index = jnp.arange(segment_ids.shape[0], dtype=jnp.int32)
    change = jnp.concatenate([jnp.ones((1,), dtype=jnp.bool_), segment_ids[1:] != segment_ids[:-1]])
    starts = jnp.where(change, index, jnp.zeros_like(index))
    return index - lax.cummax(starts, axis=0)


def allowed_pairs(segment_ids):
    index = jnp.arange(segment_ids.shape[0], dtype=jnp.int32)
    return (segment_ids[:, None] == segment_ids[None, :]) & (index[None, :] <= index[:, None])


def rms_scale(values):
    return lax.rsqrt(jnp.mean(values * values, axis=-1, keepdims=True) + EPS)


def norm_back(values, inv_root, gain, grads):
    normed = values * inv_root
    scaled = grads * gain
    result = inv_root * (scaled - normed * jnp.mean(scaled * normed, axis=-1, keepdims=True))
    return (result, jnp.sum(grads * normed, axis=0))


def matmul(left, right):
    return jnp.dot(left, right, preferred_element_type=jnp.float32)


def head_scores(query_head, key_head, allowed, scale_factor):
    scores = matmul(query_head, key_head.T) * scale_factor
    return jnp.where(allowed, scores, -1e30)


def head_forward(inputs, key_heads, value_heads, allowed, scale_factor):
    query_head, kv_slot = inputs
    scores = head_scores(query_head, key_heads[kv_slot], allowed, scale_factor)
    peak = jnp.max(scores, axis=-1, keepdims=True)
    expo = jnp.exp(scores - peak)
    total = jnp.sum(expo, axis=-1, keepdims=True)
    probs = expo / total
    mixed = matmul(probs.astype(jnp.bfloat16), value_heads[kv_slot])
    return (mixed, (peak + jnp.log(total))[:, 0])


def head_backward(inputs, key_heads, value_heads, allowed, scale_factor):
    query_head, kv_slot, grad_head, log_total = inputs
    key_head = key_heads[kv_slot]
    value_head = value_heads[kv_slot]
    scores = head_scores(query_head, key_head, allowed, scale_factor)
    probs = jnp.exp(scores - log_total[:, None])
    prob_grad = matmul(grad_head, value_head.T)
    value_grad = matmul(probs.astype(jnp.bfloat16).T, grad_head)
    inner = jnp.sum(probs * prob_grad, axis=-1, keepdims=True)
    score_grad = (probs * (prob_grad - inner)).astype(jnp.bfloat16)
    query_grad = matmul(score_grad, key_head) * scale_factor
    key_grad = matmul(score_grad.T, query_head) * scale_factor
    return (query_grad, key_grad, value_grad)


GRAD_BLOCK = 128


def split_columns(packed, widths):
    pieces = []
    offset = 0
    for width in widths:
        pieces.append(packed[:, offset : offset + width])
        offset += width
    return pieces


def gather_rows(parts):
    return lax.all_gather(jnp.concatenate(parts, axis=1), "row", axis=0, tiled=True)


def grad_block_kernel(select_ref, left_ref, right_ref, tail_ref, out_ref):
    step = pl.program_id(0)
    last = pl.num_programs(0) - 1

    @pl.when(step < last)
    def _():
        out_ref[...] = jnp.dot(
            left_ref[0], right_ref[...], preferred_element_type=jnp.float32
        ).astype(out_ref.dtype)

    @pl.when(step == last)
    def _():
        out_ref[...] = tail_ref[...]


def gain_tail_of(gain_grad):
    return jnp.concatenate(
        [gain_grad[:, None], jnp.zeros((gain_grad.shape[0], GRAD_BLOCK - 1), jnp.float32)], axis=1
    ).astype(jnp.bfloat16)


def packed_weight_grads(lefts, segments, tail):
    left_stack = jnp.stack([left.T for left in lefts])
    right = jnp.concatenate([seg for _, seg in segments], axis=1)
    column_owner = []
    for index, seg in segments:
        column_owner += [index] * seg.shape[1]
    assert len(column_owner) % GRAD_BLOCK == 0
    select = column_owner[::GRAD_BLOCK]
    assert column_owner == [owner for owner in select for _ in range(GRAD_BLOCK)]
    right_blocks = len(select)
    select.append(select[-1])
    features, tokens = left_stack.shape[1], left_stack.shape[2]
    total = right.shape[1] + GRAD_BLOCK
    return pl.pallas_call(
        grad_block_kernel,
        out_shape=jax.ShapeDtypeStruct((features, total), jnp.bfloat16),
        grid_spec=pltpu.PrefetchScalarGridSpec(
            num_scalar_prefetch=1,
            grid=(len(select),),
            in_specs=[
                pl.BlockSpec((1, features, tokens), lambda j, sel: (sel[j], 0, 0)),
                pl.BlockSpec(
                    (tokens, GRAD_BLOCK), lambda j, sel: (0, jnp.minimum(j, right_blocks - 1))
                ),
                pl.BlockSpec((features, GRAD_BLOCK), lambda j, sel: (0, 0)),
            ],
            out_specs=pl.BlockSpec((features, GRAD_BLOCK), lambda j, sel: (0, j)),
        ),
    )(jnp.asarray(select, dtype=jnp.int32), left_stack, right, tail)


def body(
    tokens,
    cotangent,
    destination,
    segment_ids,
    attn_gain,
    w_query,
    w_key,
    w_value,
    w_output,
    ffn_gain,
    w_gate,
    w_up,
    w_down,
):
    row_count = tokens.shape[0]
    quarter = tokens.shape[1]
    col_start = lax.axis_index("col") * quarter
    group_size = HEADS // KV
    send_order = jnp.argsort(destination)
    slot_ids = destination[send_order] % row_count
    arrived_pair, arrived_slots = (
        lax.all_to_all(
            jnp.stack([tokens, cotangent])[:, send_order], "row", split_axis=1, concat_axis=1, tiled=True
        ),
        lax.all_to_all(slot_ids, "row", split_axis=0, concat_axis=0, tiled=True),
    )
    placing = jnp.argsort(arrived_slots)
    attn_widths = [w_query.shape[1], w_key.shape[1], w_value.shape[1], w_output.shape[1]]
    ffn_widths = [w_gate.shape[1], w_up.shape[1], w_down.shape[1]]
    attn_packed = gather_rows([w_query, w_key, w_value, w_output])
    placed_pair, attn_packed = lax.optimization_barrier((arrived_pair[:, placing], attn_packed))
    full_pair = lax.all_gather(placed_pair, "col", axis=2, tiled=True)
    ffn_local, full_pair = lax.optimization_barrier(
        (jnp.concatenate([w_gate, w_up, w_down], axis=1), full_pair)
    )
    ffn_packed = lax.all_gather(ffn_local, "row", axis=0, tiled=True)
    full_rows, full_grads = full_pair[0], full_pair[1]
    query_w, key_w, value_w, output_w = split_columns(attn_packed, attn_widths)
    cosine, sine = rope_tables(positions_of(segment_ids))
    allowed = allowed_pairs(segment_ids)
    rows_wide = full_rows.astype(jnp.float32)
    inv_one = rms_scale(rows_wide)
    normed_one = (rows_wide * inv_one * attn_gain).astype(jnp.bfloat16)
    query = matmul(normed_one, query_w)
    key_raw = matmul(normed_one, key_w)
    value_raw = matmul(normed_one, value_w)
    query_heads_count = query.shape[1] // HD
    kv_count = key_raw.shape[1] // HD
    query_rot = (
        rotate(query.reshape(row_count, query_heads_count, HD), cosine, sine)
        .astype(jnp.bfloat16)
        .transpose(1, 0, 2)
    )
    key_rot = (
        rotate(key_raw.reshape(row_count, kv_count, HD), cosine, sine)
        .astype(jnp.bfloat16)
        .transpose(1, 0, 2)
    )
    value_heads = value_raw.astype(jnp.bfloat16).reshape(row_count, kv_count, HD).transpose(1, 0, 2)
    kv_slots = jnp.arange(query_heads_count, dtype=jnp.int32) // group_size
    scale_factor = HD ** (-0.5)
    mixed_heads, log_totals = lax.map(
        partial(
            head_forward,
            key_heads=key_rot,
            value_heads=value_heads,
            allowed=allowed,
            scale_factor=scale_factor,
        ),
        (query_rot, kv_slots),
    )
    mixed = (
        mixed_heads.transpose(1, 0, 2)
        .reshape(row_count, query_heads_count * HD)
        .astype(jnp.bfloat16)
    )
    attn_terms = matmul(mixed, output_w.T)
    attn_terms, ffn_packed = lax.optimization_barrier((attn_terms, ffn_packed))
    attn_full = lax.psum(attn_terms.astype(jnp.bfloat16), "col").astype(jnp.float32)
    resid = rows_wide + attn_full
    inv_two = rms_scale(resid)
    normed_two = (resid * inv_two * ffn_gain).astype(jnp.bfloat16)
    resid_part = lax.dynamic_slice_in_dim(resid, col_start, quarter, 1)
    gate_w, up_w, down_w = split_columns(ffn_packed, ffn_widths)
    gate = matmul(normed_two, gate_w)
    upper = matmul(normed_two, up_w)
    sigmoid_gate = jax.nn.sigmoid(gate)
    activ = (gate * sigmoid_gate * upper).astype(jnp.bfloat16)
    ffn_share = lax.psum_scatter(
        matmul(activ, down_w.T).astype(jnp.bfloat16), "col", scatter_dimension=1, tiled=True
    ).astype(jnp.float32)
    output_share = (resid_part + ffn_share).astype(jnp.bfloat16)
    act_grad = matmul(full_grads, down_w)
    gate_grad = (act_grad * upper * sigmoid_gate * (1.0 + gate * (1.0 - sigmoid_gate))).astype(
        jnp.bfloat16
    )
    up_grad = (act_grad * gate * sigmoid_gate).astype(jnp.bfloat16)
    normed_terms_two = matmul(gate_grad, gate_w.T) + matmul(up_grad, up_w.T)
    normed_grad_two = lax.psum(normed_terms_two.astype(jnp.bfloat16), "col").astype(jnp.float32)
    resid_norm_grad, ffn_gain_grad = norm_back(resid, inv_two, ffn_gain, normed_grad_two)
    ffn_grads_local = lax.psum_scatter(
        packed_weight_grads(
            [normed_two, full_grads],
            [(0, gate_grad), (0, up_grad), (1, activ)],
            gain_tail_of(ffn_gain_grad),
        ),
        "row",
        scatter_dimension=0,
        tiled=True,
    )
    resid_grad = full_grads.astype(jnp.float32) + resid_norm_grad
    attn_grad_low = resid_grad.astype(jnp.bfloat16)
    mixed_grad = matmul(attn_grad_low, output_w).astype(jnp.bfloat16)
    mixed_grad_heads = mixed_grad.reshape(row_count, query_heads_count, HD).transpose(1, 0, 2)
    query_grads, key_grads, value_grads = lax.map(
        partial(
            head_backward,
            key_heads=key_rot,
            value_heads=value_heads,
            allowed=allowed,
            scale_factor=scale_factor,
        ),
        (query_rot, kv_slots, mixed_grad_heads, log_totals),
    )
    query_grad = (
        rotate_back(query_grads.transpose(1, 0, 2), cosine, sine)
        .reshape(row_count, query_heads_count * HD)
        .astype(jnp.bfloat16)
    )
    key_sum = key_grads.reshape(kv_count, group_size, row_count, HD).sum(axis=1).transpose(1, 0, 2)
    key_grad = (
        rotate_back(key_sum, cosine, sine).reshape(row_count, kv_count * HD).astype(jnp.bfloat16)
    )
    value_sum = (
        value_grads.reshape(kv_count, group_size, row_count, HD).sum(axis=1).transpose(1, 0, 2)
    )
    value_grad = value_sum.reshape(row_count, kv_count * HD).astype(jnp.bfloat16)
    normed_terms_one = (
        matmul(query_grad, query_w.T) + matmul(key_grad, key_w.T) + matmul(value_grad, value_w.T)
    )
    normed_low_one, ffn_grads_local = lax.optimization_barrier(
        (normed_terms_one.astype(jnp.bfloat16), ffn_grads_local)
    )
    normed_grad_one = lax.psum(normed_low_one, "col").astype(jnp.float32)
    rows_norm_grad, attn_gain_grad = norm_back(rows_wide, inv_one, attn_gain, normed_grad_one)
    rows_grad = resid_grad + rows_norm_grad
    input_share = lax.dynamic_slice_in_dim(rows_grad, col_start, quarter, 1).astype(jnp.bfloat16)
    attn_grads_local = lax.psum_scatter(
        packed_weight_grads(
            [normed_one, attn_grad_low],
            [(0, query_grad), (0, key_grad), (0, value_grad), (1, mixed)],
            gain_tail_of(attn_gain_grad),
        ),
        "row",
        scatter_dimension=0,
        tiled=True,
    )
    query_result, key_result, value_result, output_result, attn_gain_result = split_columns(
        attn_grads_local.astype(jnp.float32), attn_widths + [1]
    )
    gate_result, up_result, down_result, ffn_gain_result = split_columns(
        ffn_grads_local.astype(jnp.float32), ffn_widths + [1]
    )
    attn_gain_result = attn_gain_result.reshape(-1)
    ffn_gain_result = ffn_gain_result.reshape(-1)
    back_pair = lax.all_to_all(
        jnp.stack([output_share, input_share])[:, arrived_slots],
        "row",
        split_axis=1,
        concat_axis=1,
        tiled=True,
    )
    back_rows, back_grads = back_pair[0], back_pair[1]
    restore = jnp.argsort(send_order)
    return (
        back_rows[restore],
        back_grads[restore],
        attn_gain_result,
        query_result,
        key_result,
        value_result,
        output_result,
        ffn_gain_result,
        gate_result,
        up_result,
        down_result,
    )

def solution(mesh):
    placed = (
        P("row", "col"),
        P("row", "col"),
        P("row"),
        P("row"),
        P(),
        P("row", "col"),
        P("row", "col"),
        P("row", "col"),
        P("row", "col"),
        P(),
        P("row", "col"),
        P("row", "col"),
        P("row", "col"),
    )
    return jax.shard_map(
        body,
        mesh=mesh,
        in_specs=placed,
        out_specs=(
            P("row", "col"),
            P("row", "col"),
            P("row"),
            P("row", "col"),
            P("row", "col"),
            P("row", "col"),
            P("row", "col"),
            P("row"),
            P("row", "col"),
            P("row", "col"),
            P("row", "col"),
        ),
        check_vma=False,
    )
```

```python
from functools import partial

import jax
import jax.numpy as jnp
from jax import lax
from jax.experimental import pallas as pl
from jax.experimental.pallas import tpu as pltpu
from jax.sharding import PartitionSpec as P

HEADS = 32
KV = 4
HD = 64


EPS = 1e-05
ROPE_BASE = 10000.0


def rope_tables(positions):
    half_width = HD // 2
    freqs = ROPE_BASE ** (-(jnp.arange(half_width, dtype=jnp.float32) * 2.0 / HD))
    angles = positions.astype(jnp.float32)[:, None] * freqs[None, :]
    return (jnp.cos(angles)[:, None, :], jnp.sin(angles)[:, None, :])


def rotate(values, cosine, sine):
    half_width = values.shape[-1] // 2
    first = values[..., :half_width]
    second = values[..., half_width:]
    return jnp.concatenate(
        [first * cosine - second * sine, second * cosine + first * sine], axis=-1
    )


def rotate_back(grads, cosine, sine):
    half_width = grads.shape[-1] // 2
    first = grads[..., :half_width]
    second = grads[..., half_width:]
    return jnp.concatenate(
        [first * cosine + second * sine, second * cosine - first * sine], axis=-1
    )


def positions_of(segment_ids):
    index = jnp.arange(segment_ids.shape[0], dtype=jnp.int32)
    change = jnp.concatenate([jnp.ones((1,), dtype=jnp.bool_), segment_ids[1:] != segment_ids[:-1]])
    starts = jnp.where(change, index, jnp.zeros_like(index))
    return index - lax.cummax(starts, axis=0)


def allowed_pairs(segment_ids):
    index = jnp.arange(segment_ids.shape[0], dtype=jnp.int32)
    return (segment_ids[:, None] == segment_ids[None, :]) & (index[None, :] <= index[:, None])


def rms_scale(values):
    return lax.rsqrt(jnp.mean(values * values, axis=-1, keepdims=True) + EPS)


def norm_back(values, inv_root, gain, grads):
    normed = values * inv_root
    scaled = grads * gain
    result = inv_root * (scaled - normed * jnp.mean(scaled * normed, axis=-1, keepdims=True))
    return (result, jnp.sum(grads * normed, axis=0))


def matmul(left, right):
    return jnp.dot(left, right, preferred_element_type=jnp.float32)


def head_scores(query_head, key_head, allowed, scale_factor):
    scores = matmul(query_head, key_head.T) * scale_factor
    return jnp.where(allowed, scores, -1e30)


def head_forward(inputs, key_heads, value_heads, allowed, scale_factor):
    query_head, kv_slot = inputs
    scores = head_scores(query_head, key_heads[kv_slot], allowed, scale_factor)
    peak = jnp.max(scores, axis=-1, keepdims=True)
    expo = jnp.exp(scores - peak)
    total = jnp.sum(expo, axis=-1, keepdims=True)
    probs = expo / total
    mixed = matmul(probs.astype(jnp.bfloat16), value_heads[kv_slot])
    return (mixed, (peak + jnp.log(total))[:, 0])


def head_backward(inputs, key_heads, value_heads, allowed, scale_factor):
    query_head, kv_slot, grad_head, log_total = inputs
    key_head = key_heads[kv_slot]
    value_head = value_heads[kv_slot]
    scores = head_scores(query_head, key_head, allowed, scale_factor)
    probs = jnp.exp(scores - log_total[:, None])
    prob_grad = matmul(grad_head, value_head.T)
    value_grad = matmul(probs.astype(jnp.bfloat16).T, grad_head)
    inner = jnp.sum(probs * prob_grad, axis=-1, keepdims=True)
    score_grad = (probs * (prob_grad - inner)).astype(jnp.bfloat16)
    query_grad = matmul(score_grad, key_head) * scale_factor
    key_grad = matmul(score_grad.T, query_head) * scale_factor
    return (query_grad, key_grad, value_grad)


GRAD_BLOCK = 128


def split_columns(packed, widths):
    pieces = []
    offset = 0
    for width in widths:
        pieces.append(packed[:, offset : offset + width])
        offset += width
    return pieces


def gather_rows(parts):
    return lax.all_gather(jnp.concatenate(parts, axis=1), "row", axis=0, tiled=True)


def grad_block_kernel(select_ref, left_ref, right_ref, tail_ref, out_ref):
    step = pl.program_id(0)
    last = pl.num_programs(0) - 1

    @pl.when(step < last)
    def _():
        out_ref[...] = jnp.dot(
            left_ref[0], right_ref[...], preferred_element_type=jnp.float32
        ).astype(out_ref.dtype)

    @pl.when(step == last)
    def _():
        out_ref[...] = tail_ref[...]


def grad_plain_kernel(select_ref, left_ref, right_ref, out_ref):
    out_ref[...] = jnp.dot(
        left_ref[0], right_ref[...], preferred_element_type=jnp.float32
    ).astype(out_ref.dtype)


def gain_tail_of(gain_grads):
    columns = [grad[:, None] for grad in gain_grads]
    padding = jnp.zeros((gain_grads[0].shape[0], GRAD_BLOCK - len(columns)), jnp.float32)
    return jnp.concatenate(columns + [padding], axis=1).astype(jnp.bfloat16)


def packed_weight_grads(lefts, segments, tail=None):
    left_stack = jnp.stack([left.T for left in lefts])
    right = jnp.concatenate([seg for _, seg in segments], axis=1)
    column_owner = []
    for index, seg in segments:
        column_owner += [index] * seg.shape[1]
    assert len(column_owner) % GRAD_BLOCK == 0
    select = column_owner[::GRAD_BLOCK]
    assert column_owner == [owner for owner in select for _ in range(GRAD_BLOCK)]
    right_blocks = len(select)
    features, tokens = left_stack.shape[1], left_stack.shape[2]
    in_specs = [
        pl.BlockSpec((1, features, tokens), lambda j, sel: (sel[j], 0, 0)),
        pl.BlockSpec((tokens, GRAD_BLOCK), lambda j, sel: (0, jnp.minimum(j, right_blocks - 1))),
    ]
    operands = [left_stack, right]
    kernel = grad_plain_kernel
    if tail is not None:
        select.append(select[-1])
        in_specs.append(pl.BlockSpec((features, GRAD_BLOCK), lambda j, sel: (0, 0)))
        operands.append(tail)
        kernel = grad_block_kernel
    return pl.pallas_call(
        kernel,
        out_shape=jax.ShapeDtypeStruct((features, len(select) * GRAD_BLOCK), jnp.bfloat16),
        grid_spec=pltpu.PrefetchScalarGridSpec(
            num_scalar_prefetch=1,
            grid=(len(select),),
            in_specs=in_specs,
            out_specs=pl.BlockSpec((features, GRAD_BLOCK), lambda j, sel: (0, j)),
        ),
    )(jnp.asarray(select, dtype=jnp.int32), *operands)


def body(
    tokens,
    cotangent,
    destination,
    segment_ids,
    attn_gain,
    w_query,
    w_key,
    w_value,
    w_output,
    ffn_gain,
    w_gate,
    w_up,
    w_down,
):
    row_count = tokens.shape[0]
    quarter = tokens.shape[1]
    col_start = lax.axis_index("col") * quarter
    group_size = HEADS // KV
    send_order = jnp.argsort(destination)
    slot_ids = destination[send_order] % row_count
    arrived_pair, arrived_slots = (
        lax.all_to_all(
            jnp.stack([tokens, cotangent])[:, send_order], "row", split_axis=1, concat_axis=1, tiled=True
        ),
        lax.all_to_all(slot_ids, "row", split_axis=0, concat_axis=0, tiled=True),
    )
    placing = jnp.argsort(arrived_slots)
    attn_widths = [w_query.shape[1], w_key.shape[1], w_value.shape[1], w_output.shape[1]]
    ffn_widths = [w_gate.shape[1], w_up.shape[1], w_down.shape[1]]
    attn_packed = gather_rows([w_query, w_key, w_value, w_output])
    placed_pair, attn_packed = lax.optimization_barrier((arrived_pair[:, placing], attn_packed))
    full_pair = lax.all_gather(placed_pair, "col", axis=2, tiled=True)
    ffn_local, full_pair = lax.optimization_barrier(
        (jnp.concatenate([w_gate, w_up, w_down], axis=1), full_pair)
    )
    ffn_packed = lax.all_gather(ffn_local, "row", axis=0, tiled=True)
    full_rows, full_grads = full_pair[0], full_pair[1]
    query_w, key_w, value_w, output_w = split_columns(attn_packed, attn_widths)
    cosine, sine = rope_tables(positions_of(segment_ids))
    allowed = allowed_pairs(segment_ids)
    rows_wide = full_rows.astype(jnp.float32)
    inv_one = rms_scale(rows_wide)
    normed_one = (rows_wide * inv_one * attn_gain).astype(jnp.bfloat16)
    query = matmul(normed_one, query_w)
    key_raw = matmul(normed_one, key_w)
    value_raw = matmul(normed_one, value_w)
    query_heads_count = query.shape[1] // HD
    kv_count = key_raw.shape[1] // HD
    query_rot = (
        rotate(query.reshape(row_count, query_heads_count, HD), cosine, sine)
        .astype(jnp.bfloat16)
        .transpose(1, 0, 2)
    )
    key_rot = (
        rotate(key_raw.reshape(row_count, kv_count, HD), cosine, sine)
        .astype(jnp.bfloat16)
        .transpose(1, 0, 2)
    )
    value_heads = value_raw.astype(jnp.bfloat16).reshape(row_count, kv_count, HD).transpose(1, 0, 2)
    kv_slots = jnp.arange(query_heads_count, dtype=jnp.int32) // group_size
    scale_factor = HD ** (-0.5)
    mixed_heads, log_totals = lax.map(
        partial(
            head_forward,
            key_heads=key_rot,
            value_heads=value_heads,
            allowed=allowed,
            scale_factor=scale_factor,
        ),
        (query_rot, kv_slots),
    )
    mixed = (
        mixed_heads.transpose(1, 0, 2)
        .reshape(row_count, query_heads_count * HD)
        .astype(jnp.bfloat16)
    )
    attn_terms = matmul(mixed, output_w.T)
    attn_terms, ffn_packed = lax.optimization_barrier((attn_terms, ffn_packed))
    attn_full = lax.psum(attn_terms.astype(jnp.bfloat16), "col").astype(jnp.float32)
    resid = rows_wide + attn_full
    inv_two = rms_scale(resid)
    normed_two = (resid * inv_two * ffn_gain).astype(jnp.bfloat16)
    resid_part = lax.dynamic_slice_in_dim(resid, col_start, quarter, 1)
    gate_w, up_w, down_w = split_columns(ffn_packed, ffn_widths)
    gate = matmul(normed_two, gate_w)
    upper = matmul(normed_two, up_w)
    sigmoid_gate = jax.nn.sigmoid(gate)
    activ = (gate * sigmoid_gate * upper).astype(jnp.bfloat16)
    ffn_share_low = lax.psum_scatter(
        matmul(activ, down_w.T).astype(jnp.bfloat16), "col", scatter_dimension=1, tiled=True
    )
    act_grad = matmul(full_grads, down_w)
    gate_grad = (act_grad * upper * sigmoid_gate * (1.0 + gate * (1.0 - sigmoid_gate))).astype(
        jnp.bfloat16
    )
    up_grad = (act_grad * gate * sigmoid_gate).astype(jnp.bfloat16)
    normed_terms_two = matmul(gate_grad, gate_w.T) + matmul(up_grad, up_w.T)
    normed_low_two, ffn_share_low = lax.optimization_barrier(
        (normed_terms_two.astype(jnp.bfloat16), ffn_share_low)
    )
    output_share = (resid_part + ffn_share_low.astype(jnp.float32)).astype(jnp.bfloat16)
    normed_grad_two = lax.psum(normed_low_two, "col").astype(jnp.float32)
    ffn_grads_packed = packed_weight_grads(
        [normed_two, full_grads], [(0, gate_grad), (0, up_grad), (1, activ)]
    )
    ffn_grads_packed, normed_grad_two = lax.optimization_barrier(
        (ffn_grads_packed, normed_grad_two)
    )
    resid_norm_grad, ffn_gain_grad = norm_back(resid, inv_two, ffn_gain, normed_grad_two)
    ffn_grads_local = lax.psum_scatter(ffn_grads_packed, "row", scatter_dimension=0, tiled=True)
    resid_grad = full_grads.astype(jnp.float32) + resid_norm_grad
    attn_grad_low = resid_grad.astype(jnp.bfloat16)
    mixed_grad = matmul(attn_grad_low, output_w).astype(jnp.bfloat16)
    mixed_grad_heads = mixed_grad.reshape(row_count, query_heads_count, HD).transpose(1, 0, 2)
    query_grads, key_grads, value_grads = lax.map(
        partial(
            head_backward,
            key_heads=key_rot,
            value_heads=value_heads,
            allowed=allowed,
            scale_factor=scale_factor,
        ),
        (query_rot, kv_slots, mixed_grad_heads, log_totals),
    )
    query_grad = (
        rotate_back(query_grads.transpose(1, 0, 2), cosine, sine)
        .reshape(row_count, query_heads_count * HD)
        .astype(jnp.bfloat16)
    )
    key_sum = key_grads.reshape(kv_count, group_size, row_count, HD).sum(axis=1).transpose(1, 0, 2)
    key_grad = (
        rotate_back(key_sum, cosine, sine).reshape(row_count, kv_count * HD).astype(jnp.bfloat16)
    )
    value_sum = (
        value_grads.reshape(kv_count, group_size, row_count, HD).sum(axis=1).transpose(1, 0, 2)
    )
    value_grad = value_sum.reshape(row_count, kv_count * HD).astype(jnp.bfloat16)
    normed_terms_one = (
        matmul(query_grad, query_w.T) + matmul(key_grad, key_w.T) + matmul(value_grad, value_w.T)
    )
    normed_low_one, ffn_grads_local = lax.optimization_barrier(
        (normed_terms_one.astype(jnp.bfloat16), ffn_grads_local)
    )
    normed_grad_one = lax.psum(normed_low_one, "col").astype(jnp.float32)
    rows_norm_grad, attn_gain_grad = norm_back(rows_wide, inv_one, attn_gain, normed_grad_one)
    rows_grad = resid_grad + rows_norm_grad
    input_share = lax.dynamic_slice_in_dim(rows_grad, col_start, quarter, 1).astype(jnp.bfloat16)
    attn_grads_local = lax.psum_scatter(
        packed_weight_grads(
            [normed_one, attn_grad_low],
            [(0, query_grad), (0, key_grad), (0, value_grad), (1, mixed)],
            gain_tail_of([attn_gain_grad, ffn_gain_grad]),
        ),
        "row",
        scatter_dimension=0,
        tiled=True,
    )
    (
        query_result,
        key_result,
        value_result,
        output_result,
        attn_gain_result,
        ffn_gain_result,
    ) = split_columns(attn_grads_local.astype(jnp.float32), attn_widths + [1, 1])
    gate_result, up_result, down_result = split_columns(
        ffn_grads_local.astype(jnp.float32), ffn_widths
    )
    attn_gain_result = attn_gain_result.reshape(-1)
    ffn_gain_result = ffn_gain_result.reshape(-1)
    back_pair = lax.all_to_all(
        jnp.stack([output_share, input_share])[:, arrived_slots],
        "row",
        split_axis=1,
        concat_axis=1,
        tiled=True,
    )
    back_rows, back_grads = back_pair[0], back_pair[1]
    restore = jnp.argsort(send_order)
    return (
        back_rows[restore],
        back_grads[restore],
        attn_gain_result,
        query_result,
        key_result,
        value_result,
        output_result,
        ffn_gain_result,
        gate_result,
        up_result,
        down_result,
    )

def solution(mesh):
    placed = (
        P("row", "col"),
        P("row", "col"),
        P("row"),
        P("row"),
        P(),
        P("row", "col"),
        P("row", "col"),
        P("row", "col"),
        P("row", "col"),
        P(),
        P("row", "col"),
        P("row", "col"),
        P("row", "col"),
    )
    return jax.shard_map(
        body,
        mesh=mesh,
        in_specs=placed,
        out_specs=(
            P("row", "col"),
            P("row", "col"),
            P("row"),
            P("row", "col"),
            P("row", "col"),
            P("row", "col"),
            P("row", "col"),
            P("row"),
            P("row", "col"),
            P("row", "col"),
            P("row", "col"),
        ),
        check_vma=False,
    )
```

```python
from functools import partial

import jax
import jax.numpy as jnp
from jax import lax
from jax.experimental import pallas as pl
from jax.experimental.pallas import tpu as pltpu
from jax.sharding import PartitionSpec as P

HEADS = 32
KV = 4
HD = 64


EPS = 1e-05
ROPE_BASE = 10000.0


def rope_tables(positions):
    half_width = HD // 2
    freqs = ROPE_BASE ** (-(jnp.arange(half_width, dtype=jnp.float32) * 2.0 / HD))
    angles = positions.astype(jnp.float32)[:, None] * freqs[None, :]
    return (jnp.cos(angles)[:, None, :], jnp.sin(angles)[:, None, :])


def rotate(values, cosine, sine):
    half_width = values.shape[-1] // 2
    first = values[..., :half_width]
    second = values[..., half_width:]
    return jnp.concatenate(
        [first * cosine - second * sine, second * cosine + first * sine], axis=-1
    )


def rotate_back(grads, cosine, sine):
    half_width = grads.shape[-1] // 2
    first = grads[..., :half_width]
    second = grads[..., half_width:]
    return jnp.concatenate(
        [first * cosine + second * sine, second * cosine - first * sine], axis=-1
    )


def positions_of(segment_ids):
    index = jnp.arange(segment_ids.shape[0], dtype=jnp.int32)
    change = jnp.concatenate([jnp.ones((1,), dtype=jnp.bool_), segment_ids[1:] != segment_ids[:-1]])
    starts = jnp.where(change, index, jnp.zeros_like(index))
    return index - lax.cummax(starts, axis=0)


def allowed_pairs(segment_ids):
    index = jnp.arange(segment_ids.shape[0], dtype=jnp.int32)
    return (segment_ids[:, None] == segment_ids[None, :]) & (index[None, :] <= index[:, None])


def rms_scale(values):
    return lax.rsqrt(jnp.mean(values * values, axis=-1, keepdims=True) + EPS)


def norm_back(values, inv_root, gain, grads):
    normed = values * inv_root
    scaled = grads * gain
    result = inv_root * (scaled - normed * jnp.mean(scaled * normed, axis=-1, keepdims=True))
    return (result, jnp.sum(grads * normed, axis=0))


def matmul(left, right):
    return jnp.dot(left, right, preferred_element_type=jnp.float32)


def head_scores(query_head, key_head, allowed, scale_factor):
    scores = matmul(query_head, key_head.T) * scale_factor
    return jnp.where(allowed, scores, -1e30)


def head_forward(inputs, key_heads, value_heads, allowed, scale_factor):
    query_head, kv_slot = inputs
    scores = head_scores(query_head, key_heads[kv_slot], allowed, scale_factor)
    peak = jnp.max(scores, axis=-1, keepdims=True)
    expo = jnp.exp(scores - peak)
    total = jnp.sum(expo, axis=-1, keepdims=True)
    probs = expo / total
    mixed = matmul(probs.astype(jnp.bfloat16), value_heads[kv_slot])
    return (mixed, (peak + jnp.log(total))[:, 0])


def head_backward(inputs, key_heads, value_heads, allowed, scale_factor):
    query_head, kv_slot, grad_head, log_total = inputs
    key_head = key_heads[kv_slot]
    value_head = value_heads[kv_slot]
    scores = head_scores(query_head, key_head, allowed, scale_factor)
    probs = jnp.exp(scores - log_total[:, None])
    prob_grad = matmul(grad_head, value_head.T)
    value_grad = matmul(probs.astype(jnp.bfloat16).T, grad_head)
    inner = jnp.sum(probs * prob_grad, axis=-1, keepdims=True)
    score_grad = (probs * (prob_grad - inner)).astype(jnp.bfloat16)
    query_grad = matmul(score_grad, key_head) * scale_factor
    key_grad = matmul(score_grad.T, query_head) * scale_factor
    return (query_grad, key_grad, value_grad)


GRAD_BLOCK = 128


def split_columns(packed, widths):
    pieces = []
    offset = 0
    for width in widths:
        pieces.append(packed[:, offset : offset + width])
        offset += width
    return pieces


def col_scatter(values):
    count = lax.axis_size("col")
    lead = values.shape[:-1]
    blocks = jnp.moveaxis(values.reshape(*lead, count, values.shape[-1] // count), -2, 0)
    received = lax.all_to_all(blocks, "col", split_axis=0, concat_axis=0, tiled=True)
    return jnp.sum(received.astype(jnp.float32), axis=0)


def col_gather(block):
    count = lax.axis_size("col")
    copies = jnp.broadcast_to(block[None], (count,) + block.shape)
    received = lax.all_to_all(copies, "col", split_axis=0, concat_axis=0, tiled=True)
    return jnp.moveaxis(received, 0, -2).reshape(*block.shape[:-1], count * block.shape[-1])


def col_sum(values):
    return col_gather(col_scatter(values).astype(jnp.bfloat16)).astype(jnp.float32)


def gather_rows(parts):
    return lax.all_gather(jnp.concatenate(parts, axis=1), "row", axis=0, tiled=True)


def grad_block_kernel(select_ref, left_ref, right_ref, tail_ref, out_ref):
    step = pl.program_id(0)
    last = pl.num_programs(0) - 1

    @pl.when(step < last)
    def _():
        out_ref[...] = jnp.dot(
            left_ref[0], right_ref[...], preferred_element_type=jnp.float32
        ).astype(out_ref.dtype)

    @pl.when(step == last)
    def _():
        out_ref[...] = tail_ref[...]


def grad_plain_kernel(select_ref, left_ref, right_ref, out_ref):
    out_ref[...] = jnp.dot(
        left_ref[0], right_ref[...], preferred_element_type=jnp.float32
    ).astype(out_ref.dtype)


def gain_tail_of(gain_grads):
    columns = [grad[:, None] for grad in gain_grads]
    padding = jnp.zeros((gain_grads[0].shape[0], GRAD_BLOCK - len(columns)), jnp.float32)
    return jnp.concatenate(columns + [padding], axis=1).astype(jnp.bfloat16)


def packed_weight_grads(lefts, segments, tail=None):
    left_stack = jnp.stack([left.T for left in lefts])
    right = jnp.concatenate([seg for _, seg in segments], axis=1)
    column_owner = []
    for index, seg in segments:
        column_owner += [index] * seg.shape[1]
    assert len(column_owner) % GRAD_BLOCK == 0
    select = column_owner[::GRAD_BLOCK]
    assert column_owner == [owner for owner in select for _ in range(GRAD_BLOCK)]
    right_blocks = len(select)
    features, tokens = left_stack.shape[1], left_stack.shape[2]
    in_specs = [
        pl.BlockSpec((1, features, tokens), lambda j, sel: (sel[j], 0, 0)),
        pl.BlockSpec((tokens, GRAD_BLOCK), lambda j, sel: (0, jnp.minimum(j, right_blocks - 1))),
    ]
    operands = [left_stack, right]
    kernel = grad_plain_kernel
    if tail is not None:
        select.append(select[-1])
        in_specs.append(pl.BlockSpec((features, GRAD_BLOCK), lambda j, sel: (0, 0)))
        operands.append(tail)
        kernel = grad_block_kernel
    return pl.pallas_call(
        kernel,
        out_shape=jax.ShapeDtypeStruct((features, len(select) * GRAD_BLOCK), jnp.bfloat16),
        grid_spec=pltpu.PrefetchScalarGridSpec(
            num_scalar_prefetch=1,
            grid=(len(select),),
            in_specs=in_specs,
            out_specs=pl.BlockSpec((features, GRAD_BLOCK), lambda j, sel: (0, j)),
        ),
    )(jnp.asarray(select, dtype=jnp.int32), *operands)


def body(
    tokens,
    cotangent,
    destination,
    segment_ids,
    attn_gain,
    w_query,
    w_key,
    w_value,
    w_output,
    ffn_gain,
    w_gate,
    w_up,
    w_down,
):
    row_count = tokens.shape[0]
    quarter = tokens.shape[1]
    col_start = lax.axis_index("col") * quarter
    group_size = HEADS // KV
    send_order = jnp.argsort(destination)
    slot_ids = destination[send_order] % row_count
    arrived_pair, arrived_slots = (
        lax.all_to_all(
            jnp.stack([tokens, cotangent])[:, send_order], "row", split_axis=1, concat_axis=1, tiled=True
        ),
        lax.all_to_all(slot_ids, "row", split_axis=0, concat_axis=0, tiled=True),
    )
    placing = jnp.argsort(arrived_slots)
    attn_widths = [w_query.shape[1], w_key.shape[1], w_value.shape[1], w_output.shape[1]]
    ffn_widths = [w_gate.shape[1], w_up.shape[1], w_down.shape[1]]
    attn_packed = gather_rows([w_query, w_key, w_value, w_output])
    ffn_packed = gather_rows([w_gate, w_up, w_down])
    full_pair = col_gather(arrived_pair[:, placing])
    full_rows, full_grads = full_pair[0], full_pair[1]
    query_w, key_w, value_w, output_w = split_columns(attn_packed, attn_widths)
    cosine, sine = rope_tables(positions_of(segment_ids))
    allowed = allowed_pairs(segment_ids)
    rows_wide = full_rows.astype(jnp.float32)
    inv_one = rms_scale(rows_wide)
    normed_one = (rows_wide * inv_one * attn_gain).astype(jnp.bfloat16)
    query = matmul(normed_one, query_w)
    key_raw = matmul(normed_one, key_w)
    value_raw = matmul(normed_one, value_w)
    query_heads_count = query.shape[1] // HD
    kv_count = key_raw.shape[1] // HD
    query_rot = (
        rotate(query.reshape(row_count, query_heads_count, HD), cosine, sine)
        .astype(jnp.bfloat16)
        .transpose(1, 0, 2)
    )
    key_rot = (
        rotate(key_raw.reshape(row_count, kv_count, HD), cosine, sine)
        .astype(jnp.bfloat16)
        .transpose(1, 0, 2)
    )
    value_heads = value_raw.astype(jnp.bfloat16).reshape(row_count, kv_count, HD).transpose(1, 0, 2)
    kv_slots = jnp.arange(query_heads_count, dtype=jnp.int32) // group_size
    scale_factor = HD ** (-0.5)
    mixed_heads, log_totals = lax.map(
        partial(
            head_forward,
            key_heads=key_rot,
            value_heads=value_heads,
            allowed=allowed,
            scale_factor=scale_factor,
        ),
        (query_rot, kv_slots),
    )
    mixed = (
        mixed_heads.transpose(1, 0, 2)
        .reshape(row_count, query_heads_count * HD)
        .astype(jnp.bfloat16)
    )
    attn_terms = matmul(mixed, output_w.T)
    attn_full = col_sum(attn_terms.astype(jnp.bfloat16))
    resid = rows_wide + attn_full
    inv_two = rms_scale(resid)
    normed_two = (resid * inv_two * ffn_gain).astype(jnp.bfloat16)
    resid_part = lax.dynamic_slice_in_dim(resid, col_start, quarter, 1)
    gate_w, up_w, down_w = split_columns(ffn_packed, ffn_widths)
    gate = matmul(normed_two, gate_w)
    upper = matmul(normed_two, up_w)
    sigmoid_gate = jax.nn.sigmoid(gate)
    activ = (gate * sigmoid_gate * upper).astype(jnp.bfloat16)
    ffn_share = col_scatter(matmul(activ, down_w.T).astype(jnp.bfloat16))
    act_grad = matmul(full_grads, down_w)
    gate_grad = (act_grad * upper * sigmoid_gate * (1.0 + gate * (1.0 - sigmoid_gate))).astype(
        jnp.bfloat16
    )
    up_grad = (act_grad * gate * sigmoid_gate).astype(jnp.bfloat16)
    normed_terms_two = matmul(gate_grad, gate_w.T) + matmul(up_grad, up_w.T)
    output_share = (resid_part + ffn_share.astype(jnp.bfloat16).astype(jnp.float32)).astype(
        jnp.bfloat16
    )
    normed_grad_two = col_sum(normed_terms_two.astype(jnp.bfloat16))
    ffn_grads_packed = packed_weight_grads(
        [normed_two, full_grads], [(0, gate_grad), (0, up_grad), (1, activ)]
    )
    resid_norm_grad, ffn_gain_grad = norm_back(resid, inv_two, ffn_gain, normed_grad_two)
    ffn_grads_local = lax.psum_scatter(ffn_grads_packed, "row", scatter_dimension=0, tiled=True)
    resid_grad = full_grads.astype(jnp.float32) + resid_norm_grad
    attn_grad_low = resid_grad.astype(jnp.bfloat16)
    mixed_grad = matmul(attn_grad_low, output_w).astype(jnp.bfloat16)
    mixed_grad_heads = mixed_grad.reshape(row_count, query_heads_count, HD).transpose(1, 0, 2)
    query_grads, key_grads, value_grads = lax.map(
        partial(
            head_backward,
            key_heads=key_rot,
            value_heads=value_heads,
            allowed=allowed,
            scale_factor=scale_factor,
        ),
        (query_rot, kv_slots, mixed_grad_heads, log_totals),
    )
    query_grad = (
        rotate_back(query_grads.transpose(1, 0, 2), cosine, sine)
        .reshape(row_count, query_heads_count * HD)
        .astype(jnp.bfloat16)
    )
    key_sum = key_grads.reshape(kv_count, group_size, row_count, HD).sum(axis=1).transpose(1, 0, 2)
    key_grad = (
        rotate_back(key_sum, cosine, sine).reshape(row_count, kv_count * HD).astype(jnp.bfloat16)
    )
    value_sum = (
        value_grads.reshape(kv_count, group_size, row_count, HD).sum(axis=1).transpose(1, 0, 2)
    )
    value_grad = value_sum.reshape(row_count, kv_count * HD).astype(jnp.bfloat16)
    normed_terms_one = (
        matmul(query_grad, query_w.T) + matmul(key_grad, key_w.T) + matmul(value_grad, value_w.T)
    )
    normed_grad_one = col_sum(normed_terms_one.astype(jnp.bfloat16))
    rows_norm_grad, attn_gain_grad = norm_back(rows_wide, inv_one, attn_gain, normed_grad_one)
    rows_grad = resid_grad + rows_norm_grad
    input_share = lax.dynamic_slice_in_dim(rows_grad, col_start, quarter, 1).astype(jnp.bfloat16)
    attn_grads_local = lax.psum_scatter(
        packed_weight_grads(
            [normed_one, attn_grad_low],
            [(0, query_grad), (0, key_grad), (0, value_grad), (1, mixed)],
            gain_tail_of([attn_gain_grad, ffn_gain_grad]),
        ),
        "row",
        scatter_dimension=0,
        tiled=True,
    )
    (
        query_result,
        key_result,
        value_result,
        output_result,
        attn_gain_result,
        ffn_gain_result,
    ) = split_columns(attn_grads_local.astype(jnp.float32), attn_widths + [1, 1])
    gate_result, up_result, down_result = split_columns(
        ffn_grads_local.astype(jnp.float32), ffn_widths
    )
    attn_gain_result = attn_gain_result.reshape(-1)
    ffn_gain_result = ffn_gain_result.reshape(-1)
    back_pair = lax.all_to_all(
        jnp.stack([output_share, input_share])[:, arrived_slots],
        "row",
        split_axis=1,
        concat_axis=1,
        tiled=True,
    )
    back_rows, back_grads = back_pair[0], back_pair[1]
    restore = jnp.argsort(send_order)
    return (
        back_rows[restore],
        back_grads[restore],
        attn_gain_result,
        query_result,
        key_result,
        value_result,
        output_result,
        ffn_gain_result,
        gate_result,
        up_result,
        down_result,
    )

def solution(mesh):
    placed = (
        P("row", "col"),
        P("row", "col"),
        P("row"),
        P("row"),
        P(),
        P("row", "col"),
        P("row", "col"),
        P("row", "col"),
        P("row", "col"),
        P(),
        P("row", "col"),
        P("row", "col"),
        P("row", "col"),
    )
    return jax.shard_map(
        body,
        mesh=mesh,
        in_specs=placed,
        out_specs=(
            P("row", "col"),
            P("row", "col"),
            P("row"),
            P("row", "col"),
            P("row", "col"),
            P("row", "col"),
            P("row", "col"),
            P("row"),
            P("row", "col"),
            P("row", "col"),
            P("row", "col"),
        ),
        check_vma=False,
    )
```

```python
from functools import partial

import jax
import jax.numpy as jnp
from jax import lax
from jax.experimental import pallas as pl
from jax.experimental.pallas import tpu as pltpu
from jax.sharding import PartitionSpec as P

HEADS = 32
KV = 4
HD = 64


EPS = 1e-05
ROPE_BASE = 10000.0


def rope_tables(positions):
    half_width = HD // 2
    freqs = ROPE_BASE ** (-(jnp.arange(half_width, dtype=jnp.float32) * 2.0 / HD))
    angles = positions.astype(jnp.float32)[:, None] * freqs[None, :]
    return (jnp.cos(angles)[:, None, :], jnp.sin(angles)[:, None, :])


def rotate(values, cosine, sine):
    half_width = values.shape[-1] // 2
    first = values[..., :half_width]
    second = values[..., half_width:]
    return jnp.concatenate(
        [first * cosine - second * sine, second * cosine + first * sine], axis=-1
    )


def rotate_back(grads, cosine, sine):
    half_width = grads.shape[-1] // 2
    first = grads[..., :half_width]
    second = grads[..., half_width:]
    return jnp.concatenate(
        [first * cosine + second * sine, second * cosine - first * sine], axis=-1
    )


def positions_of(segment_ids):
    index = jnp.arange(segment_ids.shape[0], dtype=jnp.int32)
    change = jnp.concatenate([jnp.ones((1,), dtype=jnp.bool_), segment_ids[1:] != segment_ids[:-1]])
    starts = jnp.where(change, index, jnp.zeros_like(index))
    return index - lax.cummax(starts, axis=0)


def allowed_pairs(segment_ids):
    index = jnp.arange(segment_ids.shape[0], dtype=jnp.int32)
    return (segment_ids[:, None] == segment_ids[None, :]) & (index[None, :] <= index[:, None])


def rms_scale(values):
    return lax.rsqrt(jnp.mean(values * values, axis=-1, keepdims=True) + EPS)


def norm_back(values, inv_root, gain, grads):
    normed = values * inv_root
    scaled = grads * gain
    result = inv_root * (scaled - normed * jnp.mean(scaled * normed, axis=-1, keepdims=True))
    return (result, jnp.sum(grads * normed, axis=0))


def matmul(left, right):
    return jnp.dot(left, right, preferred_element_type=jnp.float32)


def head_scores(query_head, key_head, allowed, scale_factor):
    scores = matmul(query_head, key_head.T) * scale_factor
    return jnp.where(allowed, scores, -1e30)


def head_forward(inputs, key_heads, value_heads, allowed, scale_factor):
    query_head, kv_slot = inputs
    scores = head_scores(query_head, key_heads[kv_slot], allowed, scale_factor)
    peak = jnp.max(scores, axis=-1, keepdims=True)
    expo = jnp.exp(scores - peak)
    total = jnp.sum(expo, axis=-1, keepdims=True)
    probs = expo / total
    mixed = matmul(probs.astype(jnp.bfloat16), value_heads[kv_slot])
    return (mixed, (peak + jnp.log(total))[:, 0])


def head_backward(inputs, key_heads, value_heads, allowed, scale_factor):
    query_head, kv_slot, grad_head, log_total = inputs
    key_head = key_heads[kv_slot]
    value_head = value_heads[kv_slot]
    scores = head_scores(query_head, key_head, allowed, scale_factor)
    probs = jnp.exp(scores - log_total[:, None])
    prob_grad = matmul(grad_head, value_head.T)
    value_grad = matmul(probs.astype(jnp.bfloat16).T, grad_head)
    inner = jnp.sum(probs * prob_grad, axis=-1, keepdims=True)
    score_grad = (probs * (prob_grad - inner)).astype(jnp.bfloat16)
    query_grad = matmul(score_grad, key_head) * scale_factor
    key_grad = matmul(score_grad.T, query_head) * scale_factor
    return (query_grad, key_grad, value_grad)


GRAD_BLOCK = 128


def split_columns(packed, widths):
    pieces = []
    offset = 0
    for width in widths:
        pieces.append(packed[:, offset : offset + width])
        offset += width
    return pieces


def col_scatter(values):
    count = lax.axis_size("col")
    lead = values.shape[:-1]
    blocks = jnp.moveaxis(values.reshape(*lead, count, values.shape[-1] // count), -2, 0)
    received = lax.all_to_all(blocks, "col", split_axis=0, concat_axis=0, tiled=True)
    return jnp.sum(received.astype(jnp.float32), axis=0)


def col_gather(block):
    count = lax.axis_size("col")
    copies = jnp.broadcast_to(block[None], (count,) + block.shape)
    received = lax.all_to_all(copies, "col", split_axis=0, concat_axis=0, tiled=True)
    return jnp.moveaxis(received, 0, -2).reshape(*block.shape[:-1], count * block.shape[-1])


def col_sum(values):
    return col_gather(col_scatter(values).astype(jnp.bfloat16)).astype(jnp.float32)


def gather_rows(parts):
    return lax.all_gather(jnp.concatenate(parts, axis=1), "row", axis=0, tiled=True)


def grad_block_kernel(select_ref, left_ref, right_ref, tail_ref, out_ref):
    step = pl.program_id(0)
    last = pl.num_programs(0) - 1

    @pl.when(step < last)
    def _():
        out_ref[...] = jnp.dot(
            left_ref[0], right_ref[...], preferred_element_type=jnp.float32
        ).astype(out_ref.dtype)

    @pl.when(step == last)
    def _():
        out_ref[...] = tail_ref[...]


def grad_plain_kernel(select_ref, left_ref, right_ref, out_ref):
    out_ref[...] = jnp.dot(
        left_ref[0], right_ref[...], preferred_element_type=jnp.float32
    ).astype(out_ref.dtype)


def gain_tail_of(gain_grads):
    columns = [grad[:, None] for grad in gain_grads]
    padding = jnp.zeros((gain_grads[0].shape[0], GRAD_BLOCK - len(columns)), jnp.float32)
    return jnp.concatenate(columns + [padding], axis=1).astype(jnp.bfloat16)


def packed_weight_grads(lefts, segments, tail=None):
    left_stack = jnp.stack([left.T for left in lefts])
    right = jnp.concatenate([seg for _, seg in segments], axis=1)
    column_owner = []
    for index, seg in segments:
        column_owner += [index] * seg.shape[1]
    assert len(column_owner) % GRAD_BLOCK == 0
    select = column_owner[::GRAD_BLOCK]
    assert column_owner == [owner for owner in select for _ in range(GRAD_BLOCK)]
    right_blocks = len(select)
    features, tokens = left_stack.shape[1], left_stack.shape[2]
    in_specs = [
        pl.BlockSpec((1, features, tokens), lambda j, sel: (sel[j], 0, 0)),
        pl.BlockSpec((tokens, GRAD_BLOCK), lambda j, sel: (0, jnp.minimum(j, right_blocks - 1))),
    ]
    operands = [left_stack, right]
    kernel = grad_plain_kernel
    if tail is not None:
        select.append(select[-1])
        in_specs.append(pl.BlockSpec((features, GRAD_BLOCK), lambda j, sel: (0, 0)))
        operands.append(tail)
        kernel = grad_block_kernel
    return pl.pallas_call(
        kernel,
        out_shape=jax.ShapeDtypeStruct((features, len(select) * GRAD_BLOCK), jnp.bfloat16),
        grid_spec=pltpu.PrefetchScalarGridSpec(
            num_scalar_prefetch=1,
            grid=(len(select),),
            in_specs=in_specs,
            out_specs=pl.BlockSpec((features, GRAD_BLOCK), lambda j, sel: (0, j)),
        ),
    )(jnp.asarray(select, dtype=jnp.int32), *operands)


def body(
    tokens,
    cotangent,
    destination,
    segment_ids,
    attn_gain,
    w_query,
    w_key,
    w_value,
    w_output,
    ffn_gain,
    w_gate,
    w_up,
    w_down,
):
    row_count = tokens.shape[0]
    quarter = tokens.shape[1]
    col_start = lax.axis_index("col") * quarter
    group_size = HEADS // KV
    send_order = jnp.argsort(destination)
    slot_ids = destination[send_order] % row_count
    arrived_pair, arrived_slots = (
        lax.all_to_all(
            jnp.stack([tokens, cotangent])[:, send_order], "row", split_axis=1, concat_axis=1, tiled=True
        ),
        lax.all_to_all(slot_ids, "row", split_axis=0, concat_axis=0, tiled=True),
    )
    placing = jnp.argsort(arrived_slots)
    attn_widths = [w_query.shape[1], w_key.shape[1], w_value.shape[1], w_output.shape[1]]
    ffn_widths = [w_gate.shape[1], w_up.shape[1], w_down.shape[1]]
    attn_packed = gather_rows([w_query, w_key, w_value, w_output])
    ffn_packed = gather_rows([w_gate, w_up, w_down])
    full_pair = col_gather(arrived_pair[:, placing])
    full_rows, full_grads = full_pair[0], full_pair[1]
    query_w, key_w, value_w, output_w = split_columns(attn_packed, attn_widths)
    cosine, sine = rope_tables(positions_of(segment_ids))
    allowed = allowed_pairs(segment_ids)
    rows_wide = full_rows.astype(jnp.float32)
    inv_one = rms_scale(rows_wide)
    normed_one = (rows_wide * inv_one * attn_gain).astype(jnp.bfloat16)
    query = matmul(normed_one, query_w)
    key_raw = matmul(normed_one, key_w)
    value_raw = matmul(normed_one, value_w)
    query_heads_count = query.shape[1] // HD
    kv_count = key_raw.shape[1] // HD
    query_rot = (
        rotate(query.reshape(row_count, query_heads_count, HD), cosine, sine)
        .astype(jnp.bfloat16)
        .transpose(1, 0, 2)
    )
    key_rot = (
        rotate(key_raw.reshape(row_count, kv_count, HD), cosine, sine)
        .astype(jnp.bfloat16)
        .transpose(1, 0, 2)
    )
    value_heads = value_raw.astype(jnp.bfloat16).reshape(row_count, kv_count, HD).transpose(1, 0, 2)
    kv_slots = jnp.arange(query_heads_count, dtype=jnp.int32) // group_size
    scale_factor = HD ** (-0.5)
    mixed_heads, log_totals = lax.map(
        partial(
            head_forward,
            key_heads=key_rot,
            value_heads=value_heads,
            allowed=allowed,
            scale_factor=scale_factor,
        ),
        (query_rot, kv_slots),
    )
    mixed = (
        mixed_heads.transpose(1, 0, 2)
        .reshape(row_count, query_heads_count * HD)
        .astype(jnp.bfloat16)
    )
    attn_terms = matmul(mixed, output_w.T)
    attn_terms, ffn_packed = lax.optimization_barrier((attn_terms, ffn_packed))
    attn_full = lax.psum(attn_terms.astype(jnp.bfloat16), "col").astype(jnp.float32)
    resid = rows_wide + attn_full
    inv_two = rms_scale(resid)
    normed_two = (resid * inv_two * ffn_gain).astype(jnp.bfloat16)
    resid_part = lax.dynamic_slice_in_dim(resid, col_start, quarter, 1)
    gate_w, up_w, down_w = split_columns(ffn_packed, ffn_widths)
    gate = matmul(normed_two, gate_w)
    upper = matmul(normed_two, up_w)
    sigmoid_gate = jax.nn.sigmoid(gate)
    activ = (gate * sigmoid_gate * upper).astype(jnp.bfloat16)
    ffn_share_low = lax.psum_scatter(
        matmul(activ, down_w.T).astype(jnp.bfloat16), "col", scatter_dimension=1, tiled=True
    )
    act_grad = matmul(full_grads, down_w)
    gate_grad = (act_grad * upper * sigmoid_gate * (1.0 + gate * (1.0 - sigmoid_gate))).astype(
        jnp.bfloat16
    )
    up_grad = (act_grad * gate * sigmoid_gate).astype(jnp.bfloat16)
    normed_terms_two = matmul(gate_grad, gate_w.T) + matmul(up_grad, up_w.T)
    normed_low_two, ffn_share_low = lax.optimization_barrier(
        (normed_terms_two.astype(jnp.bfloat16), ffn_share_low)
    )
    output_share = (resid_part + ffn_share_low.astype(jnp.float32)).astype(jnp.bfloat16)
    normed_grad_two = lax.psum(normed_low_two, "col").astype(jnp.float32)
    ffn_grads_packed = packed_weight_grads(
        [normed_two, full_grads], [(0, gate_grad), (0, up_grad), (1, activ)]
    )
    ffn_grads_packed, normed_grad_two = lax.optimization_barrier(
        (ffn_grads_packed, normed_grad_two)
    )
    resid_norm_grad, ffn_gain_grad = norm_back(resid, inv_two, ffn_gain, normed_grad_two)
    ffn_grads_local = lax.psum_scatter(ffn_grads_packed, "row", scatter_dimension=0, tiled=True)
    resid_grad = full_grads.astype(jnp.float32) + resid_norm_grad
    attn_grad_low = resid_grad.astype(jnp.bfloat16)
    mixed_grad = matmul(attn_grad_low, output_w).astype(jnp.bfloat16)
    mixed_grad_heads = mixed_grad.reshape(row_count, query_heads_count, HD).transpose(1, 0, 2)
    query_grads, key_grads, value_grads = lax.map(
        partial(
            head_backward,
            key_heads=key_rot,
            value_heads=value_heads,
            allowed=allowed,
            scale_factor=scale_factor,
        ),
        (query_rot, kv_slots, mixed_grad_heads, log_totals),
    )
    query_grad = (
        rotate_back(query_grads.transpose(1, 0, 2), cosine, sine)
        .reshape(row_count, query_heads_count * HD)
        .astype(jnp.bfloat16)
    )
    key_sum = key_grads.reshape(kv_count, group_size, row_count, HD).sum(axis=1).transpose(1, 0, 2)
    key_grad = (
        rotate_back(key_sum, cosine, sine).reshape(row_count, kv_count * HD).astype(jnp.bfloat16)
    )
    value_sum = (
        value_grads.reshape(kv_count, group_size, row_count, HD).sum(axis=1).transpose(1, 0, 2)
    )
    value_grad = value_sum.reshape(row_count, kv_count * HD).astype(jnp.bfloat16)
    normed_terms_one = (
        matmul(query_grad, query_w.T) + matmul(key_grad, key_w.T) + matmul(value_grad, value_w.T)
    )
    normed_grad_one, ffn_grads_local = lax.optimization_barrier(
        (col_sum(normed_terms_one.astype(jnp.bfloat16)), ffn_grads_local)
    )
    rows_norm_grad, attn_gain_grad = norm_back(rows_wide, inv_one, attn_gain, normed_grad_one)
    rows_grad = resid_grad + rows_norm_grad
    input_share = lax.dynamic_slice_in_dim(rows_grad, col_start, quarter, 1).astype(jnp.bfloat16)
    attn_grads_local = lax.psum_scatter(
        packed_weight_grads(
            [normed_one, attn_grad_low],
            [(0, query_grad), (0, key_grad), (0, value_grad), (1, mixed)],
            gain_tail_of([attn_gain_grad, ffn_gain_grad]),
        ),
        "row",
        scatter_dimension=0,
        tiled=True,
    )
    (
        query_result,
        key_result,
        value_result,
        output_result,
        attn_gain_result,
        ffn_gain_result,
    ) = split_columns(attn_grads_local.astype(jnp.float32), attn_widths + [1, 1])
    gate_result, up_result, down_result = split_columns(
        ffn_grads_local.astype(jnp.float32), ffn_widths
    )
    attn_gain_result = attn_gain_result.reshape(-1)
    ffn_gain_result = ffn_gain_result.reshape(-1)
    back_pair = lax.all_to_all(
        jnp.stack([output_share, input_share])[:, arrived_slots],
        "row",
        split_axis=1,
        concat_axis=1,
        tiled=True,
    )
    back_rows, back_grads = back_pair[0], back_pair[1]
    restore = jnp.argsort(send_order)
    return (
        back_rows[restore],
        back_grads[restore],
        attn_gain_result,
        query_result,
        key_result,
        value_result,
        output_result,
        ffn_gain_result,
        gate_result,
        up_result,
        down_result,
    )

def solution(mesh):
    placed = (
        P("row", "col"),
        P("row", "col"),
        P("row"),
        P("row"),
        P(),
        P("row", "col"),
        P("row", "col"),
        P("row", "col"),
        P("row", "col"),
        P(),
        P("row", "col"),
        P("row", "col"),
        P("row", "col"),
    )
    return jax.shard_map(
        body,
        mesh=mesh,
        in_specs=placed,
        out_specs=(
            P("row", "col"),
            P("row", "col"),
            P("row"),
            P("row", "col"),
            P("row", "col"),
            P("row", "col"),
            P("row", "col"),
            P("row"),
            P("row", "col"),
            P("row", "col"),
            P("row", "col"),
        ),
        check_vma=False,
    )
```

```python
from functools import partial

import jax
import jax.numpy as jnp
from jax import lax
from jax.experimental import pallas as pl
from jax.experimental.pallas import tpu as pltpu
from jax.sharding import PartitionSpec as P

HEADS = 32
KV = 4
HD = 64


EPS = 1e-05
ROPE_BASE = 10000.0


def rope_tables(positions):
    half_width = HD // 2
    freqs = ROPE_BASE ** (-(jnp.arange(half_width, dtype=jnp.float32) * 2.0 / HD))
    angles = positions.astype(jnp.float32)[:, None] * freqs[None, :]
    return (jnp.cos(angles)[:, None, :], jnp.sin(angles)[:, None, :])


def rotate(values, cosine, sine):
    half_width = values.shape[-1] // 2
    first = values[..., :half_width]
    second = values[..., half_width:]
    return jnp.concatenate(
        [first * cosine - second * sine, second * cosine + first * sine], axis=-1
    )


def rotate_back(grads, cosine, sine):
    half_width = grads.shape[-1] // 2
    first = grads[..., :half_width]
    second = grads[..., half_width:]
    return jnp.concatenate(
        [first * cosine + second * sine, second * cosine - first * sine], axis=-1
    )


def positions_of(segment_ids):
    index = jnp.arange(segment_ids.shape[0], dtype=jnp.int32)
    change = jnp.concatenate([jnp.ones((1,), dtype=jnp.bool_), segment_ids[1:] != segment_ids[:-1]])
    starts = jnp.where(change, index, jnp.zeros_like(index))
    return index - lax.cummax(starts, axis=0)


def allowed_pairs(segment_ids):
    index = jnp.arange(segment_ids.shape[0], dtype=jnp.int32)
    return (segment_ids[:, None] == segment_ids[None, :]) & (index[None, :] <= index[:, None])


def rms_scale(values):
    return lax.rsqrt(jnp.mean(values * values, axis=-1, keepdims=True) + EPS)


def norm_back(values, inv_root, gain, grads):
    normed = values * inv_root
    scaled = grads * gain
    result = inv_root * (scaled - normed * jnp.mean(scaled * normed, axis=-1, keepdims=True))
    return (result, jnp.sum(grads * normed, axis=0))


def matmul(left, right):
    return jnp.dot(left, right, preferred_element_type=jnp.float32)


def head_scores(query_head, key_head, allowed, scale_factor):
    scores = matmul(query_head, key_head.T) * scale_factor
    return jnp.where(allowed, scores, -1e30)


def head_forward(inputs, key_heads, value_heads, allowed, scale_factor):
    query_head, kv_slot = inputs
    scores = head_scores(query_head, key_heads[kv_slot], allowed, scale_factor)
    peak = jnp.max(scores, axis=-1, keepdims=True)
    expo = jnp.exp(scores - peak)
    total = jnp.sum(expo, axis=-1, keepdims=True)
    probs = expo / total
    mixed = matmul(probs.astype(jnp.bfloat16), value_heads[kv_slot])
    return (mixed, (peak + jnp.log(total))[:, 0])


def head_backward(inputs, key_heads, value_heads, allowed, scale_factor):
    query_head, kv_slot, grad_head, log_total = inputs
    key_head = key_heads[kv_slot]
    value_head = value_heads[kv_slot]
    scores = head_scores(query_head, key_head, allowed, scale_factor)
    probs = jnp.exp(scores - log_total[:, None])
    prob_grad = matmul(grad_head, value_head.T)
    value_grad = matmul(probs.astype(jnp.bfloat16).T, grad_head)
    inner = jnp.sum(probs * prob_grad, axis=-1, keepdims=True)
    score_grad = (probs * (prob_grad - inner)).astype(jnp.bfloat16)
    query_grad = matmul(score_grad, key_head) * scale_factor
    key_grad = matmul(score_grad.T, query_head) * scale_factor
    return (query_grad, key_grad, value_grad)


def grouped(heads, kv_count):
    return heads.reshape(kv_count, heads.shape[0] // kv_count, *heads.shape[1:])


def group_scores(query_groups, key_heads, allowed, scale_factor):
    scores = (
        jnp.einsum("kgqd,kpd->kgqp", query_groups, key_heads, preferred_element_type=jnp.float32)
        * scale_factor
    )
    return jnp.where(allowed, scores, -1e30)


def attention_forward(query_heads, key_heads, value_heads, allowed, scale_factor):
    query_groups = grouped(query_heads, key_heads.shape[0])
    scores = group_scores(query_groups, key_heads, allowed, scale_factor)
    peak = jnp.max(scores, axis=-1, keepdims=True)
    expo = jnp.exp(scores - peak)
    total = jnp.sum(expo, axis=-1, keepdims=True)
    probs = expo / total
    mixed = jnp.einsum(
        "kgqp,kpd->kgqd", probs.astype(jnp.bfloat16), value_heads, preferred_element_type=jnp.float32
    )
    return mixed.reshape(query_heads.shape), (peak + jnp.log(total))[..., 0]


def attention_backward(
    query_heads, key_heads, value_heads, grad_heads, log_totals, allowed, scale_factor
):
    kv_count = key_heads.shape[0]
    query_groups = grouped(query_heads, kv_count)
    grad_groups = grouped(grad_heads, kv_count)
    scores = group_scores(query_groups, key_heads, allowed, scale_factor)
    probs = jnp.exp(scores - log_totals[..., None])
    prob_grad = jnp.einsum(
        "kgqd,kpd->kgqp", grad_groups, value_heads, preferred_element_type=jnp.float32
    )
    value_grad = jnp.einsum(
        "kgqp,kgqd->kpd", probs.astype(jnp.bfloat16), grad_groups, preferred_element_type=jnp.float32
    )
    inner = jnp.sum(probs * prob_grad, axis=-1, keepdims=True)
    score_grad = (probs * (prob_grad - inner)).astype(jnp.bfloat16)
    query_grad = (
        jnp.einsum("kgqp,kpd->kgqd", score_grad, key_heads, preferred_element_type=jnp.float32)
        * scale_factor
    )
    key_grad = (
        jnp.einsum("kgqp,kgqd->kpd", score_grad, query_groups, preferred_element_type=jnp.float32)
        * scale_factor
    )
    return query_grad.reshape(query_heads.shape), key_grad, value_grad


def row_scatter_sum(vectors):
    count = lax.axis_size("row")
    blocks = jnp.moveaxis(vectors.reshape(vectors.shape[0], count, -1), 1, 0)
    return jnp.sum(lax.all_to_all(blocks, "row", split_axis=0, concat_axis=0, tiled=True), axis=0)


GRAD_BLOCK = 128


def split_columns(packed, widths):
    pieces = []
    offset = 0
    for width in widths:
        pieces.append(packed[:, offset : offset + width])
        offset += width
    return pieces


def col_scatter(values):
    count = lax.axis_size("col")
    lead = values.shape[:-1]
    blocks = jnp.moveaxis(values.reshape(*lead, count, values.shape[-1] // count), -2, 0)
    received = lax.all_to_all(blocks, "col", split_axis=0, concat_axis=0, tiled=True)
    return jnp.sum(received.astype(jnp.float32), axis=0)


def col_gather(block):
    count = lax.axis_size("col")
    copies = jnp.broadcast_to(block[None], (count,) + block.shape)
    received = lax.all_to_all(copies, "col", split_axis=0, concat_axis=0, tiled=True)
    return jnp.moveaxis(received, 0, -2).reshape(*block.shape[:-1], count * block.shape[-1])


def col_sum(values):
    return col_gather(col_scatter(values).astype(jnp.bfloat16)).astype(jnp.float32)


def gather_rows(parts):
    return lax.all_gather(jnp.concatenate(parts, axis=1), "row", axis=0, tiled=True)


def grad_block_kernel(select_ref, left_ref, right_ref, tail_ref, out_ref):
    step = pl.program_id(0)
    last = pl.num_programs(0) - 1

    @pl.when(step < last)
    def _():
        out_ref[...] = jnp.dot(
            left_ref[0], right_ref[...], preferred_element_type=jnp.float32
        ).astype(out_ref.dtype)

    @pl.when(step == last)
    def _():
        out_ref[...] = tail_ref[...]


def grad_plain_kernel(select_ref, left_ref, right_ref, out_ref):
    out_ref[...] = jnp.dot(
        left_ref[0], right_ref[...], preferred_element_type=jnp.float32
    ).astype(out_ref.dtype)


def gain_tail_of(gain_grads):
    columns = [grad[:, None] for grad in gain_grads]
    padding = jnp.zeros((gain_grads[0].shape[0], GRAD_BLOCK - len(columns)), jnp.float32)
    return jnp.concatenate(columns + [padding], axis=1).astype(jnp.bfloat16)


def packed_weight_grads(lefts, segments, tail=None):
    left_stack = jnp.stack([left.T for left in lefts])
    right = jnp.concatenate([seg for _, seg in segments], axis=1)
    column_owner = []
    for index, seg in segments:
        column_owner += [index] * seg.shape[1]
    assert len(column_owner) % GRAD_BLOCK == 0
    select = column_owner[::GRAD_BLOCK]
    assert column_owner == [owner for owner in select for _ in range(GRAD_BLOCK)]
    right_blocks = len(select)
    features, tokens = left_stack.shape[1], left_stack.shape[2]
    in_specs = [
        pl.BlockSpec((1, features, tokens), lambda j, sel: (sel[j], 0, 0)),
        pl.BlockSpec((tokens, GRAD_BLOCK), lambda j, sel: (0, jnp.minimum(j, right_blocks - 1))),
    ]
    operands = [left_stack, right]
    kernel = grad_plain_kernel
    if tail is not None:
        select.append(select[-1])
        in_specs.append(pl.BlockSpec((features, GRAD_BLOCK), lambda j, sel: (0, 0)))
        operands.append(tail)
        kernel = grad_block_kernel
    return pl.pallas_call(
        kernel,
        out_shape=jax.ShapeDtypeStruct((features, len(select) * GRAD_BLOCK), jnp.bfloat16),
        grid_spec=pltpu.PrefetchScalarGridSpec(
            num_scalar_prefetch=1,
            grid=(len(select),),
            in_specs=in_specs,
            out_specs=pl.BlockSpec((features, GRAD_BLOCK), lambda j, sel: (0, j)),
        ),
    )(jnp.asarray(select, dtype=jnp.int32), *operands)


def body(
    tokens,
    cotangent,
    destination,
    segment_ids,
    attn_gain,
    w_query,
    w_key,
    w_value,
    w_output,
    ffn_gain,
    w_gate,
    w_up,
    w_down,
):
    row_count = tokens.shape[0]
    quarter = tokens.shape[1]
    col_start = lax.axis_index("col") * quarter
    group_size = HEADS // KV
    send_order = jnp.argsort(destination)
    slot_ids = destination[send_order] % row_count
    arrived_pair, arrived_slots = (
        lax.all_to_all(
            jnp.stack([tokens, cotangent])[:, send_order], "row", split_axis=1, concat_axis=1, tiled=True
        ),
        lax.all_to_all(slot_ids, "row", split_axis=0, concat_axis=0, tiled=True),
    )
    placing = jnp.argsort(arrived_slots)
    attn_widths = [w_query.shape[1], w_key.shape[1], w_value.shape[1], w_output.shape[1]]
    ffn_widths = [w_gate.shape[1], w_up.shape[1], w_down.shape[1]]
    attn_packed = gather_rows([w_query, w_key, w_value, w_output])
    ffn_packed = gather_rows([w_gate, w_up, w_down])
    full_pair = col_gather(arrived_pair[:, placing])
    full_rows, full_grads = full_pair[0], full_pair[1]
    query_w, key_w, value_w, output_w = split_columns(attn_packed, attn_widths)
    cosine, sine = rope_tables(positions_of(segment_ids))
    allowed = allowed_pairs(segment_ids)
    rows_wide = full_rows.astype(jnp.float32)
    inv_one = rms_scale(rows_wide)
    normed_one = (rows_wide * inv_one * attn_gain).astype(jnp.bfloat16)
    query = matmul(normed_one, query_w)
    key_raw = matmul(normed_one, key_w)
    value_raw = matmul(normed_one, value_w)
    query_heads_count = query.shape[1] // HD
    kv_count = key_raw.shape[1] // HD
    query_rot = (
        rotate(query.reshape(row_count, query_heads_count, HD), cosine, sine)
        .astype(jnp.bfloat16)
        .transpose(1, 0, 2)
    )
    key_rot = (
        rotate(key_raw.reshape(row_count, kv_count, HD), cosine, sine)
        .astype(jnp.bfloat16)
        .transpose(1, 0, 2)
    )
    value_heads = value_raw.astype(jnp.bfloat16).reshape(row_count, kv_count, HD).transpose(1, 0, 2)
    scale_factor = HD ** (-0.5)
    mixed_heads, log_totals = attention_forward(
        query_rot, key_rot, value_heads, allowed, scale_factor
    )
    mixed = (
        mixed_heads.transpose(1, 0, 2)
        .reshape(row_count, query_heads_count * HD)
        .astype(jnp.bfloat16)
    )
    attn_terms = matmul(mixed, output_w.T)
    attn_terms, ffn_packed = lax.optimization_barrier((attn_terms, ffn_packed))
    attn_full = lax.psum(attn_terms.astype(jnp.bfloat16), "col").astype(jnp.float32)
    resid = rows_wide + attn_full
    inv_two = rms_scale(resid)
    normed_two = (resid * inv_two * ffn_gain).astype(jnp.bfloat16)
    resid_part = lax.dynamic_slice_in_dim(resid, col_start, quarter, 1)
    gate_w, up_w, down_w = split_columns(ffn_packed, ffn_widths)
    gate = matmul(normed_two, gate_w)
    upper = matmul(normed_two, up_w)
    sigmoid_gate = jax.nn.sigmoid(gate)
    activ = (gate * sigmoid_gate * upper).astype(jnp.bfloat16)
    ffn_share_low = lax.psum_scatter(
        matmul(activ, down_w.T).astype(jnp.bfloat16), "col", scatter_dimension=1, tiled=True
    )
    act_grad = matmul(full_grads, down_w)
    gate_grad = (act_grad * upper * sigmoid_gate * (1.0 + gate * (1.0 - sigmoid_gate))).astype(
        jnp.bfloat16
    )
    up_grad = (act_grad * gate * sigmoid_gate).astype(jnp.bfloat16)
    normed_terms_two = matmul(gate_grad, gate_w.T) + matmul(up_grad, up_w.T)
    normed_low_two, ffn_share_low = lax.optimization_barrier(
        (normed_terms_two.astype(jnp.bfloat16), ffn_share_low)
    )
    output_share = (resid_part + ffn_share_low.astype(jnp.float32)).astype(jnp.bfloat16)
    normed_grad_two = lax.psum(normed_low_two, "col").astype(jnp.float32)
    ffn_grads_packed = packed_weight_grads(
        [normed_two, full_grads], [(0, gate_grad), (0, up_grad), (1, activ)]
    )
    ffn_grads_packed, normed_grad_two = lax.optimization_barrier(
        (ffn_grads_packed, normed_grad_two)
    )
    resid_norm_grad, ffn_gain_grad = norm_back(resid, inv_two, ffn_gain, normed_grad_two)
    ffn_grads_local = lax.psum_scatter(ffn_grads_packed, "row", scatter_dimension=0, tiled=True)
    resid_grad = full_grads.astype(jnp.float32) + resid_norm_grad
    attn_grad_low = resid_grad.astype(jnp.bfloat16)
    mixed_grad = matmul(attn_grad_low, output_w).astype(jnp.bfloat16)
    mixed_grad_heads = mixed_grad.reshape(row_count, query_heads_count, HD).transpose(1, 0, 2)
    query_grads, key_grads, value_grads = attention_backward(
        query_rot, key_rot, value_heads, mixed_grad_heads, log_totals, allowed, scale_factor
    )
    query_grad = (
        rotate_back(query_grads.transpose(1, 0, 2), cosine, sine)
        .reshape(row_count, query_heads_count * HD)
        .astype(jnp.bfloat16)
    )
    key_sum = key_grads.transpose(1, 0, 2)
    key_grad = (
        rotate_back(key_sum, cosine, sine).reshape(row_count, kv_count * HD).astype(jnp.bfloat16)
    )
    value_sum = value_grads.transpose(1, 0, 2)
    value_grad = value_sum.reshape(row_count, kv_count * HD).astype(jnp.bfloat16)
    normed_terms_one = (
        matmul(query_grad, query_w.T) + matmul(key_grad, key_w.T) + matmul(value_grad, value_w.T)
    )
    attn_grads_packed, ffn_grads_local = lax.optimization_barrier(
        (
            packed_weight_grads(
                [normed_one, attn_grad_low],
                [(0, query_grad), (0, key_grad), (0, value_grad), (1, mixed)],
            ),
            ffn_grads_local,
        )
    )
    attn_grads_local = lax.psum_scatter(attn_grads_packed, "row", scatter_dimension=0, tiled=True)
    normed_grad_one = col_sum(normed_terms_one.astype(jnp.bfloat16))
    rows_norm_grad, attn_gain_grad = norm_back(rows_wide, inv_one, attn_gain, normed_grad_one)
    rows_grad = resid_grad + rows_norm_grad
    input_share = lax.dynamic_slice_in_dim(rows_grad, col_start, quarter, 1).astype(jnp.bfloat16)
    query_result, key_result, value_result, output_result = split_columns(
        attn_grads_local.astype(jnp.float32), attn_widths
    )
    attn_gain_result, ffn_gain_result = row_scatter_sum(jnp.stack([attn_gain_grad, ffn_gain_grad]))
    gate_result, up_result, down_result = split_columns(
        ffn_grads_local.astype(jnp.float32), ffn_widths
    )
    back_pair = lax.all_to_all(
        jnp.stack([output_share, input_share])[:, arrived_slots],
        "row",
        split_axis=1,
        concat_axis=1,
        tiled=True,
    )
    back_rows, back_grads = back_pair[0], back_pair[1]
    restore = jnp.argsort(send_order)
    return (
        back_rows[restore],
        back_grads[restore],
        attn_gain_result,
        query_result,
        key_result,
        value_result,
        output_result,
        ffn_gain_result,
        gate_result,
        up_result,
        down_result,
    )

def solution(mesh):
    placed = (
        P("row", "col"),
        P("row", "col"),
        P("row"),
        P("row"),
        P(),
        P("row", "col"),
        P("row", "col"),
        P("row", "col"),
        P("row", "col"),
        P(),
        P("row", "col"),
        P("row", "col"),
        P("row", "col"),
    )
    return jax.shard_map(
        body,
        mesh=mesh,
        in_specs=placed,
        out_specs=(
            P("row", "col"),
            P("row", "col"),
            P("row"),
            P("row", "col"),
            P("row", "col"),
            P("row", "col"),
            P("row", "col"),
            P("row"),
            P("row", "col"),
            P("row", "col"),
            P("row", "col"),
        ),
        check_vma=False,
    )
```

```python
from functools import partial

import jax
import jax.numpy as jnp
from jax import lax
from jax.experimental import pallas as pl
from jax.experimental.pallas import tpu as pltpu
from jax.sharding import PartitionSpec as P

HEADS = 32
KV = 4
HD = 64


EPS = 1e-05
ROPE_BASE = 10000.0


def rope_tables(positions):
    half_width = HD // 2
    freqs = ROPE_BASE ** (-(jnp.arange(half_width, dtype=jnp.float32) * 2.0 / HD))
    angles = positions.astype(jnp.float32)[:, None] * freqs[None, :]
    return (jnp.cos(angles)[:, None, :], jnp.sin(angles)[:, None, :])


def rotate(values, cosine, sine):
    half_width = values.shape[-1] // 2
    first = values[..., :half_width]
    second = values[..., half_width:]
    return jnp.concatenate(
        [first * cosine - second * sine, second * cosine + first * sine], axis=-1
    )


def rotate_back(grads, cosine, sine):
    half_width = grads.shape[-1] // 2
    first = grads[..., :half_width]
    second = grads[..., half_width:]
    return jnp.concatenate(
        [first * cosine + second * sine, second * cosine - first * sine], axis=-1
    )


def positions_of(segment_ids):
    index = jnp.arange(segment_ids.shape[0], dtype=jnp.int32)
    change = jnp.concatenate([jnp.ones((1,), dtype=jnp.bool_), segment_ids[1:] != segment_ids[:-1]])
    starts = jnp.where(change, index, jnp.zeros_like(index))
    return index - lax.cummax(starts, axis=0)


def allowed_pairs(segment_ids):
    index = jnp.arange(segment_ids.shape[0], dtype=jnp.int32)
    return (segment_ids[:, None] == segment_ids[None, :]) & (index[None, :] <= index[:, None])


def rms_scale(values):
    return lax.rsqrt(jnp.mean(values * values, axis=-1, keepdims=True) + EPS)


def norm_back(values, inv_root, gain, grads):
    normed = values * inv_root
    scaled = grads * gain
    result = inv_root * (scaled - normed * jnp.mean(scaled * normed, axis=-1, keepdims=True))
    return (result, jnp.sum(grads * normed, axis=0))


def matmul(left, right):
    return jnp.dot(left, right, preferred_element_type=jnp.float32)


def head_scores(query_head, key_head, allowed, scale_factor):
    scores = matmul(query_head, key_head.T) * scale_factor
    return jnp.where(allowed, scores, -1e30)


def head_forward(inputs, key_heads, value_heads, allowed, scale_factor):
    query_head, kv_slot = inputs
    scores = head_scores(query_head, key_heads[kv_slot], allowed, scale_factor)
    peak = jnp.max(scores, axis=-1, keepdims=True)
    expo = jnp.exp(scores - peak)
    total = jnp.sum(expo, axis=-1, keepdims=True)
    probs = expo / total
    mixed = matmul(probs.astype(jnp.bfloat16), value_heads[kv_slot])
    return (mixed, (peak + jnp.log(total))[:, 0])


def head_backward(inputs, key_heads, value_heads, allowed, scale_factor):
    query_head, kv_slot, grad_head, log_total = inputs
    key_head = key_heads[kv_slot]
    value_head = value_heads[kv_slot]
    scores = head_scores(query_head, key_head, allowed, scale_factor)
    probs = jnp.exp(scores - log_total[:, None])
    prob_grad = matmul(grad_head, value_head.T)
    value_grad = matmul(probs.astype(jnp.bfloat16).T, grad_head)
    inner = jnp.sum(probs * prob_grad, axis=-1, keepdims=True)
    score_grad = (probs * (prob_grad - inner)).astype(jnp.bfloat16)
    query_grad = matmul(score_grad, key_head) * scale_factor
    key_grad = matmul(score_grad.T, query_head) * scale_factor
    return (query_grad, key_grad, value_grad)


def grouped(heads, kv_count):
    return heads.reshape(kv_count, heads.shape[0] // kv_count, *heads.shape[1:])


def group_scores(query_groups, key_heads, allowed, scale_factor):
    scores = (
        jnp.einsum("kgqd,kpd->kgqp", query_groups, key_heads, preferred_element_type=jnp.float32)
        * scale_factor
    )
    return jnp.where(allowed, scores, -1e30)


def attention_forward(query_heads, key_heads, value_heads, allowed, scale_factor):
    query_groups = grouped(query_heads, key_heads.shape[0])
    scores = group_scores(query_groups, key_heads, allowed, scale_factor)
    peak = jnp.max(scores, axis=-1, keepdims=True)
    expo = jnp.exp(scores - peak)
    total = jnp.sum(expo, axis=-1, keepdims=True)
    probs = expo / total
    mixed = jnp.einsum(
        "kgqp,kpd->kgqd", probs.astype(jnp.bfloat16), value_heads, preferred_element_type=jnp.float32
    )
    return mixed.reshape(query_heads.shape), (peak + jnp.log(total))[..., 0]


def attention_backward(
    query_heads, key_heads, value_heads, grad_heads, log_totals, allowed, scale_factor
):
    kv_count = key_heads.shape[0]
    query_groups = grouped(query_heads, kv_count)
    grad_groups = grouped(grad_heads, kv_count)
    scores = group_scores(query_groups, key_heads, allowed, scale_factor)
    probs = jnp.exp(scores - log_totals[..., None])
    prob_grad = jnp.einsum(
        "kgqd,kpd->kgqp", grad_groups, value_heads, preferred_element_type=jnp.float32
    )
    value_grad = jnp.einsum(
        "kgqp,kgqd->kpd", probs.astype(jnp.bfloat16), grad_groups, preferred_element_type=jnp.float32
    )
    inner = jnp.sum(probs * prob_grad, axis=-1, keepdims=True)
    score_grad = (probs * (prob_grad - inner)).astype(jnp.bfloat16)
    query_grad = (
        jnp.einsum("kgqp,kpd->kgqd", score_grad, key_heads, preferred_element_type=jnp.float32)
        * scale_factor
    )
    key_grad = (
        jnp.einsum("kgqp,kgqd->kpd", score_grad, query_groups, preferred_element_type=jnp.float32)
        * scale_factor
    )
    return query_grad.reshape(query_heads.shape), key_grad, value_grad


def row_scatter_sum(vectors):
    count = lax.axis_size("row")
    blocks = jnp.moveaxis(vectors.reshape(vectors.shape[0], count, -1), 1, 0)
    return jnp.sum(lax.all_to_all(blocks, "row", split_axis=0, concat_axis=0, tiled=True), axis=0)


GRAD_BLOCK = 128


def split_columns(packed, widths):
    pieces = []
    offset = 0
    for width in widths:
        pieces.append(packed[:, offset : offset + width])
        offset += width
    return pieces


def col_scatter(values):
    count = lax.axis_size("col")
    lead = values.shape[:-1]
    blocks = jnp.moveaxis(values.reshape(*lead, count, values.shape[-1] // count), -2, 0)
    received = lax.all_to_all(blocks, "col", split_axis=0, concat_axis=0, tiled=True)
    return jnp.sum(received.astype(jnp.float32), axis=0)


def col_gather(block):
    count = lax.axis_size("col")
    copies = jnp.broadcast_to(block[None], (count,) + block.shape)
    received = lax.all_to_all(copies, "col", split_axis=0, concat_axis=0, tiled=True)
    return jnp.moveaxis(received, 0, -2).reshape(*block.shape[:-1], count * block.shape[-1])


def col_sum(values):
    return col_gather(col_scatter(values).astype(jnp.bfloat16)).astype(jnp.float32)


def gather_rows(parts):
    return lax.all_gather(jnp.concatenate(parts, axis=1), "row", axis=0, tiled=True)


def grad_plain_kernel(select_ref, left_ref, right_ref, out_ref):
    out_ref[...] = jnp.dot(
        left_ref[0], right_ref[...], preferred_element_type=jnp.float32
    ).astype(out_ref.dtype)


def packed_weight_grads(lefts, segments):
    left_stack = jnp.stack([left.T for left in lefts])
    right = jnp.concatenate([seg for _, seg in segments], axis=1)
    column_owner = []
    for index, seg in segments:
        column_owner += [index] * seg.shape[1]
    assert len(column_owner) % GRAD_BLOCK == 0
    select = column_owner[::GRAD_BLOCK]
    assert column_owner == [owner for owner in select for _ in range(GRAD_BLOCK)]
    right_blocks = len(select)
    features, tokens = left_stack.shape[1], left_stack.shape[2]
    in_specs = [
        pl.BlockSpec((1, features, tokens), lambda j, sel: (sel[j], 0, 0)),
        pl.BlockSpec((tokens, GRAD_BLOCK), lambda j, sel: (0, jnp.minimum(j, right_blocks - 1))),
    ]
    return pl.pallas_call(
        grad_plain_kernel,
        out_shape=jax.ShapeDtypeStruct((features, len(select) * GRAD_BLOCK), jnp.bfloat16),
        grid_spec=pltpu.PrefetchScalarGridSpec(
            num_scalar_prefetch=1,
            grid=(len(select),),
            in_specs=in_specs,
            out_specs=pl.BlockSpec((features, GRAD_BLOCK), lambda j, sel: (0, j)),
        ),
    )(jnp.asarray(select, dtype=jnp.int32), left_stack, right)


def body(
    tokens,
    cotangent,
    destination,
    segment_ids,
    attn_gain,
    w_query,
    w_key,
    w_value,
    w_output,
    ffn_gain,
    w_gate,
    w_up,
    w_down,
):
    row_count = tokens.shape[0]
    quarter = tokens.shape[1]
    col_start = lax.axis_index("col") * quarter
    send_order = jnp.argsort(destination)
    slot_ids = destination[send_order] % row_count
    arrived_rows, arrived_slots = (
        lax.all_to_all(tokens[send_order], "row", split_axis=0, concat_axis=0, tiled=True),
        lax.all_to_all(slot_ids, "row", split_axis=0, concat_axis=0, tiled=True),
    )
    placing = jnp.argsort(arrived_slots)
    attn_widths = [w_query.shape[1], w_key.shape[1], w_value.shape[1], w_output.shape[1]]
    ffn_widths = [w_gate.shape[1], w_up.shape[1], w_down.shape[1]]
    attn_packed = gather_rows([w_query, w_key, w_value, w_output])
    ffn_packed = gather_rows([w_gate, w_up, w_down])
    full_rows = col_gather(arrived_rows[placing])
    query_w, key_w, value_w, output_w = split_columns(attn_packed, attn_widths)
    cosine, sine = rope_tables(positions_of(segment_ids))
    allowed = allowed_pairs(segment_ids)
    rows_wide = full_rows.astype(jnp.float32)
    inv_one = rms_scale(rows_wide)
    normed_one = (rows_wide * inv_one * attn_gain).astype(jnp.bfloat16)
    query = matmul(normed_one, query_w)
    key_raw = matmul(normed_one, key_w)
    value_raw = matmul(normed_one, value_w)
    query_heads_count = query.shape[1] // HD
    kv_count = key_raw.shape[1] // HD
    query_rot = (
        rotate(query.reshape(row_count, query_heads_count, HD), cosine, sine)
        .astype(jnp.bfloat16)
        .transpose(1, 0, 2)
    )
    key_rot = (
        rotate(key_raw.reshape(row_count, kv_count, HD), cosine, sine)
        .astype(jnp.bfloat16)
        .transpose(1, 0, 2)
    )
    value_heads = value_raw.astype(jnp.bfloat16).reshape(row_count, kv_count, HD).transpose(1, 0, 2)
    scale_factor = HD ** (-0.5)
    mixed_heads, log_totals = attention_forward(
        query_rot, key_rot, value_heads, allowed, scale_factor
    )
    mixed = (
        mixed_heads.transpose(1, 0, 2)
        .reshape(row_count, query_heads_count * HD)
        .astype(jnp.bfloat16)
    )
    attn_terms = matmul(mixed, output_w.T)
    sorted_grads, attn_terms, ffn_packed = lax.optimization_barrier(
        (cotangent[send_order], attn_terms, ffn_packed)
    )
    arrived_grads = lax.all_to_all(sorted_grads, "row", split_axis=0, concat_axis=0, tiled=True)
    full_grads = col_gather(arrived_grads[placing])
    attn_full = lax.psum(attn_terms.astype(jnp.bfloat16), "col").astype(jnp.float32)
    resid = rows_wide + attn_full
    inv_two = rms_scale(resid)
    normed_two = (resid * inv_two * ffn_gain).astype(jnp.bfloat16)
    resid_part = lax.dynamic_slice_in_dim(resid, col_start, quarter, 1)
    gate_w, up_w, down_w = split_columns(ffn_packed, ffn_widths)
    gate = matmul(normed_two, gate_w)
    upper = matmul(normed_two, up_w)
    sigmoid_gate = jax.nn.sigmoid(gate)
    activ = (gate * sigmoid_gate * upper).astype(jnp.bfloat16)
    ffn_share_low = lax.psum_scatter(
        matmul(activ, down_w.T).astype(jnp.bfloat16), "col", scatter_dimension=1, tiled=True
    )
    act_grad = matmul(full_grads, down_w)
    gate_grad = (act_grad * upper * sigmoid_gate * (1.0 + gate * (1.0 - sigmoid_gate))).astype(
        jnp.bfloat16
    )
    up_grad = (act_grad * gate * sigmoid_gate).astype(jnp.bfloat16)
    normed_terms_two = matmul(gate_grad, gate_w.T) + matmul(up_grad, up_w.T)
    normed_low_two, ffn_share_low = lax.optimization_barrier(
        (normed_terms_two.astype(jnp.bfloat16), ffn_share_low)
    )
    output_share = (resid_part + ffn_share_low.astype(jnp.float32)).astype(jnp.bfloat16)
    normed_grad_two = lax.psum(normed_low_two, "col").astype(jnp.float32)
    ffn_grads_packed = packed_weight_grads(
        [normed_two, full_grads], [(0, gate_grad), (0, up_grad), (1, activ)]
    )
    ffn_grads_packed, normed_grad_two = lax.optimization_barrier(
        (ffn_grads_packed, normed_grad_two)
    )
    resid_norm_grad, ffn_gain_grad = norm_back(resid, inv_two, ffn_gain, normed_grad_two)
    ffn_grads_local = lax.psum_scatter(ffn_grads_packed, "row", scatter_dimension=0, tiled=True)
    resid_grad = full_grads.astype(jnp.float32) + resid_norm_grad
    attn_grad_low = resid_grad.astype(jnp.bfloat16)
    mixed_grad = matmul(attn_grad_low, output_w).astype(jnp.bfloat16)
    mixed_grad_heads = mixed_grad.reshape(row_count, query_heads_count, HD).transpose(1, 0, 2)
    query_grads, key_grads, value_grads = attention_backward(
        query_rot, key_rot, value_heads, mixed_grad_heads, log_totals, allowed, scale_factor
    )
    query_grad = (
        rotate_back(query_grads.transpose(1, 0, 2), cosine, sine)
        .reshape(row_count, query_heads_count * HD)
        .astype(jnp.bfloat16)
    )
    key_sum = key_grads.transpose(1, 0, 2)
    key_grad = (
        rotate_back(key_sum, cosine, sine).reshape(row_count, kv_count * HD).astype(jnp.bfloat16)
    )
    value_sum = value_grads.transpose(1, 0, 2)
    value_grad = value_sum.reshape(row_count, kv_count * HD).astype(jnp.bfloat16)
    normed_terms_one = (
        matmul(query_grad, query_w.T) + matmul(key_grad, key_w.T) + matmul(value_grad, value_w.T)
    )
    attn_grads_packed, ffn_grads_local, normed_grad_one = lax.optimization_barrier(
        (
            packed_weight_grads(
                [normed_one, attn_grad_low],
                [(0, query_grad), (0, key_grad), (0, value_grad), (1, mixed)],
            ),
            ffn_grads_local,
            col_sum(normed_terms_one.astype(jnp.bfloat16)),
        )
    )
    attn_grads_local = lax.psum_scatter(attn_grads_packed, "row", scatter_dimension=0, tiled=True)
    rows_norm_grad, attn_gain_grad = norm_back(rows_wide, inv_one, attn_gain, normed_grad_one)
    rows_grad = resid_grad + rows_norm_grad
    input_share = lax.dynamic_slice_in_dim(rows_grad, col_start, quarter, 1).astype(jnp.bfloat16)
    query_result, key_result, value_result, output_result = split_columns(
        attn_grads_local.astype(jnp.float32), attn_widths
    )
    attn_gain_result, ffn_gain_result = row_scatter_sum(jnp.stack([attn_gain_grad, ffn_gain_grad]))
    gate_result, up_result, down_result = split_columns(
        ffn_grads_local.astype(jnp.float32), ffn_widths
    )
    back_pair = lax.all_to_all(
        jnp.stack([output_share, input_share])[:, arrived_slots],
        "row",
        split_axis=1,
        concat_axis=1,
        tiled=True,
    )
    back_rows, back_grads = back_pair[0], back_pair[1]
    restore = jnp.argsort(send_order)
    return (
        back_rows[restore],
        back_grads[restore],
        attn_gain_result,
        query_result,
        key_result,
        value_result,
        output_result,
        ffn_gain_result,
        gate_result,
        up_result,
        down_result,
    )

def solution(mesh):
    placed = (
        P("row", "col"),
        P("row", "col"),
        P("row"),
        P("row"),
        P(),
        P("row", "col"),
        P("row", "col"),
        P("row", "col"),
        P("row", "col"),
        P(),
        P("row", "col"),
        P("row", "col"),
        P("row", "col"),
    )
    return jax.shard_map(
        body,
        mesh=mesh,
        in_specs=placed,
        out_specs=(
            P("row", "col"),
            P("row", "col"),
            P("row"),
            P("row", "col"),
            P("row", "col"),
            P("row", "col"),
            P("row", "col"),
            P("row"),
            P("row", "col"),
            P("row", "col"),
            P("row", "col"),
        ),
        check_vma=False,
    )
```

```python
from functools import partial

import jax
import jax.numpy as jnp
from jax import lax
from jax.experimental import pallas as pl
from jax.experimental.pallas import tpu as pltpu
from jax.sharding import PartitionSpec as P

HEADS = 32
KV = 4
HD = 64


EPS = 1e-05
ROPE_BASE = 10000.0


def rope_tables(positions):
    half_width = HD // 2
    freqs = ROPE_BASE ** (-(jnp.arange(half_width, dtype=jnp.float32) * 2.0 / HD))
    angles = positions.astype(jnp.float32)[:, None] * freqs[None, :]
    return (jnp.cos(angles)[:, None, :], jnp.sin(angles)[:, None, :])


def rotate(values, cosine, sine):
    half_width = values.shape[-1] // 2
    first = values[..., :half_width]
    second = values[..., half_width:]
    return jnp.concatenate(
        [first * cosine - second * sine, second * cosine + first * sine], axis=-1
    )


def rotate_back(grads, cosine, sine):
    half_width = grads.shape[-1] // 2
    first = grads[..., :half_width]
    second = grads[..., half_width:]
    return jnp.concatenate(
        [first * cosine + second * sine, second * cosine - first * sine], axis=-1
    )


def positions_of(segment_ids):
    index = jnp.arange(segment_ids.shape[0], dtype=jnp.int32)
    change = jnp.concatenate([jnp.ones((1,), dtype=jnp.bool_), segment_ids[1:] != segment_ids[:-1]])
    starts = jnp.where(change, index, jnp.zeros_like(index))
    return index - lax.cummax(starts, axis=0)


def allowed_pairs(segment_ids):
    index = jnp.arange(segment_ids.shape[0], dtype=jnp.int32)
    return (segment_ids[:, None] == segment_ids[None, :]) & (index[None, :] <= index[:, None])


def rms_scale(values):
    return lax.rsqrt(jnp.mean(values * values, axis=-1, keepdims=True) + EPS)


def norm_back(values, inv_root, gain, grads):
    normed = values * inv_root
    scaled = grads * gain
    result = inv_root * (scaled - normed * jnp.mean(scaled * normed, axis=-1, keepdims=True))
    return (result, jnp.sum(grads * normed, axis=0))


def matmul(left, right):
    return jnp.dot(left, right, preferred_element_type=jnp.float32)


def head_scores(query_head, key_head, allowed, scale_factor):
    scores = matmul(query_head, key_head.T) * scale_factor
    return jnp.where(allowed, scores, -1e30)


def head_forward(inputs, key_heads, value_heads, allowed, scale_factor):
    query_head, kv_slot = inputs
    scores = head_scores(query_head, key_heads[kv_slot], allowed, scale_factor)
    peak = jnp.max(scores, axis=-1, keepdims=True)
    expo = jnp.exp(scores - peak)
    total = jnp.sum(expo, axis=-1, keepdims=True)
    probs = expo / total
    mixed = matmul(probs.astype(jnp.bfloat16), value_heads[kv_slot])
    return (mixed, (peak + jnp.log(total))[:, 0])


def head_backward(inputs, key_heads, value_heads, allowed, scale_factor):
    query_head, kv_slot, grad_head, log_total = inputs
    key_head = key_heads[kv_slot]
    value_head = value_heads[kv_slot]
    scores = head_scores(query_head, key_head, allowed, scale_factor)
    probs = jnp.exp(scores - log_total[:, None])
    prob_grad = matmul(grad_head, value_head.T)
    value_grad = matmul(probs.astype(jnp.bfloat16).T, grad_head)
    inner = jnp.sum(probs * prob_grad, axis=-1, keepdims=True)
    score_grad = (probs * (prob_grad - inner)).astype(jnp.bfloat16)
    query_grad = matmul(score_grad, key_head) * scale_factor
    key_grad = matmul(score_grad.T, query_head) * scale_factor
    return (query_grad, key_grad, value_grad)


def grouped(heads, kv_count):
    return heads.reshape(kv_count, heads.shape[0] // kv_count, *heads.shape[1:])


def group_scores(query_groups, key_heads, allowed, scale_factor):
    scores = (
        jnp.einsum("kgqd,kpd->kgqp", query_groups, key_heads, preferred_element_type=jnp.float32)
        * scale_factor
    )
    return jnp.where(allowed, scores, -1e30)


def attention_forward(query_heads, key_heads, value_heads, allowed, scale_factor):
    query_groups = grouped(query_heads, key_heads.shape[0])
    scores = group_scores(query_groups, key_heads, allowed, scale_factor)
    peak = jnp.max(scores, axis=-1, keepdims=True)
    expo = jnp.exp(scores - peak)
    total = jnp.sum(expo, axis=-1, keepdims=True)
    probs = expo / total
    mixed = jnp.einsum(
        "kgqp,kpd->kgqd", probs.astype(jnp.bfloat16), value_heads, preferred_element_type=jnp.float32
    )
    return mixed.reshape(query_heads.shape), (peak + jnp.log(total))[..., 0]


def attention_backward(
    query_heads, key_heads, value_heads, grad_heads, log_totals, allowed, scale_factor
):
    kv_count = key_heads.shape[0]
    query_groups = grouped(query_heads, kv_count)
    grad_groups = grouped(grad_heads, kv_count)
    scores = group_scores(query_groups, key_heads, allowed, scale_factor)
    probs = jnp.exp(scores - log_totals[..., None])
    prob_grad = jnp.einsum(
        "kgqd,kpd->kgqp", grad_groups, value_heads, preferred_element_type=jnp.float32
    )
    value_grad = jnp.einsum(
        "kgqp,kgqd->kpd", probs.astype(jnp.bfloat16), grad_groups, preferred_element_type=jnp.float32
    )
    inner = jnp.sum(probs * prob_grad, axis=-1, keepdims=True)
    score_grad = (probs * (prob_grad - inner)).astype(jnp.bfloat16)
    query_grad = (
        jnp.einsum("kgqp,kpd->kgqd", score_grad, key_heads, preferred_element_type=jnp.float32)
        * scale_factor
    )
    key_grad = (
        jnp.einsum("kgqp,kgqd->kpd", score_grad, query_groups, preferred_element_type=jnp.float32)
        * scale_factor
    )
    return query_grad.reshape(query_heads.shape), key_grad, value_grad


def row_scatter_sum(vectors):
    count = lax.axis_size("row")
    blocks = jnp.moveaxis(vectors.reshape(vectors.shape[0], count, -1), 1, 0)
    return jnp.sum(lax.all_to_all(blocks, "row", split_axis=0, concat_axis=0, tiled=True), axis=0)


GRAD_BLOCK = 128


def split_columns(packed, widths):
    pieces = []
    offset = 0
    for width in widths:
        pieces.append(packed[:, offset : offset + width])
        offset += width
    return pieces


def col_scatter(values):
    count = lax.axis_size("col")
    lead = values.shape[:-1]
    blocks = jnp.moveaxis(values.reshape(*lead, count, values.shape[-1] // count), -2, 0)
    received = lax.all_to_all(blocks, "col", split_axis=0, concat_axis=0, tiled=True)
    return jnp.sum(received.astype(jnp.float32), axis=0)


def col_gather(block):
    count = lax.axis_size("col")
    copies = jnp.broadcast_to(block[None], (count,) + block.shape)
    received = lax.all_to_all(copies, "col", split_axis=0, concat_axis=0, tiled=True)
    return jnp.moveaxis(received, 0, -2).reshape(*block.shape[:-1], count * block.shape[-1])


def col_sum(values):
    return col_gather(col_scatter(values).astype(jnp.bfloat16)).astype(jnp.float32)


def gather_rows(parts):
    return lax.all_gather(jnp.concatenate(parts, axis=1), "row", axis=0, tiled=True)


def grad_plain_kernel(select_ref, left_ref, right_ref, out_ref):
    out_ref[...] = jnp.dot(
        left_ref[0], right_ref[...], preferred_element_type=jnp.float32
    ).astype(out_ref.dtype)


def packed_weight_grads(lefts, segments):
    left_stack = jnp.stack([left.T for left in lefts])
    right = jnp.concatenate([seg for _, seg in segments], axis=1)
    column_owner = []
    for index, seg in segments:
        column_owner += [index] * seg.shape[1]
    assert len(column_owner) % GRAD_BLOCK == 0
    select = column_owner[::GRAD_BLOCK]
    assert column_owner == [owner for owner in select for _ in range(GRAD_BLOCK)]
    right_blocks = len(select)
    features, tokens = left_stack.shape[1], left_stack.shape[2]
    in_specs = [
        pl.BlockSpec((1, features, tokens), lambda j, sel: (sel[j], 0, 0)),
        pl.BlockSpec((tokens, GRAD_BLOCK), lambda j, sel: (0, jnp.minimum(j, right_blocks - 1))),
    ]
    return pl.pallas_call(
        grad_plain_kernel,
        out_shape=jax.ShapeDtypeStruct((features, len(select) * GRAD_BLOCK), jnp.bfloat16),
        grid_spec=pltpu.PrefetchScalarGridSpec(
            num_scalar_prefetch=1,
            grid=(len(select),),
            in_specs=in_specs,
            out_specs=pl.BlockSpec((features, GRAD_BLOCK), lambda j, sel: (0, j)),
        ),
    )(jnp.asarray(select, dtype=jnp.int32), left_stack, right)


def body(
    tokens,
    cotangent,
    destination,
    segment_ids,
    attn_gain,
    w_query,
    w_key,
    w_value,
    w_output,
    ffn_gain,
    w_gate,
    w_up,
    w_down,
):
    row_count = tokens.shape[0]
    quarter = tokens.shape[1]
    col_start = lax.axis_index("col") * quarter
    send_order = jnp.argsort(destination)
    slot_ids = destination[send_order] % row_count
    arrived_pair, arrived_slots = (
        lax.all_to_all(
            jnp.stack([tokens, cotangent])[:, send_order], "row", split_axis=1, concat_axis=1, tiled=True
        ),
        lax.all_to_all(slot_ids, "row", split_axis=0, concat_axis=0, tiled=True),
    )
    placing = jnp.argsort(arrived_slots)
    attn_widths = [w_query.shape[1], w_key.shape[1], w_value.shape[1], w_output.shape[1]]
    ffn_widths = [w_gate.shape[1], w_up.shape[1], w_down.shape[1]]
    attn_packed = gather_rows([w_query, w_key, w_value, w_output])
    ffn_packed = gather_rows([w_gate, w_up, w_down])
    placed_pair = arrived_pair[:, placing]
    full_rows = col_gather(placed_pair[0])
    query_w, key_w, value_w, output_w = split_columns(attn_packed, attn_widths)
    cosine, sine = rope_tables(positions_of(segment_ids))
    allowed = allowed_pairs(segment_ids)
    rows_wide = full_rows.astype(jnp.float32)
    inv_one = rms_scale(rows_wide)
    normed_one = (rows_wide * inv_one * attn_gain).astype(jnp.bfloat16)
    query = matmul(normed_one, query_w)
    key_raw = matmul(normed_one, key_w)
    value_raw = matmul(normed_one, value_w)
    query_heads_count = query.shape[1] // HD
    kv_count = key_raw.shape[1] // HD
    query_rot = (
        rotate(query.reshape(row_count, query_heads_count, HD), cosine, sine)
        .astype(jnp.bfloat16)
        .transpose(1, 0, 2)
    )
    key_rot = (
        rotate(key_raw.reshape(row_count, kv_count, HD), cosine, sine)
        .astype(jnp.bfloat16)
        .transpose(1, 0, 2)
    )
    value_heads = value_raw.astype(jnp.bfloat16).reshape(row_count, kv_count, HD).transpose(1, 0, 2)
    scale_factor = HD ** (-0.5)
    mixed_heads, log_totals = attention_forward(
        query_rot, key_rot, value_heads, allowed, scale_factor
    )
    mixed = (
        mixed_heads.transpose(1, 0, 2)
        .reshape(row_count, query_heads_count * HD)
        .astype(jnp.bfloat16)
    )
    attn_terms = matmul(mixed, output_w.T)
    placed_grads, attn_terms, ffn_packed = lax.optimization_barrier(
        (placed_pair[1], attn_terms, ffn_packed)
    )
    full_grads = col_gather(placed_grads)
    attn_full = lax.psum(attn_terms.astype(jnp.bfloat16), "col").astype(jnp.float32)
    resid = rows_wide + attn_full
    inv_two = rms_scale(resid)
    normed_two = (resid * inv_two * ffn_gain).astype(jnp.bfloat16)
    resid_part = lax.dynamic_slice_in_dim(resid, col_start, quarter, 1)
    gate_w, up_w, down_w = split_columns(ffn_packed, ffn_widths)
    gate = matmul(normed_two, gate_w)
    upper = matmul(normed_two, up_w)
    sigmoid_gate = jax.nn.sigmoid(gate)
    activ = (gate * sigmoid_gate * upper).astype(jnp.bfloat16)
    ffn_share_low = col_scatter(matmul(activ, down_w.T).astype(jnp.bfloat16)).astype(jnp.bfloat16)
    act_grad = matmul(full_grads, down_w)
    gate_grad = (act_grad * upper * sigmoid_gate * (1.0 + gate * (1.0 - sigmoid_gate))).astype(
        jnp.bfloat16
    )
    up_grad = (act_grad * gate * sigmoid_gate).astype(jnp.bfloat16)
    normed_terms_two = matmul(gate_grad, gate_w.T) + matmul(up_grad, up_w.T)
    normed_low_two, ffn_share_low = lax.optimization_barrier(
        (normed_terms_two.astype(jnp.bfloat16), ffn_share_low)
    )
    output_share = (resid_part + ffn_share_low.astype(jnp.float32)).astype(jnp.bfloat16)
    normed_grad_two = lax.psum(normed_low_two, "col").astype(jnp.float32)
    ffn_grads_packed = packed_weight_grads(
        [normed_two, full_grads], [(0, gate_grad), (0, up_grad), (1, activ)]
    )
    ffn_grads_packed, normed_grad_two = lax.optimization_barrier(
        (ffn_grads_packed, normed_grad_two)
    )
    resid_norm_grad, ffn_gain_grad = norm_back(resid, inv_two, ffn_gain, normed_grad_two)
    ffn_grads_local = lax.psum_scatter(ffn_grads_packed, "row", scatter_dimension=0, tiled=True)
    resid_grad = full_grads.astype(jnp.float32) + resid_norm_grad
    attn_grad_low = resid_grad.astype(jnp.bfloat16)
    mixed_grad = matmul(attn_grad_low, output_w).astype(jnp.bfloat16)
    mixed_grad_heads = mixed_grad.reshape(row_count, query_heads_count, HD).transpose(1, 0, 2)
    query_grads, key_grads, value_grads = attention_backward(
        query_rot, key_rot, value_heads, mixed_grad_heads, log_totals, allowed, scale_factor
    )
    query_grad = (
        rotate_back(query_grads.transpose(1, 0, 2), cosine, sine)
        .reshape(row_count, query_heads_count * HD)
        .astype(jnp.bfloat16)
    )
    key_sum = key_grads.transpose(1, 0, 2)
    key_grad = (
        rotate_back(key_sum, cosine, sine).reshape(row_count, kv_count * HD).astype(jnp.bfloat16)
    )
    value_sum = value_grads.transpose(1, 0, 2)
    value_grad = value_sum.reshape(row_count, kv_count * HD).astype(jnp.bfloat16)
    normed_terms_one = (
        matmul(query_grad, query_w.T) + matmul(key_grad, key_w.T) + matmul(value_grad, value_w.T)
    )
    attn_grads_packed, ffn_grads_local, normed_grad_one = lax.optimization_barrier(
        (
            packed_weight_grads(
                [normed_one, attn_grad_low],
                [(0, query_grad), (0, key_grad), (0, value_grad), (1, mixed)],
            ),
            ffn_grads_local,
            col_sum(normed_terms_one.astype(jnp.bfloat16)),
        )
    )
    attn_grads_local = lax.psum_scatter(attn_grads_packed, "row", scatter_dimension=0, tiled=True)
    rows_norm_grad, attn_gain_grad = norm_back(rows_wide, inv_one, attn_gain, normed_grad_one)
    rows_grad = resid_grad + rows_norm_grad
    input_share = lax.dynamic_slice_in_dim(rows_grad, col_start, quarter, 1).astype(jnp.bfloat16)
    query_result, key_result, value_result, output_result = split_columns(
        attn_grads_local.astype(jnp.float32), attn_widths
    )
    attn_gain_result, ffn_gain_result = row_scatter_sum(jnp.stack([attn_gain_grad, ffn_gain_grad]))
    gate_result, up_result, down_result = split_columns(
        ffn_grads_local.astype(jnp.float32), ffn_widths
    )
    back_pair = lax.all_to_all(
        jnp.stack([output_share, input_share])[:, arrived_slots],
        "row",
        split_axis=1,
        concat_axis=1,
        tiled=True,
    )
    back_rows, back_grads = back_pair[0], back_pair[1]
    restore = jnp.argsort(send_order)
    return (
        back_rows[restore],
        back_grads[restore],
        attn_gain_result,
        query_result,
        key_result,
        value_result,
        output_result,
        ffn_gain_result,
        gate_result,
        up_result,
        down_result,
    )

def solution(mesh):
    placed = (
        P("row", "col"),
        P("row", "col"),
        P("row"),
        P("row"),
        P(),
        P("row", "col"),
        P("row", "col"),
        P("row", "col"),
        P("row", "col"),
        P(),
        P("row", "col"),
        P("row", "col"),
        P("row", "col"),
    )
    return jax.shard_map(
        body,
        mesh=mesh,
        in_specs=placed,
        out_specs=(
            P("row", "col"),
            P("row", "col"),
            P("row"),
            P("row", "col"),
            P("row", "col"),
            P("row", "col"),
            P("row", "col"),
            P("row"),
            P("row", "col"),
            P("row", "col"),
            P("row", "col"),
        ),
        check_vma=False,
    )
```

```python
from functools import partial

import jax
import jax.numpy as jnp
from jax import lax
from jax.experimental import pallas as pl
from jax.experimental.pallas import tpu as pltpu
from jax.sharding import PartitionSpec as P

HEADS = 32
KV = 4
HD = 64


EPS = 1e-05
ROPE_BASE = 10000.0


def rope_tables(positions):
    half_width = HD // 2
    freqs = ROPE_BASE ** (-(jnp.arange(half_width, dtype=jnp.float32) * 2.0 / HD))
    angles = positions.astype(jnp.float32)[:, None] * freqs[None, :]
    return (jnp.cos(angles)[:, None, :], jnp.sin(angles)[:, None, :])


def rotate(values, cosine, sine):
    half_width = values.shape[-1] // 2
    first = values[..., :half_width]
    second = values[..., half_width:]
    return jnp.concatenate(
        [first * cosine - second * sine, second * cosine + first * sine], axis=-1
    )


def rotate_back(grads, cosine, sine):
    half_width = grads.shape[-1] // 2
    first = grads[..., :half_width]
    second = grads[..., half_width:]
    return jnp.concatenate(
        [first * cosine + second * sine, second * cosine - first * sine], axis=-1
    )


def positions_of(segment_ids):
    index = jnp.arange(segment_ids.shape[0], dtype=jnp.int32)
    change = jnp.concatenate([jnp.ones((1,), dtype=jnp.bool_), segment_ids[1:] != segment_ids[:-1]])
    starts = jnp.where(change, index, jnp.zeros_like(index))
    return index - lax.cummax(starts, axis=0)


def allowed_pairs(segment_ids):
    index = jnp.arange(segment_ids.shape[0], dtype=jnp.int32)
    return (segment_ids[:, None] == segment_ids[None, :]) & (index[None, :] <= index[:, None])


def rms_scale(values):
    return lax.rsqrt(jnp.mean(values * values, axis=-1, keepdims=True) + EPS)


def norm_back(values, inv_root, gain, grads):
    normed = values * inv_root
    scaled = grads * gain
    result = inv_root * (scaled - normed * jnp.mean(scaled * normed, axis=-1, keepdims=True))
    return (result, jnp.sum(grads * normed, axis=0))


def matmul(left, right):
    return jnp.dot(left, right, preferred_element_type=jnp.float32)


def head_scores(query_head, key_head, allowed, scale_factor):
    scores = matmul(query_head, key_head.T) * scale_factor
    return jnp.where(allowed, scores, -1e30)


def head_forward(inputs, key_heads, value_heads, allowed, scale_factor):
    query_head, kv_slot = inputs
    scores = head_scores(query_head, key_heads[kv_slot], allowed, scale_factor)
    peak = jnp.max(scores, axis=-1, keepdims=True)
    expo = jnp.exp(scores - peak)
    total = jnp.sum(expo, axis=-1, keepdims=True)
    probs = expo / total
    mixed = matmul(probs.astype(jnp.bfloat16), value_heads[kv_slot])
    return (mixed, (peak + jnp.log(total))[:, 0])


def head_backward(inputs, key_heads, value_heads, allowed, scale_factor):
    query_head, kv_slot, grad_head, log_total = inputs
    key_head = key_heads[kv_slot]
    value_head = value_heads[kv_slot]
    scores = head_scores(query_head, key_head, allowed, scale_factor)
    probs = jnp.exp(scores - log_total[:, None])
    prob_grad = matmul(grad_head, value_head.T)
    value_grad = matmul(probs.astype(jnp.bfloat16).T, grad_head)
    inner = jnp.sum(probs * prob_grad, axis=-1, keepdims=True)
    score_grad = (probs * (prob_grad - inner)).astype(jnp.bfloat16)
    query_grad = matmul(score_grad, key_head) * scale_factor
    key_grad = matmul(score_grad.T, query_head) * scale_factor
    return (query_grad, key_grad, value_grad)


def grouped(heads, kv_count):
    return heads.reshape(kv_count, heads.shape[0] // kv_count, *heads.shape[1:])


def group_scores(query_groups, key_heads, allowed, scale_factor):
    scores = (
        jnp.einsum("kgqd,kpd->kgqp", query_groups, key_heads, preferred_element_type=jnp.float32)
        * scale_factor
    )
    return jnp.where(allowed, scores, -1e30)


def attention_forward(query_heads, key_heads, value_heads, allowed, scale_factor):
    query_groups = grouped(query_heads, key_heads.shape[0])
    scores = group_scores(query_groups, key_heads, allowed, scale_factor)
    peak = jnp.max(scores, axis=-1, keepdims=True)
    expo = jnp.exp(scores - peak)
    total = jnp.sum(expo, axis=-1, keepdims=True)
    probs = expo / total
    mixed = jnp.einsum(
        "kgqp,kpd->kgqd", probs.astype(jnp.bfloat16), value_heads, preferred_element_type=jnp.float32
    )
    return mixed.reshape(query_heads.shape), (peak + jnp.log(total))[..., 0]


def attention_backward(
    query_heads, key_heads, value_heads, grad_heads, log_totals, allowed, scale_factor
):
    kv_count = key_heads.shape[0]
    query_groups = grouped(query_heads, kv_count)
    grad_groups = grouped(grad_heads, kv_count)
    scores = group_scores(query_groups, key_heads, allowed, scale_factor)
    probs = jnp.exp(scores - log_totals[..., None])
    prob_grad = jnp.einsum(
        "kgqd,kpd->kgqp", grad_groups, value_heads, preferred_element_type=jnp.float32
    )
    value_grad = jnp.einsum(
        "kgqp,kgqd->kpd", probs.astype(jnp.bfloat16), grad_groups, preferred_element_type=jnp.float32
    )
    inner = jnp.sum(probs * prob_grad, axis=-1, keepdims=True)
    score_grad = (probs * (prob_grad - inner)).astype(jnp.bfloat16)
    query_grad = (
        jnp.einsum("kgqp,kpd->kgqd", score_grad, key_heads, preferred_element_type=jnp.float32)
        * scale_factor
    )
    key_grad = (
        jnp.einsum("kgqp,kgqd->kpd", score_grad, query_groups, preferred_element_type=jnp.float32)
        * scale_factor
    )
    return query_grad.reshape(query_heads.shape), key_grad, value_grad


def row_scatter_sum(vectors):
    count = lax.axis_size("row")
    blocks = jnp.moveaxis(vectors.reshape(vectors.shape[0], count, -1), 1, 0)
    return jnp.sum(lax.all_to_all(blocks, "row", split_axis=0, concat_axis=0, tiled=True), axis=0)


GRAD_BLOCK = 128


def split_columns(packed, widths):
    pieces = []
    offset = 0
    for width in widths:
        pieces.append(packed[:, offset : offset + width])
        offset += width
    return pieces


def col_scatter(values):
    count = lax.axis_size("col")
    lead = values.shape[:-1]
    blocks = jnp.moveaxis(values.reshape(*lead, count, values.shape[-1] // count), -2, 0)
    received = lax.all_to_all(blocks, "col", split_axis=0, concat_axis=0, tiled=True)
    return jnp.sum(received.astype(jnp.float32), axis=0)


def col_gather(block):
    count = lax.axis_size("col")
    copies = jnp.broadcast_to(block[None], (count,) + block.shape)
    received = lax.all_to_all(copies, "col", split_axis=0, concat_axis=0, tiled=True)
    return jnp.moveaxis(received, 0, -2).reshape(*block.shape[:-1], count * block.shape[-1])


def col_sum(values):
    return col_gather(col_scatter(values).astype(jnp.bfloat16)).astype(jnp.float32)


def gather_rows(parts):
    return lax.all_gather(jnp.concatenate(parts, axis=1), "row", axis=0, tiled=True)


def grad_plain_kernel(select_ref, left_ref, right_ref, out_ref):
    out_ref[...] = jnp.dot(
        left_ref[0], right_ref[...], preferred_element_type=jnp.float32
    ).astype(out_ref.dtype)


def packed_weight_grads(lefts, segments):
    left_stack = jnp.stack([left.T for left in lefts])
    right = jnp.concatenate([seg for _, seg in segments], axis=1)
    column_owner = []
    for index, seg in segments:
        column_owner += [index] * seg.shape[1]
    assert len(column_owner) % GRAD_BLOCK == 0
    select = column_owner[::GRAD_BLOCK]
    assert column_owner == [owner for owner in select for _ in range(GRAD_BLOCK)]
    right_blocks = len(select)
    features, tokens = left_stack.shape[1], left_stack.shape[2]
    in_specs = [
        pl.BlockSpec((1, features, tokens), lambda j, sel: (sel[j], 0, 0)),
        pl.BlockSpec((tokens, GRAD_BLOCK), lambda j, sel: (0, jnp.minimum(j, right_blocks - 1))),
    ]
    return pl.pallas_call(
        grad_plain_kernel,
        out_shape=jax.ShapeDtypeStruct((features, len(select) * GRAD_BLOCK), jnp.bfloat16),
        grid_spec=pltpu.PrefetchScalarGridSpec(
            num_scalar_prefetch=1,
            grid=(len(select),),
            in_specs=in_specs,
            out_specs=pl.BlockSpec((features, GRAD_BLOCK), lambda j, sel: (0, j)),
        ),
    )(jnp.asarray(select, dtype=jnp.int32), left_stack, right)


def body(
    tokens,
    cotangent,
    destination,
    segment_ids,
    attn_gain,
    w_query,
    w_key,
    w_value,
    w_output,
    ffn_gain,
    w_gate,
    w_up,
    w_down,
):
    row_count = tokens.shape[0]
    quarter = tokens.shape[1]
    col_start = lax.axis_index("col") * quarter
    send_order = jnp.argsort(destination)
    slot_ids = destination[send_order] % row_count
    arrived_pair, arrived_slots = (
        lax.all_to_all(
            jnp.stack([tokens, cotangent])[:, send_order], "row", split_axis=1, concat_axis=1, tiled=True
        ),
        lax.all_to_all(slot_ids, "row", split_axis=0, concat_axis=0, tiled=True),
    )
    placing = jnp.argsort(arrived_slots)
    attn_widths = [w_query.shape[1], w_key.shape[1], w_value.shape[1], w_output.shape[1]]
    ffn_widths = [w_gate.shape[1], w_up.shape[1], w_down.shape[1]]
    weights_packed = gather_rows([w_query, w_key, w_value, w_output, w_gate, w_up, w_down])
    attn_packed = weights_packed[:, : sum(attn_widths)]
    ffn_packed = weights_packed[:, sum(attn_widths) :]
    placed_pair = arrived_pair[:, placing]
    full_rows = col_gather(placed_pair[0])
    full_grads = col_gather(placed_pair[1])
    query_w, key_w, value_w, output_w = split_columns(attn_packed, attn_widths)
    cosine, sine = rope_tables(positions_of(segment_ids))
    allowed = allowed_pairs(segment_ids)
    rows_wide = full_rows.astype(jnp.float32)
    inv_one = rms_scale(rows_wide)
    normed_one = (rows_wide * inv_one * attn_gain).astype(jnp.bfloat16)
    query = matmul(normed_one, query_w)
    key_raw = matmul(normed_one, key_w)
    value_raw = matmul(normed_one, value_w)
    query_heads_count = query.shape[1] // HD
    kv_count = key_raw.shape[1] // HD
    query_rot = (
        rotate(query.reshape(row_count, query_heads_count, HD), cosine, sine)
        .astype(jnp.bfloat16)
        .transpose(1, 0, 2)
    )
    key_rot = (
        rotate(key_raw.reshape(row_count, kv_count, HD), cosine, sine)
        .astype(jnp.bfloat16)
        .transpose(1, 0, 2)
    )
    value_heads = value_raw.astype(jnp.bfloat16).reshape(row_count, kv_count, HD).transpose(1, 0, 2)
    scale_factor = HD ** (-0.5)
    mixed_heads, log_totals = attention_forward(
        query_rot, key_rot, value_heads, allowed, scale_factor
    )
    mixed = (
        mixed_heads.transpose(1, 0, 2)
        .reshape(row_count, query_heads_count * HD)
        .astype(jnp.bfloat16)
    )
    attn_terms = matmul(mixed, output_w.T)
    attn_full = lax.psum(attn_terms.astype(jnp.bfloat16), "col").astype(jnp.float32)
    resid = rows_wide + attn_full
    inv_two = rms_scale(resid)
    normed_two = (resid * inv_two * ffn_gain).astype(jnp.bfloat16)
    resid_part = lax.dynamic_slice_in_dim(resid, col_start, quarter, 1)
    gate_w, up_w, down_w = split_columns(ffn_packed, ffn_widths)
    gate = matmul(normed_two, gate_w)
    upper = matmul(normed_two, up_w)
    sigmoid_gate = jax.nn.sigmoid(gate)
    activ = (gate * sigmoid_gate * upper).astype(jnp.bfloat16)
    ffn_share_low = col_scatter(matmul(activ, down_w.T).astype(jnp.bfloat16)).astype(jnp.bfloat16)
    act_grad = matmul(full_grads, down_w)
    gate_grad = (act_grad * upper * sigmoid_gate * (1.0 + gate * (1.0 - sigmoid_gate))).astype(
        jnp.bfloat16
    )
    up_grad = (act_grad * gate * sigmoid_gate).astype(jnp.bfloat16)
    normed_terms_two = matmul(gate_grad, gate_w.T) + matmul(up_grad, up_w.T)
    normed_low_two, ffn_share_low = lax.optimization_barrier(
        (normed_terms_two.astype(jnp.bfloat16), ffn_share_low)
    )
    output_share = (resid_part + ffn_share_low.astype(jnp.float32)).astype(jnp.bfloat16)
    normed_grad_two = lax.psum(normed_low_two, "col").astype(jnp.float32)
    ffn_grads_packed = packed_weight_grads(
        [normed_two, full_grads], [(0, gate_grad), (0, up_grad), (1, activ)]
    )
    ffn_grads_packed, normed_grad_two = lax.optimization_barrier(
        (ffn_grads_packed, normed_grad_two)
    )
    resid_norm_grad, ffn_gain_grad = norm_back(resid, inv_two, ffn_gain, normed_grad_two)
    ffn_grads_local = lax.psum_scatter(ffn_grads_packed, "row", scatter_dimension=0, tiled=True)
    resid_grad = full_grads.astype(jnp.float32) + resid_norm_grad
    attn_grad_low = resid_grad.astype(jnp.bfloat16)
    mixed_grad = matmul(attn_grad_low, output_w).astype(jnp.bfloat16)
    mixed_grad_heads = mixed_grad.reshape(row_count, query_heads_count, HD).transpose(1, 0, 2)
    query_grads, key_grads, value_grads = attention_backward(
        query_rot, key_rot, value_heads, mixed_grad_heads, log_totals, allowed, scale_factor
    )
    query_grad = (
        rotate_back(query_grads.transpose(1, 0, 2), cosine, sine)
        .reshape(row_count, query_heads_count * HD)
        .astype(jnp.bfloat16)
    )
    key_sum = key_grads.transpose(1, 0, 2)
    key_grad = (
        rotate_back(key_sum, cosine, sine).reshape(row_count, kv_count * HD).astype(jnp.bfloat16)
    )
    value_sum = value_grads.transpose(1, 0, 2)
    value_grad = value_sum.reshape(row_count, kv_count * HD).astype(jnp.bfloat16)
    normed_terms_one = (
        matmul(query_grad, query_w.T) + matmul(key_grad, key_w.T) + matmul(value_grad, value_w.T)
    )
    attn_grads_packed, ffn_grads_local, normed_grad_one = lax.optimization_barrier(
        (
            packed_weight_grads(
                [normed_one, attn_grad_low],
                [(0, query_grad), (0, key_grad), (0, value_grad), (1, mixed)],
            ),
            ffn_grads_local,
            col_sum(normed_terms_one.astype(jnp.bfloat16)),
        )
    )
    attn_grads_local = lax.psum_scatter(attn_grads_packed, "row", scatter_dimension=0, tiled=True)
    rows_norm_grad, attn_gain_grad = norm_back(rows_wide, inv_one, attn_gain, normed_grad_one)
    rows_grad = resid_grad + rows_norm_grad
    input_share = lax.dynamic_slice_in_dim(rows_grad, col_start, quarter, 1).astype(jnp.bfloat16)
    query_result, key_result, value_result, output_result = split_columns(
        attn_grads_local.astype(jnp.float32), attn_widths
    )
    attn_gain_result, ffn_gain_result = row_scatter_sum(jnp.stack([attn_gain_grad, ffn_gain_grad]))
    gate_result, up_result, down_result = split_columns(
        ffn_grads_local.astype(jnp.float32), ffn_widths
    )
    back_pair = lax.all_to_all(
        jnp.stack([output_share, input_share])[:, arrived_slots],
        "row",
        split_axis=1,
        concat_axis=1,
        tiled=True,
    )
    back_rows, back_grads = back_pair[0], back_pair[1]
    restore = jnp.argsort(send_order)
    return (
        back_rows[restore],
        back_grads[restore],
        attn_gain_result,
        query_result,
        key_result,
        value_result,
        output_result,
        ffn_gain_result,
        gate_result,
        up_result,
        down_result,
    )

def solution(mesh):
    placed = (
        P("row", "col"),
        P("row", "col"),
        P("row"),
        P("row"),
        P(),
        P("row", "col"),
        P("row", "col"),
        P("row", "col"),
        P("row", "col"),
        P(),
        P("row", "col"),
        P("row", "col"),
        P("row", "col"),
    )
    return jax.shard_map(
        body,
        mesh=mesh,
        in_specs=placed,
        out_specs=(
            P("row", "col"),
            P("row", "col"),
            P("row"),
            P("row", "col"),
            P("row", "col"),
            P("row", "col"),
            P("row", "col"),
            P("row"),
            P("row", "col"),
            P("row", "col"),
            P("row", "col"),
        ),
        check_vma=False,
    )
```

```python
from functools import partial

import jax
import jax.numpy as jnp
from jax import lax
from jax.experimental import pallas as pl
from jax.experimental.pallas import tpu as pltpu
from jax.sharding import PartitionSpec as P

HEADS = 32
KV = 4
HD = 64


EPS = 1e-05
ROPE_BASE = 10000.0


def rope_tables(positions):
    half_width = HD // 2
    freqs = ROPE_BASE ** (-(jnp.arange(half_width, dtype=jnp.float32) * 2.0 / HD))
    angles = positions.astype(jnp.float32)[:, None] * freqs[None, :]
    return (jnp.cos(angles)[:, None, :], jnp.sin(angles)[:, None, :])


def rotate(values, cosine, sine):
    half_width = values.shape[-1] // 2
    first = values[..., :half_width]
    second = values[..., half_width:]
    return jnp.concatenate(
        [first * cosine - second * sine, second * cosine + first * sine], axis=-1
    )


def rotate_back(grads, cosine, sine):
    half_width = grads.shape[-1] // 2
    first = grads[..., :half_width]
    second = grads[..., half_width:]
    return jnp.concatenate(
        [first * cosine + second * sine, second * cosine - first * sine], axis=-1
    )


def positions_of(segment_ids):
    index = jnp.arange(segment_ids.shape[0], dtype=jnp.int32)
    change = jnp.concatenate([jnp.ones((1,), dtype=jnp.bool_), segment_ids[1:] != segment_ids[:-1]])
    starts = jnp.where(change, index, jnp.zeros_like(index))
    return index - lax.cummax(starts, axis=0)


def allowed_pairs(segment_ids):
    index = jnp.arange(segment_ids.shape[0], dtype=jnp.int32)
    return (segment_ids[:, None] == segment_ids[None, :]) & (index[None, :] <= index[:, None])


def rms_scale(values):
    return lax.rsqrt(jnp.mean(values * values, axis=-1, keepdims=True) + EPS)


def norm_back(values, inv_root, gain, grads):
    normed = values * inv_root
    scaled = grads * gain
    result = inv_root * (scaled - normed * jnp.mean(scaled * normed, axis=-1, keepdims=True))
    return (result, jnp.sum(grads * normed, axis=0))


def matmul(left, right):
    return jnp.dot(left, right, preferred_element_type=jnp.float32)


def head_scores(query_head, key_head, allowed, scale_factor):
    scores = matmul(query_head, key_head.T) * scale_factor
    return jnp.where(allowed, scores, -1e30)


def head_forward(inputs, key_heads, value_heads, allowed, scale_factor):
    query_head, kv_slot = inputs
    scores = head_scores(query_head, key_heads[kv_slot], allowed, scale_factor)
    peak = jnp.max(scores, axis=-1, keepdims=True)
    expo = jnp.exp(scores - peak)
    total = jnp.sum(expo, axis=-1, keepdims=True)
    probs = expo / total
    mixed = matmul(probs.astype(jnp.bfloat16), value_heads[kv_slot])
    return (mixed, (peak + jnp.log(total))[:, 0])


def head_backward(inputs, key_heads, value_heads, allowed, scale_factor):
    query_head, kv_slot, grad_head, log_total = inputs
    key_head = key_heads[kv_slot]
    value_head = value_heads[kv_slot]
    scores = head_scores(query_head, key_head, allowed, scale_factor)
    probs = jnp.exp(scores - log_total[:, None])
    prob_grad = matmul(grad_head, value_head.T)
    value_grad = matmul(probs.astype(jnp.bfloat16).T, grad_head)
    inner = jnp.sum(probs * prob_grad, axis=-1, keepdims=True)
    score_grad = (probs * (prob_grad - inner)).astype(jnp.bfloat16)
    query_grad = matmul(score_grad, key_head) * scale_factor
    key_grad = matmul(score_grad.T, query_head) * scale_factor
    return (query_grad, key_grad, value_grad)


def grouped(heads, kv_count):
    return heads.reshape(kv_count, heads.shape[0] // kv_count, *heads.shape[1:])


def group_scores(query_groups, key_heads, allowed, scale_factor):
    scores = (
        jnp.einsum("kgqd,kpd->kgqp", query_groups, key_heads, preferred_element_type=jnp.float32)
        * scale_factor
    )
    return jnp.where(allowed, scores, -1e30)


def attention_forward(query_heads, key_heads, value_heads, allowed, scale_factor):
    query_groups = grouped(query_heads, key_heads.shape[0])
    scores = group_scores(query_groups, key_heads, allowed, scale_factor)
    peak = jnp.max(scores, axis=-1, keepdims=True)
    expo = jnp.exp(scores - peak)
    total = jnp.sum(expo, axis=-1, keepdims=True)
    probs = expo / total
    mixed = jnp.einsum(
        "kgqp,kpd->kgqd", probs.astype(jnp.bfloat16), value_heads, preferred_element_type=jnp.float32
    )
    return mixed.reshape(query_heads.shape), (peak + jnp.log(total))[..., 0]


def attention_backward(
    query_heads, key_heads, value_heads, grad_heads, log_totals, allowed, scale_factor
):
    kv_count = key_heads.shape[0]
    query_groups = grouped(query_heads, kv_count)
    grad_groups = grouped(grad_heads, kv_count)
    scores = group_scores(query_groups, key_heads, allowed, scale_factor)
    probs = jnp.exp(scores - log_totals[..., None])
    prob_grad = jnp.einsum(
        "kgqd,kpd->kgqp", grad_groups, value_heads, preferred_element_type=jnp.float32
    )
    value_grad = jnp.einsum(
        "kgqp,kgqd->kpd", probs.astype(jnp.bfloat16), grad_groups, preferred_element_type=jnp.float32
    )
    inner = jnp.sum(probs * prob_grad, axis=-1, keepdims=True)
    score_grad = (probs * (prob_grad - inner)).astype(jnp.bfloat16)
    query_grad = (
        jnp.einsum("kgqp,kpd->kgqd", score_grad, key_heads, preferred_element_type=jnp.float32)
        * scale_factor
    )
    key_grad = (
        jnp.einsum("kgqp,kgqd->kpd", score_grad, query_groups, preferred_element_type=jnp.float32)
        * scale_factor
    )
    return query_grad.reshape(query_heads.shape), key_grad, value_grad


def row_scatter_sum(vectors):
    count = lax.axis_size("row")
    blocks = jnp.moveaxis(vectors.reshape(vectors.shape[0], count, -1), 1, 0)
    return jnp.sum(lax.all_to_all(blocks, "row", split_axis=0, concat_axis=0, tiled=True), axis=0)


GRAD_BLOCK = 128


def split_columns(packed, widths):
    pieces = []
    offset = 0
    for width in widths:
        pieces.append(packed[:, offset : offset + width])
        offset += width
    return pieces


def col_scatter(values):
    count = lax.axis_size("col")
    lead = values.shape[:-1]
    blocks = jnp.moveaxis(values.reshape(*lead, count, values.shape[-1] // count), -2, 0)
    received = lax.all_to_all(blocks, "col", split_axis=0, concat_axis=0, tiled=True)
    return jnp.sum(received.astype(jnp.float32), axis=0)


def col_gather(block):
    count = lax.axis_size("col")
    copies = jnp.broadcast_to(block[None], (count,) + block.shape)
    received = lax.all_to_all(copies, "col", split_axis=0, concat_axis=0, tiled=True)
    return jnp.moveaxis(received, 0, -2).reshape(*block.shape[:-1], count * block.shape[-1])


def col_sum(values):
    return col_gather(col_scatter(values).astype(jnp.bfloat16)).astype(jnp.float32)


def gather_rows(parts):
    return lax.all_gather(jnp.concatenate(parts, axis=1), "row", axis=0, tiled=True)


def grad_plain_kernel(select_ref, left_ref, right_ref, out_ref):
    out_ref[...] = jnp.dot(
        left_ref[0], right_ref[...], preferred_element_type=jnp.float32
    ).astype(out_ref.dtype)


def packed_weight_grads(lefts, segments):
    left_stack = jnp.stack([left.T for left in lefts])
    right = jnp.concatenate([seg for _, seg in segments], axis=1)
    column_owner = []
    for index, seg in segments:
        column_owner += [index] * seg.shape[1]
    assert len(column_owner) % GRAD_BLOCK == 0
    select = column_owner[::GRAD_BLOCK]
    assert column_owner == [owner for owner in select for _ in range(GRAD_BLOCK)]
    right_blocks = len(select)
    features, tokens = left_stack.shape[1], left_stack.shape[2]
    in_specs = [
        pl.BlockSpec((1, features, tokens), lambda j, sel: (sel[j], 0, 0)),
        pl.BlockSpec((tokens, GRAD_BLOCK), lambda j, sel: (0, jnp.minimum(j, right_blocks - 1))),
    ]
    return pl.pallas_call(
        grad_plain_kernel,
        out_shape=jax.ShapeDtypeStruct((features, len(select) * GRAD_BLOCK), jnp.bfloat16),
        grid_spec=pltpu.PrefetchScalarGridSpec(
            num_scalar_prefetch=1,
            grid=(len(select),),
            in_specs=in_specs,
            out_specs=pl.BlockSpec((features, GRAD_BLOCK), lambda j, sel: (0, j)),
        ),
    )(jnp.asarray(select, dtype=jnp.int32), left_stack, right)


def body(
    tokens,
    cotangent,
    destination,
    segment_ids,
    attn_gain,
    w_query,
    w_key,
    w_value,
    w_output,
    ffn_gain,
    w_gate,
    w_up,
    w_down,
):
    row_count = tokens.shape[0]
    quarter = tokens.shape[1]
    col_start = lax.axis_index("col") * quarter
    send_order = jnp.argsort(destination)
    slot_ids = destination[send_order] % row_count
    arrived_pair, arrived_slots = (
        lax.all_to_all(
            jnp.stack([tokens, cotangent])[:, send_order], "row", split_axis=1, concat_axis=1, tiled=True
        ),
        lax.all_to_all(slot_ids, "row", split_axis=0, concat_axis=0, tiled=True),
    )
    placing = jnp.argsort(arrived_slots)
    attn_widths = [w_query.shape[1], w_key.shape[1], w_value.shape[1], w_output.shape[1]]
    ffn_widths = [w_gate.shape[1], w_up.shape[1], w_down.shape[1]]
    weights_packed = gather_rows([w_query, w_key, w_value, w_output, w_gate, w_up, w_down])
    attn_packed = weights_packed[:, : sum(attn_widths)]
    ffn_packed = weights_packed[:, sum(attn_widths) :]
    placed_pair = arrived_pair[:, placing]
    full_rows = col_gather(placed_pair[0])
    full_grads = col_gather(placed_pair[1])
    query_w, key_w, value_w, output_w = split_columns(attn_packed, attn_widths)
    cosine, sine = rope_tables(positions_of(segment_ids))
    allowed = allowed_pairs(segment_ids)
    rows_wide = full_rows.astype(jnp.float32)
    inv_one = rms_scale(rows_wide)
    normed_one = (rows_wide * inv_one * attn_gain).astype(jnp.bfloat16)
    query = matmul(normed_one, query_w)
    key_raw = matmul(normed_one, key_w)
    value_raw = matmul(normed_one, value_w)
    query_heads_count = query.shape[1] // HD
    kv_count = key_raw.shape[1] // HD
    query_rot = (
        rotate(query.reshape(row_count, query_heads_count, HD), cosine, sine)
        .astype(jnp.bfloat16)
        .transpose(1, 0, 2)
    )
    key_rot = (
        rotate(key_raw.reshape(row_count, kv_count, HD), cosine, sine)
        .astype(jnp.bfloat16)
        .transpose(1, 0, 2)
    )
    value_heads = value_raw.astype(jnp.bfloat16).reshape(row_count, kv_count, HD).transpose(1, 0, 2)
    scale_factor = HD ** (-0.5)
    mixed_heads, log_totals = attention_forward(
        query_rot, key_rot, value_heads, allowed, scale_factor
    )
    mixed = (
        mixed_heads.transpose(1, 0, 2)
        .reshape(row_count, query_heads_count * HD)
        .astype(jnp.bfloat16)
    )
    attn_terms = matmul(mixed, output_w.T)
    attn_full = lax.psum(attn_terms.astype(jnp.bfloat16), "col").astype(jnp.float32)
    resid = rows_wide + attn_full
    inv_two = rms_scale(resid)
    normed_two = (resid * inv_two * ffn_gain).astype(jnp.bfloat16)
    resid_part = lax.dynamic_slice_in_dim(resid, col_start, quarter, 1)
    gate_w, up_w, down_w = split_columns(ffn_packed, ffn_widths)
    gate = matmul(normed_two, gate_w)
    upper = matmul(normed_two, up_w)
    sigmoid_gate = jax.nn.sigmoid(gate)
    activ = (gate * sigmoid_gate * upper).astype(jnp.bfloat16)
    ffn_share_low = col_scatter(matmul(activ, down_w.T).astype(jnp.bfloat16)).astype(jnp.bfloat16)
    act_grad = matmul(full_grads, down_w)
    gate_grad = (act_grad * upper * sigmoid_gate * (1.0 + gate * (1.0 - sigmoid_gate))).astype(
        jnp.bfloat16
    )
    up_grad = (act_grad * gate * sigmoid_gate).astype(jnp.bfloat16)
    normed_terms_two = matmul(gate_grad, gate_w.T) + matmul(up_grad, up_w.T)
    output_share = (resid_part + ffn_share_low.astype(jnp.float32)).astype(jnp.bfloat16)
    ffn_grads_packed = packed_weight_grads(
        [normed_two, full_grads], [(0, gate_grad), (0, up_grad), (1, activ)]
    )
    normed_low_two, ffn_grads_packed = lax.optimization_barrier(
        (normed_terms_two.astype(jnp.bfloat16), ffn_grads_packed)
    )
    normed_grad_two = col_sum(normed_low_two)
    resid_norm_grad, ffn_gain_grad = norm_back(resid, inv_two, ffn_gain, normed_grad_two)
    ffn_grads_local = lax.psum_scatter(ffn_grads_packed, "row", scatter_dimension=0, tiled=True)
    resid_grad = full_grads.astype(jnp.float32) + resid_norm_grad
    attn_grad_low = resid_grad.astype(jnp.bfloat16)
    mixed_grad = matmul(attn_grad_low, output_w).astype(jnp.bfloat16)
    mixed_grad_heads = mixed_grad.reshape(row_count, query_heads_count, HD).transpose(1, 0, 2)
    query_grads, key_grads, value_grads = attention_backward(
        query_rot, key_rot, value_heads, mixed_grad_heads, log_totals, allowed, scale_factor
    )
    query_grad = (
        rotate_back(query_grads.transpose(1, 0, 2), cosine, sine)
        .reshape(row_count, query_heads_count * HD)
        .astype(jnp.bfloat16)
    )
    key_sum = key_grads.transpose(1, 0, 2)
    key_grad = (
        rotate_back(key_sum, cosine, sine).reshape(row_count, kv_count * HD).astype(jnp.bfloat16)
    )
    value_sum = value_grads.transpose(1, 0, 2)
    value_grad = value_sum.reshape(row_count, kv_count * HD).astype(jnp.bfloat16)
    normed_terms_one = (
        matmul(query_grad, query_w.T) + matmul(key_grad, key_w.T) + matmul(value_grad, value_w.T)
    )
    attn_grads_packed, ffn_grads_local, normed_grad_one = lax.optimization_barrier(
        (
            packed_weight_grads(
                [normed_one, attn_grad_low],
                [(0, query_grad), (0, key_grad), (0, value_grad), (1, mixed)],
            ),
            ffn_grads_local,
            col_sum(normed_terms_one.astype(jnp.bfloat16)),
        )
    )
    attn_grads_local = lax.psum_scatter(attn_grads_packed, "row", scatter_dimension=0, tiled=True)
    rows_norm_grad, attn_gain_grad = norm_back(rows_wide, inv_one, attn_gain, normed_grad_one)
    rows_grad = resid_grad + rows_norm_grad
    input_share = lax.dynamic_slice_in_dim(rows_grad, col_start, quarter, 1).astype(jnp.bfloat16)
    query_result, key_result, value_result, output_result = split_columns(
        attn_grads_local.astype(jnp.float32), attn_widths
    )
    attn_gain_result, ffn_gain_result = row_scatter_sum(jnp.stack([attn_gain_grad, ffn_gain_grad]))
    gate_result, up_result, down_result = split_columns(
        ffn_grads_local.astype(jnp.float32), ffn_widths
    )
    back_pair = lax.all_to_all(
        jnp.stack([output_share, input_share])[:, arrived_slots],
        "row",
        split_axis=1,
        concat_axis=1,
        tiled=True,
    )
    back_rows, back_grads = back_pair[0], back_pair[1]
    restore = jnp.argsort(send_order)
    return (
        back_rows[restore],
        back_grads[restore],
        attn_gain_result,
        query_result,
        key_result,
        value_result,
        output_result,
        ffn_gain_result,
        gate_result,
        up_result,
        down_result,
    )

def solution(mesh):
    placed = (
        P("row", "col"),
        P("row", "col"),
        P("row"),
        P("row"),
        P(),
        P("row", "col"),
        P("row", "col"),
        P("row", "col"),
        P("row", "col"),
        P(),
        P("row", "col"),
        P("row", "col"),
        P("row", "col"),
    )
    return jax.shard_map(
        body,
        mesh=mesh,
        in_specs=placed,
        out_specs=(
            P("row", "col"),
            P("row", "col"),
            P("row"),
            P("row", "col"),
            P("row", "col"),
            P("row", "col"),
            P("row", "col"),
            P("row"),
            P("row", "col"),
            P("row", "col"),
            P("row", "col"),
        ),
        check_vma=False,
    )
```

```python
from functools import partial

import jax
import jax.numpy as jnp
from jax import lax
from jax.experimental import pallas as pl
from jax.experimental.pallas import tpu as pltpu
from jax.sharding import PartitionSpec as P

HEADS = 32
KV = 4
HD = 64


EPS = 1e-05
ROPE_BASE = 10000.0


def rope_tables(positions):
    half_width = HD // 2
    freqs = ROPE_BASE ** (-(jnp.arange(half_width, dtype=jnp.float32) * 2.0 / HD))
    angles = positions.astype(jnp.float32)[:, None] * freqs[None, :]
    return (jnp.cos(angles)[:, None, :], jnp.sin(angles)[:, None, :])


def rotate(values, cosine, sine):
    half_width = values.shape[-1] // 2
    first = values[..., :half_width]
    second = values[..., half_width:]
    return jnp.concatenate(
        [first * cosine - second * sine, second * cosine + first * sine], axis=-1
    )


def rotate_back(grads, cosine, sine):
    half_width = grads.shape[-1] // 2
    first = grads[..., :half_width]
    second = grads[..., half_width:]
    return jnp.concatenate(
        [first * cosine + second * sine, second * cosine - first * sine], axis=-1
    )


def positions_of(segment_ids):
    index = jnp.arange(segment_ids.shape[0], dtype=jnp.int32)
    change = jnp.concatenate([jnp.ones((1,), dtype=jnp.bool_), segment_ids[1:] != segment_ids[:-1]])
    starts = jnp.where(change, index, jnp.zeros_like(index))
    return index - lax.cummax(starts, axis=0)


def allowed_pairs(segment_ids):
    index = jnp.arange(segment_ids.shape[0], dtype=jnp.int32)
    return (segment_ids[:, None] == segment_ids[None, :]) & (index[None, :] <= index[:, None])


def rms_scale(values):
    return lax.rsqrt(jnp.mean(values * values, axis=-1, keepdims=True) + EPS)


def norm_back(values, inv_root, gain, grads):
    normed = values * inv_root
    scaled = grads * gain
    result = inv_root * (scaled - normed * jnp.mean(scaled * normed, axis=-1, keepdims=True))
    return (result, jnp.sum(grads * normed, axis=0))


def matmul(left, right):
    return jnp.dot(left, right, preferred_element_type=jnp.float32)


def head_scores(query_head, key_head, allowed, scale_factor):
    scores = matmul(query_head, key_head.T) * scale_factor
    return jnp.where(allowed, scores, -1e30)


def head_forward(inputs, key_heads, value_heads, allowed, scale_factor):
    query_head, kv_slot = inputs
    scores = head_scores(query_head, key_heads[kv_slot], allowed, scale_factor)
    peak = jnp.max(scores, axis=-1, keepdims=True)
    expo = jnp.exp(scores - peak)
    total = jnp.sum(expo, axis=-1, keepdims=True)
    probs = expo / total
    mixed = matmul(probs.astype(jnp.bfloat16), value_heads[kv_slot])
    return (mixed, (peak + jnp.log(total))[:, 0])


def head_backward(inputs, key_heads, value_heads, allowed, scale_factor):
    query_head, kv_slot, grad_head, log_total = inputs
    key_head = key_heads[kv_slot]
    value_head = value_heads[kv_slot]
    scores = head_scores(query_head, key_head, allowed, scale_factor)
    probs = jnp.exp(scores - log_total[:, None])
    prob_grad = matmul(grad_head, value_head.T)
    value_grad = matmul(probs.astype(jnp.bfloat16).T, grad_head)
    inner = jnp.sum(probs * prob_grad, axis=-1, keepdims=True)
    score_grad = (probs * (prob_grad - inner)).astype(jnp.bfloat16)
    query_grad = matmul(score_grad, key_head) * scale_factor
    key_grad = matmul(score_grad.T, query_head) * scale_factor
    return (query_grad, key_grad, value_grad)


def grouped(heads, kv_count):
    return heads.reshape(kv_count, heads.shape[0] // kv_count, *heads.shape[1:])


def group_scores(query_groups, key_heads, allowed, scale_factor):
    scores = (
        jnp.einsum("kgqd,kpd->kgqp", query_groups, key_heads, preferred_element_type=jnp.float32)
        * scale_factor
    )
    return jnp.where(allowed, scores, -1e30)


def attention_forward(query_heads, key_heads, value_heads, allowed, scale_factor):
    query_groups = grouped(query_heads, key_heads.shape[0])
    scores = group_scores(query_groups, key_heads, allowed, scale_factor)
    peak = jnp.max(scores, axis=-1, keepdims=True)
    expo = jnp.exp(scores - peak)
    total = jnp.sum(expo, axis=-1, keepdims=True)
    probs = expo / total
    mixed = jnp.einsum(
        "kgqp,kpd->kgqd", probs.astype(jnp.bfloat16), value_heads, preferred_element_type=jnp.float32
    )
    return mixed.reshape(query_heads.shape), (peak + jnp.log(total))[..., 0]


def attention_backward(
    query_heads, key_heads, value_heads, grad_heads, log_totals, allowed, scale_factor
):
    kv_count = key_heads.shape[0]
    query_groups = grouped(query_heads, kv_count)
    grad_groups = grouped(grad_heads, kv_count)
    scores = group_scores(query_groups, key_heads, allowed, scale_factor)
    probs = jnp.exp(scores - log_totals[..., None])
    prob_grad = jnp.einsum(
        "kgqd,kpd->kgqp", grad_groups, value_heads, preferred_element_type=jnp.float32
    )
    value_grad = jnp.einsum(
        "kgqp,kgqd->kpd", probs.astype(jnp.bfloat16), grad_groups, preferred_element_type=jnp.float32
    )
    inner = jnp.sum(probs * prob_grad, axis=-1, keepdims=True)
    score_grad = (probs * (prob_grad - inner)).astype(jnp.bfloat16)
    query_grad = (
        jnp.einsum("kgqp,kpd->kgqd", score_grad, key_heads, preferred_element_type=jnp.float32)
        * scale_factor
    )
    key_grad = (
        jnp.einsum("kgqp,kgqd->kpd", score_grad, query_groups, preferred_element_type=jnp.float32)
        * scale_factor
    )
    return query_grad.reshape(query_heads.shape), key_grad, value_grad


def row_scatter_sum(vectors):
    count = lax.axis_size("row")
    blocks = jnp.moveaxis(vectors.reshape(vectors.shape[0], count, -1), 1, 0)
    return jnp.sum(lax.all_to_all(blocks, "row", split_axis=0, concat_axis=0, tiled=True), axis=0)


GRAD_BLOCK = 128


def split_columns(packed, widths):
    pieces = []
    offset = 0
    for width in widths:
        pieces.append(packed[:, offset : offset + width])
        offset += width
    return pieces


def col_scatter(values):
    count = lax.axis_size("col")
    lead = values.shape[:-1]
    blocks = jnp.moveaxis(values.reshape(*lead, count, values.shape[-1] // count), -2, 0)
    received = lax.all_to_all(blocks, "col", split_axis=0, concat_axis=0, tiled=True)
    return jnp.sum(received.astype(jnp.float32), axis=0)


def col_gather(block):
    count = lax.axis_size("col")
    copies = jnp.broadcast_to(block[None], (count,) + block.shape)
    received = lax.all_to_all(copies, "col", split_axis=0, concat_axis=0, tiled=True)
    return jnp.moveaxis(received, 0, -2).reshape(*block.shape[:-1], count * block.shape[-1])


def col_sum(values):
    return col_gather(col_scatter(values).astype(jnp.bfloat16)).astype(jnp.float32)


def gather_rows(parts):
    return lax.all_gather(jnp.concatenate(parts, axis=1), "row", axis=0, tiled=True)


def grad_plain_kernel(select_ref, left_ref, right_ref, out_ref):
    out_ref[...] = jnp.dot(
        left_ref[0], right_ref[...], preferred_element_type=jnp.float32
    ).astype(out_ref.dtype)


def grad_tail_kernel(select_ref, left_ref, right_ref, tail_ref, out_ref):
    step = pl.program_id(0)
    last = pl.num_programs(0) - 1

    @pl.when(step < last)
    def _():
        grad_plain_kernel(select_ref, left_ref, right_ref, out_ref)

    @pl.when(step == last)
    def _():
        out_ref[...] = tail_ref[...]


def gain_tail_of(gain_grads):
    columns = [grad[:, None] for grad in gain_grads]
    padding = jnp.zeros((gain_grads[0].shape[0], GRAD_BLOCK - len(columns)), jnp.float32)
    return jnp.concatenate(columns + [padding], axis=1).astype(jnp.bfloat16)


def packed_weight_grads(lefts, segments, tail=None):
    left_stack = jnp.stack([left.T for left in lefts])
    right = jnp.concatenate([seg for _, seg in segments], axis=1)
    column_owner = []
    for index, seg in segments:
        column_owner += [index] * seg.shape[1]
    assert len(column_owner) % GRAD_BLOCK == 0
    select = column_owner[::GRAD_BLOCK]
    assert column_owner == [owner for owner in select for _ in range(GRAD_BLOCK)]
    right_blocks = len(select)
    features, tokens = left_stack.shape[1], left_stack.shape[2]
    in_specs = [
        pl.BlockSpec((1, features, tokens), lambda j, sel: (sel[j], 0, 0)),
        pl.BlockSpec((tokens, GRAD_BLOCK), lambda j, sel: (0, jnp.minimum(j, right_blocks - 1))),
    ]
    operands = [left_stack, right]
    kernel = grad_plain_kernel
    if tail is not None:
        select.append(select[-1])
        in_specs.append(pl.BlockSpec((features, GRAD_BLOCK), lambda j, sel: (0, 0)))
        operands.append(tail)
        kernel = grad_tail_kernel
    return pl.pallas_call(
        kernel,
        out_shape=jax.ShapeDtypeStruct((features, len(select) * GRAD_BLOCK), jnp.bfloat16),
        grid_spec=pltpu.PrefetchScalarGridSpec(
            num_scalar_prefetch=1,
            grid=(len(select),),
            in_specs=in_specs,
            out_specs=pl.BlockSpec((features, GRAD_BLOCK), lambda j, sel: (0, j)),
        ),
    )(jnp.asarray(select, dtype=jnp.int32), *operands)


def body(
    tokens,
    cotangent,
    destination,
    segment_ids,
    attn_gain,
    w_query,
    w_key,
    w_value,
    w_output,
    ffn_gain,
    w_gate,
    w_up,
    w_down,
):
    row_count = tokens.shape[0]
    quarter = tokens.shape[1]
    col_start = lax.axis_index("col") * quarter
    send_order = jnp.argsort(destination)
    slot_ids = destination[send_order] % row_count
    arrived_pair, arrived_slots = (
        lax.all_to_all(
            jnp.stack([tokens, cotangent])[:, send_order], "row", split_axis=1, concat_axis=1, tiled=True
        ),
        lax.all_to_all(slot_ids, "row", split_axis=0, concat_axis=0, tiled=True),
    )
    placing = jnp.argsort(arrived_slots)
    attn_widths = [w_query.shape[1], w_key.shape[1], w_value.shape[1], w_output.shape[1]]
    ffn_widths = [w_gate.shape[1], w_up.shape[1], w_down.shape[1]]
    weights_packed = gather_rows([w_query, w_key, w_value, w_output, w_gate, w_up, w_down])
    attn_packed = weights_packed[:, : sum(attn_widths)]
    ffn_packed = weights_packed[:, sum(attn_widths) :]
    placed_pair = arrived_pair[:, placing]
    full_rows = col_gather(placed_pair[0])
    full_grads = col_gather(placed_pair[1])
    query_w, key_w, value_w, output_w = split_columns(attn_packed, attn_widths)
    cosine, sine = rope_tables(positions_of(segment_ids))
    allowed = allowed_pairs(segment_ids)
    rows_wide = full_rows.astype(jnp.float32)
    inv_one = rms_scale(rows_wide)
    normed_one = (rows_wide * inv_one * attn_gain).astype(jnp.bfloat16)
    query = matmul(normed_one, query_w)
    key_raw = matmul(normed_one, key_w)
    value_raw = matmul(normed_one, value_w)
    query_heads_count = query.shape[1] // HD
    kv_count = key_raw.shape[1] // HD
    query_rot = (
        rotate(query.reshape(row_count, query_heads_count, HD), cosine, sine)
        .astype(jnp.bfloat16)
        .transpose(1, 0, 2)
    )
    key_rot = (
        rotate(key_raw.reshape(row_count, kv_count, HD), cosine, sine)
        .astype(jnp.bfloat16)
        .transpose(1, 0, 2)
    )
    value_heads = value_raw.astype(jnp.bfloat16).reshape(row_count, kv_count, HD).transpose(1, 0, 2)
    scale_factor = HD ** (-0.5)
    mixed_heads, log_totals = attention_forward(
        query_rot, key_rot, value_heads, allowed, scale_factor
    )
    mixed = (
        mixed_heads.transpose(1, 0, 2)
        .reshape(row_count, query_heads_count * HD)
        .astype(jnp.bfloat16)
    )
    attn_terms = matmul(mixed, output_w.T)
    attn_full = lax.psum(attn_terms.astype(jnp.bfloat16), "col").astype(jnp.float32)
    resid = rows_wide + attn_full
    inv_two = rms_scale(resid)
    normed_two = (resid * inv_two * ffn_gain).astype(jnp.bfloat16)
    resid_part = lax.dynamic_slice_in_dim(resid, col_start, quarter, 1)
    gate_w, up_w, down_w = split_columns(ffn_packed, ffn_widths)
    gate = matmul(normed_two, gate_w)
    upper = matmul(normed_two, up_w)
    sigmoid_gate = jax.nn.sigmoid(gate)
    activ = (gate * sigmoid_gate * upper).astype(jnp.bfloat16)
    ffn_share_low = col_scatter(matmul(activ, down_w.T).astype(jnp.bfloat16)).astype(jnp.bfloat16)
    act_grad = matmul(full_grads, down_w)
    gate_grad = (act_grad * upper * sigmoid_gate * (1.0 + gate * (1.0 - sigmoid_gate))).astype(
        jnp.bfloat16
    )
    up_grad = (act_grad * gate * sigmoid_gate).astype(jnp.bfloat16)
    normed_terms_two = matmul(gate_grad, gate_w.T) + matmul(up_grad, up_w.T)
    output_share = (resid_part + ffn_share_low.astype(jnp.float32)).astype(jnp.bfloat16)
    ffn_grads_packed = packed_weight_grads(
        [normed_two, full_grads], [(0, gate_grad), (0, up_grad), (1, activ)]
    )
    normed_low_two, ffn_grads_packed, output_share = lax.optimization_barrier(
        (normed_terms_two.astype(jnp.bfloat16), ffn_grads_packed, output_share)
    )
    back_rows = lax.all_to_all(
        output_share[arrived_slots], "row", split_axis=0, concat_axis=0, tiled=True
    )
    normed_grad_two = col_sum(normed_low_two)
    resid_norm_grad, ffn_gain_grad = norm_back(resid, inv_two, ffn_gain, normed_grad_two)
    ffn_grads_local = lax.psum_scatter(ffn_grads_packed, "row", scatter_dimension=0, tiled=True)
    resid_grad = full_grads.astype(jnp.float32) + resid_norm_grad
    attn_grad_low = resid_grad.astype(jnp.bfloat16)
    mixed_grad = matmul(attn_grad_low, output_w).astype(jnp.bfloat16)
    mixed_grad_heads = mixed_grad.reshape(row_count, query_heads_count, HD).transpose(1, 0, 2)
    query_grads, key_grads, value_grads = attention_backward(
        query_rot, key_rot, value_heads, mixed_grad_heads, log_totals, allowed, scale_factor
    )
    query_grad = (
        rotate_back(query_grads.transpose(1, 0, 2), cosine, sine)
        .reshape(row_count, query_heads_count * HD)
        .astype(jnp.bfloat16)
    )
    key_sum = key_grads.transpose(1, 0, 2)
    key_grad = (
        rotate_back(key_sum, cosine, sine).reshape(row_count, kv_count * HD).astype(jnp.bfloat16)
    )
    value_sum = value_grads.transpose(1, 0, 2)
    value_grad = value_sum.reshape(row_count, kv_count * HD).astype(jnp.bfloat16)
    normed_terms_one = (
        matmul(query_grad, query_w.T) + matmul(key_grad, key_w.T) + matmul(value_grad, value_w.T)
    )
    normed_grad_one, ffn_grads_local, back_rows = lax.optimization_barrier(
        (col_sum(normed_terms_one.astype(jnp.bfloat16)), ffn_grads_local, back_rows)
    )
    rows_norm_grad, attn_gain_grad = norm_back(rows_wide, inv_one, attn_gain, normed_grad_one)
    attn_grads_local = lax.psum_scatter(
        packed_weight_grads(
            [normed_one, attn_grad_low],
            [(0, query_grad), (0, key_grad), (0, value_grad), (1, mixed)],
            gain_tail_of([attn_gain_grad, ffn_gain_grad]),
        ),
        "row",
        scatter_dimension=0,
        tiled=True,
    )
    rows_grad = resid_grad + rows_norm_grad
    input_share = lax.dynamic_slice_in_dim(rows_grad, col_start, quarter, 1).astype(jnp.bfloat16)
    (
        query_result,
        key_result,
        value_result,
        output_result,
        attn_gain_result,
        ffn_gain_result,
    ) = split_columns(attn_grads_local.astype(jnp.float32), attn_widths + [1, 1])
    attn_gain_result = attn_gain_result.reshape(-1)
    ffn_gain_result = ffn_gain_result.reshape(-1)
    gate_result, up_result, down_result = split_columns(
        ffn_grads_local.astype(jnp.float32), ffn_widths
    )
    back_grads = lax.all_to_all(
        input_share[arrived_slots], "row", split_axis=0, concat_axis=0, tiled=True
    )
    restore = jnp.argsort(send_order)
    return (
        back_rows[restore],
        back_grads[restore],
        attn_gain_result,
        query_result,
        key_result,
        value_result,
        output_result,
        ffn_gain_result,
        gate_result,
        up_result,
        down_result,
    )

def solution(mesh):
    placed = (
        P("row", "col"),
        P("row", "col"),
        P("row"),
        P("row"),
        P(),
        P("row", "col"),
        P("row", "col"),
        P("row", "col"),
        P("row", "col"),
        P(),
        P("row", "col"),
        P("row", "col"),
        P("row", "col"),
    )
    return jax.shard_map(
        body,
        mesh=mesh,
        in_specs=placed,
        out_specs=(
            P("row", "col"),
            P("row", "col"),
            P("row"),
            P("row", "col"),
            P("row", "col"),
            P("row", "col"),
            P("row", "col"),
            P("row"),
            P("row", "col"),
            P("row", "col"),
            P("row", "col"),
        ),
        check_vma=False,
    )
```

```python
from functools import partial

import jax
import jax.numpy as jnp
from jax import lax
from jax.experimental import pallas as pl
from jax.experimental.pallas import tpu as pltpu
from jax.sharding import PartitionSpec as P

HEADS = 32
KV = 4
HD = 64


EPS = 1e-05
ROPE_BASE = 10000.0


def rope_tables(positions):
    half_width = HD // 2
    freqs = ROPE_BASE ** (-(jnp.arange(half_width, dtype=jnp.float32) * 2.0 / HD))
    angles = positions.astype(jnp.float32)[:, None] * freqs[None, :]
    return (jnp.cos(angles)[:, None, :], jnp.sin(angles)[:, None, :])


def rotate(values, cosine, sine):
    half_width = values.shape[-1] // 2
    first = values[..., :half_width]
    second = values[..., half_width:]
    return jnp.concatenate(
        [first * cosine - second * sine, second * cosine + first * sine], axis=-1
    )


def rotate_back(grads, cosine, sine):
    half_width = grads.shape[-1] // 2
    first = grads[..., :half_width]
    second = grads[..., half_width:]
    return jnp.concatenate(
        [first * cosine + second * sine, second * cosine - first * sine], axis=-1
    )


def positions_of(segment_ids):
    index = jnp.arange(segment_ids.shape[0], dtype=jnp.int32)
    change = jnp.concatenate([jnp.ones((1,), dtype=jnp.bool_), segment_ids[1:] != segment_ids[:-1]])
    starts = jnp.where(change, index, jnp.zeros_like(index))
    return index - lax.cummax(starts, axis=0)


def allowed_pairs(segment_ids):
    index = jnp.arange(segment_ids.shape[0], dtype=jnp.int32)
    return (segment_ids[:, None] == segment_ids[None, :]) & (index[None, :] <= index[:, None])


def rms_scale(values):
    return lax.rsqrt(jnp.mean(values * values, axis=-1, keepdims=True) + EPS)


def norm_back(values, inv_root, gain, grads):
    normed = values * inv_root
    scaled = grads * gain
    result = inv_root * (scaled - normed * jnp.mean(scaled * normed, axis=-1, keepdims=True))
    return (result, jnp.sum(grads * normed, axis=0))


def matmul(left, right):
    return jnp.dot(left, right, preferred_element_type=jnp.float32)


def head_scores(query_head, key_head, allowed, scale_factor):
    scores = matmul(query_head, key_head.T) * scale_factor
    return jnp.where(allowed, scores, -1e30)


def head_forward(inputs, key_heads, value_heads, allowed, scale_factor):
    query_head, kv_slot = inputs
    scores = head_scores(query_head, key_heads[kv_slot], allowed, scale_factor)
    peak = jnp.max(scores, axis=-1, keepdims=True)
    expo = jnp.exp(scores - peak)
    total = jnp.sum(expo, axis=-1, keepdims=True)
    probs = expo / total
    mixed = matmul(probs.astype(jnp.bfloat16), value_heads[kv_slot])
    return (mixed, (peak + jnp.log(total))[:, 0])


def head_backward(inputs, key_heads, value_heads, allowed, scale_factor):
    query_head, kv_slot, grad_head, log_total = inputs
    key_head = key_heads[kv_slot]
    value_head = value_heads[kv_slot]
    scores = head_scores(query_head, key_head, allowed, scale_factor)
    probs = jnp.exp(scores - log_total[:, None])
    prob_grad = matmul(grad_head, value_head.T)
    value_grad = matmul(probs.astype(jnp.bfloat16).T, grad_head)
    inner = jnp.sum(probs * prob_grad, axis=-1, keepdims=True)
    score_grad = (probs * (prob_grad - inner)).astype(jnp.bfloat16)
    query_grad = matmul(score_grad, key_head) * scale_factor
    key_grad = matmul(score_grad.T, query_head) * scale_factor
    return (query_grad, key_grad, value_grad)


def grouped(heads, kv_count):
    return heads.reshape(kv_count, heads.shape[0] // kv_count, *heads.shape[1:])


def group_scores(query_groups, key_heads, allowed, scale_factor):
    scores = (
        jnp.einsum("kgqd,kpd->kgqp", query_groups, key_heads, preferred_element_type=jnp.float32)
        * scale_factor
    )
    return jnp.where(allowed, scores, -1e30)


def attention_forward(query_heads, key_heads, value_heads, allowed, scale_factor):
    query_groups = grouped(query_heads, key_heads.shape[0])
    scores = group_scores(query_groups, key_heads, allowed, scale_factor)
    peak = jnp.max(scores, axis=-1, keepdims=True)
    expo = jnp.exp(scores - peak)
    total = jnp.sum(expo, axis=-1, keepdims=True)
    probs = expo / total
    mixed = jnp.einsum(
        "kgqp,kpd->kgqd", probs.astype(jnp.bfloat16), value_heads, preferred_element_type=jnp.float32
    )
    return mixed.reshape(query_heads.shape), (peak + jnp.log(total))[..., 0]


def attention_backward(
    query_heads, key_heads, value_heads, grad_heads, log_totals, allowed, scale_factor
):
    kv_count = key_heads.shape[0]
    query_groups = grouped(query_heads, kv_count)
    grad_groups = grouped(grad_heads, kv_count)
    scores = group_scores(query_groups, key_heads, allowed, scale_factor)
    probs = jnp.exp(scores - log_totals[..., None])
    prob_grad = jnp.einsum(
        "kgqd,kpd->kgqp", grad_groups, value_heads, preferred_element_type=jnp.float32
    )
    value_grad = jnp.einsum(
        "kgqp,kgqd->kpd", probs.astype(jnp.bfloat16), grad_groups, preferred_element_type=jnp.float32
    )
    inner = jnp.sum(probs * prob_grad, axis=-1, keepdims=True)
    score_grad = (probs * (prob_grad - inner)).astype(jnp.bfloat16)
    query_grad = (
        jnp.einsum("kgqp,kpd->kgqd", score_grad, key_heads, preferred_element_type=jnp.float32)
        * scale_factor
    )
    key_grad = (
        jnp.einsum("kgqp,kgqd->kpd", score_grad, query_groups, preferred_element_type=jnp.float32)
        * scale_factor
    )
    return query_grad.reshape(query_heads.shape), key_grad, value_grad


def row_scatter_sum(vectors):
    count = lax.axis_size("row")
    blocks = jnp.moveaxis(vectors.reshape(vectors.shape[0], count, -1), 1, 0)
    return jnp.sum(lax.all_to_all(blocks, "row", split_axis=0, concat_axis=0, tiled=True), axis=0)


GRAD_BLOCK = 128


def split_columns(packed, widths):
    pieces = []
    offset = 0
    for width in widths:
        pieces.append(packed[:, offset : offset + width])
        offset += width
    return pieces


def col_scatter(values):
    count = lax.axis_size("col")
    lead = values.shape[:-1]
    blocks = jnp.moveaxis(values.reshape(*lead, count, values.shape[-1] // count), -2, 0)
    received = lax.all_to_all(blocks, "col", split_axis=0, concat_axis=0, tiled=True)
    return jnp.sum(received.astype(jnp.float32), axis=0)


def col_gather(block):
    count = lax.axis_size("col")
    copies = jnp.broadcast_to(block[None], (count,) + block.shape)
    received = lax.all_to_all(copies, "col", split_axis=0, concat_axis=0, tiled=True)
    return jnp.moveaxis(received, 0, -2).reshape(*block.shape[:-1], count * block.shape[-1])


def col_sum(values):
    return col_gather(col_scatter(values).astype(jnp.bfloat16)).astype(jnp.float32)


def gather_rows(parts):
    return lax.all_gather(jnp.concatenate(parts, axis=1), "row", axis=0, tiled=True)


def grad_plain_kernel(select_ref, left_ref, right_ref, out_ref):
    out_ref[...] = jnp.dot(
        left_ref[0], right_ref[...], preferred_element_type=jnp.float32
    ).astype(out_ref.dtype)


def packed_weight_grads(lefts, segments):
    left_stack = jnp.stack([left.T for left in lefts])
    right = jnp.concatenate([seg for _, seg in segments], axis=1)
    column_owner = []
    for index, seg in segments:
        column_owner += [index] * seg.shape[1]
    assert len(column_owner) % GRAD_BLOCK == 0
    select = column_owner[::GRAD_BLOCK]
    assert column_owner == [owner for owner in select for _ in range(GRAD_BLOCK)]
    right_blocks = len(select)
    features, tokens = left_stack.shape[1], left_stack.shape[2]
    in_specs = [
        pl.BlockSpec((1, features, tokens), lambda j, sel: (sel[j], 0, 0)),
        pl.BlockSpec((tokens, GRAD_BLOCK), lambda j, sel: (0, jnp.minimum(j, right_blocks - 1))),
    ]
    return pl.pallas_call(
        grad_plain_kernel,
        out_shape=jax.ShapeDtypeStruct((features, len(select) * GRAD_BLOCK), jnp.bfloat16),
        grid_spec=pltpu.PrefetchScalarGridSpec(
            num_scalar_prefetch=1,
            grid=(len(select),),
            in_specs=in_specs,
            out_specs=pl.BlockSpec((features, GRAD_BLOCK), lambda j, sel: (0, j)),
        ),
    )(jnp.asarray(select, dtype=jnp.int32), left_stack, right)


def body(
    tokens,
    cotangent,
    destination,
    segment_ids,
    attn_gain,
    w_query,
    w_key,
    w_value,
    w_output,
    ffn_gain,
    w_gate,
    w_up,
    w_down,
):
    row_count = tokens.shape[0]
    quarter = tokens.shape[1]
    col_start = lax.axis_index("col") * quarter
    send_order = jnp.argsort(destination)
    slot_ids = destination[send_order] % row_count
    arrived_pair, arrived_slots = (
        lax.all_to_all(
            jnp.stack([tokens, cotangent])[:, send_order], "row", split_axis=1, concat_axis=1, tiled=True
        ),
        lax.all_to_all(slot_ids, "row", split_axis=0, concat_axis=0, tiled=True),
    )
    placing = jnp.argsort(arrived_slots)
    attn_widths = [w_query.shape[1], w_key.shape[1], w_value.shape[1], w_output.shape[1]]
    ffn_widths = [w_gate.shape[1], w_up.shape[1], w_down.shape[1]]
    weights_packed = gather_rows([w_query, w_key, w_value, w_output, w_gate, w_up, w_down])
    attn_packed = weights_packed[:, : sum(attn_widths)]
    ffn_packed = weights_packed[:, sum(attn_widths) :]
    placed_pair = arrived_pair[:, placing]
    full_rows = col_gather(placed_pair[0])
    full_grads = col_gather(placed_pair[1])
    query_w, key_w, value_w, output_w = split_columns(attn_packed, attn_widths)
    cosine, sine = rope_tables(positions_of(segment_ids))
    allowed = allowed_pairs(segment_ids)
    rows_wide = full_rows.astype(jnp.float32)
    inv_one = rms_scale(rows_wide)
    normed_one = (rows_wide * inv_one * attn_gain).astype(jnp.bfloat16)
    query = matmul(normed_one, query_w)
    key_raw = matmul(normed_one, key_w)
    value_raw = matmul(normed_one, value_w)
    query_heads_count = query.shape[1] // HD
    kv_count = key_raw.shape[1] // HD
    query_rot = (
        rotate(query.reshape(row_count, query_heads_count, HD), cosine, sine)
        .astype(jnp.bfloat16)
        .transpose(1, 0, 2)
    )
    key_rot = (
        rotate(key_raw.reshape(row_count, kv_count, HD), cosine, sine)
        .astype(jnp.bfloat16)
        .transpose(1, 0, 2)
    )
    value_heads = value_raw.astype(jnp.bfloat16).reshape(row_count, kv_count, HD).transpose(1, 0, 2)
    scale_factor = HD ** (-0.5)
    mixed_heads, log_totals = attention_forward(
        query_rot, key_rot, value_heads, allowed, scale_factor
    )
    mixed = (
        mixed_heads.transpose(1, 0, 2)
        .reshape(row_count, query_heads_count * HD)
        .astype(jnp.bfloat16)
    )
    attn_terms = matmul(mixed, output_w.T)
    attn_full = lax.psum(attn_terms.astype(jnp.bfloat16), "col").astype(jnp.float32)
    resid = rows_wide + attn_full
    inv_two = rms_scale(resid)
    normed_two = (resid * inv_two * ffn_gain).astype(jnp.bfloat16)
    resid_part = lax.dynamic_slice_in_dim(resid, col_start, quarter, 1)
    gate_w, up_w, down_w = split_columns(ffn_packed, ffn_widths)
    gate = matmul(normed_two, gate_w)
    upper = matmul(normed_two, up_w)
    sigmoid_gate = jax.nn.sigmoid(gate)
    activ = (gate * sigmoid_gate * upper).astype(jnp.bfloat16)
    ffn_share_low = col_scatter(matmul(activ, down_w.T).astype(jnp.bfloat16)).astype(jnp.bfloat16)
    act_grad = matmul(full_grads, down_w)
    gate_grad = (act_grad * upper * sigmoid_gate * (1.0 + gate * (1.0 - sigmoid_gate))).astype(
        jnp.bfloat16
    )
    up_grad = (act_grad * gate * sigmoid_gate).astype(jnp.bfloat16)
    normed_terms_two = matmul(gate_grad, gate_w.T) + matmul(up_grad, up_w.T)
    ffn_grads_packed = packed_weight_grads(
        [normed_two, full_grads], [(0, gate_grad), (0, up_grad), (1, activ)]
    )
    normed_low_two, ffn_grads_packed = lax.optimization_barrier(
        (normed_terms_two.astype(jnp.bfloat16), ffn_grads_packed)
    )
    normed_grad_two = col_sum(normed_low_two)
    resid_norm_grad, ffn_gain_grad = norm_back(resid, inv_two, ffn_gain, normed_grad_two)
    ffn_grads_local = lax.psum_scatter(ffn_grads_packed, "row", scatter_dimension=0, tiled=True)
    resid_grad = full_grads.astype(jnp.float32) + resid_norm_grad
    attn_grad_low = resid_grad.astype(jnp.bfloat16)
    mixed_grad = matmul(attn_grad_low, output_w).astype(jnp.bfloat16)
    mixed_grad_heads = mixed_grad.reshape(row_count, query_heads_count, HD).transpose(1, 0, 2)
    query_grads, key_grads, value_grads = attention_backward(
        query_rot, key_rot, value_heads, mixed_grad_heads, log_totals, allowed, scale_factor
    )
    query_grad = (
        rotate_back(query_grads.transpose(1, 0, 2), cosine, sine)
        .reshape(row_count, query_heads_count * HD)
        .astype(jnp.bfloat16)
    )
    key_sum = key_grads.transpose(1, 0, 2)
    key_grad = (
        rotate_back(key_sum, cosine, sine).reshape(row_count, kv_count * HD).astype(jnp.bfloat16)
    )
    value_sum = value_grads.transpose(1, 0, 2)
    value_grad = value_sum.reshape(row_count, kv_count * HD).astype(jnp.bfloat16)
    normed_terms_one = (
        matmul(query_grad, query_w.T) + matmul(key_grad, key_w.T) + matmul(value_grad, value_w.T)
    )
    attn_grads_packed, ffn_grads_local, ffn_share_low = lax.optimization_barrier(
        (
            packed_weight_grads(
                [normed_one, attn_grad_low],
                [(0, query_grad), (0, key_grad), (0, value_grad), (1, mixed)],
            ),
            ffn_grads_local,
            ffn_share_low,
        )
    )
    attn_grads_local = lax.psum_scatter(attn_grads_packed, "row", scatter_dimension=0, tiled=True)
    normed_grad_one = col_sum(normed_terms_one.astype(jnp.bfloat16))
    rows_norm_grad, attn_gain_grad = norm_back(rows_wide, inv_one, attn_gain, normed_grad_one)
    rows_grad = resid_grad + rows_norm_grad
    input_share = lax.dynamic_slice_in_dim(rows_grad, col_start, quarter, 1).astype(jnp.bfloat16)
    output_share = (resid_part + ffn_share_low.astype(jnp.float32)).astype(jnp.bfloat16)
    query_result, key_result, value_result, output_result = split_columns(
        attn_grads_local.astype(jnp.float32), attn_widths
    )
    attn_gain_result, ffn_gain_result = row_scatter_sum(jnp.stack([attn_gain_grad, ffn_gain_grad]))
    gate_result, up_result, down_result = split_columns(
        ffn_grads_local.astype(jnp.float32), ffn_widths
    )
    back_pair = lax.all_to_all(
        jnp.stack([output_share, input_share])[:, arrived_slots],
        "row",
        split_axis=1,
        concat_axis=1,
        tiled=True,
    )
    back_rows, back_grads = back_pair[0], back_pair[1]
    restore = jnp.argsort(send_order)
    return (
        back_rows[restore],
        back_grads[restore],
        attn_gain_result,
        query_result,
        key_result,
        value_result,
        output_result,
        ffn_gain_result,
        gate_result,
        up_result,
        down_result,
    )

def solution(mesh):
    placed = (
        P("row", "col"),
        P("row", "col"),
        P("row"),
        P("row"),
        P(),
        P("row", "col"),
        P("row", "col"),
        P("row", "col"),
        P("row", "col"),
        P(),
        P("row", "col"),
        P("row", "col"),
        P("row", "col"),
    )
    return jax.shard_map(
        body,
        mesh=mesh,
        in_specs=placed,
        out_specs=(
            P("row", "col"),
            P("row", "col"),
            P("row"),
            P("row", "col"),
            P("row", "col"),
            P("row", "col"),
            P("row", "col"),
            P("row"),
            P("row", "col"),
            P("row", "col"),
            P("row", "col"),
        ),
        check_vma=False,
    )
```

```python
from functools import partial

import jax
import jax.numpy as jnp
from jax import lax
from jax.experimental import pallas as pl
from jax.experimental.pallas import tpu as pltpu
from jax.sharding import PartitionSpec as P

HEADS = 32
KV = 4
HD = 64


EPS = 1e-05
ROPE_BASE = 10000.0


def rope_tables(positions):
    half_width = HD // 2
    freqs = ROPE_BASE ** (-(jnp.arange(half_width, dtype=jnp.float32) * 2.0 / HD))
    angles = positions.astype(jnp.float32)[:, None] * freqs[None, :]
    return (jnp.cos(angles)[:, None, :], jnp.sin(angles)[:, None, :])


def rotate(values, cosine, sine):
    half_width = values.shape[-1] // 2
    first = values[..., :half_width]
    second = values[..., half_width:]
    return jnp.concatenate(
        [first * cosine - second * sine, second * cosine + first * sine], axis=-1
    )


def rotate_back(grads, cosine, sine):
    half_width = grads.shape[-1] // 2
    first = grads[..., :half_width]
    second = grads[..., half_width:]
    return jnp.concatenate(
        [first * cosine + second * sine, second * cosine - first * sine], axis=-1
    )


def positions_of(segment_ids):
    index = jnp.arange(segment_ids.shape[0], dtype=jnp.int32)
    change = jnp.concatenate([jnp.ones((1,), dtype=jnp.bool_), segment_ids[1:] != segment_ids[:-1]])
    starts = jnp.where(change, index, jnp.zeros_like(index))
    return index - lax.cummax(starts, axis=0)


def allowed_pairs(segment_ids):
    index = jnp.arange(segment_ids.shape[0], dtype=jnp.int32)
    return (segment_ids[:, None] == segment_ids[None, :]) & (index[None, :] <= index[:, None])


def rms_scale(values):
    return lax.rsqrt(jnp.mean(values * values, axis=-1, keepdims=True) + EPS)


def norm_back(values, inv_root, gain, grads):
    normed = values * inv_root
    scaled = grads * gain
    result = inv_root * (scaled - normed * jnp.mean(scaled * normed, axis=-1, keepdims=True))
    return (result, jnp.sum(grads * normed, axis=0))


def matmul(left, right):
    return jnp.dot(left, right, preferred_element_type=jnp.float32)


def head_scores(query_head, key_head, allowed, scale_factor):
    scores = matmul(query_head, key_head.T) * scale_factor
    return jnp.where(allowed, scores, -1e30)


def head_forward(inputs, key_heads, value_heads, allowed, scale_factor):
    query_head, kv_slot = inputs
    scores = head_scores(query_head, key_heads[kv_slot], allowed, scale_factor)
    peak = jnp.max(scores, axis=-1, keepdims=True)
    expo = jnp.exp(scores - peak)
    total = jnp.sum(expo, axis=-1, keepdims=True)
    probs = expo / total
    mixed = matmul(probs.astype(jnp.bfloat16), value_heads[kv_slot])
    return (mixed, (peak + jnp.log(total))[:, 0])


def head_backward(inputs, key_heads, value_heads, allowed, scale_factor):
    query_head, kv_slot, grad_head, log_total = inputs
    key_head = key_heads[kv_slot]
    value_head = value_heads[kv_slot]
    scores = head_scores(query_head, key_head, allowed, scale_factor)
    probs = jnp.exp(scores - log_total[:, None])
    prob_grad = matmul(grad_head, value_head.T)
    value_grad = matmul(probs.astype(jnp.bfloat16).T, grad_head)
    inner = jnp.sum(probs * prob_grad, axis=-1, keepdims=True)
    score_grad = (probs * (prob_grad - inner)).astype(jnp.bfloat16)
    query_grad = matmul(score_grad, key_head) * scale_factor
    key_grad = matmul(score_grad.T, query_head) * scale_factor
    return (query_grad, key_grad, value_grad)


def grouped(heads, kv_count):
    return heads.reshape(kv_count, heads.shape[0] // kv_count, *heads.shape[1:])


def group_scores(query_groups, key_heads, allowed, scale_factor):
    scores = (
        jnp.einsum("kgqd,kpd->kgqp", query_groups, key_heads, preferred_element_type=jnp.float32)
        * scale_factor
    )
    return jnp.where(allowed, scores, -1e30)


def attention_forward(query_heads, key_heads, value_heads, allowed, scale_factor):
    query_groups = grouped(query_heads, key_heads.shape[0])
    scores = group_scores(query_groups, key_heads, allowed, scale_factor)
    peak = jnp.max(scores, axis=-1, keepdims=True)
    expo = jnp.exp(scores - peak)
    total = jnp.sum(expo, axis=-1, keepdims=True)
    probs = expo / total
    mixed = jnp.einsum(
        "kgqp,kpd->kgqd", probs.astype(jnp.bfloat16), value_heads, preferred_element_type=jnp.float32
    )
    return mixed.reshape(query_heads.shape), (peak + jnp.log(total))[..., 0]


def attention_backward(
    query_heads, key_heads, value_heads, grad_heads, log_totals, allowed, scale_factor
):
    kv_count = key_heads.shape[0]
    query_groups = grouped(query_heads, kv_count)
    grad_groups = grouped(grad_heads, kv_count)
    scores = group_scores(query_groups, key_heads, allowed, scale_factor)
    probs = jnp.exp(scores - log_totals[..., None])
    prob_grad = jnp.einsum(
        "kgqd,kpd->kgqp", grad_groups, value_heads, preferred_element_type=jnp.float32
    )
    value_grad = jnp.einsum(
        "kgqp,kgqd->kpd", probs.astype(jnp.bfloat16), grad_groups, preferred_element_type=jnp.float32
    )
    inner = jnp.sum(probs * prob_grad, axis=-1, keepdims=True)
    score_grad = (probs * (prob_grad - inner)).astype(jnp.bfloat16)
    query_grad = (
        jnp.einsum("kgqp,kpd->kgqd", score_grad, key_heads, preferred_element_type=jnp.float32)
        * scale_factor
    )
    key_grad = (
        jnp.einsum("kgqp,kgqd->kpd", score_grad, query_groups, preferred_element_type=jnp.float32)
        * scale_factor
    )
    return query_grad.reshape(query_heads.shape), key_grad, value_grad


def row_scatter_sum(vectors):
    count = lax.axis_size("row")
    blocks = jnp.moveaxis(vectors.reshape(vectors.shape[0], count, -1), 1, 0)
    return jnp.sum(lax.all_to_all(blocks, "row", split_axis=0, concat_axis=0, tiled=True), axis=0)


GRAD_BLOCK = 128


def split_columns(packed, widths):
    pieces = []
    offset = 0
    for width in widths:
        pieces.append(packed[:, offset : offset + width])
        offset += width
    return pieces


def col_scatter(values):
    count = lax.axis_size("col")
    lead = values.shape[:-1]
    blocks = jnp.moveaxis(values.reshape(*lead, count, values.shape[-1] // count), -2, 0)
    received = lax.all_to_all(blocks, "col", split_axis=0, concat_axis=0, tiled=True)
    return jnp.sum(received.astype(jnp.float32), axis=0)


def col_gather(block):
    count = lax.axis_size("col")
    copies = jnp.broadcast_to(block[None], (count,) + block.shape)
    received = lax.all_to_all(copies, "col", split_axis=0, concat_axis=0, tiled=True)
    return jnp.moveaxis(received, 0, -2).reshape(*block.shape[:-1], count * block.shape[-1])


def col_sum(values):
    return col_gather(col_scatter(values).astype(jnp.bfloat16)).astype(jnp.float32)


def gather_rows(parts):
    return lax.all_gather(jnp.concatenate(parts, axis=1), "row", axis=0, tiled=True)


def grad_plain_kernel(select_ref, left_ref, right_ref, out_ref):
    out_ref[...] = jnp.dot(
        left_ref[0], right_ref[...], preferred_element_type=jnp.float32
    ).astype(out_ref.dtype)


def packed_weight_grads(lefts, segments):
    left_stack = jnp.stack([left.T for left in lefts])
    right = jnp.concatenate([seg for _, seg in segments], axis=1)
    column_owner = []
    for index, seg in segments:
        column_owner += [index] * seg.shape[1]
    assert len(column_owner) % GRAD_BLOCK == 0
    select = column_owner[::GRAD_BLOCK]
    assert column_owner == [owner for owner in select for _ in range(GRAD_BLOCK)]
    right_blocks = len(select)
    features, tokens = left_stack.shape[1], left_stack.shape[2]
    in_specs = [
        pl.BlockSpec((1, features, tokens), lambda j, sel: (sel[j], 0, 0)),
        pl.BlockSpec((tokens, GRAD_BLOCK), lambda j, sel: (0, jnp.minimum(j, right_blocks - 1))),
    ]
    return pl.pallas_call(
        grad_plain_kernel,
        out_shape=jax.ShapeDtypeStruct((features, len(select) * GRAD_BLOCK), jnp.bfloat16),
        grid_spec=pltpu.PrefetchScalarGridSpec(
            num_scalar_prefetch=1,
            grid=(len(select),),
            in_specs=in_specs,
            out_specs=pl.BlockSpec((features, GRAD_BLOCK), lambda j, sel: (0, j)),
        ),
    )(jnp.asarray(select, dtype=jnp.int32), left_stack, right)


def body(
    tokens,
    cotangent,
    destination,
    segment_ids,
    attn_gain,
    w_query,
    w_key,
    w_value,
    w_output,
    ffn_gain,
    w_gate,
    w_up,
    w_down,
):
    row_count = tokens.shape[0]
    quarter = tokens.shape[1]
    col_start = lax.axis_index("col") * quarter
    send_order = jnp.argsort(destination)
    slot_ids = destination[send_order] % row_count
    arrived_pair, arrived_slots = (
        lax.all_to_all(
            jnp.stack([tokens, cotangent])[:, send_order], "row", split_axis=1, concat_axis=1, tiled=True
        ),
        lax.all_to_all(slot_ids, "row", split_axis=0, concat_axis=0, tiled=True),
    )
    placing = jnp.argsort(arrived_slots)
    attn_widths = [w_query.shape[1], w_key.shape[1], w_value.shape[1], w_output.shape[1]]
    ffn_widths = [w_gate.shape[1], w_up.shape[1], w_down.shape[1]]
    weights_packed = gather_rows([w_query, w_key, w_value, w_output, w_gate, w_up, w_down])
    attn_packed = weights_packed[:, : sum(attn_widths)]
    ffn_packed = weights_packed[:, sum(attn_widths) :]
    placed_pair = arrived_pair[:, placing]
    full_rows = col_gather(placed_pair[0])
    full_grads = col_gather(placed_pair[1])
    query_w, key_w, value_w, output_w = split_columns(attn_packed, attn_widths)
    cosine, sine = rope_tables(positions_of(segment_ids))
    allowed = allowed_pairs(segment_ids)
    rows_wide = full_rows.astype(jnp.float32)
    inv_one = rms_scale(rows_wide)
    normed_one = (rows_wide * inv_one * attn_gain).astype(jnp.bfloat16)
    query = matmul(normed_one, query_w)
    key_raw = matmul(normed_one, key_w)
    value_raw = matmul(normed_one, value_w)
    query_heads_count = query.shape[1] // HD
    kv_count = key_raw.shape[1] // HD
    query_rot = (
        rotate(query.reshape(row_count, query_heads_count, HD), cosine, sine)
        .astype(jnp.bfloat16)
        .transpose(1, 0, 2)
    )
    key_rot = (
        rotate(key_raw.reshape(row_count, kv_count, HD), cosine, sine)
        .astype(jnp.bfloat16)
        .transpose(1, 0, 2)
    )
    value_heads = value_raw.astype(jnp.bfloat16).reshape(row_count, kv_count, HD).transpose(1, 0, 2)
    scale_factor = HD ** (-0.5)
    mixed_heads, log_totals = attention_forward(
        query_rot, key_rot, value_heads, allowed, scale_factor
    )
    mixed = (
        mixed_heads.transpose(1, 0, 2)
        .reshape(row_count, query_heads_count * HD)
        .astype(jnp.bfloat16)
    )
    attn_terms = matmul(mixed, output_w.T)
    attn_full = lax.psum(attn_terms.astype(jnp.bfloat16), "col").astype(jnp.float32)
    resid = rows_wide + attn_full
    inv_two = rms_scale(resid)
    normed_two = (resid * inv_two * ffn_gain).astype(jnp.bfloat16)
    resid_part = lax.dynamic_slice_in_dim(resid, col_start, quarter, 1)
    gate_w, up_w, down_w = split_columns(ffn_packed, ffn_widths)
    gate = matmul(normed_two, gate_w)
    upper = matmul(normed_two, up_w)
    sigmoid_gate = jax.nn.sigmoid(gate)
    activ = (gate * sigmoid_gate * upper).astype(jnp.bfloat16)
    ffn_share_low = lax.psum_scatter(
        matmul(activ, down_w.T).astype(jnp.bfloat16), "col", scatter_dimension=1, tiled=True
    )
    act_grad = matmul(full_grads, down_w)
    gate_grad = (act_grad * upper * sigmoid_gate * (1.0 + gate * (1.0 - sigmoid_gate))).astype(
        jnp.bfloat16
    )
    up_grad = (act_grad * gate * sigmoid_gate).astype(jnp.bfloat16)
    normed_terms_two = matmul(gate_grad, gate_w.T) + matmul(up_grad, up_w.T)
    ffn_grads_packed = packed_weight_grads(
        [normed_two, full_grads], [(0, gate_grad), (0, up_grad), (1, activ)]
    )
    ffn_grads_packed, ffn_share_low = lax.optimization_barrier((ffn_grads_packed, ffn_share_low))
    normed_low_two, ffn_grads_packed = lax.optimization_barrier(
        (normed_terms_two.astype(jnp.bfloat16), ffn_grads_packed)
    )
    normed_grad_two = col_sum(normed_low_two)
    resid_norm_grad, ffn_gain_grad = norm_back(resid, inv_two, ffn_gain, normed_grad_two)
    ffn_grads_local = lax.psum_scatter(ffn_grads_packed, "row", scatter_dimension=0, tiled=True)
    resid_grad = full_grads.astype(jnp.float32) + resid_norm_grad
    attn_grad_low = resid_grad.astype(jnp.bfloat16)
    mixed_grad = matmul(attn_grad_low, output_w).astype(jnp.bfloat16)
    mixed_grad_heads = mixed_grad.reshape(row_count, query_heads_count, HD).transpose(1, 0, 2)
    query_grads, key_grads, value_grads = attention_backward(
        query_rot, key_rot, value_heads, mixed_grad_heads, log_totals, allowed, scale_factor
    )
    query_grad = (
        rotate_back(query_grads.transpose(1, 0, 2), cosine, sine)
        .reshape(row_count, query_heads_count * HD)
        .astype(jnp.bfloat16)
    )
    key_sum = key_grads.transpose(1, 0, 2)
    key_grad = (
        rotate_back(key_sum, cosine, sine).reshape(row_count, kv_count * HD).astype(jnp.bfloat16)
    )
    value_sum = value_grads.transpose(1, 0, 2)
    value_grad = value_sum.reshape(row_count, kv_count * HD).astype(jnp.bfloat16)
    normed_terms_one = (
        matmul(query_grad, query_w.T) + matmul(key_grad, key_w.T) + matmul(value_grad, value_w.T)
    )
    attn_grads_packed, ffn_grads_local = lax.optimization_barrier(
        (
            packed_weight_grads(
                [normed_one, attn_grad_low],
                [(0, query_grad), (0, key_grad), (0, value_grad), (1, mixed)],
            ),
            ffn_grads_local,
        )
    )
    attn_grads_local = lax.psum_scatter(attn_grads_packed, "row", scatter_dimension=0, tiled=True)
    normed_grad_one = col_sum(normed_terms_one.astype(jnp.bfloat16))
    rows_norm_grad, attn_gain_grad = norm_back(rows_wide, inv_one, attn_gain, normed_grad_one)
    rows_grad = resid_grad + rows_norm_grad
    input_share = lax.dynamic_slice_in_dim(rows_grad, col_start, quarter, 1).astype(jnp.bfloat16)
    output_share = (resid_part + ffn_share_low.astype(jnp.float32)).astype(jnp.bfloat16)
    query_result, key_result, value_result, output_result = split_columns(
        attn_grads_local.astype(jnp.float32), attn_widths
    )
    attn_gain_result, ffn_gain_result = row_scatter_sum(jnp.stack([attn_gain_grad, ffn_gain_grad]))
    gate_result, up_result, down_result = split_columns(
        ffn_grads_local.astype(jnp.float32), ffn_widths
    )
    back_pair = lax.all_to_all(
        jnp.stack([output_share, input_share])[:, arrived_slots],
        "row",
        split_axis=1,
        concat_axis=1,
        tiled=True,
    )
    back_rows, back_grads = back_pair[0], back_pair[1]
    restore = jnp.argsort(send_order)
    return (
        back_rows[restore],
        back_grads[restore],
        attn_gain_result,
        query_result,
        key_result,
        value_result,
        output_result,
        ffn_gain_result,
        gate_result,
        up_result,
        down_result,
    )

def solution(mesh):
    placed = (
        P("row", "col"),
        P("row", "col"),
        P("row"),
        P("row"),
        P(),
        P("row", "col"),
        P("row", "col"),
        P("row", "col"),
        P("row", "col"),
        P(),
        P("row", "col"),
        P("row", "col"),
        P("row", "col"),
    )
    return jax.shard_map(
        body,
        mesh=mesh,
        in_specs=placed,
        out_specs=(
            P("row", "col"),
            P("row", "col"),
            P("row"),
            P("row", "col"),
            P("row", "col"),
            P("row", "col"),
            P("row", "col"),
            P("row"),
            P("row", "col"),
            P("row", "col"),
            P("row", "col"),
        ),
        check_vma=False,
    )
```

```python
from functools import partial

import jax
import jax.numpy as jnp
from jax import lax
from jax.experimental import pallas as pl
from jax.experimental.pallas import tpu as pltpu
from jax.sharding import PartitionSpec as P

HEADS = 32
KV = 4
HD = 64


EPS = 1e-05
ROPE_BASE = 10000.0


def rope_tables(positions):
    half_width = HD // 2
    freqs = ROPE_BASE ** (-(jnp.arange(half_width, dtype=jnp.float32) * 2.0 / HD))
    angles = positions.astype(jnp.float32)[:, None] * freqs[None, :]
    return (jnp.cos(angles)[:, None, :], jnp.sin(angles)[:, None, :])


def rotate(values, cosine, sine):
    half_width = values.shape[-1] // 2
    first = values[..., :half_width]
    second = values[..., half_width:]
    return jnp.concatenate(
        [first * cosine - second * sine, second * cosine + first * sine], axis=-1
    )


def rotate_back(grads, cosine, sine):
    half_width = grads.shape[-1] // 2
    first = grads[..., :half_width]
    second = grads[..., half_width:]
    return jnp.concatenate(
        [first * cosine + second * sine, second * cosine - first * sine], axis=-1
    )


def positions_of(segment_ids):
    index = jnp.arange(segment_ids.shape[0], dtype=jnp.int32)
    change = jnp.concatenate([jnp.ones((1,), dtype=jnp.bool_), segment_ids[1:] != segment_ids[:-1]])
    starts = jnp.where(change, index, jnp.zeros_like(index))
    return index - lax.cummax(starts, axis=0)


def allowed_pairs(segment_ids):
    index = jnp.arange(segment_ids.shape[0], dtype=jnp.int32)
    return (segment_ids[:, None] == segment_ids[None, :]) & (index[None, :] <= index[:, None])


def rms_scale(values):
    return lax.rsqrt(jnp.mean(values * values, axis=-1, keepdims=True) + EPS)


def norm_back(values, inv_root, gain, grads):
    normed = values * inv_root
    scaled = grads * gain
    result = inv_root * (scaled - normed * jnp.mean(scaled * normed, axis=-1, keepdims=True))
    return (result, jnp.sum(grads * normed, axis=0))


def matmul(left, right):
    return jnp.dot(left, right, preferred_element_type=jnp.float32)


def head_scores(query_head, key_head, allowed, scale_factor):
    scores = matmul(query_head, key_head.T) * scale_factor
    return jnp.where(allowed, scores, -1e30)


def head_forward(inputs, key_heads, value_heads, allowed, scale_factor):
    query_head, kv_slot = inputs
    scores = head_scores(query_head, key_heads[kv_slot], allowed, scale_factor)
    peak = jnp.max(scores, axis=-1, keepdims=True)
    expo = jnp.exp(scores - peak)
    total = jnp.sum(expo, axis=-1, keepdims=True)
    probs = expo / total
    mixed = matmul(probs.astype(jnp.bfloat16), value_heads[kv_slot])
    return (mixed, (peak + jnp.log(total))[:, 0])


def head_backward(inputs, key_heads, value_heads, allowed, scale_factor):
    query_head, kv_slot, grad_head, log_total = inputs
    key_head = key_heads[kv_slot]
    value_head = value_heads[kv_slot]
    scores = head_scores(query_head, key_head, allowed, scale_factor)
    probs = jnp.exp(scores - log_total[:, None])
    prob_grad = matmul(grad_head, value_head.T)
    value_grad = matmul(probs.astype(jnp.bfloat16).T, grad_head)
    inner = jnp.sum(probs * prob_grad, axis=-1, keepdims=True)
    score_grad = (probs * (prob_grad - inner)).astype(jnp.bfloat16)
    query_grad = matmul(score_grad, key_head) * scale_factor
    key_grad = matmul(score_grad.T, query_head) * scale_factor
    return (query_grad, key_grad, value_grad)


def grouped(heads, kv_count):
    return heads.reshape(kv_count, heads.shape[0] // kv_count, *heads.shape[1:])


def group_scores(query_groups, key_heads, allowed, scale_factor):
    scores = (
        jnp.einsum("kgqd,kpd->kgqp", query_groups, key_heads, preferred_element_type=jnp.float32)
        * scale_factor
    )
    return jnp.where(allowed, scores, -1e30)


def attention_forward(query_heads, key_heads, value_heads, allowed, scale_factor):
    query_groups = grouped(query_heads, key_heads.shape[0])
    scores = group_scores(query_groups, key_heads, allowed, scale_factor)
    peak = jnp.max(scores, axis=-1, keepdims=True)
    expo = jnp.exp(scores - peak)
    total = jnp.sum(expo, axis=-1, keepdims=True)
    probs = expo / total
    mixed = jnp.einsum(
        "kgqp,kpd->kgqd", probs.astype(jnp.bfloat16), value_heads, preferred_element_type=jnp.float32
    )
    return mixed.reshape(query_heads.shape), (peak + jnp.log(total))[..., 0]


def attention_backward(
    query_heads, key_heads, value_heads, grad_heads, log_totals, allowed, scale_factor
):
    kv_count = key_heads.shape[0]
    query_groups = grouped(query_heads, kv_count)
    grad_groups = grouped(grad_heads, kv_count)
    scores = group_scores(query_groups, key_heads, allowed, scale_factor)
    probs = jnp.exp(scores - log_totals[..., None])
    prob_grad = jnp.einsum(
        "kgqd,kpd->kgqp", grad_groups, value_heads, preferred_element_type=jnp.float32
    )
    value_grad = jnp.einsum(
        "kgqp,kgqd->kpd", probs.astype(jnp.bfloat16), grad_groups, preferred_element_type=jnp.float32
    )
    inner = jnp.sum(probs * prob_grad, axis=-1, keepdims=True)
    score_grad = (probs * (prob_grad - inner)).astype(jnp.bfloat16)
    query_grad = (
        jnp.einsum("kgqp,kpd->kgqd", score_grad, key_heads, preferred_element_type=jnp.float32)
        * scale_factor
    )
    key_grad = (
        jnp.einsum("kgqp,kgqd->kpd", score_grad, query_groups, preferred_element_type=jnp.float32)
        * scale_factor
    )
    return query_grad.reshape(query_heads.shape), key_grad, value_grad


def row_scatter_sum(vectors):
    count = lax.axis_size("row")
    blocks = jnp.moveaxis(vectors.reshape(vectors.shape[0], count, -1), 1, 0)
    return jnp.sum(lax.all_to_all(blocks, "row", split_axis=0, concat_axis=0, tiled=True), axis=0)


GRAD_BLOCK = 128


def split_columns(packed, widths):
    pieces = []
    offset = 0
    for width in widths:
        pieces.append(packed[:, offset : offset + width])
        offset += width
    return pieces


def col_scatter(values):
    count = lax.axis_size("col")
    lead = values.shape[:-1]
    blocks = jnp.moveaxis(values.reshape(*lead, count, values.shape[-1] // count), -2, 0)
    received = lax.all_to_all(blocks, "col", split_axis=0, concat_axis=0, tiled=True)
    return jnp.sum(received.astype(jnp.float32), axis=0)


def col_gather(block):
    count = lax.axis_size("col")
    copies = jnp.broadcast_to(block[None], (count,) + block.shape)
    received = lax.all_to_all(copies, "col", split_axis=0, concat_axis=0, tiled=True)
    return jnp.moveaxis(received, 0, -2).reshape(*block.shape[:-1], count * block.shape[-1])


def col_sum_ring(values):
    count = lax.axis_size("col")
    me = lax.axis_index("col")
    lead = values.shape[:-1]
    blocks = jnp.moveaxis(values.reshape(*lead, count, values.shape[-1] // count), -2, 0)
    ordered = jnp.roll(blocks, -me, axis=0)
    total = ordered[0].astype(jnp.float32)
    for shift in range(1, count):
        pairs = [(i, (i + shift) % count) for i in range(count)]
        total = total + lax.ppermute(ordered[shift], "col", pairs).astype(jnp.float32)
    reduced = total.astype(jnp.bfloat16)
    pieces = [reduced]
    for shift in range(1, count):
        pairs = [(i, (i - shift) % count) for i in range(count)]
        pieces.append(lax.ppermute(reduced, "col", pairs))
    full = jnp.roll(jnp.stack(pieces), me, axis=0)
    return jnp.moveaxis(full, 0, -2).reshape(values.shape).astype(jnp.float32)


def col_sum(values):
    return col_gather(col_scatter(values).astype(jnp.bfloat16)).astype(jnp.float32)


def gather_rows(parts):
    return lax.all_gather(jnp.concatenate(parts, axis=1), "row", axis=0, tiled=True)


def grad_plain_kernel(select_ref, left_ref, right_ref, out_ref):
    out_ref[...] = jnp.dot(
        left_ref[0], right_ref[...], preferred_element_type=jnp.float32
    ).astype(out_ref.dtype)


def packed_weight_grads(lefts, segments):
    left_stack = jnp.stack([left.T for left in lefts])
    right = jnp.concatenate([seg for _, seg in segments], axis=1)
    column_owner = []
    for index, seg in segments:
        column_owner += [index] * seg.shape[1]
    assert len(column_owner) % GRAD_BLOCK == 0
    select = column_owner[::GRAD_BLOCK]
    assert column_owner == [owner for owner in select for _ in range(GRAD_BLOCK)]
    right_blocks = len(select)
    features, tokens = left_stack.shape[1], left_stack.shape[2]
    in_specs = [
        pl.BlockSpec((1, features, tokens), lambda j, sel: (sel[j], 0, 0)),
        pl.BlockSpec((tokens, GRAD_BLOCK), lambda j, sel: (0, jnp.minimum(j, right_blocks - 1))),
    ]
    return pl.pallas_call(
        grad_plain_kernel,
        out_shape=jax.ShapeDtypeStruct((features, len(select) * GRAD_BLOCK), jnp.bfloat16),
        grid_spec=pltpu.PrefetchScalarGridSpec(
            num_scalar_prefetch=1,
            grid=(len(select),),
            in_specs=in_specs,
            out_specs=pl.BlockSpec((features, GRAD_BLOCK), lambda j, sel: (0, j)),
        ),
    )(jnp.asarray(select, dtype=jnp.int32), left_stack, right)


def body(
    tokens,
    cotangent,
    destination,
    segment_ids,
    attn_gain,
    w_query,
    w_key,
    w_value,
    w_output,
    ffn_gain,
    w_gate,
    w_up,
    w_down,
):
    row_count = tokens.shape[0]
    quarter = tokens.shape[1]
    col_start = lax.axis_index("col") * quarter
    send_order = jnp.argsort(destination)
    slot_ids = destination[send_order] % row_count
    arrived_pair, arrived_slots = (
        lax.all_to_all(
            jnp.stack([tokens, cotangent])[:, send_order], "row", split_axis=1, concat_axis=1, tiled=True
        ),
        lax.all_to_all(slot_ids, "row", split_axis=0, concat_axis=0, tiled=True),
    )
    placing = jnp.argsort(arrived_slots)
    attn_widths = [w_query.shape[1], w_key.shape[1], w_value.shape[1], w_output.shape[1]]
    ffn_widths = [w_gate.shape[1], w_up.shape[1], w_down.shape[1]]
    weights_packed = gather_rows([w_query, w_key, w_value, w_output, w_gate, w_up, w_down])
    attn_packed = weights_packed[:, : sum(attn_widths)]
    ffn_packed = weights_packed[:, sum(attn_widths) :]
    placed_pair = arrived_pair[:, placing]
    full_rows = col_gather(placed_pair[0])
    full_grads = col_gather(placed_pair[1])
    query_w, key_w, value_w, output_w = split_columns(attn_packed, attn_widths)
    cosine, sine = rope_tables(positions_of(segment_ids))
    allowed = allowed_pairs(segment_ids)
    rows_wide = full_rows.astype(jnp.float32)
    inv_one = rms_scale(rows_wide)
    normed_one = (rows_wide * inv_one * attn_gain).astype(jnp.bfloat16)
    query = matmul(normed_one, query_w)
    key_raw = matmul(normed_one, key_w)
    value_raw = matmul(normed_one, value_w)
    query_heads_count = query.shape[1] // HD
    kv_count = key_raw.shape[1] // HD
    query_rot = (
        rotate(query.reshape(row_count, query_heads_count, HD), cosine, sine)
        .astype(jnp.bfloat16)
        .transpose(1, 0, 2)
    )
    key_rot = (
        rotate(key_raw.reshape(row_count, kv_count, HD), cosine, sine)
        .astype(jnp.bfloat16)
        .transpose(1, 0, 2)
    )
    value_heads = value_raw.astype(jnp.bfloat16).reshape(row_count, kv_count, HD).transpose(1, 0, 2)
    scale_factor = HD ** (-0.5)
    mixed_heads, log_totals = attention_forward(
        query_rot, key_rot, value_heads, allowed, scale_factor
    )
    mixed = (
        mixed_heads.transpose(1, 0, 2)
        .reshape(row_count, query_heads_count * HD)
        .astype(jnp.bfloat16)
    )
    attn_terms = matmul(mixed, output_w.T)
    attn_full = lax.psum(attn_terms.astype(jnp.bfloat16), "col").astype(jnp.float32)
    resid = rows_wide + attn_full
    inv_two = rms_scale(resid)
    normed_two = (resid * inv_two * ffn_gain).astype(jnp.bfloat16)
    resid_part = lax.dynamic_slice_in_dim(resid, col_start, quarter, 1)
    gate_w, up_w, down_w = split_columns(ffn_packed, ffn_widths)
    gate = matmul(normed_two, gate_w)
    upper = matmul(normed_two, up_w)
    sigmoid_gate = jax.nn.sigmoid(gate)
    activ = (gate * sigmoid_gate * upper).astype(jnp.bfloat16)
    ffn_share_low = lax.psum_scatter(
        matmul(activ, down_w.T).astype(jnp.bfloat16), "col", scatter_dimension=1, tiled=True
    )
    act_grad = matmul(full_grads, down_w)
    gate_grad = (act_grad * upper * sigmoid_gate * (1.0 + gate * (1.0 - sigmoid_gate))).astype(
        jnp.bfloat16
    )
    up_grad = (act_grad * gate * sigmoid_gate).astype(jnp.bfloat16)
    normed_terms_two = matmul(gate_grad, gate_w.T) + matmul(up_grad, up_w.T)
    ffn_grads_packed = packed_weight_grads(
        [normed_two, full_grads], [(0, gate_grad), (0, up_grad), (1, activ)]
    )
    ffn_grads_packed, ffn_share_low = lax.optimization_barrier((ffn_grads_packed, ffn_share_low))
    normed_low_two, ffn_grads_packed = lax.optimization_barrier(
        (normed_terms_two.astype(jnp.bfloat16), ffn_grads_packed)
    )
    normed_grad_two = col_sum(normed_low_two)
    resid_norm_grad, ffn_gain_grad = norm_back(resid, inv_two, ffn_gain, normed_grad_two)
    ffn_grads_local = lax.psum_scatter(ffn_grads_packed, "row", scatter_dimension=0, tiled=True)
    resid_grad = full_grads.astype(jnp.float32) + resid_norm_grad
    attn_grad_low = resid_grad.astype(jnp.bfloat16)
    mixed_grad = matmul(attn_grad_low, output_w).astype(jnp.bfloat16)
    mixed_grad_heads = mixed_grad.reshape(row_count, query_heads_count, HD).transpose(1, 0, 2)
    query_grads, key_grads, value_grads = attention_backward(
        query_rot, key_rot, value_heads, mixed_grad_heads, log_totals, allowed, scale_factor
    )
    query_grad = (
        rotate_back(query_grads.transpose(1, 0, 2), cosine, sine)
        .reshape(row_count, query_heads_count * HD)
        .astype(jnp.bfloat16)
    )
    key_sum = key_grads.transpose(1, 0, 2)
    key_grad = (
        rotate_back(key_sum, cosine, sine).reshape(row_count, kv_count * HD).astype(jnp.bfloat16)
    )
    value_sum = value_grads.transpose(1, 0, 2)
    value_grad = value_sum.reshape(row_count, kv_count * HD).astype(jnp.bfloat16)
    normed_terms_one = (
        matmul(query_grad, query_w.T) + matmul(key_grad, key_w.T) + matmul(value_grad, value_w.T)
    )
    attn_grads_packed, ffn_grads_local = lax.optimization_barrier(
        (
            packed_weight_grads(
                [normed_one, attn_grad_low],
                [(0, query_grad), (0, key_grad), (0, value_grad), (1, mixed)],
            ),
            ffn_grads_local,
        )
    )
    attn_grads_local = lax.psum_scatter(attn_grads_packed, "row", scatter_dimension=0, tiled=True)
    normed_grad_one = col_sum_ring(normed_terms_one.astype(jnp.bfloat16))
    rows_norm_grad, attn_gain_grad = norm_back(rows_wide, inv_one, attn_gain, normed_grad_one)
    rows_grad = resid_grad + rows_norm_grad
    input_share = lax.dynamic_slice_in_dim(rows_grad, col_start, quarter, 1).astype(jnp.bfloat16)
    output_share = (resid_part + ffn_share_low.astype(jnp.float32)).astype(jnp.bfloat16)
    query_result, key_result, value_result, output_result = split_columns(
        attn_grads_local.astype(jnp.float32), attn_widths
    )
    attn_gain_result, ffn_gain_result = row_scatter_sum(jnp.stack([attn_gain_grad, ffn_gain_grad]))
    gate_result, up_result, down_result = split_columns(
        ffn_grads_local.astype(jnp.float32), ffn_widths
    )
    back_pair = lax.all_to_all(
        jnp.stack([output_share, input_share])[:, arrived_slots],
        "row",
        split_axis=1,
        concat_axis=1,
        tiled=True,
    )
    back_rows, back_grads = back_pair[0], back_pair[1]
    restore = jnp.argsort(send_order)
    return (
        back_rows[restore],
        back_grads[restore],
        attn_gain_result,
        query_result,
        key_result,
        value_result,
        output_result,
        ffn_gain_result,
        gate_result,
        up_result,
        down_result,
    )

def solution(mesh):
    placed = (
        P("row", "col"),
        P("row", "col"),
        P("row"),
        P("row"),
        P(),
        P("row", "col"),
        P("row", "col"),
        P("row", "col"),
        P("row", "col"),
        P(),
        P("row", "col"),
        P("row", "col"),
        P("row", "col"),
    )
    return jax.shard_map(
        body,
        mesh=mesh,
        in_specs=placed,
        out_specs=(
            P("row", "col"),
            P("row", "col"),
            P("row"),
            P("row", "col"),
            P("row", "col"),
            P("row", "col"),
            P("row", "col"),
            P("row"),
            P("row", "col"),
            P("row", "col"),
            P("row", "col"),
        ),
        check_vma=False,
    )
```

```python
from functools import partial

import jax
import jax.numpy as jnp
from jax import lax
from jax.experimental import pallas as pl
from jax.experimental.pallas import tpu as pltpu
from jax.sharding import PartitionSpec as P

HEADS = 32
KV = 4
HD = 64


EPS = 1e-05
ROPE_BASE = 10000.0


def rope_tables(positions):
    half_width = HD // 2
    freqs = ROPE_BASE ** (-(jnp.arange(half_width, dtype=jnp.float32) * 2.0 / HD))
    angles = positions.astype(jnp.float32)[:, None] * freqs[None, :]
    return (jnp.cos(angles)[:, None, :], jnp.sin(angles)[:, None, :])


def rotate(values, cosine, sine):
    half_width = values.shape[-1] // 2
    first = values[..., :half_width]
    second = values[..., half_width:]
    return jnp.concatenate(
        [first * cosine - second * sine, second * cosine + first * sine], axis=-1
    )


def rotate_back(grads, cosine, sine):
    half_width = grads.shape[-1] // 2
    first = grads[..., :half_width]
    second = grads[..., half_width:]
    return jnp.concatenate(
        [first * cosine + second * sine, second * cosine - first * sine], axis=-1
    )


def positions_of(segment_ids):
    index = jnp.arange(segment_ids.shape[0], dtype=jnp.int32)
    change = jnp.concatenate([jnp.ones((1,), dtype=jnp.bool_), segment_ids[1:] != segment_ids[:-1]])
    starts = jnp.where(change, index, jnp.zeros_like(index))
    return index - lax.cummax(starts, axis=0)


def allowed_pairs(segment_ids):
    index = jnp.arange(segment_ids.shape[0], dtype=jnp.int32)
    return (segment_ids[:, None] == segment_ids[None, :]) & (index[None, :] <= index[:, None])


def rms_scale(values):
    return lax.rsqrt(jnp.mean(values * values, axis=-1, keepdims=True) + EPS)


def norm_back(values, inv_root, gain, grads):
    normed = values * inv_root
    scaled = grads * gain
    result = inv_root * (scaled - normed * jnp.mean(scaled * normed, axis=-1, keepdims=True))
    return (result, jnp.sum(grads * normed, axis=0))


def matmul(left, right):
    return jnp.dot(left, right, preferred_element_type=jnp.float32)


def head_scores(query_head, key_head, allowed, scale_factor):
    scores = matmul(query_head, key_head.T) * scale_factor
    return jnp.where(allowed, scores, -1e30)


def head_forward(inputs, key_heads, value_heads, allowed, scale_factor):
    query_head, kv_slot = inputs
    scores = head_scores(query_head, key_heads[kv_slot], allowed, scale_factor)
    peak = jnp.max(scores, axis=-1, keepdims=True)
    expo = jnp.exp(scores - peak)
    total = jnp.sum(expo, axis=-1, keepdims=True)
    probs = expo / total
    mixed = matmul(probs.astype(jnp.bfloat16), value_heads[kv_slot])
    return (mixed, (peak + jnp.log(total))[:, 0])


def head_backward(inputs, key_heads, value_heads, allowed, scale_factor):
    query_head, kv_slot, grad_head, log_total = inputs
    key_head = key_heads[kv_slot]
    value_head = value_heads[kv_slot]
    scores = head_scores(query_head, key_head, allowed, scale_factor)
    probs = jnp.exp(scores - log_total[:, None])
    prob_grad = matmul(grad_head, value_head.T)
    value_grad = matmul(probs.astype(jnp.bfloat16).T, grad_head)
    inner = jnp.sum(probs * prob_grad, axis=-1, keepdims=True)
    score_grad = (probs * (prob_grad - inner)).astype(jnp.bfloat16)
    query_grad = matmul(score_grad, key_head) * scale_factor
    key_grad = matmul(score_grad.T, query_head) * scale_factor
    return (query_grad, key_grad, value_grad)


def grouped(heads, kv_count):
    return heads.reshape(kv_count, heads.shape[0] // kv_count, *heads.shape[1:])


def group_scores(query_groups, key_heads, allowed, scale_factor):
    scores = (
        jnp.einsum("kgqd,kpd->kgqp", query_groups, key_heads, preferred_element_type=jnp.float32)
        * scale_factor
    )
    return jnp.where(allowed, scores, -1e30)


def attention_forward(query_heads, key_heads, value_heads, allowed, scale_factor):
    query_groups = grouped(query_heads, key_heads.shape[0])
    scores = group_scores(query_groups, key_heads, allowed, scale_factor)
    peak = jnp.max(scores, axis=-1, keepdims=True)
    expo = jnp.exp(scores - peak)
    total = jnp.sum(expo, axis=-1, keepdims=True)
    probs = expo / total
    mixed = jnp.einsum(
        "kgqp,kpd->kgqd", probs.astype(jnp.bfloat16), value_heads, preferred_element_type=jnp.float32
    )
    return mixed.reshape(query_heads.shape), (peak + jnp.log(total))[..., 0]


def attention_backward(
    query_heads, key_heads, value_heads, grad_heads, log_totals, allowed, scale_factor
):
    kv_count = key_heads.shape[0]
    query_groups = grouped(query_heads, kv_count)
    grad_groups = grouped(grad_heads, kv_count)
    scores = group_scores(query_groups, key_heads, allowed, scale_factor)
    probs = jnp.exp(scores - log_totals[..., None])
    prob_grad = jnp.einsum(
        "kgqd,kpd->kgqp", grad_groups, value_heads, preferred_element_type=jnp.float32
    )
    value_grad = jnp.einsum(
        "kgqp,kgqd->kpd", probs.astype(jnp.bfloat16), grad_groups, preferred_element_type=jnp.float32
    )
    inner = jnp.sum(probs * prob_grad, axis=-1, keepdims=True)
    score_grad = (probs * (prob_grad - inner)).astype(jnp.bfloat16)
    query_grad = (
        jnp.einsum("kgqp,kpd->kgqd", score_grad, key_heads, preferred_element_type=jnp.float32)
        * scale_factor
    )
    key_grad = (
        jnp.einsum("kgqp,kgqd->kpd", score_grad, query_groups, preferred_element_type=jnp.float32)
        * scale_factor
    )
    return query_grad.reshape(query_heads.shape), key_grad, value_grad


def row_scatter_sum(vectors):
    count = lax.axis_size("row")
    blocks = jnp.moveaxis(vectors.reshape(vectors.shape[0], count, -1), 1, 0)
    return jnp.sum(lax.all_to_all(blocks, "row", split_axis=0, concat_axis=0, tiled=True), axis=0)


GRAD_BLOCK = 128


def split_columns(packed, widths):
    pieces = []
    offset = 0
    for width in widths:
        pieces.append(packed[:, offset : offset + width])
        offset += width
    return pieces


def col_scatter(values):
    count = lax.axis_size("col")
    lead = values.shape[:-1]
    blocks = jnp.moveaxis(values.reshape(*lead, count, values.shape[-1] // count), -2, 0)
    received = lax.all_to_all(blocks, "col", split_axis=0, concat_axis=0, tiled=True)
    return jnp.sum(received.astype(jnp.float32), axis=0)


def col_gather(block):
    count = lax.axis_size("col")
    copies = jnp.broadcast_to(block[None], (count,) + block.shape)
    received = lax.all_to_all(copies, "col", split_axis=0, concat_axis=0, tiled=True)
    return jnp.moveaxis(received, 0, -2).reshape(*block.shape[:-1], count * block.shape[-1])


def col_sum(values):
    return col_gather(col_scatter(values).astype(jnp.bfloat16)).astype(jnp.float32)


def gather_rows(parts):
    return lax.all_gather(jnp.concatenate(parts, axis=1), "row", axis=0, tiled=True)


def grad_plain_kernel(select_ref, left_ref, right_ref, out_ref):
    out_ref[...] = jnp.dot(
        left_ref[0], right_ref[...], preferred_element_type=jnp.float32
    ).astype(out_ref.dtype)


def packed_weight_grads(lefts, segments):
    left_stack = jnp.stack([left.T for left in lefts])
    right = jnp.concatenate([seg for _, seg in segments], axis=1)
    column_owner = []
    for index, seg in segments:
        column_owner += [index] * seg.shape[1]
    assert len(column_owner) % GRAD_BLOCK == 0
    select = column_owner[::GRAD_BLOCK]
    assert column_owner == [owner for owner in select for _ in range(GRAD_BLOCK)]
    right_blocks = len(select)
    features, tokens = left_stack.shape[1], left_stack.shape[2]
    in_specs = [
        pl.BlockSpec((1, features, tokens), lambda j, sel: (sel[j], 0, 0)),
        pl.BlockSpec((tokens, GRAD_BLOCK), lambda j, sel: (0, jnp.minimum(j, right_blocks - 1))),
    ]
    return pl.pallas_call(
        grad_plain_kernel,
        out_shape=jax.ShapeDtypeStruct((features, len(select) * GRAD_BLOCK), jnp.bfloat16),
        grid_spec=pltpu.PrefetchScalarGridSpec(
            num_scalar_prefetch=1,
            grid=(len(select),),
            in_specs=in_specs,
            out_specs=pl.BlockSpec((features, GRAD_BLOCK), lambda j, sel: (0, j)),
        ),
    )(jnp.asarray(select, dtype=jnp.int32), left_stack, right)


def body(
    tokens,
    cotangent,
    destination,
    segment_ids,
    attn_gain,
    w_query,
    w_key,
    w_value,
    w_output,
    ffn_gain,
    w_gate,
    w_up,
    w_down,
):
    row_count = tokens.shape[0]
    quarter = tokens.shape[1]
    col_start = lax.axis_index("col") * quarter
    send_order = jnp.argsort(destination)
    slot_ids = destination[send_order] % row_count
    arrived_pair, arrived_slots = (
        lax.all_to_all(
            jnp.stack([tokens, cotangent])[:, send_order], "row", split_axis=1, concat_axis=1, tiled=True
        ),
        lax.all_to_all(slot_ids, "row", split_axis=0, concat_axis=0, tiled=True),
    )
    placing = jnp.argsort(arrived_slots)
    attn_widths = [w_query.shape[1], w_key.shape[1], w_value.shape[1], w_output.shape[1]]
    ffn_widths = [w_gate.shape[1], w_up.shape[1], w_down.shape[1]]
    weights_packed = gather_rows([w_query, w_key, w_value, w_output, w_gate, w_up, w_down])
    attn_packed = weights_packed[:, : sum(attn_widths)]
    ffn_packed = weights_packed[:, sum(attn_widths) :]
    placed_pair = arrived_pair[:, placing]
    full_rows = col_gather(placed_pair[0])
    full_grads = col_gather(placed_pair[1])
    query_w, key_w, value_w, output_w = split_columns(attn_packed, attn_widths)
    cosine, sine = rope_tables(positions_of(segment_ids))
    allowed = allowed_pairs(segment_ids)
    rows_wide = full_rows.astype(jnp.float32)
    inv_one = rms_scale(rows_wide)
    normed_one = (rows_wide * inv_one * attn_gain).astype(jnp.bfloat16)
    query = matmul(normed_one, query_w)
    key_raw = matmul(normed_one, key_w)
    value_raw = matmul(normed_one, value_w)
    query_heads_count = query.shape[1] // HD
    kv_count = key_raw.shape[1] // HD
    query_rot = (
        rotate(query.reshape(row_count, query_heads_count, HD), cosine, sine)
        .astype(jnp.bfloat16)
        .transpose(1, 0, 2)
    )
    key_rot = (
        rotate(key_raw.reshape(row_count, kv_count, HD), cosine, sine)
        .astype(jnp.bfloat16)
        .transpose(1, 0, 2)
    )
    value_heads = value_raw.astype(jnp.bfloat16).reshape(row_count, kv_count, HD).transpose(1, 0, 2)
    scale_factor = HD ** (-0.5)
    mixed_heads, log_totals = attention_forward(
        query_rot, key_rot, value_heads, allowed, scale_factor
    )
    mixed = (
        mixed_heads.transpose(1, 0, 2)
        .reshape(row_count, query_heads_count * HD)
        .astype(jnp.bfloat16)
    )
    attn_terms = matmul(mixed, output_w.T)
    attn_full = lax.psum(attn_terms.astype(jnp.bfloat16), "col").astype(jnp.float32)
    resid = rows_wide + attn_full
    inv_two = rms_scale(resid)
    normed_two = (resid * inv_two * ffn_gain).astype(jnp.bfloat16)
    resid_part = lax.dynamic_slice_in_dim(resid, col_start, quarter, 1)
    gate_w, up_w, down_w = split_columns(ffn_packed, ffn_widths)
    gate = matmul(normed_two, gate_w)
    upper = matmul(normed_two, up_w)
    sigmoid_gate = jax.nn.sigmoid(gate)
    activ = (gate * sigmoid_gate * upper).astype(jnp.bfloat16)
    ffn_share_low = lax.psum_scatter(
        matmul(activ, down_w.T).astype(jnp.bfloat16), "col", scatter_dimension=1, tiled=True
    )
    act_grad = matmul(full_grads, down_w)
    gate_grad = (act_grad * upper * sigmoid_gate * (1.0 + gate * (1.0 - sigmoid_gate))).astype(
        jnp.bfloat16
    )
    up_grad = (act_grad * gate * sigmoid_gate).astype(jnp.bfloat16)
    normed_terms_two = matmul(gate_grad, gate_w.T) + matmul(up_grad, up_w.T)
    ffn_grads_packed = packed_weight_grads(
        [normed_two, full_grads], [(0, gate_grad), (0, up_grad), (1, activ)]
    )
    ffn_grads_packed, ffn_share_low = lax.optimization_barrier((ffn_grads_packed, ffn_share_low))
    normed_low_two, ffn_grads_packed = lax.optimization_barrier(
        (normed_terms_two.astype(jnp.bfloat16), ffn_grads_packed)
    )
    normed_grad_two = col_sum(normed_low_two)
    resid_norm_grad, ffn_gain_grad = norm_back(resid, inv_two, ffn_gain, normed_grad_two)
    ffn_grads_local = lax.psum_scatter(ffn_grads_packed, "row", scatter_dimension=0, tiled=True)
    resid_grad = full_grads.astype(jnp.float32) + resid_norm_grad
    attn_grad_low = resid_grad.astype(jnp.bfloat16)
    mixed_grad = matmul(attn_grad_low, output_w).astype(jnp.bfloat16)
    mixed_grad_heads = mixed_grad.reshape(row_count, query_heads_count, HD).transpose(1, 0, 2)
    query_grads, key_grads, value_grads = attention_backward(
        query_rot, key_rot, value_heads, mixed_grad_heads, log_totals, allowed, scale_factor
    )
    query_grad = (
        rotate_back(query_grads.transpose(1, 0, 2), cosine, sine)
        .reshape(row_count, query_heads_count * HD)
        .astype(jnp.bfloat16)
    )
    key_sum = key_grads.transpose(1, 0, 2)
    key_grad = (
        rotate_back(key_sum, cosine, sine).reshape(row_count, kv_count * HD).astype(jnp.bfloat16)
    )
    value_sum = value_grads.transpose(1, 0, 2)
    value_grad = value_sum.reshape(row_count, kv_count * HD).astype(jnp.bfloat16)
    normed_terms_one = (
        matmul(query_grad, query_w.T) + matmul(key_grad, key_w.T) + matmul(value_grad, value_w.T)
    )
    output_share = (resid_part + ffn_share_low.astype(jnp.float32)).astype(jnp.bfloat16)
    back_rows = lax.all_to_all(
        output_share[arrived_slots], "row", split_axis=0, concat_axis=0, tiled=True
    )
    attn_grads_packed, ffn_grads_local, back_rows, normed_low_one = lax.optimization_barrier(
        (
            packed_weight_grads(
                [normed_one, attn_grad_low],
                [(0, query_grad), (0, key_grad), (0, value_grad), (1, mixed)],
            ),
            ffn_grads_local,
            back_rows,
            normed_terms_one.astype(jnp.bfloat16),
        )
    )
    attn_grads_local = lax.psum_scatter(attn_grads_packed, "row", scatter_dimension=0, tiled=True)
    normed_grad_one = col_sum(normed_low_one)
    rows_norm_grad, attn_gain_grad = norm_back(rows_wide, inv_one, attn_gain, normed_grad_one)
    rows_grad = resid_grad + rows_norm_grad
    input_share = lax.dynamic_slice_in_dim(rows_grad, col_start, quarter, 1).astype(jnp.bfloat16)
    query_result, key_result, value_result, output_result = split_columns(
        attn_grads_local.astype(jnp.float32), attn_widths
    )
    gate_result, up_result, down_result = split_columns(
        ffn_grads_local.astype(jnp.float32), ffn_widths
    )
    row_devices = lax.axis_size("row")
    gains = jnp.stack([attn_gain_grad, ffn_gain_grad])
    gain_blocks = jnp.moveaxis(gains.reshape(2, row_devices, -1), 1, 0).reshape(row_devices, -1)
    gain_width = gain_blocks.shape[1]
    assert gain_width <= quarter
    gain_rows = jnp.pad(gain_blocks, ((0, 0), (0, quarter - gain_width)))[:, None, :]
    token_rows = input_share[arrived_slots].reshape(row_devices, -1, quarter)
    received = lax.all_to_all(
        jnp.concatenate([token_rows, gain_rows.astype(jnp.bfloat16)], axis=1),
        "row",
        split_axis=0,
        concat_axis=0,
        tiled=True,
    )
    back_grads = received[:, :-1].reshape(row_count, quarter)
    gain_sums = jnp.sum(received[:, -1, :gain_width].astype(jnp.float32), axis=0).reshape(2, -1)
    attn_gain_result, ffn_gain_result = gain_sums[0], gain_sums[1]
    restore = jnp.argsort(send_order)
    return (
        back_rows[restore],
        back_grads[restore],
        attn_gain_result,
        query_result,
        key_result,
        value_result,
        output_result,
        ffn_gain_result,
        gate_result,
        up_result,
        down_result,
    )

def solution(mesh):
    placed = (
        P("row", "col"),
        P("row", "col"),
        P("row"),
        P("row"),
        P(),
        P("row", "col"),
        P("row", "col"),
        P("row", "col"),
        P("row", "col"),
        P(),
        P("row", "col"),
        P("row", "col"),
        P("row", "col"),
    )
    return jax.shard_map(
        body,
        mesh=mesh,
        in_specs=placed,
        out_specs=(
            P("row", "col"),
            P("row", "col"),
            P("row"),
            P("row", "col"),
            P("row", "col"),
            P("row", "col"),
            P("row", "col"),
            P("row"),
            P("row", "col"),
            P("row", "col"),
            P("row", "col"),
        ),
        check_vma=False,
    )
```

```python
from functools import partial

import jax
import jax.numpy as jnp
from jax import lax
from jax.experimental import pallas as pl
from jax.experimental.pallas import tpu as pltpu
from jax.sharding import PartitionSpec as P

HEADS = 32
KV = 4
HD = 64


EPS = 1e-05
ROPE_BASE = 10000.0


def rope_tables(positions):
    half_width = HD // 2
    freqs = ROPE_BASE ** (-(jnp.arange(half_width, dtype=jnp.float32) * 2.0 / HD))
    angles = positions.astype(jnp.float32)[:, None] * freqs[None, :]
    return (jnp.cos(angles)[:, None, :], jnp.sin(angles)[:, None, :])


def rotate(values, cosine, sine):
    half_width = values.shape[-1] // 2
    first = values[..., :half_width]
    second = values[..., half_width:]
    return jnp.concatenate(
        [first * cosine - second * sine, second * cosine + first * sine], axis=-1
    )


def rotate_back(grads, cosine, sine):
    half_width = grads.shape[-1] // 2
    first = grads[..., :half_width]
    second = grads[..., half_width:]
    return jnp.concatenate(
        [first * cosine + second * sine, second * cosine - first * sine], axis=-1
    )


def positions_of(segment_ids):
    index = jnp.arange(segment_ids.shape[0], dtype=jnp.int32)
    change = jnp.concatenate([jnp.ones((1,), dtype=jnp.bool_), segment_ids[1:] != segment_ids[:-1]])
    starts = jnp.where(change, index, jnp.zeros_like(index))
    return index - lax.cummax(starts, axis=0)


def allowed_pairs(segment_ids):
    index = jnp.arange(segment_ids.shape[0], dtype=jnp.int32)
    return (segment_ids[:, None] == segment_ids[None, :]) & (index[None, :] <= index[:, None])


def rms_scale(values):
    return lax.rsqrt(jnp.mean(values * values, axis=-1, keepdims=True) + EPS)


def norm_back(values, inv_root, gain, grads):
    normed = values * inv_root
    scaled = grads * gain
    result = inv_root * (scaled - normed * jnp.mean(scaled * normed, axis=-1, keepdims=True))
    return (result, jnp.sum(grads * normed, axis=0))


def matmul(left, right):
    return jnp.dot(left, right, preferred_element_type=jnp.float32)


def head_scores(query_head, key_head, allowed, scale_factor):
    scores = matmul(query_head, key_head.T) * scale_factor
    return jnp.where(allowed, scores, -1e30)


def head_forward(inputs, key_heads, value_heads, allowed, scale_factor):
    query_head, kv_slot = inputs
    scores = head_scores(query_head, key_heads[kv_slot], allowed, scale_factor)
    peak = jnp.max(scores, axis=-1, keepdims=True)
    expo = jnp.exp(scores - peak)
    total = jnp.sum(expo, axis=-1, keepdims=True)
    probs = expo / total
    mixed = matmul(probs.astype(jnp.bfloat16), value_heads[kv_slot])
    return (mixed, (peak + jnp.log(total))[:, 0])


def head_backward(inputs, key_heads, value_heads, allowed, scale_factor):
    query_head, kv_slot, grad_head, log_total = inputs
    key_head = key_heads[kv_slot]
    value_head = value_heads[kv_slot]
    scores = head_scores(query_head, key_head, allowed, scale_factor)
    probs = jnp.exp(scores - log_total[:, None])
    prob_grad = matmul(grad_head, value_head.T)
    value_grad = matmul(probs.astype(jnp.bfloat16).T, grad_head)
    inner = jnp.sum(probs * prob_grad, axis=-1, keepdims=True)
    score_grad = (probs * (prob_grad - inner)).astype(jnp.bfloat16)
    query_grad = matmul(score_grad, key_head) * scale_factor
    key_grad = matmul(score_grad.T, query_head) * scale_factor
    return (query_grad, key_grad, value_grad)


def grouped(heads, kv_count):
    return heads.reshape(kv_count, heads.shape[0] // kv_count, *heads.shape[1:])


def group_scores(query_groups, key_heads, allowed, scale_factor):
    scores = (
        jnp.einsum("kgqd,kpd->kgqp", query_groups, key_heads, preferred_element_type=jnp.float32)
        * scale_factor
    )
    return jnp.where(allowed, scores, -1e30)


def attention_forward(query_heads, key_heads, value_heads, allowed, scale_factor):
    query_groups = grouped(query_heads, key_heads.shape[0])
    scores = group_scores(query_groups, key_heads, allowed, scale_factor)
    peak = jnp.max(scores, axis=-1, keepdims=True)
    expo = jnp.exp(scores - peak)
    total = jnp.sum(expo, axis=-1, keepdims=True)
    probs = expo / total
    mixed = jnp.einsum(
        "kgqp,kpd->kgqd", probs.astype(jnp.bfloat16), value_heads, preferred_element_type=jnp.float32
    )
    return mixed.reshape(query_heads.shape), (peak + jnp.log(total))[..., 0]


def attention_backward(
    query_heads, key_heads, value_heads, grad_heads, log_totals, allowed, scale_factor
):
    kv_count = key_heads.shape[0]
    query_groups = grouped(query_heads, kv_count)
    grad_groups = grouped(grad_heads, kv_count)
    scores = group_scores(query_groups, key_heads, allowed, scale_factor)
    probs = jnp.exp(scores - log_totals[..., None])
    prob_grad = jnp.einsum(
        "kgqd,kpd->kgqp", grad_groups, value_heads, preferred_element_type=jnp.float32
    )
    value_grad = jnp.einsum(
        "kgqp,kgqd->kpd", probs.astype(jnp.bfloat16), grad_groups, preferred_element_type=jnp.float32
    )
    inner = jnp.sum(probs * prob_grad, axis=-1, keepdims=True)
    score_grad = (probs * (prob_grad - inner)).astype(jnp.bfloat16)
    query_grad = (
        jnp.einsum("kgqp,kpd->kgqd", score_grad, key_heads, preferred_element_type=jnp.float32)
        * scale_factor
    )
    key_grad = (
        jnp.einsum("kgqp,kgqd->kpd", score_grad, query_groups, preferred_element_type=jnp.float32)
        * scale_factor
    )
    return query_grad.reshape(query_heads.shape), key_grad, value_grad


def row_scatter_sum(vectors):
    count = lax.axis_size("row")
    blocks = jnp.moveaxis(vectors.reshape(vectors.shape[0], count, -1), 1, 0)
    return jnp.sum(lax.all_to_all(blocks, "row", split_axis=0, concat_axis=0, tiled=True), axis=0)


GRAD_BLOCK = 128


def split_columns(packed, widths):
    pieces = []
    offset = 0
    for width in widths:
        pieces.append(packed[:, offset : offset + width])
        offset += width
    return pieces


def col_scatter(values):
    count = lax.axis_size("col")
    lead = values.shape[:-1]
    blocks = jnp.moveaxis(values.reshape(*lead, count, values.shape[-1] // count), -2, 0)
    received = lax.all_to_all(blocks, "col", split_axis=0, concat_axis=0, tiled=True)
    return jnp.sum(received.astype(jnp.float32), axis=0)


def col_gather(block):
    count = lax.axis_size("col")
    copies = jnp.broadcast_to(block[None], (count,) + block.shape)
    received = lax.all_to_all(copies, "col", split_axis=0, concat_axis=0, tiled=True)
    return jnp.moveaxis(received, 0, -2).reshape(*block.shape[:-1], count * block.shape[-1])


def col_sum(values):
    return col_gather(col_scatter(values).astype(jnp.bfloat16)).astype(jnp.float32)


def gather_rows(parts):
    return lax.all_gather(jnp.concatenate(parts, axis=1), "row", axis=0, tiled=True)


def grad_wide_kernel(select_ref, left_ref, right_ref, out_ref):
    step = pl.program_id(0)
    parts = out_ref.shape[1] // GRAD_BLOCK
    for part in range(parts):
        owner = select_ref[step * parts + part]
        columns = slice(part * GRAD_BLOCK, (part + 1) * GRAD_BLOCK)
        out_ref[:, columns] = jnp.dot(
            left_ref[owner], right_ref[:, columns], preferred_element_type=jnp.float32
        ).astype(out_ref.dtype)


def packed_weight_grads(lefts, segments):
    left_stack = jnp.stack([left.T for left in lefts])
    right = jnp.concatenate([seg for _, seg in segments], axis=1)
    column_owner = []
    for index, seg in segments:
        column_owner += [index] * seg.shape[1]
    assert len(column_owner) % GRAD_BLOCK == 0
    select = column_owner[::GRAD_BLOCK]
    assert column_owner == [owner for owner in select for _ in range(GRAD_BLOCK)]
    parts = next(m for m in (4, 3, 2, 1) if len(select) % m == 0)
    width = parts * GRAD_BLOCK
    features, tokens = left_stack.shape[1], left_stack.shape[2]
    in_specs = [
        pl.BlockSpec(left_stack.shape, lambda j, sel: (0, 0, 0)),
        pl.BlockSpec((tokens, width), lambda j, sel: (0, j)),
    ]
    return pl.pallas_call(
        grad_wide_kernel,
        out_shape=jax.ShapeDtypeStruct((features, right.shape[1]), jnp.bfloat16),
        grid_spec=pltpu.PrefetchScalarGridSpec(
            num_scalar_prefetch=1,
            grid=(len(select) // parts,),
            in_specs=in_specs,
            out_specs=pl.BlockSpec((features, width), lambda j, sel: (0, j)),
        ),
    )(jnp.asarray(select, dtype=jnp.int32), left_stack, right)


def body(
    tokens,
    cotangent,
    destination,
    segment_ids,
    attn_gain,
    w_query,
    w_key,
    w_value,
    w_output,
    ffn_gain,
    w_gate,
    w_up,
    w_down,
):
    row_count = tokens.shape[0]
    quarter = tokens.shape[1]
    col_start = lax.axis_index("col") * quarter
    send_order = jnp.argsort(destination)
    slot_ids = destination[send_order] % row_count
    arrived_pair, arrived_slots = (
        lax.all_to_all(
            jnp.stack([tokens, cotangent])[:, send_order], "row", split_axis=1, concat_axis=1, tiled=True
        ),
        lax.all_to_all(slot_ids, "row", split_axis=0, concat_axis=0, tiled=True),
    )
    placing = jnp.argsort(arrived_slots)
    attn_widths = [w_query.shape[1], w_key.shape[1], w_value.shape[1], w_output.shape[1]]
    ffn_widths = [w_gate.shape[1], w_up.shape[1], w_down.shape[1]]
    weights_packed = gather_rows([w_query, w_key, w_value, w_output, w_gate, w_up, w_down])
    attn_packed = weights_packed[:, : sum(attn_widths)]
    ffn_packed = weights_packed[:, sum(attn_widths) :]
    placed_pair = arrived_pair[:, placing]
    full_rows = col_gather(placed_pair[0])
    full_grads = col_gather(placed_pair[1])
    query_w, key_w, value_w, output_w = split_columns(attn_packed, attn_widths)
    cosine, sine = rope_tables(positions_of(segment_ids))
    allowed = allowed_pairs(segment_ids)
    rows_wide = full_rows.astype(jnp.float32)
    inv_one = rms_scale(rows_wide)
    normed_one = (rows_wide * inv_one * attn_gain).astype(jnp.bfloat16)
    query = matmul(normed_one, query_w)
    key_raw = matmul(normed_one, key_w)
    value_raw = matmul(normed_one, value_w)
    query_heads_count = query.shape[1] // HD
    kv_count = key_raw.shape[1] // HD
    query_rot = (
        rotate(query.reshape(row_count, query_heads_count, HD), cosine, sine)
        .astype(jnp.bfloat16)
        .transpose(1, 0, 2)
    )
    key_rot = (
        rotate(key_raw.reshape(row_count, kv_count, HD), cosine, sine)
        .astype(jnp.bfloat16)
        .transpose(1, 0, 2)
    )
    value_heads = value_raw.astype(jnp.bfloat16).reshape(row_count, kv_count, HD).transpose(1, 0, 2)
    scale_factor = HD ** (-0.5)
    mixed_heads, log_totals = attention_forward(
        query_rot, key_rot, value_heads, allowed, scale_factor
    )
    mixed = (
        mixed_heads.transpose(1, 0, 2)
        .reshape(row_count, query_heads_count * HD)
        .astype(jnp.bfloat16)
    )
    attn_terms = matmul(mixed, output_w.T)
    attn_full = lax.psum(attn_terms.astype(jnp.bfloat16), "col").astype(jnp.float32)
    resid = rows_wide + attn_full
    inv_two = rms_scale(resid)
    normed_two = (resid * inv_two * ffn_gain).astype(jnp.bfloat16)
    resid_part = lax.dynamic_slice_in_dim(resid, col_start, quarter, 1)
    gate_w, up_w, down_w = split_columns(ffn_packed, ffn_widths)
    gate = matmul(normed_two, gate_w)
    upper = matmul(normed_two, up_w)
    sigmoid_gate = jax.nn.sigmoid(gate)
    activ = (gate * sigmoid_gate * upper).astype(jnp.bfloat16)
    ffn_share_low = lax.psum_scatter(
        matmul(activ, down_w.T).astype(jnp.bfloat16), "col", scatter_dimension=1, tiled=True
    )
    act_grad = matmul(full_grads, down_w)
    gate_grad = (act_grad * upper * sigmoid_gate * (1.0 + gate * (1.0 - sigmoid_gate))).astype(
        jnp.bfloat16
    )
    up_grad = (act_grad * gate * sigmoid_gate).astype(jnp.bfloat16)
    normed_terms_two = matmul(gate_grad, gate_w.T) + matmul(up_grad, up_w.T)
    ffn_grads_packed = packed_weight_grads(
        [normed_two, full_grads], [(0, gate_grad), (0, up_grad), (1, activ)]
    )
    ffn_grads_packed, ffn_share_low = lax.optimization_barrier((ffn_grads_packed, ffn_share_low))
    normed_low_two, ffn_grads_packed = lax.optimization_barrier(
        (normed_terms_two.astype(jnp.bfloat16), ffn_grads_packed)
    )
    normed_grad_two = col_sum(normed_low_two)
    resid_norm_grad, ffn_gain_grad = norm_back(resid, inv_two, ffn_gain, normed_grad_two)
    ffn_grads_local = lax.psum_scatter(ffn_grads_packed, "row", scatter_dimension=0, tiled=True)
    resid_grad = full_grads.astype(jnp.float32) + resid_norm_grad
    attn_grad_low = resid_grad.astype(jnp.bfloat16)
    mixed_grad = matmul(attn_grad_low, output_w).astype(jnp.bfloat16)
    mixed_grad_heads = mixed_grad.reshape(row_count, query_heads_count, HD).transpose(1, 0, 2)
    query_grads, key_grads, value_grads = attention_backward(
        query_rot, key_rot, value_heads, mixed_grad_heads, log_totals, allowed, scale_factor
    )
    query_grad = (
        rotate_back(query_grads.transpose(1, 0, 2), cosine, sine)
        .reshape(row_count, query_heads_count * HD)
        .astype(jnp.bfloat16)
    )
    key_sum = key_grads.transpose(1, 0, 2)
    key_grad = (
        rotate_back(key_sum, cosine, sine).reshape(row_count, kv_count * HD).astype(jnp.bfloat16)
    )
    value_sum = value_grads.transpose(1, 0, 2)
    value_grad = value_sum.reshape(row_count, kv_count * HD).astype(jnp.bfloat16)
    normed_terms_one = (
        matmul(query_grad, query_w.T) + matmul(key_grad, key_w.T) + matmul(value_grad, value_w.T)
    )
    output_share = (resid_part + ffn_share_low.astype(jnp.float32)).astype(jnp.bfloat16)
    back_rows = lax.all_to_all(
        output_share[arrived_slots], "row", split_axis=0, concat_axis=0, tiled=True
    )
    attn_grads_packed, ffn_grads_local, back_rows, normed_low_one = lax.optimization_barrier(
        (
            packed_weight_grads(
                [normed_one, attn_grad_low],
                [(0, query_grad), (0, key_grad), (0, value_grad), (1, mixed)],
            ),
            ffn_grads_local,
            back_rows,
            normed_terms_one.astype(jnp.bfloat16),
        )
    )
    attn_grads_local = lax.psum_scatter(attn_grads_packed, "row", scatter_dimension=0, tiled=True)
    normed_grad_one = col_sum(normed_low_one)
    rows_norm_grad, attn_gain_grad = norm_back(rows_wide, inv_one, attn_gain, normed_grad_one)
    rows_grad = resid_grad + rows_norm_grad
    input_share = lax.dynamic_slice_in_dim(rows_grad, col_start, quarter, 1).astype(jnp.bfloat16)
    query_result, key_result, value_result, output_result = split_columns(
        attn_grads_local.astype(jnp.float32), attn_widths
    )
    gate_result, up_result, down_result = split_columns(
        ffn_grads_local.astype(jnp.float32), ffn_widths
    )
    row_devices = lax.axis_size("row")
    gains = jnp.stack([attn_gain_grad, ffn_gain_grad])
    gain_blocks = jnp.moveaxis(gains.reshape(2, row_devices, -1), 1, 0).reshape(row_devices, -1)
    gain_width = gain_blocks.shape[1]
    assert gain_width <= quarter
    gain_rows = jnp.pad(gain_blocks, ((0, 0), (0, quarter - gain_width)))[:, None, :]
    token_rows = input_share[arrived_slots].reshape(row_devices, -1, quarter)
    received = lax.all_to_all(
        jnp.concatenate([token_rows, gain_rows.astype(jnp.bfloat16)], axis=1),
        "row",
        split_axis=0,
        concat_axis=0,
        tiled=True,
    )
    back_grads = received[:, :-1].reshape(row_count, quarter)
    gain_sums = jnp.sum(received[:, -1, :gain_width].astype(jnp.float32), axis=0).reshape(2, -1)
    attn_gain_result, ffn_gain_result = gain_sums[0], gain_sums[1]
    restore = jnp.argsort(send_order)
    return (
        back_rows[restore],
        back_grads[restore],
        attn_gain_result,
        query_result,
        key_result,
        value_result,
        output_result,
        ffn_gain_result,
        gate_result,
        up_result,
        down_result,
    )

def solution(mesh):
    placed = (
        P("row", "col"),
        P("row", "col"),
        P("row"),
        P("row"),
        P(),
        P("row", "col"),
        P("row", "col"),
        P("row", "col"),
        P("row", "col"),
        P(),
        P("row", "col"),
        P("row", "col"),
        P("row", "col"),
    )
    return jax.shard_map(
        body,
        mesh=mesh,
        in_specs=placed,
        out_specs=(
            P("row", "col"),
            P("row", "col"),
            P("row"),
            P("row", "col"),
            P("row", "col"),
            P("row", "col"),
            P("row", "col"),
            P("row"),
            P("row", "col"),
            P("row", "col"),
            P("row", "col"),
        ),
        check_vma=False,
    )
```

```python
from functools import partial

import jax
import jax.numpy as jnp
from jax import lax
from jax.experimental import pallas as pl
from jax.experimental.pallas import tpu as pltpu
from jax.sharding import PartitionSpec as P

HEADS = 32
KV = 4
HD = 64


EPS = 1e-05
ROPE_BASE = 10000.0


def rope_tables(positions):
    half_width = HD // 2
    freqs = ROPE_BASE ** (-(jnp.arange(half_width, dtype=jnp.float32) * 2.0 / HD))
    angles = positions.astype(jnp.float32)[:, None] * freqs[None, :]
    return (jnp.cos(angles)[:, None, :], jnp.sin(angles)[:, None, :])


def rotate(values, cosine, sine):
    half_width = values.shape[-1] // 2
    first = values[..., :half_width]
    second = values[..., half_width:]
    return jnp.concatenate(
        [first * cosine - second * sine, second * cosine + first * sine], axis=-1
    )


def rotate_back(grads, cosine, sine):
    half_width = grads.shape[-1] // 2
    first = grads[..., :half_width]
    second = grads[..., half_width:]
    return jnp.concatenate(
        [first * cosine + second * sine, second * cosine - first * sine], axis=-1
    )


def positions_of(segment_ids):
    index = jnp.arange(segment_ids.shape[0], dtype=jnp.int32)
    change = jnp.concatenate([jnp.ones((1,), dtype=jnp.bool_), segment_ids[1:] != segment_ids[:-1]])
    starts = jnp.where(change, index, jnp.zeros_like(index))
    return index - lax.cummax(starts, axis=0)


def allowed_pairs(segment_ids):
    index = jnp.arange(segment_ids.shape[0], dtype=jnp.int32)
    return (segment_ids[:, None] == segment_ids[None, :]) & (index[None, :] <= index[:, None])


def rms_scale(values):
    return lax.rsqrt(jnp.mean(values * values, axis=-1, keepdims=True) + EPS)


def norm_back(values, inv_root, gain, grads):
    normed = values * inv_root
    scaled = grads * gain
    result = inv_root * (scaled - normed * jnp.mean(scaled * normed, axis=-1, keepdims=True))
    return (result, jnp.sum(grads * normed, axis=0))


def matmul(left, right):
    return jnp.dot(left, right, preferred_element_type=jnp.float32)


def head_scores(query_head, key_head, allowed, scale_factor):
    scores = matmul(query_head, key_head.T) * scale_factor
    return jnp.where(allowed, scores, -1e30)


def head_forward(inputs, key_heads, value_heads, allowed, scale_factor):
    query_head, kv_slot = inputs
    scores = head_scores(query_head, key_heads[kv_slot], allowed, scale_factor)
    peak = jnp.max(scores, axis=-1, keepdims=True)
    expo = jnp.exp(scores - peak)
    total = jnp.sum(expo, axis=-1, keepdims=True)
    probs = expo / total
    mixed = matmul(probs.astype(jnp.bfloat16), value_heads[kv_slot])
    return (mixed, (peak + jnp.log(total))[:, 0])


def head_backward(inputs, key_heads, value_heads, allowed, scale_factor):
    query_head, kv_slot, grad_head, log_total = inputs
    key_head = key_heads[kv_slot]
    value_head = value_heads[kv_slot]
    scores = head_scores(query_head, key_head, allowed, scale_factor)
    probs = jnp.exp(scores - log_total[:, None])
    prob_grad = matmul(grad_head, value_head.T)
    value_grad = matmul(probs.astype(jnp.bfloat16).T, grad_head)
    inner = jnp.sum(probs * prob_grad, axis=-1, keepdims=True)
    score_grad = (probs * (prob_grad - inner)).astype(jnp.bfloat16)
    query_grad = matmul(score_grad, key_head) * scale_factor
    key_grad = matmul(score_grad.T, query_head) * scale_factor
    return (query_grad, key_grad, value_grad)


def grouped(heads, kv_count):
    return heads.reshape(kv_count, heads.shape[0] // kv_count, *heads.shape[1:])


def group_scores(query_groups, key_heads, allowed, scale_factor):
    scores = (
        jnp.einsum("kgqd,kpd->kgqp", query_groups, key_heads, preferred_element_type=jnp.float32)
        * scale_factor
    )
    return jnp.where(allowed, scores, -1e30)


def attention_forward(query_heads, key_heads, value_heads, allowed, scale_factor):
    query_groups = grouped(query_heads, key_heads.shape[0])
    scores = group_scores(query_groups, key_heads, allowed, scale_factor)
    peak = jnp.max(scores, axis=-1, keepdims=True)
    expo = jnp.exp(scores - peak)
    total = jnp.sum(expo, axis=-1, keepdims=True)
    probs = expo / total
    mixed = jnp.einsum(
        "kgqp,kpd->kgqd", probs.astype(jnp.bfloat16), value_heads, preferred_element_type=jnp.float32
    )
    return mixed.reshape(query_heads.shape), (peak + jnp.log(total))[..., 0]


def attention_backward(
    query_heads, key_heads, value_heads, grad_heads, log_totals, allowed, scale_factor
):
    kv_count = key_heads.shape[0]
    query_groups = grouped(query_heads, kv_count)
    grad_groups = grouped(grad_heads, kv_count)
    scores = group_scores(query_groups, key_heads, allowed, scale_factor)
    probs = jnp.exp(scores - log_totals[..., None])
    prob_grad = jnp.einsum(
        "kgqd,kpd->kgqp", grad_groups, value_heads, preferred_element_type=jnp.float32
    )
    value_grad = jnp.einsum(
        "kgqp,kgqd->kpd", probs.astype(jnp.bfloat16), grad_groups, preferred_element_type=jnp.float32
    )
    inner = jnp.sum(probs * prob_grad, axis=-1, keepdims=True)
    score_grad = (probs * (prob_grad - inner)).astype(jnp.bfloat16)
    query_grad = (
        jnp.einsum("kgqp,kpd->kgqd", score_grad, key_heads, preferred_element_type=jnp.float32)
        * scale_factor
    )
    key_grad = (
        jnp.einsum("kgqp,kgqd->kpd", score_grad, query_groups, preferred_element_type=jnp.float32)
        * scale_factor
    )
    return query_grad.reshape(query_heads.shape), key_grad, value_grad


def row_scatter_sum(vectors):
    count = lax.axis_size("row")
    blocks = jnp.moveaxis(vectors.reshape(vectors.shape[0], count, -1), 1, 0)
    return jnp.sum(lax.all_to_all(blocks, "row", split_axis=0, concat_axis=0, tiled=True), axis=0)


GRAD_BLOCK = 128


def split_columns(packed, widths):
    pieces = []
    offset = 0
    for width in widths:
        pieces.append(packed[:, offset : offset + width])
        offset += width
    return pieces


def col_scatter(values):
    count = lax.axis_size("col")
    lead = values.shape[:-1]
    blocks = jnp.moveaxis(values.reshape(*lead, count, values.shape[-1] // count), -2, 0)
    received = lax.all_to_all(blocks, "col", split_axis=0, concat_axis=0, tiled=True)
    return jnp.sum(received.astype(jnp.float32), axis=0)


def col_gather(block):
    count = lax.axis_size("col")
    copies = jnp.broadcast_to(block[None], (count,) + block.shape)
    received = lax.all_to_all(copies, "col", split_axis=0, concat_axis=0, tiled=True)
    return jnp.moveaxis(received, 0, -2).reshape(*block.shape[:-1], count * block.shape[-1])


def col_sum(values):
    return col_gather(col_scatter(values).astype(jnp.bfloat16)).astype(jnp.float32)


def gather_rows(parts):
    return lax.all_gather(jnp.concatenate(parts, axis=1), "row", axis=0, tiled=True)


def grad_wide_kernel(select_ref, left_ref, right_ref, out_ref):
    step = pl.program_id(0)
    parts = out_ref.shape[1] // GRAD_BLOCK
    for part in range(parts):
        owner = select_ref[step * parts + part]
        columns = slice(part * GRAD_BLOCK, (part + 1) * GRAD_BLOCK)
        out_ref[:, columns] = jnp.dot(
            left_ref[owner], right_ref[:, columns], preferred_element_type=jnp.float32
        ).astype(out_ref.dtype)


def packed_weight_grads(lefts, segments):
    left_stack = jnp.stack([left.T for left in lefts])
    right = jnp.concatenate([seg for _, seg in segments], axis=1)
    column_owner = []
    for index, seg in segments:
        column_owner += [index] * seg.shape[1]
    assert len(column_owner) % GRAD_BLOCK == 0
    select = column_owner[::GRAD_BLOCK]
    assert column_owner == [owner for owner in select for _ in range(GRAD_BLOCK)]
    parts = next(m for m in (4, 3, 2, 1) if len(select) % m == 0)
    width = parts * GRAD_BLOCK
    features, tokens = left_stack.shape[1], left_stack.shape[2]
    in_specs = [
        pl.BlockSpec(left_stack.shape, lambda j, sel: (0, 0, 0)),
        pl.BlockSpec((tokens, width), lambda j, sel: (0, j)),
    ]
    return pl.pallas_call(
        grad_wide_kernel,
        out_shape=jax.ShapeDtypeStruct((features, right.shape[1]), jnp.bfloat16),
        grid_spec=pltpu.PrefetchScalarGridSpec(
            num_scalar_prefetch=1,
            grid=(len(select) // parts,),
            in_specs=in_specs,
            out_specs=pl.BlockSpec((features, width), lambda j, sel: (0, j)),
        ),
    )(jnp.asarray(select, dtype=jnp.int32), left_stack, right)


def body(
    tokens,
    cotangent,
    destination,
    segment_ids,
    attn_gain,
    w_query,
    w_key,
    w_value,
    w_output,
    ffn_gain,
    w_gate,
    w_up,
    w_down,
):
    row_count = tokens.shape[0]
    quarter = tokens.shape[1]
    col_start = lax.axis_index("col") * quarter
    send_order = jnp.argsort(destination)
    slot_ids = destination[send_order] % row_count
    arrived_pair, arrived_slots = (
        lax.all_to_all(
            jnp.stack([tokens, cotangent])[:, send_order], "row", split_axis=1, concat_axis=1, tiled=True
        ),
        lax.all_to_all(slot_ids, "row", split_axis=0, concat_axis=0, tiled=True),
    )
    placing = jnp.argsort(arrived_slots)
    attn_widths = [w_query.shape[1], w_key.shape[1], w_value.shape[1], w_output.shape[1]]
    ffn_widths = [w_gate.shape[1], w_up.shape[1], w_down.shape[1]]
    weights_packed = gather_rows([w_query, w_key, w_value, w_output, w_gate, w_up, w_down])
    attn_packed = weights_packed[:, : sum(attn_widths)]
    ffn_packed = weights_packed[:, sum(attn_widths) :]
    placed_pair = arrived_pair[:, placing]
    full_rows = col_gather(placed_pair[0])
    full_grads = col_gather(placed_pair[1])
    query_w, key_w, value_w, output_w = split_columns(attn_packed, attn_widths)
    cosine, sine = rope_tables(positions_of(segment_ids))
    allowed = allowed_pairs(segment_ids)
    rows_wide = full_rows.astype(jnp.float32)
    inv_one = rms_scale(rows_wide)
    normed_one = (rows_wide * inv_one * attn_gain).astype(jnp.bfloat16)
    query = matmul(normed_one, query_w)
    key_raw = matmul(normed_one, key_w)
    value_raw = matmul(normed_one, value_w)
    query_heads_count = query.shape[1] // HD
    kv_count = key_raw.shape[1] // HD
    query_rot = (
        rotate(query.reshape(row_count, query_heads_count, HD), cosine, sine)
        .astype(jnp.bfloat16)
        .transpose(1, 0, 2)
    )
    key_rot = (
        rotate(key_raw.reshape(row_count, kv_count, HD), cosine, sine)
        .astype(jnp.bfloat16)
        .transpose(1, 0, 2)
    )
    value_heads = value_raw.astype(jnp.bfloat16).reshape(row_count, kv_count, HD).transpose(1, 0, 2)
    scale_factor = HD ** (-0.5)
    mixed_heads, log_totals = attention_forward(
        query_rot, key_rot, value_heads, allowed, scale_factor
    )
    mixed = (
        mixed_heads.transpose(1, 0, 2)
        .reshape(row_count, query_heads_count * HD)
        .astype(jnp.bfloat16)
    )
    attn_terms = matmul(mixed, output_w.T)
    attn_full = lax.psum(attn_terms.astype(jnp.bfloat16), "col").astype(jnp.float32)
    resid = rows_wide + attn_full
    inv_two = rms_scale(resid)
    normed_two = (resid * inv_two * ffn_gain).astype(jnp.bfloat16)
    resid_part = lax.dynamic_slice_in_dim(resid, col_start, quarter, 1)
    gate_w, up_w, down_w = split_columns(ffn_packed, ffn_widths)
    gate = matmul(normed_two, gate_w)
    upper = matmul(normed_two, up_w)
    sigmoid_gate = jax.nn.sigmoid(gate)
    activ = (gate * sigmoid_gate * upper).astype(jnp.bfloat16)
    ffn_share_low = lax.psum_scatter(
        matmul(activ, down_w.T).astype(jnp.bfloat16), "col", scatter_dimension=1, tiled=True
    )
    act_grad = matmul(full_grads, down_w)
    gate_grad = (act_grad * upper * sigmoid_gate * (1.0 + gate * (1.0 - sigmoid_gate))).astype(
        jnp.bfloat16
    )
    up_grad = (act_grad * gate * sigmoid_gate).astype(jnp.bfloat16)
    normed_terms_two = matmul(gate_grad, gate_w.T) + matmul(up_grad, up_w.T)
    ffn_grads_packed = packed_weight_grads(
        [normed_two, full_grads], [(0, gate_grad), (0, up_grad), (1, activ)]
    )
    ffn_grads_packed, ffn_share_low = lax.optimization_barrier((ffn_grads_packed, ffn_share_low))
    normed_low_two, ffn_grads_packed = lax.optimization_barrier(
        (normed_terms_two.astype(jnp.bfloat16), ffn_grads_packed)
    )
    normed_grad_two = col_sum(normed_low_two)
    resid_norm_grad, ffn_gain_grad = norm_back(resid, inv_two, ffn_gain, normed_grad_two)
    ffn_grads_local = lax.psum_scatter(ffn_grads_packed, "row", scatter_dimension=0, tiled=True)
    resid_grad = full_grads.astype(jnp.float32) + resid_norm_grad
    attn_grad_low = resid_grad.astype(jnp.bfloat16)
    mixed_grad = matmul(attn_grad_low, output_w).astype(jnp.bfloat16)
    mixed_grad_heads = mixed_grad.reshape(row_count, query_heads_count, HD).transpose(1, 0, 2)
    query_grads, key_grads, value_grads = attention_backward(
        query_rot, key_rot, value_heads, mixed_grad_heads, log_totals, allowed, scale_factor
    )
    query_grad = (
        rotate_back(query_grads.transpose(1, 0, 2), cosine, sine)
        .reshape(row_count, query_heads_count * HD)
        .astype(jnp.bfloat16)
    )
    key_sum = key_grads.transpose(1, 0, 2)
    key_grad = (
        rotate_back(key_sum, cosine, sine).reshape(row_count, kv_count * HD).astype(jnp.bfloat16)
    )
    value_sum = value_grads.transpose(1, 0, 2)
    value_grad = value_sum.reshape(row_count, kv_count * HD).astype(jnp.bfloat16)
    normed_terms_one = (
        matmul(query_grad, query_w.T) + matmul(key_grad, key_w.T) + matmul(value_grad, value_w.T)
    )
    output_share = (resid_part + ffn_share_low.astype(jnp.float32)).astype(jnp.bfloat16)
    back_rows = lax.all_to_all(
        output_share[arrived_slots], "row", split_axis=0, concat_axis=0, tiled=True
    )
    attn_grads_packed, ffn_grads_local, back_rows, normed_low_one = lax.optimization_barrier(
        (
            packed_weight_grads(
                [normed_one, attn_grad_low],
                [(0, query_grad), (0, key_grad), (0, value_grad), (1, mixed)],
            ),
            ffn_grads_local,
            back_rows,
            normed_terms_one.astype(jnp.bfloat16),
        )
    )
    attn_grads_local = lax.psum_scatter(attn_grads_packed, "row", scatter_dimension=0, tiled=True)
    normed_grad_block = col_scatter(normed_low_one)
    normed_block = lax.dynamic_slice_in_dim(rows_wide, col_start, quarter, 1) * inv_one
    scaled_block = normed_grad_block * lax.dynamic_slice_in_dim(attn_gain, col_start, quarter, 0)
    token_part = jnp.sum(scaled_block * normed_block, axis=-1)
    gain_part = jnp.sum(normed_grad_block * normed_block, axis=0)
    exchanged = col_gather(jnp.concatenate([token_part, gain_part])).reshape(
        -1, token_part.shape[0] + gain_part.shape[0]
    )
    row_mean = jnp.sum(exchanged[:, : token_part.shape[0]], axis=0) / rows_wide.shape[-1]
    attn_gain_grad = exchanged[:, token_part.shape[0] :].reshape(-1)
    input_block = lax.dynamic_slice_in_dim(resid_grad, col_start, quarter, 1) + inv_one * (
        scaled_block - normed_block * row_mean[:, None]
    )
    input_share = input_block.astype(jnp.bfloat16)
    query_result, key_result, value_result, output_result = split_columns(
        attn_grads_local.astype(jnp.float32), attn_widths
    )
    gate_result, up_result, down_result = split_columns(
        ffn_grads_local.astype(jnp.float32), ffn_widths
    )
    row_devices = lax.axis_size("row")
    gains = jnp.stack([attn_gain_grad, ffn_gain_grad])
    gain_blocks = jnp.moveaxis(gains.reshape(2, row_devices, -1), 1, 0).reshape(row_devices, -1)
    gain_width = gain_blocks.shape[1]
    assert gain_width <= quarter
    gain_rows = jnp.pad(gain_blocks, ((0, 0), (0, quarter - gain_width)))[:, None, :]
    token_rows = input_share[arrived_slots].reshape(row_devices, -1, quarter)
    received = lax.all_to_all(
        jnp.concatenate([token_rows, gain_rows.astype(jnp.bfloat16)], axis=1),
        "row",
        split_axis=0,
        concat_axis=0,
        tiled=True,
    )
    back_grads = received[:, :-1].reshape(row_count, quarter)
    gain_sums = jnp.sum(received[:, -1, :gain_width].astype(jnp.float32), axis=0).reshape(2, -1)
    attn_gain_result, ffn_gain_result = gain_sums[0], gain_sums[1]
    restore = jnp.argsort(send_order)
    return (
        back_rows[restore],
        back_grads[restore],
        attn_gain_result,
        query_result,
        key_result,
        value_result,
        output_result,
        ffn_gain_result,
        gate_result,
        up_result,
        down_result,
    )

def solution(mesh):
    placed = (
        P("row", "col"),
        P("row", "col"),
        P("row"),
        P("row"),
        P(),
        P("row", "col"),
        P("row", "col"),
        P("row", "col"),
        P("row", "col"),
        P(),
        P("row", "col"),
        P("row", "col"),
        P("row", "col"),
    )
    return jax.shard_map(
        body,
        mesh=mesh,
        in_specs=placed,
        out_specs=(
            P("row", "col"),
            P("row", "col"),
            P("row"),
            P("row", "col"),
            P("row", "col"),
            P("row", "col"),
            P("row", "col"),
            P("row"),
            P("row", "col"),
            P("row", "col"),
            P("row", "col"),
        ),
        check_vma=False,
    )
```

```python
from functools import partial

import jax
import jax.numpy as jnp
from jax import lax
from jax.experimental import pallas as pl
from jax.experimental.pallas import tpu as pltpu
from jax.sharding import PartitionSpec as P

HEADS = 32
KV = 4
HD = 64


EPS = 1e-05
ROPE_BASE = 10000.0


def rope_tables(positions):
    half_width = HD // 2
    freqs = ROPE_BASE ** (-(jnp.arange(half_width, dtype=jnp.float32) * 2.0 / HD))
    angles = positions.astype(jnp.float32)[:, None] * freqs[None, :]
    return (jnp.cos(angles)[:, None, :], jnp.sin(angles)[:, None, :])


def rotate(values, cosine, sine):
    half_width = values.shape[-1] // 2
    first = values[..., :half_width]
    second = values[..., half_width:]
    return jnp.concatenate(
        [first * cosine - second * sine, second * cosine + first * sine], axis=-1
    )


def rotate_back(grads, cosine, sine):
    half_width = grads.shape[-1] // 2
    first = grads[..., :half_width]
    second = grads[..., half_width:]
    return jnp.concatenate(
        [first * cosine + second * sine, second * cosine - first * sine], axis=-1
    )


def positions_of(segment_ids):
    index = jnp.arange(segment_ids.shape[0], dtype=jnp.int32)
    change = jnp.concatenate([jnp.ones((1,), dtype=jnp.bool_), segment_ids[1:] != segment_ids[:-1]])
    starts = jnp.where(change, index, jnp.zeros_like(index))
    return index - lax.cummax(starts, axis=0)


def allowed_pairs(segment_ids):
    index = jnp.arange(segment_ids.shape[0], dtype=jnp.int32)
    return (segment_ids[:, None] == segment_ids[None, :]) & (index[None, :] <= index[:, None])


def rms_scale(values):
    return lax.rsqrt(jnp.mean(values * values, axis=-1, keepdims=True) + EPS)


def norm_back(values, inv_root, gain, grads):
    normed = values * inv_root
    scaled = grads * gain
    result = inv_root * (scaled - normed * jnp.mean(scaled * normed, axis=-1, keepdims=True))
    return (result, jnp.sum(grads * normed, axis=0))


def matmul(left, right):
    return jnp.dot(left, right, preferred_element_type=jnp.float32)


def head_scores(query_head, key_head, allowed, scale_factor):
    scores = matmul(query_head, key_head.T) * scale_factor
    return jnp.where(allowed, scores, -1e30)


def head_forward(inputs, key_heads, value_heads, allowed, scale_factor):
    query_head, kv_slot = inputs
    scores = head_scores(query_head, key_heads[kv_slot], allowed, scale_factor)
    peak = jnp.max(scores, axis=-1, keepdims=True)
    expo = jnp.exp(scores - peak)
    total = jnp.sum(expo, axis=-1, keepdims=True)
    probs = expo / total
    mixed = matmul(probs.astype(jnp.bfloat16), value_heads[kv_slot])
    return (mixed, (peak + jnp.log(total))[:, 0])


def head_backward(inputs, key_heads, value_heads, allowed, scale_factor):
    query_head, kv_slot, grad_head, log_total = inputs
    key_head = key_heads[kv_slot]
    value_head = value_heads[kv_slot]
    scores = head_scores(query_head, key_head, allowed, scale_factor)
    probs = jnp.exp(scores - log_total[:, None])
    prob_grad = matmul(grad_head, value_head.T)
    value_grad = matmul(probs.astype(jnp.bfloat16).T, grad_head)
    inner = jnp.sum(probs * prob_grad, axis=-1, keepdims=True)
    score_grad = (probs * (prob_grad - inner)).astype(jnp.bfloat16)
    query_grad = matmul(score_grad, key_head) * scale_factor
    key_grad = matmul(score_grad.T, query_head) * scale_factor
    return (query_grad, key_grad, value_grad)


def grouped(heads, kv_count):
    return heads.reshape(kv_count, heads.shape[0] // kv_count, *heads.shape[1:])


def group_scores(query_groups, key_heads, allowed, scale_factor):
    scores = (
        jnp.einsum("kgqd,kpd->kgqp", query_groups, key_heads, preferred_element_type=jnp.float32)
        * scale_factor
    )
    return jnp.where(allowed, scores, -1e30)


def attention_forward(query_heads, key_heads, value_heads, allowed, scale_factor):
    query_groups = grouped(query_heads, key_heads.shape[0])
    scores = group_scores(query_groups, key_heads, allowed, scale_factor)
    peak = jnp.max(scores, axis=-1, keepdims=True)
    expo = jnp.exp(scores - peak)
    total = jnp.sum(expo, axis=-1, keepdims=True)
    probs = expo / total
    mixed = jnp.einsum(
        "kgqp,kpd->kgqd", probs.astype(jnp.bfloat16), value_heads, preferred_element_type=jnp.float32
    )
    return mixed.reshape(query_heads.shape), (peak + jnp.log(total))[..., 0]


def attention_backward(
    query_heads, key_heads, value_heads, grad_heads, log_totals, allowed, scale_factor
):
    kv_count = key_heads.shape[0]
    query_groups = grouped(query_heads, kv_count)
    grad_groups = grouped(grad_heads, kv_count)
    scores = group_scores(query_groups, key_heads, allowed, scale_factor)
    probs = jnp.exp(scores - log_totals[..., None])
    prob_grad = jnp.einsum(
        "kgqd,kpd->kgqp", grad_groups, value_heads, preferred_element_type=jnp.float32
    )
    value_grad = jnp.einsum(
        "kgqp,kgqd->kpd", probs.astype(jnp.bfloat16), grad_groups, preferred_element_type=jnp.float32
    )
    inner = jnp.sum(probs * prob_grad, axis=-1, keepdims=True)
    score_grad = (probs * (prob_grad - inner)).astype(jnp.bfloat16)
    query_grad = (
        jnp.einsum("kgqp,kpd->kgqd", score_grad, key_heads, preferred_element_type=jnp.float32)
        * scale_factor
    )
    key_grad = (
        jnp.einsum("kgqp,kgqd->kpd", score_grad, query_groups, preferred_element_type=jnp.float32)
        * scale_factor
    )
    return query_grad.reshape(query_heads.shape), key_grad, value_grad


def row_scatter_sum(vectors):
    count = lax.axis_size("row")
    blocks = jnp.moveaxis(vectors.reshape(vectors.shape[0], count, -1), 1, 0)
    return jnp.sum(lax.all_to_all(blocks, "row", split_axis=0, concat_axis=0, tiled=True), axis=0)


GRAD_BLOCK = 128


def split_columns(packed, widths):
    pieces = []
    offset = 0
    for width in widths:
        pieces.append(packed[:, offset : offset + width])
        offset += width
    return pieces


def col_scatter(values):
    count = lax.axis_size("col")
    lead = values.shape[:-1]
    blocks = jnp.moveaxis(values.reshape(*lead, count, values.shape[-1] // count), -2, 0)
    received = lax.all_to_all(blocks, "col", split_axis=0, concat_axis=0, tiled=True)
    return jnp.sum(received.astype(jnp.float32), axis=0)


def col_gather(block):
    count = lax.axis_size("col")
    copies = jnp.broadcast_to(block[None], (count,) + block.shape)
    received = lax.all_to_all(copies, "col", split_axis=0, concat_axis=0, tiled=True)
    return jnp.moveaxis(received, 0, -2).reshape(*block.shape[:-1], count * block.shape[-1])


def col_sum(values):
    return col_gather(col_scatter(values).astype(jnp.bfloat16)).astype(jnp.float32)


def gather_rows(parts):
    return lax.all_gather(jnp.concatenate(parts, axis=1), "row", axis=0, tiled=True)


def grad_wide_kernel(select_ref, left_ref, right_ref, out_ref):
    step = pl.program_id(0)
    parts = out_ref.shape[1] // GRAD_BLOCK
    for part in range(parts):
        owner = select_ref[step * parts + part]
        columns = slice(part * GRAD_BLOCK, (part + 1) * GRAD_BLOCK)
        out_ref[:, columns] = jnp.dot(
            left_ref[owner], right_ref[:, columns], preferred_element_type=jnp.float32
        ).astype(out_ref.dtype)


def packed_weight_grads(lefts, segments):
    left_stack = jnp.stack([left.T for left in lefts])
    right = jnp.concatenate([seg for _, seg in segments], axis=1)
    column_owner = []
    for index, seg in segments:
        column_owner += [index] * seg.shape[1]
    assert len(column_owner) % GRAD_BLOCK == 0
    select = column_owner[::GRAD_BLOCK]
    assert column_owner == [owner for owner in select for _ in range(GRAD_BLOCK)]
    parts = max(m for m in range(1, 12) if len(select) % m == 0 and len(select) // m >= 3)
    width = parts * GRAD_BLOCK
    features, tokens = left_stack.shape[1], left_stack.shape[2]
    in_specs = [
        pl.BlockSpec(left_stack.shape, lambda j, sel: (0, 0, 0)),
        pl.BlockSpec((tokens, width), lambda j, sel: (0, j)),
    ]
    return pl.pallas_call(
        grad_wide_kernel,
        out_shape=jax.ShapeDtypeStruct((features, right.shape[1]), jnp.bfloat16),
        grid_spec=pltpu.PrefetchScalarGridSpec(
            num_scalar_prefetch=1,
            grid=(len(select) // parts,),
            in_specs=in_specs,
            out_specs=pl.BlockSpec((features, width), lambda j, sel: (0, j)),
        ),
    )(jnp.asarray(select, dtype=jnp.int32), left_stack, right)


def body(
    tokens,
    cotangent,
    destination,
    segment_ids,
    attn_gain,
    w_query,
    w_key,
    w_value,
    w_output,
    ffn_gain,
    w_gate,
    w_up,
    w_down,
):
    row_count = tokens.shape[0]
    quarter = tokens.shape[1]
    col_start = lax.axis_index("col") * quarter
    send_order = jnp.argsort(destination)
    slot_ids = destination[send_order] % row_count
    arrived_pair, arrived_slots = (
        lax.all_to_all(
            jnp.stack([tokens, cotangent])[:, send_order], "row", split_axis=1, concat_axis=1, tiled=True
        ),
        lax.all_to_all(slot_ids, "row", split_axis=0, concat_axis=0, tiled=True),
    )
    placing = jnp.argsort(arrived_slots)
    attn_widths = [w_query.shape[1], w_key.shape[1], w_value.shape[1], w_output.shape[1]]
    ffn_widths = [w_gate.shape[1], w_up.shape[1], w_down.shape[1]]
    weights_packed = gather_rows([w_query, w_key, w_value, w_output, w_gate, w_up, w_down])
    attn_packed = weights_packed[:, : sum(attn_widths)]
    ffn_packed = weights_packed[:, sum(attn_widths) :]
    placed_pair = arrived_pair[:, placing]
    full_rows = col_gather(placed_pair[0])
    full_grads = col_gather(placed_pair[1])
    query_w, key_w, value_w, output_w = split_columns(attn_packed, attn_widths)
    cosine, sine = rope_tables(positions_of(segment_ids))
    allowed = allowed_pairs(segment_ids)
    rows_wide = full_rows.astype(jnp.float32)
    inv_one = rms_scale(rows_wide)
    normed_one = (rows_wide * inv_one * attn_gain).astype(jnp.bfloat16)
    query = matmul(normed_one, query_w)
    key_raw = matmul(normed_one, key_w)
    value_raw = matmul(normed_one, value_w)
    query_heads_count = query.shape[1] // HD
    kv_count = key_raw.shape[1] // HD
    query_rot = (
        rotate(query.reshape(row_count, query_heads_count, HD), cosine, sine)
        .astype(jnp.bfloat16)
        .transpose(1, 0, 2)
    )
    key_rot = (
        rotate(key_raw.reshape(row_count, kv_count, HD), cosine, sine)
        .astype(jnp.bfloat16)
        .transpose(1, 0, 2)
    )
    value_heads = value_raw.astype(jnp.bfloat16).reshape(row_count, kv_count, HD).transpose(1, 0, 2)
    scale_factor = HD ** (-0.5)
    mixed_heads, log_totals = attention_forward(
        query_rot, key_rot, value_heads, allowed, scale_factor
    )
    mixed = (
        mixed_heads.transpose(1, 0, 2)
        .reshape(row_count, query_heads_count * HD)
        .astype(jnp.bfloat16)
    )
    attn_terms = matmul(mixed, output_w.T)
    attn_full = lax.psum(attn_terms.astype(jnp.bfloat16), "col").astype(jnp.float32)
    resid = rows_wide + attn_full
    inv_two = rms_scale(resid)
    normed_two = (resid * inv_two * ffn_gain).astype(jnp.bfloat16)
    resid_part = lax.dynamic_slice_in_dim(resid, col_start, quarter, 1)
    gate_w, up_w, down_w = split_columns(ffn_packed, ffn_widths)
    gate = matmul(normed_two, gate_w)
    upper = matmul(normed_two, up_w)
    sigmoid_gate = jax.nn.sigmoid(gate)
    activ = (gate * sigmoid_gate * upper).astype(jnp.bfloat16)
    ffn_share_low = lax.psum_scatter(
        matmul(activ, down_w.T).astype(jnp.bfloat16), "col", scatter_dimension=1, tiled=True
    )
    act_grad = matmul(full_grads, down_w)
    gate_grad = (act_grad * upper * sigmoid_gate * (1.0 + gate * (1.0 - sigmoid_gate))).astype(
        jnp.bfloat16
    )
    up_grad = (act_grad * gate * sigmoid_gate).astype(jnp.bfloat16)
    normed_terms_two = matmul(gate_grad, gate_w.T) + matmul(up_grad, up_w.T)
    ffn_grads_packed = packed_weight_grads(
        [normed_two, full_grads], [(0, gate_grad), (0, up_grad), (1, activ)]
    )
    ffn_grads_packed, ffn_share_low = lax.optimization_barrier((ffn_grads_packed, ffn_share_low))
    normed_low_two, ffn_grads_packed = lax.optimization_barrier(
        (normed_terms_two.astype(jnp.bfloat16), ffn_grads_packed)
    )
    normed_grad_two = col_sum(normed_low_two)
    resid_norm_grad, ffn_gain_grad = norm_back(resid, inv_two, ffn_gain, normed_grad_two)
    ffn_grads_local = lax.psum_scatter(ffn_grads_packed, "row", scatter_dimension=0, tiled=True)
    resid_grad = full_grads.astype(jnp.float32) + resid_norm_grad
    attn_grad_low = resid_grad.astype(jnp.bfloat16)
    mixed_grad = matmul(attn_grad_low, output_w).astype(jnp.bfloat16)
    mixed_grad_heads = mixed_grad.reshape(row_count, query_heads_count, HD).transpose(1, 0, 2)
    query_grads, key_grads, value_grads = attention_backward(
        query_rot, key_rot, value_heads, mixed_grad_heads, log_totals, allowed, scale_factor
    )
    query_grad = (
        rotate_back(query_grads.transpose(1, 0, 2), cosine, sine)
        .reshape(row_count, query_heads_count * HD)
        .astype(jnp.bfloat16)
    )
    key_sum = key_grads.transpose(1, 0, 2)
    key_grad = (
        rotate_back(key_sum, cosine, sine).reshape(row_count, kv_count * HD).astype(jnp.bfloat16)
    )
    value_sum = value_grads.transpose(1, 0, 2)
    value_grad = value_sum.reshape(row_count, kv_count * HD).astype(jnp.bfloat16)
    normed_terms_one = (
        matmul(query_grad, query_w.T) + matmul(key_grad, key_w.T) + matmul(value_grad, value_w.T)
    )
    output_share = (resid_part + ffn_share_low.astype(jnp.float32)).astype(jnp.bfloat16)
    back_rows = lax.all_to_all(
        output_share[arrived_slots], "row", split_axis=0, concat_axis=0, tiled=True
    )
    attn_grads_packed, ffn_grads_local, back_rows, normed_low_one = lax.optimization_barrier(
        (
            packed_weight_grads(
                [normed_one, attn_grad_low],
                [(0, query_grad), (0, key_grad), (0, value_grad), (1, mixed)],
            ),
            ffn_grads_local,
            back_rows,
            normed_terms_one.astype(jnp.bfloat16),
        )
    )
    attn_grads_local = lax.psum_scatter(attn_grads_packed, "row", scatter_dimension=0, tiled=True)
    normed_grad_block = col_scatter(normed_low_one)
    normed_block = lax.dynamic_slice_in_dim(rows_wide, col_start, quarter, 1) * inv_one
    scaled_block = normed_grad_block * lax.dynamic_slice_in_dim(attn_gain, col_start, quarter, 0)
    token_part = jnp.sum(scaled_block * normed_block, axis=-1)
    gain_part = jnp.sum(normed_grad_block * normed_block, axis=0)
    exchanged = col_gather(jnp.concatenate([token_part, gain_part])).reshape(
        -1, token_part.shape[0] + gain_part.shape[0]
    )
    row_mean = jnp.sum(exchanged[:, : token_part.shape[0]], axis=0) / rows_wide.shape[-1]
    attn_gain_grad = exchanged[:, token_part.shape[0] :].reshape(-1)
    input_block = lax.dynamic_slice_in_dim(resid_grad, col_start, quarter, 1) + inv_one * (
        scaled_block - normed_block * row_mean[:, None]
    )
    input_share = input_block.astype(jnp.bfloat16)
    query_result, key_result, value_result, output_result = split_columns(
        attn_grads_local.astype(jnp.float32), attn_widths
    )
    gate_result, up_result, down_result = split_columns(
        ffn_grads_local.astype(jnp.float32), ffn_widths
    )
    row_devices = lax.axis_size("row")
    gains = jnp.stack([attn_gain_grad, ffn_gain_grad])
    gain_blocks = jnp.moveaxis(gains.reshape(2, row_devices, -1), 1, 0).reshape(row_devices, -1)
    gain_width = gain_blocks.shape[1]
    assert gain_width <= quarter
    gain_rows = jnp.pad(gain_blocks, ((0, 0), (0, quarter - gain_width)))[:, None, :]
    token_rows = input_share[arrived_slots].reshape(row_devices, -1, quarter)
    received = lax.all_to_all(
        jnp.concatenate([token_rows, gain_rows.astype(jnp.bfloat16)], axis=1),
        "row",
        split_axis=0,
        concat_axis=0,
        tiled=True,
    )
    back_grads = received[:, :-1].reshape(row_count, quarter)
    gain_sums = jnp.sum(received[:, -1, :gain_width].astype(jnp.float32), axis=0).reshape(2, -1)
    attn_gain_result, ffn_gain_result = gain_sums[0], gain_sums[1]
    restore = jnp.argsort(send_order)
    return (
        back_rows[restore],
        back_grads[restore],
        attn_gain_result,
        query_result,
        key_result,
        value_result,
        output_result,
        ffn_gain_result,
        gate_result,
        up_result,
        down_result,
    )

def solution(mesh):
    placed = (
        P("row", "col"),
        P("row", "col"),
        P("row"),
        P("row"),
        P(),
        P("row", "col"),
        P("row", "col"),
        P("row", "col"),
        P("row", "col"),
        P(),
        P("row", "col"),
        P("row", "col"),
        P("row", "col"),
    )
    return jax.shard_map(
        body,
        mesh=mesh,
        in_specs=placed,
        out_specs=(
            P("row", "col"),
            P("row", "col"),
            P("row"),
            P("row", "col"),
            P("row", "col"),
            P("row", "col"),
            P("row", "col"),
            P("row"),
            P("row", "col"),
            P("row", "col"),
            P("row", "col"),
        ),
        check_vma=False,
    )
```

```python
from functools import partial

import jax
import jax.numpy as jnp
from jax import lax
from jax.experimental import pallas as pl
from jax.experimental.pallas import tpu as pltpu
from jax.sharding import PartitionSpec as P

HEADS = 32
KV = 4
HD = 64


EPS = 1e-05
ROPE_BASE = 10000.0


def rope_tables(positions):
    half_width = HD // 2
    freqs = ROPE_BASE ** (-(jnp.arange(half_width, dtype=jnp.float32) * 2.0 / HD))
    angles = positions.astype(jnp.float32)[:, None] * freqs[None, :]
    return (jnp.cos(angles)[:, None, :], jnp.sin(angles)[:, None, :])


def rotate(values, cosine, sine):
    half_width = values.shape[-1] // 2
    first = values[..., :half_width]
    second = values[..., half_width:]
    return jnp.concatenate(
        [first * cosine - second * sine, second * cosine + first * sine], axis=-1
    )


def rotate_back(grads, cosine, sine):
    half_width = grads.shape[-1] // 2
    first = grads[..., :half_width]
    second = grads[..., half_width:]
    return jnp.concatenate(
        [first * cosine + second * sine, second * cosine - first * sine], axis=-1
    )


def positions_of(segment_ids):
    index = jnp.arange(segment_ids.shape[0], dtype=jnp.int32)
    change = jnp.concatenate([jnp.ones((1,), dtype=jnp.bool_), segment_ids[1:] != segment_ids[:-1]])
    starts = jnp.where(change, index, jnp.zeros_like(index))
    return index - lax.cummax(starts, axis=0)


def allowed_pairs(segment_ids):
    index = jnp.arange(segment_ids.shape[0], dtype=jnp.int32)
    return (segment_ids[:, None] == segment_ids[None, :]) & (index[None, :] <= index[:, None])


def rms_scale(values):
    return lax.rsqrt(jnp.mean(values * values, axis=-1, keepdims=True) + EPS)


def norm_back(values, inv_root, gain, grads):
    normed = values * inv_root
    scaled = grads * gain
    result = inv_root * (scaled - normed * jnp.mean(scaled * normed, axis=-1, keepdims=True))
    return (result, jnp.sum(grads * normed, axis=0))


def matmul(left, right):
    return jnp.dot(left, right, preferred_element_type=jnp.float32)


def head_scores(query_head, key_head, allowed, scale_factor):
    scores = matmul(query_head, key_head.T) * scale_factor
    return jnp.where(allowed, scores, -1e30)


def head_forward(inputs, key_heads, value_heads, allowed, scale_factor):
    query_head, kv_slot = inputs
    scores = head_scores(query_head, key_heads[kv_slot], allowed, scale_factor)
    peak = jnp.max(scores, axis=-1, keepdims=True)
    expo = jnp.exp(scores - peak)
    total = jnp.sum(expo, axis=-1, keepdims=True)
    probs = expo / total
    mixed = matmul(probs.astype(jnp.bfloat16), value_heads[kv_slot])
    return (mixed, (peak + jnp.log(total))[:, 0])


def head_backward(inputs, key_heads, value_heads, allowed, scale_factor):
    query_head, kv_slot, grad_head, log_total = inputs
    key_head = key_heads[kv_slot]
    value_head = value_heads[kv_slot]
    scores = head_scores(query_head, key_head, allowed, scale_factor)
    probs = jnp.exp(scores - log_total[:, None])
    prob_grad = matmul(grad_head, value_head.T)
    value_grad = matmul(probs.astype(jnp.bfloat16).T, grad_head)
    inner = jnp.sum(probs * prob_grad, axis=-1, keepdims=True)
    score_grad = (probs * (prob_grad - inner)).astype(jnp.bfloat16)
    query_grad = matmul(score_grad, key_head) * scale_factor
    key_grad = matmul(score_grad.T, query_head) * scale_factor
    return (query_grad, key_grad, value_grad)


def grouped(heads, kv_count):
    return heads.reshape(kv_count, heads.shape[0] // kv_count, *heads.shape[1:])


def group_scores(query_groups, key_heads, allowed, scale_factor):
    scores = (
        jnp.einsum("kgqd,kpd->kgqp", query_groups, key_heads, preferred_element_type=jnp.float32)
        * scale_factor
    )
    return jnp.where(allowed, scores, -1e30)


def attention_forward(query_heads, key_heads, value_heads, allowed, scale_factor):
    query_groups = grouped(query_heads, key_heads.shape[0])
    scores = group_scores(query_groups, key_heads, allowed, scale_factor)
    peak = jnp.max(scores, axis=-1, keepdims=True)
    expo = jnp.exp(scores - peak)
    total = jnp.sum(expo, axis=-1, keepdims=True)
    probs = expo / total
    mixed = jnp.einsum(
        "kgqp,kpd->kgqd", probs.astype(jnp.bfloat16), value_heads, preferred_element_type=jnp.float32
    )
    return mixed.reshape(query_heads.shape), (peak + jnp.log(total))[..., 0]


def attention_backward(
    query_heads, key_heads, value_heads, grad_heads, log_totals, allowed, scale_factor
):
    kv_count = key_heads.shape[0]
    query_groups = grouped(query_heads, kv_count)
    grad_groups = grouped(grad_heads, kv_count)
    scores = group_scores(query_groups, key_heads, allowed, scale_factor)
    probs = jnp.exp(scores - log_totals[..., None])
    prob_grad = jnp.einsum(
        "kgqd,kpd->kgqp", grad_groups, value_heads, preferred_element_type=jnp.float32
    )
    value_grad = jnp.einsum(
        "kgqp,kgqd->kpd", probs.astype(jnp.bfloat16), grad_groups, preferred_element_type=jnp.float32
    )
    inner = jnp.sum(probs * prob_grad, axis=-1, keepdims=True)
    score_grad = (probs * (prob_grad - inner)).astype(jnp.bfloat16)
    query_grad = (
        jnp.einsum("kgqp,kpd->kgqd", score_grad, key_heads, preferred_element_type=jnp.float32)
        * scale_factor
    )
    key_grad = (
        jnp.einsum("kgqp,kgqd->kpd", score_grad, query_groups, preferred_element_type=jnp.float32)
        * scale_factor
    )
    return query_grad.reshape(query_heads.shape), key_grad, value_grad


def row_scatter_sum(vectors):
    count = lax.axis_size("row")
    blocks = jnp.moveaxis(vectors.reshape(vectors.shape[0], count, -1), 1, 0)
    return jnp.sum(lax.all_to_all(blocks, "row", split_axis=0, concat_axis=0, tiled=True), axis=0)


GRAD_BLOCK = 128


def split_columns(packed, widths):
    pieces = []
    offset = 0
    for width in widths:
        pieces.append(packed[:, offset : offset + width])
        offset += width
    return pieces


def col_scatter(values):
    count = lax.axis_size("col")
    lead = values.shape[:-1]
    blocks = jnp.moveaxis(values.reshape(*lead, count, values.shape[-1] // count), -2, 0)
    received = lax.all_to_all(blocks, "col", split_axis=0, concat_axis=0, tiled=True)
    return jnp.sum(received.astype(jnp.float32), axis=0)


def col_gather(block):
    count = lax.axis_size("col")
    copies = jnp.broadcast_to(block[None], (count,) + block.shape)
    received = lax.all_to_all(copies, "col", split_axis=0, concat_axis=0, tiled=True)
    return jnp.moveaxis(received, 0, -2).reshape(*block.shape[:-1], count * block.shape[-1])


def col_sum(values):
    return col_gather(col_scatter(values).astype(jnp.bfloat16)).astype(jnp.float32)


def gather_rows(parts):
    return lax.all_gather(jnp.concatenate(parts, axis=1), "row", axis=0, tiled=True)


def grad_wide_kernel(select_ref, left_ref, right_ref, out_ref, uniform):
    step = pl.program_id(0)
    parts = out_ref.shape[1] // GRAD_BLOCK
    if uniform:
        out_ref[...] = jnp.dot(
            left_ref[select_ref[step * parts]], right_ref[...], preferred_element_type=jnp.float32
        ).astype(out_ref.dtype)
        return
    for part in range(parts):
        owner = select_ref[step * parts + part]
        columns = slice(part * GRAD_BLOCK, (part + 1) * GRAD_BLOCK)
        out_ref[:, columns] = jnp.dot(
            left_ref[owner], right_ref[:, columns], preferred_element_type=jnp.float32
        ).astype(out_ref.dtype)


def packed_weight_grads(lefts, segments):
    left_stack = jnp.stack([left.T for left in lefts])
    right = jnp.concatenate([seg for _, seg in segments], axis=1)
    column_owner = []
    for index, seg in segments:
        column_owner += [index] * seg.shape[1]
    assert len(column_owner) % GRAD_BLOCK == 0
    select = column_owner[::GRAD_BLOCK]
    assert column_owner == [owner for owner in select for _ in range(GRAD_BLOCK)]
    parts = max(m for m in range(1, 12) if len(select) % m == 0 and len(select) // m >= 3)
    width = parts * GRAD_BLOCK
    uniform = all(
        len(set(select[start : start + parts])) == 1 for start in range(0, len(select), parts)
    )
    features, tokens = left_stack.shape[1], left_stack.shape[2]
    in_specs = [
        pl.BlockSpec(left_stack.shape, lambda j, sel: (0, 0, 0)),
        pl.BlockSpec((tokens, width), lambda j, sel: (0, j)),
    ]
    return pl.pallas_call(
        partial(grad_wide_kernel, uniform=uniform),
        out_shape=jax.ShapeDtypeStruct((features, right.shape[1]), jnp.bfloat16),
        grid_spec=pltpu.PrefetchScalarGridSpec(
            num_scalar_prefetch=1,
            grid=(len(select) // parts,),
            in_specs=in_specs,
            out_specs=pl.BlockSpec((features, width), lambda j, sel: (0, j)),
        ),
    )(jnp.asarray(select, dtype=jnp.int32), left_stack, right)


def body(
    tokens,
    cotangent,
    destination,
    segment_ids,
    attn_gain,
    w_query,
    w_key,
    w_value,
    w_output,
    ffn_gain,
    w_gate,
    w_up,
    w_down,
):
    row_count = tokens.shape[0]
    quarter = tokens.shape[1]
    col_start = lax.axis_index("col") * quarter
    send_order = jnp.argsort(destination)
    slot_ids = destination[send_order] % row_count
    arrived_pair, arrived_slots = (
        lax.all_to_all(
            jnp.stack([tokens, cotangent])[:, send_order], "row", split_axis=1, concat_axis=1, tiled=True
        ),
        lax.all_to_all(slot_ids, "row", split_axis=0, concat_axis=0, tiled=True),
    )
    placing = jnp.argsort(arrived_slots)
    attn_widths = [w_query.shape[1], w_key.shape[1], w_value.shape[1], w_output.shape[1]]
    ffn_widths = [w_gate.shape[1], w_up.shape[1], w_down.shape[1]]
    weights_packed = gather_rows([w_query, w_key, w_value, w_output, w_gate, w_up, w_down])
    attn_packed = weights_packed[:, : sum(attn_widths)]
    ffn_packed = weights_packed[:, sum(attn_widths) :]
    placed_pair = arrived_pair[:, placing]
    full_rows = col_gather(placed_pair[0])
    full_grads = col_gather(placed_pair[1])
    query_w, key_w, value_w, output_w = split_columns(attn_packed, attn_widths)
    cosine, sine = rope_tables(positions_of(segment_ids))
    allowed = allowed_pairs(segment_ids)
    rows_wide = full_rows.astype(jnp.float32)
    inv_one = rms_scale(rows_wide)
    normed_one = (rows_wide * inv_one * attn_gain).astype(jnp.bfloat16)
    query = matmul(normed_one, query_w)
    key_raw = matmul(normed_one, key_w)
    value_raw = matmul(normed_one, value_w)
    query_heads_count = query.shape[1] // HD
    kv_count = key_raw.shape[1] // HD
    query_rot = (
        rotate(query.reshape(row_count, query_heads_count, HD), cosine, sine)
        .astype(jnp.bfloat16)
        .transpose(1, 0, 2)
    )
    key_rot = (
        rotate(key_raw.reshape(row_count, kv_count, HD), cosine, sine)
        .astype(jnp.bfloat16)
        .transpose(1, 0, 2)
    )
    value_heads = value_raw.astype(jnp.bfloat16).reshape(row_count, kv_count, HD).transpose(1, 0, 2)
    scale_factor = HD ** (-0.5)
    mixed_heads, log_totals = attention_forward(
        query_rot, key_rot, value_heads, allowed, scale_factor
    )
    mixed = (
        mixed_heads.transpose(1, 0, 2)
        .reshape(row_count, query_heads_count * HD)
        .astype(jnp.bfloat16)
    )
    attn_terms = matmul(mixed, output_w.T)
    attn_full = lax.psum(attn_terms.astype(jnp.bfloat16), "col").astype(jnp.float32)
    resid = rows_wide + attn_full
    inv_two = rms_scale(resid)
    normed_two = (resid * inv_two * ffn_gain).astype(jnp.bfloat16)
    resid_part = lax.dynamic_slice_in_dim(resid, col_start, quarter, 1)
    gate_w, up_w, down_w = split_columns(ffn_packed, ffn_widths)
    gate = matmul(normed_two, gate_w)
    upper = matmul(normed_two, up_w)
    sigmoid_gate = jax.nn.sigmoid(gate)
    activ = (gate * sigmoid_gate * upper).astype(jnp.bfloat16)
    ffn_share_low = lax.psum_scatter(
        matmul(activ, down_w.T).astype(jnp.bfloat16), "col", scatter_dimension=1, tiled=True
    )
    act_grad = matmul(full_grads, down_w)
    gate_grad = (act_grad * upper * sigmoid_gate * (1.0 + gate * (1.0 - sigmoid_gate))).astype(
        jnp.bfloat16
    )
    up_grad = (act_grad * gate * sigmoid_gate).astype(jnp.bfloat16)
    normed_terms_two = matmul(gate_grad, gate_w.T) + matmul(up_grad, up_w.T)
    ffn_grads_packed = packed_weight_grads(
        [normed_two, full_grads], [(0, gate_grad), (0, up_grad), (1, activ)]
    )
    ffn_grads_packed, ffn_share_low = lax.optimization_barrier((ffn_grads_packed, ffn_share_low))
    normed_low_two, ffn_grads_packed = lax.optimization_barrier(
        (normed_terms_two.astype(jnp.bfloat16), ffn_grads_packed)
    )
    normed_grad_two = col_sum(normed_low_two)
    resid_norm_grad, ffn_gain_grad = norm_back(resid, inv_two, ffn_gain, normed_grad_two)
    ffn_grads_local = lax.psum_scatter(ffn_grads_packed, "row", scatter_dimension=0, tiled=True)
    resid_grad = full_grads.astype(jnp.float32) + resid_norm_grad
    attn_grad_low = resid_grad.astype(jnp.bfloat16)
    mixed_grad = matmul(attn_grad_low, output_w).astype(jnp.bfloat16)
    mixed_grad_heads = mixed_grad.reshape(row_count, query_heads_count, HD).transpose(1, 0, 2)
    query_grads, key_grads, value_grads = attention_backward(
        query_rot, key_rot, value_heads, mixed_grad_heads, log_totals, allowed, scale_factor
    )
    query_grad = (
        rotate_back(query_grads.transpose(1, 0, 2), cosine, sine)
        .reshape(row_count, query_heads_count * HD)
        .astype(jnp.bfloat16)
    )
    key_sum = key_grads.transpose(1, 0, 2)
    key_grad = (
        rotate_back(key_sum, cosine, sine).reshape(row_count, kv_count * HD).astype(jnp.bfloat16)
    )
    value_sum = value_grads.transpose(1, 0, 2)
    value_grad = value_sum.reshape(row_count, kv_count * HD).astype(jnp.bfloat16)
    normed_terms_one = (
        matmul(query_grad, query_w.T) + matmul(key_grad, key_w.T) + matmul(value_grad, value_w.T)
    )
    output_share = (resid_part + ffn_share_low.astype(jnp.float32)).astype(jnp.bfloat16)
    back_rows = lax.all_to_all(
        output_share[arrived_slots], "row", split_axis=0, concat_axis=0, tiled=True
    )
    attn_grads_packed, ffn_grads_local, back_rows, normed_low_one = lax.optimization_barrier(
        (
            packed_weight_grads(
                [normed_one, attn_grad_low],
                [(0, query_grad), (0, key_grad), (0, value_grad), (1, mixed)],
            ),
            ffn_grads_local,
            back_rows,
            normed_terms_one.astype(jnp.bfloat16),
        )
    )
    attn_grads_local = lax.psum_scatter(attn_grads_packed, "row", scatter_dimension=0, tiled=True)
    normed_grad_block = col_scatter(normed_low_one)
    normed_block = lax.dynamic_slice_in_dim(rows_wide, col_start, quarter, 1) * inv_one
    scaled_block = normed_grad_block * lax.dynamic_slice_in_dim(attn_gain, col_start, quarter, 0)
    token_part = jnp.sum(scaled_block * normed_block, axis=-1)
    gain_part = jnp.sum(normed_grad_block * normed_block, axis=0)
    exchanged = col_gather(jnp.concatenate([token_part, gain_part])).reshape(
        -1, token_part.shape[0] + gain_part.shape[0]
    )
    row_mean = jnp.sum(exchanged[:, : token_part.shape[0]], axis=0) / rows_wide.shape[-1]
    attn_gain_grad = exchanged[:, token_part.shape[0] :].reshape(-1)
    input_block = lax.dynamic_slice_in_dim(resid_grad, col_start, quarter, 1) + inv_one * (
        scaled_block - normed_block * row_mean[:, None]
    )
    input_share = input_block.astype(jnp.bfloat16)
    query_result, key_result, value_result, output_result = split_columns(
        attn_grads_local.astype(jnp.float32), attn_widths
    )
    gate_result, up_result, down_result = split_columns(
        ffn_grads_local.astype(jnp.float32), ffn_widths
    )
    row_devices = lax.axis_size("row")
    gains = jnp.stack([attn_gain_grad, ffn_gain_grad])
    gain_blocks = jnp.moveaxis(gains.reshape(2, row_devices, -1), 1, 0).reshape(row_devices, -1)
    gain_width = gain_blocks.shape[1]
    assert gain_width <= quarter
    gain_rows = jnp.pad(gain_blocks, ((0, 0), (0, quarter - gain_width)))[:, None, :]
    token_rows = input_share[arrived_slots].reshape(row_devices, -1, quarter)
    received = lax.all_to_all(
        jnp.concatenate([token_rows, gain_rows.astype(jnp.bfloat16)], axis=1),
        "row",
        split_axis=0,
        concat_axis=0,
        tiled=True,
    )
    back_grads = received[:, :-1].reshape(row_count, quarter)
    gain_sums = jnp.sum(received[:, -1, :gain_width].astype(jnp.float32), axis=0).reshape(2, -1)
    attn_gain_result, ffn_gain_result = gain_sums[0], gain_sums[1]
    restore = jnp.argsort(send_order)
    return (
        back_rows[restore],
        back_grads[restore],
        attn_gain_result,
        query_result,
        key_result,
        value_result,
        output_result,
        ffn_gain_result,
        gate_result,
        up_result,
        down_result,
    )

def solution(mesh):
    placed = (
        P("row", "col"),
        P("row", "col"),
        P("row"),
        P("row"),
        P(),
        P("row", "col"),
        P("row", "col"),
        P("row", "col"),
        P("row", "col"),
        P(),
        P("row", "col"),
        P("row", "col"),
        P("row", "col"),
    )
    return jax.shard_map(
        body,
        mesh=mesh,
        in_specs=placed,
        out_specs=(
            P("row", "col"),
            P("row", "col"),
            P("row"),
            P("row", "col"),
            P("row", "col"),
            P("row", "col"),
            P("row", "col"),
            P("row"),
            P("row", "col"),
            P("row", "col"),
            P("row", "col"),
        ),
        check_vma=False,
    )
```

```python
from functools import partial

import jax
import jax.numpy as jnp
from jax import lax
from jax.experimental import pallas as pl
from jax.experimental.pallas import tpu as pltpu
from jax.sharding import PartitionSpec as P

HEADS = 32
KV = 4
HD = 64


EPS = 1e-05
ROPE_BASE = 10000.0


def rope_tables(positions):
    half_width = HD // 2
    freqs = ROPE_BASE ** (-(jnp.arange(half_width, dtype=jnp.float32) * 2.0 / HD))
    angles = positions.astype(jnp.float32)[:, None] * freqs[None, :]
    return (jnp.cos(angles)[:, None, :], jnp.sin(angles)[:, None, :])


def rotate(values, cosine, sine):
    half_width = values.shape[-1] // 2
    first = values[..., :half_width]
    second = values[..., half_width:]
    return jnp.concatenate(
        [first * cosine - second * sine, second * cosine + first * sine], axis=-1
    )


def rotate_back(grads, cosine, sine):
    half_width = grads.shape[-1] // 2
    first = grads[..., :half_width]
    second = grads[..., half_width:]
    return jnp.concatenate(
        [first * cosine + second * sine, second * cosine - first * sine], axis=-1
    )


def positions_of(segment_ids):
    index = jnp.arange(segment_ids.shape[0], dtype=jnp.int32)
    change = jnp.concatenate([jnp.ones((1,), dtype=jnp.bool_), segment_ids[1:] != segment_ids[:-1]])
    starts = jnp.where(change, index, jnp.zeros_like(index))
    return index - lax.cummax(starts, axis=0)


def allowed_pairs(segment_ids):
    index = jnp.arange(segment_ids.shape[0], dtype=jnp.int32)
    return (segment_ids[:, None] == segment_ids[None, :]) & (index[None, :] <= index[:, None])


def rms_scale(values):
    return lax.rsqrt(jnp.mean(values * values, axis=-1, keepdims=True) + EPS)


def norm_back(values, inv_root, gain, grads):
    normed = values * inv_root
    scaled = grads * gain
    result = inv_root * (scaled - normed * jnp.mean(scaled * normed, axis=-1, keepdims=True))
    return (result, jnp.sum(grads * normed, axis=0))


def matmul(left, right):
    return jnp.dot(left, right, preferred_element_type=jnp.float32)


def head_scores(query_head, key_head, allowed, scale_factor):
    scores = matmul(query_head, key_head.T) * scale_factor
    return jnp.where(allowed, scores, -1e30)


def head_forward(inputs, key_heads, value_heads, allowed, scale_factor):
    query_head, kv_slot = inputs
    scores = head_scores(query_head, key_heads[kv_slot], allowed, scale_factor)
    peak = jnp.max(scores, axis=-1, keepdims=True)
    expo = jnp.exp(scores - peak)
    total = jnp.sum(expo, axis=-1, keepdims=True)
    probs = expo / total
    mixed = matmul(probs.astype(jnp.bfloat16), value_heads[kv_slot])
    return (mixed, (peak + jnp.log(total))[:, 0])


def head_backward(inputs, key_heads, value_heads, allowed, scale_factor):
    query_head, kv_slot, grad_head, log_total = inputs
    key_head = key_heads[kv_slot]
    value_head = value_heads[kv_slot]
    scores = head_scores(query_head, key_head, allowed, scale_factor)
    probs = jnp.exp(scores - log_total[:, None])
    prob_grad = matmul(grad_head, value_head.T)
    value_grad = matmul(probs.astype(jnp.bfloat16).T, grad_head)
    inner = jnp.sum(probs * prob_grad, axis=-1, keepdims=True)
    score_grad = (probs * (prob_grad - inner)).astype(jnp.bfloat16)
    query_grad = matmul(score_grad, key_head) * scale_factor
    key_grad = matmul(score_grad.T, query_head) * scale_factor
    return (query_grad, key_grad, value_grad)


def grouped(heads, kv_count):
    return heads.reshape(kv_count, heads.shape[0] // kv_count, *heads.shape[1:])


def group_scores(query_groups, key_heads, allowed, scale_factor):
    scores = (
        jnp.einsum("kgqd,kpd->kgqp", query_groups, key_heads, preferred_element_type=jnp.float32)
        * scale_factor
    )
    return jnp.where(allowed, scores, -1e30)


def attention_forward(query_heads, key_heads, value_heads, allowed, scale_factor):
    query_groups = grouped(query_heads, key_heads.shape[0])
    scores = group_scores(query_groups, key_heads, allowed, scale_factor)
    peak = jnp.max(scores, axis=-1, keepdims=True)
    expo = jnp.exp(scores - peak)
    total = jnp.sum(expo, axis=-1, keepdims=True)
    probs = expo / total
    mixed = jnp.einsum(
        "kgqp,kpd->kgqd", probs.astype(jnp.bfloat16), value_heads, preferred_element_type=jnp.float32
    )
    return mixed.reshape(query_heads.shape), (peak + jnp.log(total))[..., 0]


def attention_backward(
    query_heads, key_heads, value_heads, grad_heads, log_totals, allowed, scale_factor
):
    kv_count = key_heads.shape[0]
    query_groups = grouped(query_heads, kv_count)
    grad_groups = grouped(grad_heads, kv_count)
    scores = group_scores(query_groups, key_heads, allowed, scale_factor)
    probs = jnp.exp(scores - log_totals[..., None])
    prob_grad = jnp.einsum(
        "kgqd,kpd->kgqp", grad_groups, value_heads, preferred_element_type=jnp.float32
    )
    value_grad = jnp.einsum(
        "kgqp,kgqd->kpd", probs.astype(jnp.bfloat16), grad_groups, preferred_element_type=jnp.float32
    )
    inner = jnp.sum(probs * prob_grad, axis=-1, keepdims=True)
    score_grad = (probs * (prob_grad - inner)).astype(jnp.bfloat16)
    query_grad = (
        jnp.einsum("kgqp,kpd->kgqd", score_grad, key_heads, preferred_element_type=jnp.float32)
        * scale_factor
    )
    key_grad = (
        jnp.einsum("kgqp,kgqd->kpd", score_grad, query_groups, preferred_element_type=jnp.float32)
        * scale_factor
    )
    return query_grad.reshape(query_heads.shape), key_grad, value_grad


def row_scatter_sum(vectors):
    count = lax.axis_size("row")
    blocks = jnp.moveaxis(vectors.reshape(vectors.shape[0], count, -1), 1, 0)
    return jnp.sum(lax.all_to_all(blocks, "row", split_axis=0, concat_axis=0, tiled=True), axis=0)


GRAD_BLOCK = 128


def split_columns(packed, widths):
    pieces = []
    offset = 0
    for width in widths:
        pieces.append(packed[:, offset : offset + width])
        offset += width
    return pieces


def col_scatter(values):
    count = lax.axis_size("col")
    lead = values.shape[:-1]
    blocks = jnp.moveaxis(values.reshape(*lead, count, values.shape[-1] // count), -2, 0)
    received = lax.all_to_all(blocks, "col", split_axis=0, concat_axis=0, tiled=True)
    return jnp.sum(received.astype(jnp.float32), axis=0)


def col_gather(block):
    count = lax.axis_size("col")
    copies = jnp.broadcast_to(block[None], (count,) + block.shape)
    received = lax.all_to_all(copies, "col", split_axis=0, concat_axis=0, tiled=True)
    return jnp.moveaxis(received, 0, -2).reshape(*block.shape[:-1], count * block.shape[-1])


def col_sum(values):
    return col_gather(col_scatter(values).astype(jnp.bfloat16)).astype(jnp.float32)


def gather_rows(parts):
    return lax.all_gather(jnp.concatenate(parts, axis=1), "row", axis=0, tiled=True)


def grad_wide_kernel(select_ref, left_ref, right_ref, out_ref, uniform):
    step = pl.program_id(0)
    parts = out_ref.shape[1] // GRAD_BLOCK
    if uniform:
        out_ref[...] = jnp.dot(
            left_ref[select_ref[step * parts]], right_ref[...], preferred_element_type=jnp.float32
        ).astype(out_ref.dtype)
        return
    for part in range(parts):
        owner = select_ref[step * parts + part]
        columns = slice(part * GRAD_BLOCK, (part + 1) * GRAD_BLOCK)
        out_ref[:, columns] = jnp.dot(
            left_ref[owner], right_ref[:, columns], preferred_element_type=jnp.float32
        ).astype(out_ref.dtype)


def packed_weight_grads(lefts, segments):
    left_stack = jnp.stack([left.T for left in lefts])
    right = jnp.concatenate([seg for _, seg in segments], axis=1)
    column_owner = []
    for index, seg in segments:
        column_owner += [index] * seg.shape[1]
    assert len(column_owner) % GRAD_BLOCK == 0
    select = column_owner[::GRAD_BLOCK]
    assert column_owner == [owner for owner in select for _ in range(GRAD_BLOCK)]
    count = len(select)
    divisors = [m for m in range(1, count + 1) if count % m == 0 and count // m >= 2]
    uniform_parts = [
        m for m in divisors if all(len(set(select[s : s + m])) == 1 for s in range(0, count, m))
    ]
    parts = max(uniform_parts) if uniform_parts else max(
        m for m in divisors if m <= 11 and count // m >= 3
    )
    width = parts * GRAD_BLOCK
    uniform = all(
        len(set(select[start : start + parts])) == 1 for start in range(0, len(select), parts)
    )
    features, tokens = left_stack.shape[1], left_stack.shape[2]
    in_specs = [
        pl.BlockSpec(left_stack.shape, lambda j, sel: (0, 0, 0)),
        pl.BlockSpec((tokens, width), lambda j, sel: (0, j)),
    ]
    return pl.pallas_call(
        partial(grad_wide_kernel, uniform=uniform),
        out_shape=jax.ShapeDtypeStruct((features, right.shape[1]), jnp.bfloat16),
        grid_spec=pltpu.PrefetchScalarGridSpec(
            num_scalar_prefetch=1,
            grid=(len(select) // parts,),
            in_specs=in_specs,
            out_specs=pl.BlockSpec((features, width), lambda j, sel: (0, j)),
        ),
    )(jnp.asarray(select, dtype=jnp.int32), left_stack, right)


def body(
    tokens,
    cotangent,
    destination,
    segment_ids,
    attn_gain,
    w_query,
    w_key,
    w_value,
    w_output,
    ffn_gain,
    w_gate,
    w_up,
    w_down,
):
    row_count = tokens.shape[0]
    quarter = tokens.shape[1]
    col_start = lax.axis_index("col") * quarter
    send_order = jnp.argsort(destination)
    slot_ids = destination[send_order] % row_count
    arrived_pair, arrived_slots = (
        lax.all_to_all(
            jnp.stack([tokens, cotangent])[:, send_order], "row", split_axis=1, concat_axis=1, tiled=True
        ),
        lax.all_to_all(slot_ids, "row", split_axis=0, concat_axis=0, tiled=True),
    )
    placing = jnp.argsort(arrived_slots)
    attn_widths = [w_query.shape[1], w_key.shape[1], w_value.shape[1], w_output.shape[1]]
    ffn_widths = [w_gate.shape[1], w_up.shape[1], w_down.shape[1]]
    weights_packed = gather_rows([w_query, w_key, w_value, w_output, w_gate, w_up, w_down])
    attn_packed = weights_packed[:, : sum(attn_widths)]
    ffn_packed = weights_packed[:, sum(attn_widths) :]
    placed_pair = arrived_pair[:, placing]
    full_rows = col_gather(placed_pair[0])
    full_grads = col_gather(placed_pair[1])
    query_w, key_w, value_w, output_w = split_columns(attn_packed, attn_widths)
    cosine, sine = rope_tables(positions_of(segment_ids))
    allowed = allowed_pairs(segment_ids)
    rows_wide = full_rows.astype(jnp.float32)
    inv_one = rms_scale(rows_wide)
    normed_one = (rows_wide * inv_one * attn_gain).astype(jnp.bfloat16)
    query = matmul(normed_one, query_w)
    key_raw = matmul(normed_one, key_w)
    value_raw = matmul(normed_one, value_w)
    query_heads_count = query.shape[1] // HD
    kv_count = key_raw.shape[1] // HD
    query_rot = (
        rotate(query.reshape(row_count, query_heads_count, HD), cosine, sine)
        .astype(jnp.bfloat16)
        .transpose(1, 0, 2)
    )
    key_rot = (
        rotate(key_raw.reshape(row_count, kv_count, HD), cosine, sine)
        .astype(jnp.bfloat16)
        .transpose(1, 0, 2)
    )
    value_heads = value_raw.astype(jnp.bfloat16).reshape(row_count, kv_count, HD).transpose(1, 0, 2)
    scale_factor = HD ** (-0.5)
    mixed_heads, log_totals = attention_forward(
        query_rot, key_rot, value_heads, allowed, scale_factor
    )
    mixed = (
        mixed_heads.transpose(1, 0, 2)
        .reshape(row_count, query_heads_count * HD)
        .astype(jnp.bfloat16)
    )
    attn_terms = matmul(mixed, output_w.T)
    attn_full = lax.psum(attn_terms.astype(jnp.bfloat16), "col").astype(jnp.float32)
    resid = rows_wide + attn_full
    inv_two = rms_scale(resid)
    normed_two = (resid * inv_two * ffn_gain).astype(jnp.bfloat16)
    resid_part = lax.dynamic_slice_in_dim(resid, col_start, quarter, 1)
    gate_w, up_w, down_w = split_columns(ffn_packed, ffn_widths)
    gate = matmul(normed_two, gate_w)
    upper = matmul(normed_two, up_w)
    sigmoid_gate = jax.nn.sigmoid(gate)
    activ = (gate * sigmoid_gate * upper).astype(jnp.bfloat16)
    ffn_share_low = lax.psum_scatter(
        matmul(activ, down_w.T).astype(jnp.bfloat16), "col", scatter_dimension=1, tiled=True
    )
    act_grad = matmul(full_grads, down_w)
    gate_grad = (act_grad * upper * sigmoid_gate * (1.0 + gate * (1.0 - sigmoid_gate))).astype(
        jnp.bfloat16
    )
    up_grad = (act_grad * gate * sigmoid_gate).astype(jnp.bfloat16)
    normed_terms_two = matmul(gate_grad, gate_w.T) + matmul(up_grad, up_w.T)
    normed_low_two, gate_grad_late, up_grad_late, activ_late = lax.optimization_barrier(
        (normed_terms_two.astype(jnp.bfloat16), gate_grad, up_grad, activ)
    )
    ffn_grads_packed = packed_weight_grads(
        [normed_two, full_grads], [(0, gate_grad_late), (0, up_grad_late), (1, activ_late)]
    )
    ffn_grads_packed, ffn_share_low = lax.optimization_barrier((ffn_grads_packed, ffn_share_low))
    normed_low_two, ffn_grads_packed = lax.optimization_barrier((normed_low_two, ffn_grads_packed))
    normed_grad_two = col_sum(normed_low_two)
    resid_norm_grad, ffn_gain_grad = norm_back(resid, inv_two, ffn_gain, normed_grad_two)
    ffn_grads_local = lax.psum_scatter(ffn_grads_packed, "row", scatter_dimension=0, tiled=True)
    resid_grad = full_grads.astype(jnp.float32) + resid_norm_grad
    attn_grad_low = resid_grad.astype(jnp.bfloat16)
    mixed_grad = matmul(attn_grad_low, output_w).astype(jnp.bfloat16)
    mixed_grad_heads = mixed_grad.reshape(row_count, query_heads_count, HD).transpose(1, 0, 2)
    query_grads, key_grads, value_grads = attention_backward(
        query_rot, key_rot, value_heads, mixed_grad_heads, log_totals, allowed, scale_factor
    )
    query_grad = (
        rotate_back(query_grads.transpose(1, 0, 2), cosine, sine)
        .reshape(row_count, query_heads_count * HD)
        .astype(jnp.bfloat16)
    )
    key_sum = key_grads.transpose(1, 0, 2)
    key_grad = (
        rotate_back(key_sum, cosine, sine).reshape(row_count, kv_count * HD).astype(jnp.bfloat16)
    )
    value_sum = value_grads.transpose(1, 0, 2)
    value_grad = value_sum.reshape(row_count, kv_count * HD).astype(jnp.bfloat16)
    normed_terms_one = (
        matmul(query_grad, query_w.T) + matmul(key_grad, key_w.T) + matmul(value_grad, value_w.T)
    )
    run_gap = max(
        query_grad.shape[1] + key_grad.shape[1] + value_grad.shape[1] - mixed.shape[1], 0
    )
    output_share = (resid_part + ffn_share_low.astype(jnp.float32)).astype(jnp.bfloat16)
    back_rows = lax.all_to_all(
        output_share[arrived_slots], "row", split_axis=0, concat_axis=0, tiled=True
    )
    attn_grads_packed, ffn_grads_local, back_rows, normed_low_one = lax.optimization_barrier(
        (
            packed_weight_grads(
                [normed_one, attn_grad_low],
                [
                    (0, query_grad),
                    (0, key_grad),
                    (0, value_grad),
                    (1, jnp.pad(mixed, ((0, 0), (0, run_gap)))),
                ],
            ),
            ffn_grads_local,
            back_rows,
            normed_terms_one.astype(jnp.bfloat16),
        )
    )
    attn_grads_local = lax.psum_scatter(attn_grads_packed, "row", scatter_dimension=0, tiled=True)
    normed_grad_block = col_scatter(normed_low_one)
    normed_block = lax.dynamic_slice_in_dim(rows_wide, col_start, quarter, 1) * inv_one
    scaled_block = normed_grad_block * lax.dynamic_slice_in_dim(attn_gain, col_start, quarter, 0)
    token_part = jnp.sum(scaled_block * normed_block, axis=-1)
    gain_part = jnp.sum(normed_grad_block * normed_block, axis=0)
    exchanged = col_gather(jnp.concatenate([token_part, gain_part])).reshape(
        -1, token_part.shape[0] + gain_part.shape[0]
    )
    row_mean = jnp.sum(exchanged[:, : token_part.shape[0]], axis=0) / rows_wide.shape[-1]
    attn_gain_grad = exchanged[:, token_part.shape[0] :].reshape(-1)
    input_block = lax.dynamic_slice_in_dim(resid_grad, col_start, quarter, 1) + inv_one * (
        scaled_block - normed_block * row_mean[:, None]
    )
    input_share = input_block.astype(jnp.bfloat16)
    query_result, key_result, value_result, output_result = split_columns(
        attn_grads_local.astype(jnp.float32), attn_widths + [run_gap]
    )[:4]
    gate_result, up_result, down_result = split_columns(
        ffn_grads_local.astype(jnp.float32), ffn_widths
    )
    row_devices = lax.axis_size("row")
    gains = jnp.stack([attn_gain_grad, ffn_gain_grad])
    gain_blocks = jnp.moveaxis(gains.reshape(2, row_devices, -1), 1, 0).reshape(row_devices, -1)
    gain_width = gain_blocks.shape[1]
    assert gain_width <= quarter
    gain_rows = jnp.pad(gain_blocks, ((0, 0), (0, quarter - gain_width)))[:, None, :]
    token_rows = input_share[arrived_slots].reshape(row_devices, -1, quarter)
    received = lax.all_to_all(
        jnp.concatenate([token_rows, gain_rows.astype(jnp.bfloat16)], axis=1),
        "row",
        split_axis=0,
        concat_axis=0,
        tiled=True,
    )
    back_grads = received[:, :-1].reshape(row_count, quarter)
    gain_sums = jnp.sum(received[:, -1, :gain_width].astype(jnp.float32), axis=0).reshape(2, -1)
    attn_gain_result, ffn_gain_result = gain_sums[0], gain_sums[1]
    restore = jnp.argsort(send_order)
    return (
        back_rows[restore],
        back_grads[restore],
        attn_gain_result,
        query_result,
        key_result,
        value_result,
        output_result,
        ffn_gain_result,
        gate_result,
        up_result,
        down_result,
    )

def solution(mesh):
    placed = (
        P("row", "col"),
        P("row", "col"),
        P("row"),
        P("row"),
        P(),
        P("row", "col"),
        P("row", "col"),
        P("row", "col"),
        P("row", "col"),
        P(),
        P("row", "col"),
        P("row", "col"),
        P("row", "col"),
    )
    return jax.shard_map(
        body,
        mesh=mesh,
        in_specs=placed,
        out_specs=(
            P("row", "col"),
            P("row", "col"),
            P("row"),
            P("row", "col"),
            P("row", "col"),
            P("row", "col"),
            P("row", "col"),
            P("row"),
            P("row", "col"),
            P("row", "col"),
            P("row", "col"),
        ),
        check_vma=False,
    )
```

```python
from functools import partial

import jax
import jax.numpy as jnp
from jax import lax
from jax.experimental import pallas as pl
from jax.experimental.pallas import tpu as pltpu
from jax.sharding import PartitionSpec as P

HEADS = 32
KV = 4
HD = 64


EPS = 1e-05
ROPE_BASE = 10000.0


def rope_tables(positions):
    half_width = HD // 2
    freqs = ROPE_BASE ** (-(jnp.arange(half_width, dtype=jnp.float32) * 2.0 / HD))
    angles = positions.astype(jnp.float32)[:, None] * freqs[None, :]
    return (jnp.cos(angles)[:, None, :], jnp.sin(angles)[:, None, :])


def rotate(values, cosine, sine):
    half_width = values.shape[-1] // 2
    first = values[..., :half_width]
    second = values[..., half_width:]
    return jnp.concatenate(
        [first * cosine - second * sine, second * cosine + first * sine], axis=-1
    )


def rotate_back(grads, cosine, sine):
    half_width = grads.shape[-1] // 2
    first = grads[..., :half_width]
    second = grads[..., half_width:]
    return jnp.concatenate(
        [first * cosine + second * sine, second * cosine - first * sine], axis=-1
    )


def positions_of(segment_ids):
    index = jnp.arange(segment_ids.shape[0], dtype=jnp.int32)
    change = jnp.concatenate([jnp.ones((1,), dtype=jnp.bool_), segment_ids[1:] != segment_ids[:-1]])
    starts = jnp.where(change, index, jnp.zeros_like(index))
    return index - lax.cummax(starts, axis=0)


def allowed_pairs(segment_ids):
    index = jnp.arange(segment_ids.shape[0], dtype=jnp.int32)
    return (segment_ids[:, None] == segment_ids[None, :]) & (index[None, :] <= index[:, None])


def rms_scale(values):
    return lax.rsqrt(jnp.mean(values * values, axis=-1, keepdims=True) + EPS)


def norm_back(values, inv_root, gain, grads):
    normed = values * inv_root
    scaled = grads * gain
    result = inv_root * (scaled - normed * jnp.mean(scaled * normed, axis=-1, keepdims=True))
    return (result, jnp.sum(grads * normed, axis=0))


def matmul(left, right):
    return jnp.dot(left, right, preferred_element_type=jnp.float32)


def head_scores(query_head, key_head, allowed, scale_factor):
    scores = matmul(query_head, key_head.T) * scale_factor
    return jnp.where(allowed, scores, -1e30)


def head_forward(inputs, key_heads, value_heads, allowed, scale_factor):
    query_head, kv_slot = inputs
    scores = head_scores(query_head, key_heads[kv_slot], allowed, scale_factor)
    peak = jnp.max(scores, axis=-1, keepdims=True)
    expo = jnp.exp(scores - peak)
    total = jnp.sum(expo, axis=-1, keepdims=True)
    probs = expo / total
    mixed = matmul(probs.astype(jnp.bfloat16), value_heads[kv_slot])
    return (mixed, (peak + jnp.log(total))[:, 0])


def head_backward(inputs, key_heads, value_heads, allowed, scale_factor):
    query_head, kv_slot, grad_head, log_total = inputs
    key_head = key_heads[kv_slot]
    value_head = value_heads[kv_slot]
    scores = head_scores(query_head, key_head, allowed, scale_factor)
    probs = jnp.exp(scores - log_total[:, None])
    prob_grad = matmul(grad_head, value_head.T)
    value_grad = matmul(probs.astype(jnp.bfloat16).T, grad_head)
    inner = jnp.sum(probs * prob_grad, axis=-1, keepdims=True)
    score_grad = (probs * (prob_grad - inner)).astype(jnp.bfloat16)
    query_grad = matmul(score_grad, key_head) * scale_factor
    key_grad = matmul(score_grad.T, query_head) * scale_factor
    return (query_grad, key_grad, value_grad)


def grouped(heads, kv_count):
    return heads.reshape(kv_count, heads.shape[0] // kv_count, *heads.shape[1:])


def group_scores(query_groups, key_heads, allowed, scale_factor):
    scores = (
        jnp.einsum("kgqd,kpd->kgqp", query_groups, key_heads, preferred_element_type=jnp.float32)
        * scale_factor
    )
    return jnp.where(allowed, scores, -1e30)


def attention_forward(query_heads, key_heads, value_heads, allowed, scale_factor):
    query_groups = grouped(query_heads, key_heads.shape[0])
    scores = group_scores(query_groups, key_heads, allowed, scale_factor)
    peak = jnp.max(scores, axis=-1, keepdims=True)
    expo = jnp.exp(scores - peak)
    total = jnp.sum(expo, axis=-1, keepdims=True)
    probs = expo / total
    mixed = jnp.einsum(
        "kgqp,kpd->kgqd", probs.astype(jnp.bfloat16), value_heads, preferred_element_type=jnp.float32
    )
    return mixed.reshape(query_heads.shape), (peak + jnp.log(total))[..., 0]


def attention_backward(
    query_heads, key_heads, value_heads, grad_heads, log_totals, allowed, scale_factor
):
    kv_count = key_heads.shape[0]
    query_groups = grouped(query_heads, kv_count)
    grad_groups = grouped(grad_heads, kv_count)
    scores = group_scores(query_groups, key_heads, allowed, scale_factor)
    probs = jnp.exp(scores - log_totals[..., None])
    prob_grad = jnp.einsum(
        "kgqd,kpd->kgqp", grad_groups, value_heads, preferred_element_type=jnp.float32
    )
    value_grad = jnp.einsum(
        "kgqp,kgqd->kpd", probs.astype(jnp.bfloat16), grad_groups, preferred_element_type=jnp.float32
    )
    inner = jnp.sum(probs * prob_grad, axis=-1, keepdims=True)
    score_grad = (probs * (prob_grad - inner)).astype(jnp.bfloat16)
    query_grad = (
        jnp.einsum("kgqp,kpd->kgqd", score_grad, key_heads, preferred_element_type=jnp.float32)
        * scale_factor
    )
    key_grad = (
        jnp.einsum("kgqp,kgqd->kpd", score_grad, query_groups, preferred_element_type=jnp.float32)
        * scale_factor
    )
    return query_grad.reshape(query_heads.shape), key_grad, value_grad


def row_scatter_sum(vectors):
    count = lax.axis_size("row")
    blocks = jnp.moveaxis(vectors.reshape(vectors.shape[0], count, -1), 1, 0)
    return jnp.sum(lax.all_to_all(blocks, "row", split_axis=0, concat_axis=0, tiled=True), axis=0)


GRAD_BLOCK = 128


def split_columns(packed, widths):
    pieces = []
    offset = 0
    for width in widths:
        pieces.append(packed[:, offset : offset + width])
        offset += width
    return pieces


def col_scatter(values):
    count = lax.axis_size("col")
    lead = values.shape[:-1]
    blocks = jnp.moveaxis(values.reshape(*lead, count, values.shape[-1] // count), -2, 0)
    received = lax.all_to_all(blocks, "col", split_axis=0, concat_axis=0, tiled=True)
    return jnp.sum(received.astype(jnp.float32), axis=0)


def col_gather(block):
    count = lax.axis_size("col")
    copies = jnp.broadcast_to(block[None], (count,) + block.shape)
    received = lax.all_to_all(copies, "col", split_axis=0, concat_axis=0, tiled=True)
    return jnp.moveaxis(received, 0, -2).reshape(*block.shape[:-1], count * block.shape[-1])


def col_sum(values):
    return col_gather(col_scatter(values).astype(jnp.bfloat16)).astype(jnp.float32)


def gather_rows(parts):
    return lax.all_gather(jnp.concatenate(parts, axis=1), "row", axis=0, tiled=True)


def grad_wide_kernel(select_ref, left_ref, right_ref, out_ref, uniform):
    step = pl.program_id(0)
    parts = out_ref.shape[1] // GRAD_BLOCK
    if uniform:
        out_ref[...] = jnp.dot(
            left_ref[select_ref[step * parts]], right_ref[...], preferred_element_type=jnp.float32
        ).astype(out_ref.dtype)
        return
    for part in range(parts):
        owner = select_ref[step * parts + part]
        columns = slice(part * GRAD_BLOCK, (part + 1) * GRAD_BLOCK)
        out_ref[:, columns] = jnp.dot(
            left_ref[owner], right_ref[:, columns], preferred_element_type=jnp.float32
        ).astype(out_ref.dtype)


def packed_weight_grads(lefts, segments):
    left_stack = jnp.stack([left.T for left in lefts])
    right = jnp.concatenate([seg for _, seg in segments], axis=1)
    column_owner = []
    for index, seg in segments:
        column_owner += [index] * seg.shape[1]
    assert len(column_owner) % GRAD_BLOCK == 0
    select = column_owner[::GRAD_BLOCK]
    assert column_owner == [owner for owner in select for _ in range(GRAD_BLOCK)]
    parts = max(m for m in range(1, 12) if len(select) % m == 0 and len(select) // m >= 3)
    width = parts * GRAD_BLOCK
    uniform = all(
        len(set(select[start : start + parts])) == 1 for start in range(0, len(select), parts)
    )
    features, tokens = left_stack.shape[1], left_stack.shape[2]
    in_specs = [
        pl.BlockSpec(left_stack.shape, lambda j, sel: (0, 0, 0)),
        pl.BlockSpec((tokens, width), lambda j, sel: (0, j)),
    ]
    return pl.pallas_call(
        partial(grad_wide_kernel, uniform=uniform),
        out_shape=jax.ShapeDtypeStruct((features, right.shape[1]), jnp.bfloat16),
        grid_spec=pltpu.PrefetchScalarGridSpec(
            num_scalar_prefetch=1,
            grid=(len(select) // parts,),
            in_specs=in_specs,
            out_specs=pl.BlockSpec((features, width), lambda j, sel: (0, j)),
        ),
    )(jnp.asarray(select, dtype=jnp.int32), left_stack, right)


def body(
    tokens,
    cotangent,
    destination,
    segment_ids,
    attn_gain,
    w_query,
    w_key,
    w_value,
    w_output,
    ffn_gain,
    w_gate,
    w_up,
    w_down,
):
    row_count = tokens.shape[0]
    quarter = tokens.shape[1]
    col_start = lax.axis_index("col") * quarter
    send_order = jnp.argsort(destination)
    slot_ids = destination[send_order] % row_count
    arrived_pair, arrived_slots = (
        lax.all_to_all(
            jnp.stack([tokens, cotangent])[:, send_order], "row", split_axis=1, concat_axis=1, tiled=True
        ),
        lax.all_to_all(slot_ids, "row", split_axis=0, concat_axis=0, tiled=True),
    )
    placing = jnp.argsort(arrived_slots)
    attn_widths = [w_query.shape[1], w_key.shape[1], w_value.shape[1], w_output.shape[1]]
    ffn_widths = [w_gate.shape[1], w_up.shape[1], w_down.shape[1]]
    weights_packed = gather_rows([w_query, w_key, w_value, w_output, w_gate, w_up, w_down])
    attn_packed = weights_packed[:, : sum(attn_widths)]
    ffn_packed = weights_packed[:, sum(attn_widths) :]
    placed_pair = arrived_pair[:, placing]
    full_rows = col_gather(placed_pair[0])
    full_grads = col_gather(placed_pair[1])
    query_w, key_w, value_w, output_w = split_columns(attn_packed, attn_widths)
    cosine, sine = rope_tables(positions_of(segment_ids))
    allowed = allowed_pairs(segment_ids)
    rows_wide = full_rows.astype(jnp.float32)
    inv_one = rms_scale(rows_wide)
    normed_one = (rows_wide * inv_one * attn_gain).astype(jnp.bfloat16)
    query = matmul(normed_one, query_w)
    key_raw = matmul(normed_one, key_w)
    value_raw = matmul(normed_one, value_w)
    query_heads_count = query.shape[1] // HD
    kv_count = key_raw.shape[1] // HD
    query_rot = (
        rotate(query.reshape(row_count, query_heads_count, HD), cosine, sine)
        .astype(jnp.bfloat16)
        .transpose(1, 0, 2)
    )
    key_rot = (
        rotate(key_raw.reshape(row_count, kv_count, HD), cosine, sine)
        .astype(jnp.bfloat16)
        .transpose(1, 0, 2)
    )
    value_heads = value_raw.astype(jnp.bfloat16).reshape(row_count, kv_count, HD).transpose(1, 0, 2)
    scale_factor = HD ** (-0.5)
    mixed_heads, log_totals = attention_forward(
        query_rot, key_rot, value_heads, allowed, scale_factor
    )
    mixed = (
        mixed_heads.transpose(1, 0, 2)
        .reshape(row_count, query_heads_count * HD)
        .astype(jnp.bfloat16)
    )
    attn_terms = matmul(mixed, output_w.T)
    attn_full = lax.psum(attn_terms.astype(jnp.bfloat16), "col").astype(jnp.float32)
    resid = rows_wide + attn_full
    inv_two = rms_scale(resid)
    normed_two = (resid * inv_two * ffn_gain).astype(jnp.bfloat16)
    resid_part = lax.dynamic_slice_in_dim(resid, col_start, quarter, 1)
    gate_w, up_w, down_w = split_columns(ffn_packed, ffn_widths)
    gate = matmul(normed_two, gate_w)
    upper = matmul(normed_two, up_w)
    sigmoid_gate = jax.nn.sigmoid(gate)
    activ = (gate * sigmoid_gate * upper).astype(jnp.bfloat16)
    ffn_share_low = lax.psum_scatter(
        matmul(activ, down_w.T).astype(jnp.bfloat16), "col", scatter_dimension=1, tiled=True
    )
    act_grad = matmul(full_grads, down_w)
    gate_grad = (act_grad * upper * sigmoid_gate * (1.0 + gate * (1.0 - sigmoid_gate))).astype(
        jnp.bfloat16
    )
    up_grad = (act_grad * gate * sigmoid_gate).astype(jnp.bfloat16)
    ffn_grads_packed = packed_weight_grads(
        [normed_two, full_grads], [(0, gate_grad), (0, up_grad), (1, activ)]
    )
    ffn_grads_packed, ffn_share_low = lax.optimization_barrier((ffn_grads_packed, ffn_share_low))
    kernel_done, gate_grad_late, up_grad_late = lax.optimization_barrier(
        (ffn_grads_packed, gate_grad, up_grad)
    )
    normed_terms_two = matmul(gate_grad_late, gate_w.T) + matmul(up_grad_late, up_w.T)
    normed_grad_two = col_sum(normed_terms_two.astype(jnp.bfloat16))
    resid_norm_grad, ffn_gain_grad = norm_back(resid, inv_two, ffn_gain, normed_grad_two)
    ffn_grads_local = lax.psum_scatter(ffn_grads_packed, "row", scatter_dimension=0, tiled=True)
    resid_grad = full_grads.astype(jnp.float32) + resid_norm_grad
    attn_grad_low = resid_grad.astype(jnp.bfloat16)
    mixed_grad = matmul(attn_grad_low, output_w).astype(jnp.bfloat16)
    mixed_grad_heads = mixed_grad.reshape(row_count, query_heads_count, HD).transpose(1, 0, 2)
    query_grads, key_grads, value_grads = attention_backward(
        query_rot, key_rot, value_heads, mixed_grad_heads, log_totals, allowed, scale_factor
    )
    query_grad = (
        rotate_back(query_grads.transpose(1, 0, 2), cosine, sine)
        .reshape(row_count, query_heads_count * HD)
        .astype(jnp.bfloat16)
    )
    key_sum = key_grads.transpose(1, 0, 2)
    key_grad = (
        rotate_back(key_sum, cosine, sine).reshape(row_count, kv_count * HD).astype(jnp.bfloat16)
    )
    value_sum = value_grads.transpose(1, 0, 2)
    value_grad = value_sum.reshape(row_count, kv_count * HD).astype(jnp.bfloat16)
    normed_terms_one = (
        matmul(query_grad, query_w.T) + matmul(key_grad, key_w.T) + matmul(value_grad, value_w.T)
    )
    output_share = (resid_part + ffn_share_low.astype(jnp.float32)).astype(jnp.bfloat16)
    back_rows = lax.all_to_all(
        output_share[arrived_slots], "row", split_axis=0, concat_axis=0, tiled=True
    )
    attn_grads_packed, ffn_grads_local, back_rows, normed_low_one = lax.optimization_barrier(
        (
            packed_weight_grads(
                [normed_one, attn_grad_low],
                [(0, query_grad), (0, key_grad), (0, value_grad), (1, mixed)],
            ),
            ffn_grads_local,
            back_rows,
            normed_terms_one.astype(jnp.bfloat16),
        )
    )
    attn_grads_local = lax.psum_scatter(attn_grads_packed, "row", scatter_dimension=0, tiled=True)
    normed_grad_block = col_scatter(normed_low_one)
    normed_block = lax.dynamic_slice_in_dim(rows_wide, col_start, quarter, 1) * inv_one
    scaled_block = normed_grad_block * lax.dynamic_slice_in_dim(attn_gain, col_start, quarter, 0)
    token_part = jnp.sum(scaled_block * normed_block, axis=-1)
    gain_part = jnp.sum(normed_grad_block * normed_block, axis=0)
    exchanged = col_gather(jnp.concatenate([token_part, gain_part])).reshape(
        -1, token_part.shape[0] + gain_part.shape[0]
    )
    row_mean = jnp.sum(exchanged[:, : token_part.shape[0]], axis=0) / rows_wide.shape[-1]
    attn_gain_grad = exchanged[:, token_part.shape[0] :].reshape(-1)
    input_block = lax.dynamic_slice_in_dim(resid_grad, col_start, quarter, 1) + inv_one * (
        scaled_block - normed_block * row_mean[:, None]
    )
    input_share = input_block.astype(jnp.bfloat16)
    query_result, key_result, value_result, output_result = split_columns(
        attn_grads_local.astype(jnp.float32), attn_widths
    )
    gate_result, up_result, down_result = split_columns(
        ffn_grads_local.astype(jnp.float32), ffn_widths
    )
    row_devices = lax.axis_size("row")
    gains = jnp.stack([attn_gain_grad, ffn_gain_grad])
    gain_blocks = jnp.moveaxis(gains.reshape(2, row_devices, -1), 1, 0).reshape(row_devices, -1)
    gain_width = gain_blocks.shape[1]
    assert gain_width <= quarter
    gain_rows = jnp.pad(gain_blocks, ((0, 0), (0, quarter - gain_width)))[:, None, :]
    token_rows = input_share[arrived_slots].reshape(row_devices, -1, quarter)
    received = lax.all_to_all(
        jnp.concatenate([token_rows, gain_rows.astype(jnp.bfloat16)], axis=1),
        "row",
        split_axis=0,
        concat_axis=0,
        tiled=True,
    )
    back_grads = received[:, :-1].reshape(row_count, quarter)
    gain_sums = jnp.sum(received[:, -1, :gain_width].astype(jnp.float32), axis=0).reshape(2, -1)
    attn_gain_result, ffn_gain_result = gain_sums[0], gain_sums[1]
    restore = jnp.argsort(send_order)
    return (
        back_rows[restore],
        back_grads[restore],
        attn_gain_result,
        query_result,
        key_result,
        value_result,
        output_result,
        ffn_gain_result,
        gate_result,
        up_result,
        down_result,
    )

def solution(mesh):
    placed = (
        P("row", "col"),
        P("row", "col"),
        P("row"),
        P("row"),
        P(),
        P("row", "col"),
        P("row", "col"),
        P("row", "col"),
        P("row", "col"),
        P(),
        P("row", "col"),
        P("row", "col"),
        P("row", "col"),
    )
    return jax.shard_map(
        body,
        mesh=mesh,
        in_specs=placed,
        out_specs=(
            P("row", "col"),
            P("row", "col"),
            P("row"),
            P("row", "col"),
            P("row", "col"),
            P("row", "col"),
            P("row", "col"),
            P("row"),
            P("row", "col"),
            P("row", "col"),
            P("row", "col"),
        ),
        check_vma=False,
    )
```

```python
from functools import partial

import jax
import jax.numpy as jnp
from jax import lax
from jax.experimental import pallas as pl
from jax.experimental.pallas import tpu as pltpu
from jax.sharding import PartitionSpec as P

HEADS = 32
KV = 4
HD = 64


EPS = 1e-05
ROPE_BASE = 10000.0


def rope_tables(positions):
    half_width = HD // 2
    freqs = ROPE_BASE ** (-(jnp.arange(half_width, dtype=jnp.float32) * 2.0 / HD))
    angles = positions.astype(jnp.float32)[:, None] * freqs[None, :]
    return (jnp.cos(angles)[:, None, :], jnp.sin(angles)[:, None, :])


def rotate(values, cosine, sine):
    half_width = values.shape[-1] // 2
    first = values[..., :half_width]
    second = values[..., half_width:]
    return jnp.concatenate(
        [first * cosine - second * sine, second * cosine + first * sine], axis=-1
    )


def rotate_back(grads, cosine, sine):
    half_width = grads.shape[-1] // 2
    first = grads[..., :half_width]
    second = grads[..., half_width:]
    return jnp.concatenate(
        [first * cosine + second * sine, second * cosine - first * sine], axis=-1
    )


def positions_of(segment_ids):
    index = jnp.arange(segment_ids.shape[0], dtype=jnp.int32)
    change = jnp.concatenate([jnp.ones((1,), dtype=jnp.bool_), segment_ids[1:] != segment_ids[:-1]])
    starts = jnp.where(change, index, jnp.zeros_like(index))
    return index - lax.cummax(starts, axis=0)


def allowed_pairs(segment_ids):
    index = jnp.arange(segment_ids.shape[0], dtype=jnp.int32)
    return (segment_ids[:, None] == segment_ids[None, :]) & (index[None, :] <= index[:, None])


def rms_scale(values):
    return lax.rsqrt(jnp.mean(values * values, axis=-1, keepdims=True) + EPS)


def norm_back(values, inv_root, gain, grads):
    normed = values * inv_root
    scaled = grads * gain
    result = inv_root * (scaled - normed * jnp.mean(scaled * normed, axis=-1, keepdims=True))
    return (result, jnp.sum(grads * normed, axis=0))


def matmul(left, right):
    return jnp.dot(left, right, preferred_element_type=jnp.float32)


def head_scores(query_head, key_head, allowed, scale_factor):
    scores = matmul(query_head, key_head.T) * scale_factor
    return jnp.where(allowed, scores, -1e30)


def head_forward(inputs, key_heads, value_heads, allowed, scale_factor):
    query_head, kv_slot = inputs
    scores = head_scores(query_head, key_heads[kv_slot], allowed, scale_factor)
    peak = jnp.max(scores, axis=-1, keepdims=True)
    expo = jnp.exp(scores - peak)
    total = jnp.sum(expo, axis=-1, keepdims=True)
    probs = expo / total
    mixed = matmul(probs.astype(jnp.bfloat16), value_heads[kv_slot])
    return (mixed, (peak + jnp.log(total))[:, 0])


def head_backward(inputs, key_heads, value_heads, allowed, scale_factor):
    query_head, kv_slot, grad_head, log_total = inputs
    key_head = key_heads[kv_slot]
    value_head = value_heads[kv_slot]
    scores = head_scores(query_head, key_head, allowed, scale_factor)
    probs = jnp.exp(scores - log_total[:, None])
    prob_grad = matmul(grad_head, value_head.T)
    value_grad = matmul(probs.astype(jnp.bfloat16).T, grad_head)
    inner = jnp.sum(probs * prob_grad, axis=-1, keepdims=True)
    score_grad = (probs * (prob_grad - inner)).astype(jnp.bfloat16)
    query_grad = matmul(score_grad, key_head) * scale_factor
    key_grad = matmul(score_grad.T, query_head) * scale_factor
    return (query_grad, key_grad, value_grad)


def grouped(heads, kv_count):
    return heads.reshape(kv_count, heads.shape[0] // kv_count, *heads.shape[1:])


def group_scores(query_groups, key_heads, allowed, scale_factor):
    scores = (
        jnp.einsum("kgqd,kpd->kgqp", query_groups, key_heads, preferred_element_type=jnp.float32)
        * scale_factor
    )
    return jnp.where(allowed, scores, -1e30)


def attention_forward(query_heads, key_heads, value_heads, allowed, scale_factor):
    query_groups = grouped(query_heads, key_heads.shape[0])
    scores = group_scores(query_groups, key_heads, allowed, scale_factor)
    peak = jnp.max(scores, axis=-1, keepdims=True)
    expo = jnp.exp(scores - peak)
    total = jnp.sum(expo, axis=-1, keepdims=True)
    probs = expo / total
    mixed = jnp.einsum(
        "kgqp,kpd->kgqd", probs.astype(jnp.bfloat16), value_heads, preferred_element_type=jnp.float32
    )
    return mixed.reshape(query_heads.shape), (peak + jnp.log(total))[..., 0]


def attention_backward(
    query_heads, key_heads, value_heads, grad_heads, log_totals, allowed, scale_factor
):
    kv_count = key_heads.shape[0]
    query_groups = grouped(query_heads, kv_count)
    grad_groups = grouped(grad_heads, kv_count)
    scores = group_scores(query_groups, key_heads, allowed, scale_factor)
    probs = jnp.exp(scores - log_totals[..., None])
    prob_grad = jnp.einsum(
        "kgqd,kpd->kgqp", grad_groups, value_heads, preferred_element_type=jnp.float32
    )
    value_grad = jnp.einsum(
        "kgqp,kgqd->kpd", probs.astype(jnp.bfloat16), grad_groups, preferred_element_type=jnp.float32
    )
    inner = jnp.sum(probs * prob_grad, axis=-1, keepdims=True)
    score_grad = (probs * (prob_grad - inner)).astype(jnp.bfloat16)
    query_grad = (
        jnp.einsum("kgqp,kpd->kgqd", score_grad, key_heads, preferred_element_type=jnp.float32)
        * scale_factor
    )
    key_grad = (
        jnp.einsum("kgqp,kgqd->kpd", score_grad, query_groups, preferred_element_type=jnp.float32)
        * scale_factor
    )
    return query_grad.reshape(query_heads.shape), key_grad, value_grad


def row_scatter_sum(vectors):
    count = lax.axis_size("row")
    blocks = jnp.moveaxis(vectors.reshape(vectors.shape[0], count, -1), 1, 0)
    return jnp.sum(lax.all_to_all(blocks, "row", split_axis=0, concat_axis=0, tiled=True), axis=0)


GRAD_BLOCK = 128


def split_columns(packed, widths):
    pieces = []
    offset = 0
    for width in widths:
        pieces.append(packed[:, offset : offset + width])
        offset += width
    return pieces


def col_scatter(values):
    count = lax.axis_size("col")
    lead = values.shape[:-1]
    blocks = jnp.moveaxis(values.reshape(*lead, count, values.shape[-1] // count), -2, 0)
    received = lax.all_to_all(blocks, "col", split_axis=0, concat_axis=0, tiled=True)
    return jnp.sum(received.astype(jnp.float32), axis=0)


def col_gather(block):
    count = lax.axis_size("col")
    copies = jnp.broadcast_to(block[None], (count,) + block.shape)
    received = lax.all_to_all(copies, "col", split_axis=0, concat_axis=0, tiled=True)
    return jnp.moveaxis(received, 0, -2).reshape(*block.shape[:-1], count * block.shape[-1])


def col_sum(values):
    return col_gather(col_scatter(values).astype(jnp.bfloat16)).astype(jnp.float32)


def gather_rows(parts):
    return lax.all_gather(jnp.concatenate(parts, axis=1), "row", axis=0, tiled=True)


def grad_wide_kernel(select_ref, left_ref, right_ref, out_ref, uniform):
    step = pl.program_id(0)
    parts = out_ref.shape[1] // GRAD_BLOCK
    if uniform:
        out_ref[...] = jnp.dot(
            left_ref[select_ref[step * parts]], right_ref[...], preferred_element_type=jnp.float32
        ).astype(out_ref.dtype)
        return
    for part in range(parts):
        owner = select_ref[step * parts + part]
        columns = slice(part * GRAD_BLOCK, (part + 1) * GRAD_BLOCK)
        out_ref[:, columns] = jnp.dot(
            left_ref[owner], right_ref[:, columns], preferred_element_type=jnp.float32
        ).astype(out_ref.dtype)


def packed_weight_grads(lefts, segments):
    left_stack = jnp.stack([left.T for left in lefts])
    right = jnp.concatenate([seg for _, seg in segments], axis=1)
    column_owner = []
    for index, seg in segments:
        column_owner += [index] * seg.shape[1]
    assert len(column_owner) % GRAD_BLOCK == 0
    select = column_owner[::GRAD_BLOCK]
    assert column_owner == [owner for owner in select for _ in range(GRAD_BLOCK)]
    parts = max(m for m in range(1, 12) if len(select) % m == 0 and len(select) // m >= 3)
    width = parts * GRAD_BLOCK
    uniform = all(
        len(set(select[start : start + parts])) == 1 for start in range(0, len(select), parts)
    )
    features, tokens = left_stack.shape[1], left_stack.shape[2]
    in_specs = [
        pl.BlockSpec(left_stack.shape, lambda j, sel: (0, 0, 0)),
        pl.BlockSpec((tokens, width), lambda j, sel: (0, j)),
    ]
    return pl.pallas_call(
        partial(grad_wide_kernel, uniform=uniform),
        out_shape=jax.ShapeDtypeStruct((features, right.shape[1]), jnp.bfloat16),
        grid_spec=pltpu.PrefetchScalarGridSpec(
            num_scalar_prefetch=1,
            grid=(len(select) // parts,),
            in_specs=in_specs,
            out_specs=pl.BlockSpec((features, width), lambda j, sel: (0, j)),
        ),
    )(jnp.asarray(select, dtype=jnp.int32), left_stack, right)


def body(
    tokens,
    cotangent,
    destination,
    segment_ids,
    attn_gain,
    w_query,
    w_key,
    w_value,
    w_output,
    ffn_gain,
    w_gate,
    w_up,
    w_down,
):
    row_count = tokens.shape[0]
    quarter = tokens.shape[1]
    col_start = lax.axis_index("col") * quarter
    send_order = jnp.argsort(destination)
    slot_ids = destination[send_order] % row_count
    arrived_pair, arrived_slots = (
        lax.all_to_all(
            jnp.stack([tokens, cotangent])[:, send_order], "row", split_axis=1, concat_axis=1, tiled=True
        ),
        lax.all_to_all(slot_ids, "row", split_axis=0, concat_axis=0, tiled=True),
    )
    placing = jnp.argsort(arrived_slots)
    attn_widths = [w_query.shape[1], w_key.shape[1], w_value.shape[1], w_output.shape[1]]
    ffn_widths = [w_gate.shape[1], w_up.shape[1], w_down.shape[1]]
    weights_packed = gather_rows([w_query, w_key, w_value, w_output, w_gate, w_up, w_down])
    attn_packed = weights_packed[:, : sum(attn_widths)]
    ffn_packed = weights_packed[:, sum(attn_widths) :]
    placed_pair = arrived_pair[:, placing]
    full_rows = col_gather(placed_pair[0])
    full_grads = col_gather(placed_pair[1])
    query_w, key_w, value_w, output_w = split_columns(attn_packed, attn_widths)
    cosine, sine = rope_tables(positions_of(segment_ids))
    allowed = allowed_pairs(segment_ids)
    rows_wide = full_rows.astype(jnp.float32)
    inv_one = rms_scale(rows_wide)
    normed_one = (rows_wide * inv_one * attn_gain).astype(jnp.bfloat16)
    query = matmul(normed_one, query_w)
    key_raw = matmul(normed_one, key_w)
    value_raw = matmul(normed_one, value_w)
    query_heads_count = query.shape[1] // HD
    kv_count = key_raw.shape[1] // HD
    query_rot = (
        rotate(query.reshape(row_count, query_heads_count, HD), cosine, sine)
        .astype(jnp.bfloat16)
        .transpose(1, 0, 2)
    )
    key_rot = (
        rotate(key_raw.reshape(row_count, kv_count, HD), cosine, sine)
        .astype(jnp.bfloat16)
        .transpose(1, 0, 2)
    )
    value_heads = value_raw.astype(jnp.bfloat16).reshape(row_count, kv_count, HD).transpose(1, 0, 2)
    scale_factor = HD ** (-0.5)
    mixed_heads, log_totals = attention_forward(
        query_rot, key_rot, value_heads, allowed, scale_factor
    )
    mixed = (
        mixed_heads.transpose(1, 0, 2)
        .reshape(row_count, query_heads_count * HD)
        .astype(jnp.bfloat16)
    )
    attn_terms = matmul(mixed, output_w.T)
    attn_full = lax.psum(attn_terms.astype(jnp.bfloat16), "col").astype(jnp.float32)
    resid = rows_wide + attn_full
    inv_two = rms_scale(resid)
    normed_two = (resid * inv_two * ffn_gain).astype(jnp.bfloat16)
    resid_part = lax.dynamic_slice_in_dim(resid, col_start, quarter, 1)
    gate_w, up_w, down_w = split_columns(ffn_packed, ffn_widths)
    gate = matmul(normed_two, gate_w)
    upper = matmul(normed_two, up_w)
    sigmoid_gate = jax.nn.sigmoid(gate)
    activ = (gate * sigmoid_gate * upper).astype(jnp.bfloat16)
    ffn_share_low = lax.psum_scatter(
        matmul(activ, down_w.T).astype(jnp.bfloat16), "col", scatter_dimension=1, tiled=True
    )
    act_grad = matmul(full_grads, down_w)
    gate_grad = (act_grad * upper * sigmoid_gate * (1.0 + gate * (1.0 - sigmoid_gate))).astype(
        jnp.bfloat16
    )
    up_grad = (act_grad * gate * sigmoid_gate).astype(jnp.bfloat16)
    normed_terms_two = matmul(gate_grad, gate_w.T) + matmul(up_grad, up_w.T)
    ffn_grads_packed = packed_weight_grads(
        [normed_two, full_grads], [(0, gate_grad), (0, up_grad), (1, activ)]
    )
    ffn_grads_packed, ffn_share_low = lax.optimization_barrier((ffn_grads_packed, ffn_share_low))
    normed_low_two, ffn_grads_packed = lax.optimization_barrier(
        (normed_terms_two.astype(jnp.bfloat16), ffn_grads_packed)
    )
    normed_grad_two = col_sum(normed_low_two)
    resid_norm_grad, ffn_gain_grad = norm_back(resid, inv_two, ffn_gain, normed_grad_two)
    ffn_grads_local = lax.psum_scatter(ffn_grads_packed, "row", scatter_dimension=0, tiled=True)
    resid_grad = full_grads.astype(jnp.float32) + resid_norm_grad
    attn_grad_low = resid_grad.astype(jnp.bfloat16)
    mixed_grad = matmul(attn_grad_low, output_w).astype(jnp.bfloat16)
    mixed_grad_heads = mixed_grad.reshape(row_count, query_heads_count, HD).transpose(1, 0, 2)
    query_grads, key_grads, value_grads = attention_backward(
        query_rot, key_rot, value_heads, mixed_grad_heads, log_totals, allowed, scale_factor
    )
    query_grad = (
        rotate_back(query_grads.transpose(1, 0, 2), cosine, sine)
        .reshape(row_count, query_heads_count * HD)
        .astype(jnp.bfloat16)
    )
    key_sum = key_grads.transpose(1, 0, 2)
    key_grad = (
        rotate_back(key_sum, cosine, sine).reshape(row_count, kv_count * HD).astype(jnp.bfloat16)
    )
    value_sum = value_grads.transpose(1, 0, 2)
    value_grad = value_sum.reshape(row_count, kv_count * HD).astype(jnp.bfloat16)
    output_share = (resid_part + ffn_share_low.astype(jnp.float32)).astype(jnp.bfloat16)
    back_rows = lax.all_to_all(
        output_share[arrived_slots], "row", split_axis=0, concat_axis=0, tiled=True
    )
    (
        attn_grads_packed,
        ffn_grads_local,
        back_rows,
        query_grad_late,
        key_grad_late,
        value_grad_late,
    ) = lax.optimization_barrier(
        (
            packed_weight_grads(
                [normed_one, attn_grad_low],
                [(0, query_grad), (0, key_grad), (0, value_grad), (1, mixed)],
            ),
            ffn_grads_local,
            back_rows,
            query_grad,
            key_grad,
            value_grad,
        )
    )
    normed_low_one = (
        matmul(query_grad_late, query_w.T)
        + matmul(key_grad_late, key_w.T)
        + matmul(value_grad_late, value_w.T)
    ).astype(jnp.bfloat16)
    attn_grads_local = lax.psum_scatter(attn_grads_packed, "row", scatter_dimension=0, tiled=True)
    normed_grad_block = col_scatter(normed_low_one)
    normed_block = lax.dynamic_slice_in_dim(rows_wide, col_start, quarter, 1) * inv_one
    scaled_block = normed_grad_block * lax.dynamic_slice_in_dim(attn_gain, col_start, quarter, 0)
    token_part = jnp.sum(scaled_block * normed_block, axis=-1)
    gain_part = jnp.sum(normed_grad_block * normed_block, axis=0)
    exchanged = col_gather(jnp.concatenate([token_part, gain_part])).reshape(
        -1, token_part.shape[0] + gain_part.shape[0]
    )
    row_mean = jnp.sum(exchanged[:, : token_part.shape[0]], axis=0) / rows_wide.shape[-1]
    attn_gain_grad = exchanged[:, token_part.shape[0] :].reshape(-1)
    input_block = lax.dynamic_slice_in_dim(resid_grad, col_start, quarter, 1) + inv_one * (
        scaled_block - normed_block * row_mean[:, None]
    )
    input_share = input_block.astype(jnp.bfloat16)
    query_result, key_result, value_result, output_result = split_columns(
        attn_grads_local.astype(jnp.float32), attn_widths
    )
    gate_result, up_result, down_result = split_columns(
        ffn_grads_local.astype(jnp.float32), ffn_widths
    )
    row_devices = lax.axis_size("row")
    gains = jnp.stack([attn_gain_grad, ffn_gain_grad])
    gain_blocks = jnp.moveaxis(gains.reshape(2, row_devices, -1), 1, 0).reshape(row_devices, -1)
    gain_width = gain_blocks.shape[1]
    assert gain_width <= quarter
    gain_rows = jnp.pad(gain_blocks, ((0, 0), (0, quarter - gain_width)))[:, None, :]
    token_rows = input_share[arrived_slots].reshape(row_devices, -1, quarter)
    received = lax.all_to_all(
        jnp.concatenate([token_rows, gain_rows.astype(jnp.bfloat16)], axis=1),
        "row",
        split_axis=0,
        concat_axis=0,
        tiled=True,
    )
    back_grads = received[:, :-1].reshape(row_count, quarter)
    gain_sums = jnp.sum(received[:, -1, :gain_width].astype(jnp.float32), axis=0).reshape(2, -1)
    attn_gain_result, ffn_gain_result = gain_sums[0], gain_sums[1]
    restore = jnp.argsort(send_order)
    return (
        back_rows[restore],
        back_grads[restore],
        attn_gain_result,
        query_result,
        key_result,
        value_result,
        output_result,
        ffn_gain_result,
        gate_result,
        up_result,
        down_result,
    )

def solution(mesh):
    placed = (
        P("row", "col"),
        P("row", "col"),
        P("row"),
        P("row"),
        P(),
        P("row", "col"),
        P("row", "col"),
        P("row", "col"),
        P("row", "col"),
        P(),
        P("row", "col"),
        P("row", "col"),
        P("row", "col"),
    )
    return jax.shard_map(
        body,
        mesh=mesh,
        in_specs=placed,
        out_specs=(
            P("row", "col"),
            P("row", "col"),
            P("row"),
            P("row", "col"),
            P("row", "col"),
            P("row", "col"),
            P("row", "col"),
            P("row"),
            P("row", "col"),
            P("row", "col"),
            P("row", "col"),
        ),
        check_vma=False,
    )
```

```python
from functools import partial

import jax
import jax.numpy as jnp
from jax import lax
from jax.experimental import pallas as pl
from jax.experimental.pallas import tpu as pltpu
from jax.sharding import PartitionSpec as P

HEADS = 32
KV = 4
HD = 64


EPS = 1e-05
ROPE_BASE = 10000.0


def rope_tables(positions):
    half_width = HD // 2
    freqs = ROPE_BASE ** (-(jnp.arange(half_width, dtype=jnp.float32) * 2.0 / HD))
    angles = positions.astype(jnp.float32)[:, None] * freqs[None, :]
    return (jnp.cos(angles)[:, None, :], jnp.sin(angles)[:, None, :])


def rotate(values, cosine, sine):
    half_width = values.shape[-1] // 2
    first = values[..., :half_width]
    second = values[..., half_width:]
    return jnp.concatenate(
        [first * cosine - second * sine, second * cosine + first * sine], axis=-1
    )


def rotate_back(grads, cosine, sine):
    half_width = grads.shape[-1] // 2
    first = grads[..., :half_width]
    second = grads[..., half_width:]
    return jnp.concatenate(
        [first * cosine + second * sine, second * cosine - first * sine], axis=-1
    )


def positions_of(segment_ids):
    index = jnp.arange(segment_ids.shape[0], dtype=jnp.int32)
    change = jnp.concatenate([jnp.ones((1,), dtype=jnp.bool_), segment_ids[1:] != segment_ids[:-1]])
    starts = jnp.where(change, index, jnp.zeros_like(index))
    return index - lax.cummax(starts, axis=0)


def allowed_pairs(segment_ids):
    index = jnp.arange(segment_ids.shape[0], dtype=jnp.int32)
    return (segment_ids[:, None] == segment_ids[None, :]) & (index[None, :] <= index[:, None])


def rms_scale(values):
    return lax.rsqrt(jnp.mean(values * values, axis=-1, keepdims=True) + EPS)


def norm_back(values, inv_root, gain, grads):
    normed = values * inv_root
    scaled = grads * gain
    result = inv_root * (scaled - normed * jnp.mean(scaled * normed, axis=-1, keepdims=True))
    return (result, jnp.sum(grads * normed, axis=0))


def matmul(left, right):
    return jnp.dot(left, right, preferred_element_type=jnp.float32)


def head_scores(query_head, key_head, allowed, scale_factor):
    scores = matmul(query_head, key_head.T) * scale_factor
    return jnp.where(allowed, scores, -1e30)


def head_forward(inputs, key_heads, value_heads, allowed, scale_factor):
    query_head, kv_slot = inputs
    scores = head_scores(query_head, key_heads[kv_slot], allowed, scale_factor)
    peak = jnp.max(scores, axis=-1, keepdims=True)
    expo = jnp.exp(scores - peak)
    total = jnp.sum(expo, axis=-1, keepdims=True)
    probs = expo / total
    mixed = matmul(probs.astype(jnp.bfloat16), value_heads[kv_slot])
    return (mixed, (peak + jnp.log(total))[:, 0])


def head_backward(inputs, key_heads, value_heads, allowed, scale_factor):
    query_head, kv_slot, grad_head, log_total = inputs
    key_head = key_heads[kv_slot]
    value_head = value_heads[kv_slot]
    scores = head_scores(query_head, key_head, allowed, scale_factor)
    probs = jnp.exp(scores - log_total[:, None])
    prob_grad = matmul(grad_head, value_head.T)
    value_grad = matmul(probs.astype(jnp.bfloat16).T, grad_head)
    inner = jnp.sum(probs * prob_grad, axis=-1, keepdims=True)
    score_grad = (probs * (prob_grad - inner)).astype(jnp.bfloat16)
    query_grad = matmul(score_grad, key_head) * scale_factor
    key_grad = matmul(score_grad.T, query_head) * scale_factor
    return (query_grad, key_grad, value_grad)


def grouped(heads, kv_count):
    return heads.reshape(kv_count, heads.shape[0] // kv_count, *heads.shape[1:])


def group_scores(query_groups, key_heads, allowed, scale_factor):
    scores = (
        jnp.einsum("kgqd,kpd->kgqp", query_groups, key_heads, preferred_element_type=jnp.float32)
        * scale_factor
    )
    return jnp.where(allowed, scores, -1e30)


def attention_forward(query_heads, key_heads, value_heads, allowed, scale_factor):
    query_groups = grouped(query_heads, key_heads.shape[0])
    scores = group_scores(query_groups, key_heads, allowed, scale_factor)
    peak = jnp.max(scores, axis=-1, keepdims=True)
    expo = jnp.exp(scores - peak)
    total = jnp.sum(expo, axis=-1, keepdims=True)
    probs = expo / total
    mixed = jnp.einsum(
        "kgqp,kpd->kgqd", probs.astype(jnp.bfloat16), value_heads, preferred_element_type=jnp.float32
    )
    return mixed.reshape(query_heads.shape), (peak + jnp.log(total))[..., 0]


def attention_backward(
    query_heads, key_heads, value_heads, grad_heads, log_totals, allowed, scale_factor
):
    kv_count = key_heads.shape[0]
    query_groups = grouped(query_heads, kv_count)
    grad_groups = grouped(grad_heads, kv_count)
    scores = group_scores(query_groups, key_heads, allowed, scale_factor)
    probs = jnp.exp(scores - log_totals[..., None])
    prob_grad = jnp.einsum(
        "kgqd,kpd->kgqp", grad_groups, value_heads, preferred_element_type=jnp.float32
    )
    value_grad = jnp.einsum(
        "kgqp,kgqd->kpd", probs.astype(jnp.bfloat16), grad_groups, preferred_element_type=jnp.float32
    )
    inner = jnp.sum(probs * prob_grad, axis=-1, keepdims=True)
    score_grad = (probs * (prob_grad - inner)).astype(jnp.bfloat16)
    query_grad = (
        jnp.einsum("kgqp,kpd->kgqd", score_grad, key_heads, preferred_element_type=jnp.float32)
        * scale_factor
    )
    key_grad = (
        jnp.einsum("kgqp,kgqd->kpd", score_grad, query_groups, preferred_element_type=jnp.float32)
        * scale_factor
    )
    return query_grad.reshape(query_heads.shape), key_grad, value_grad


def row_scatter_sum(vectors):
    count = lax.axis_size("row")
    blocks = jnp.moveaxis(vectors.reshape(vectors.shape[0], count, -1), 1, 0)
    return jnp.sum(lax.all_to_all(blocks, "row", split_axis=0, concat_axis=0, tiled=True), axis=0)


GRAD_BLOCK = 128


def split_columns(packed, widths):
    pieces = []
    offset = 0
    for width in widths:
        pieces.append(packed[:, offset : offset + width])
        offset += width
    return pieces


def col_scatter(values):
    count = lax.axis_size("col")
    lead = values.shape[:-1]
    blocks = jnp.moveaxis(values.reshape(*lead, count, values.shape[-1] // count), -2, 0)
    received = lax.all_to_all(blocks, "col", split_axis=0, concat_axis=0, tiled=True)
    return jnp.sum(received.astype(jnp.float32), axis=0)


def col_gather(block):
    count = lax.axis_size("col")
    copies = jnp.broadcast_to(block[None], (count,) + block.shape)
    received = lax.all_to_all(copies, "col", split_axis=0, concat_axis=0, tiled=True)
    return jnp.moveaxis(received, 0, -2).reshape(*block.shape[:-1], count * block.shape[-1])


def col_sum(values):
    return col_gather(col_scatter(values).astype(jnp.bfloat16)).astype(jnp.float32)


def gather_rows(parts):
    return lax.all_gather(jnp.concatenate(parts, axis=1), "row", axis=0, tiled=True)


def grad_wide_kernel(select_ref, left_ref, right_ref, out_ref, uniform):
    step = pl.program_id(0)
    parts = out_ref.shape[1] // GRAD_BLOCK
    if uniform:
        out_ref[...] = jnp.dot(
            left_ref[select_ref[step * parts]], right_ref[...], preferred_element_type=jnp.float32
        ).astype(out_ref.dtype)
        return
    for part in range(parts):
        owner = select_ref[step * parts + part]
        columns = slice(part * GRAD_BLOCK, (part + 1) * GRAD_BLOCK)
        out_ref[:, columns] = jnp.dot(
            left_ref[owner], right_ref[:, columns], preferred_element_type=jnp.float32
        ).astype(out_ref.dtype)


def grad_runs_kernel(left_ref, right_ref, out_ref, runs):
    for owner, start, width in runs:
        out_ref[:, start : start + width] = jnp.dot(
            left_ref[owner], right_ref[:, start : start + width], preferred_element_type=jnp.float32
        ).astype(out_ref.dtype)


def packed_weight_grads(lefts, segments):
    left_stack = jnp.stack([left.T for left in lefts])
    right = jnp.concatenate([seg for _, seg in segments], axis=1)
    column_owner = []
    for index, seg in segments:
        column_owner += [index] * seg.shape[1]
    assert len(column_owner) % GRAD_BLOCK == 0
    select = column_owner[::GRAD_BLOCK]
    assert column_owner == [owner for owner in select for _ in range(GRAD_BLOCK)]
    if len(select) <= 10:
        runs = []
        for owner, seg in segments:
            if runs and runs[-1][0] == owner:
                runs[-1][2] += seg.shape[1]
            else:
                start = runs[-1][1] + runs[-1][2] if runs else 0
                runs.append([owner, start, seg.shape[1]])
        return pl.pallas_call(
            partial(grad_runs_kernel, runs=[tuple(run) for run in runs]),
            out_shape=jax.ShapeDtypeStruct((left_stack.shape[1], right.shape[1]), jnp.bfloat16),
            grid=(1,),
            in_specs=[
                pl.BlockSpec(left_stack.shape, lambda j: (0, 0, 0)),
                pl.BlockSpec(right.shape, lambda j: (0, 0)),
            ],
            out_specs=pl.BlockSpec((left_stack.shape[1], right.shape[1]), lambda j: (0, 0)),
        )(left_stack, right)
    parts = max(m for m in range(1, 12) if len(select) % m == 0 and len(select) // m >= 3)
    width = parts * GRAD_BLOCK
    uniform = all(
        len(set(select[start : start + parts])) == 1 for start in range(0, len(select), parts)
    )
    features, tokens = left_stack.shape[1], left_stack.shape[2]
    in_specs = [
        pl.BlockSpec(left_stack.shape, lambda j, sel: (0, 0, 0)),
        pl.BlockSpec((tokens, width), lambda j, sel: (0, j)),
    ]
    return pl.pallas_call(
        partial(grad_wide_kernel, uniform=uniform),
        out_shape=jax.ShapeDtypeStruct((features, right.shape[1]), jnp.bfloat16),
        grid_spec=pltpu.PrefetchScalarGridSpec(
            num_scalar_prefetch=1,
            grid=(len(select) // parts,),
            in_specs=in_specs,
            out_specs=pl.BlockSpec((features, width), lambda j, sel: (0, j)),
        ),
    )(jnp.asarray(select, dtype=jnp.int32), left_stack, right)


def body(
    tokens,
    cotangent,
    destination,
    segment_ids,
    attn_gain,
    w_query,
    w_key,
    w_value,
    w_output,
    ffn_gain,
    w_gate,
    w_up,
    w_down,
):
    row_count = tokens.shape[0]
    quarter = tokens.shape[1]
    col_start = lax.axis_index("col") * quarter
    send_order = jnp.argsort(destination)
    slot_ids = destination[send_order] % row_count
    arrived_pair, arrived_slots = (
        lax.all_to_all(
            jnp.stack([tokens, cotangent])[:, send_order], "row", split_axis=1, concat_axis=1, tiled=True
        ),
        lax.all_to_all(slot_ids, "row", split_axis=0, concat_axis=0, tiled=True),
    )
    placing = jnp.argsort(arrived_slots)
    attn_widths = [w_query.shape[1], w_key.shape[1], w_value.shape[1], w_output.shape[1]]
    ffn_widths = [w_gate.shape[1], w_up.shape[1], w_down.shape[1]]
    weights_packed = gather_rows([w_query, w_key, w_value, w_output, w_gate, w_up, w_down])
    attn_packed = weights_packed[:, : sum(attn_widths)]
    ffn_packed = weights_packed[:, sum(attn_widths) :]
    placed_pair = arrived_pair[:, placing]
    full_rows = col_gather(placed_pair[0])
    full_grads = col_gather(placed_pair[1])
    query_w, key_w, value_w, output_w = split_columns(attn_packed, attn_widths)
    cosine, sine = rope_tables(positions_of(segment_ids))
    allowed = allowed_pairs(segment_ids)
    rows_wide = full_rows.astype(jnp.float32)
    inv_one = rms_scale(rows_wide)
    normed_one = (rows_wide * inv_one * attn_gain).astype(jnp.bfloat16)
    query = matmul(normed_one, query_w)
    key_raw = matmul(normed_one, key_w)
    value_raw = matmul(normed_one, value_w)
    query_heads_count = query.shape[1] // HD
    kv_count = key_raw.shape[1] // HD
    query_rot = (
        rotate(query.reshape(row_count, query_heads_count, HD), cosine, sine)
        .astype(jnp.bfloat16)
        .transpose(1, 0, 2)
    )
    key_rot = (
        rotate(key_raw.reshape(row_count, kv_count, HD), cosine, sine)
        .astype(jnp.bfloat16)
        .transpose(1, 0, 2)
    )
    value_heads = value_raw.astype(jnp.bfloat16).reshape(row_count, kv_count, HD).transpose(1, 0, 2)
    scale_factor = HD ** (-0.5)
    mixed_heads, log_totals = attention_forward(
        query_rot, key_rot, value_heads, allowed, scale_factor
    )
    mixed = (
        mixed_heads.transpose(1, 0, 2)
        .reshape(row_count, query_heads_count * HD)
        .astype(jnp.bfloat16)
    )
    attn_terms = matmul(mixed, output_w.T)
    attn_full = lax.psum(attn_terms.astype(jnp.bfloat16), "col").astype(jnp.float32)
    resid = rows_wide + attn_full
    inv_two = rms_scale(resid)
    normed_two = (resid * inv_two * ffn_gain).astype(jnp.bfloat16)
    resid_part = lax.dynamic_slice_in_dim(resid, col_start, quarter, 1)
    gate_w, up_w, down_w = split_columns(ffn_packed, ffn_widths)
    gate = matmul(normed_two, gate_w)
    upper = matmul(normed_two, up_w)
    sigmoid_gate = jax.nn.sigmoid(gate)
    activ = (gate * sigmoid_gate * upper).astype(jnp.bfloat16)
    ffn_share_low = lax.psum_scatter(
        matmul(activ, down_w.T).astype(jnp.bfloat16), "col", scatter_dimension=1, tiled=True
    )
    act_grad = matmul(full_grads, down_w)
    gate_grad = (act_grad * upper * sigmoid_gate * (1.0 + gate * (1.0 - sigmoid_gate))).astype(
        jnp.bfloat16
    )
    up_grad = (act_grad * gate * sigmoid_gate).astype(jnp.bfloat16)
    normed_terms_two = matmul(gate_grad, gate_w.T) + matmul(up_grad, up_w.T)
    ffn_grads_packed = packed_weight_grads(
        [normed_two, full_grads], [(0, gate_grad), (0, up_grad), (1, activ)]
    )
    ffn_grads_packed, ffn_share_low = lax.optimization_barrier((ffn_grads_packed, ffn_share_low))
    normed_low_two, ffn_grads_packed = lax.optimization_barrier(
        (normed_terms_two.astype(jnp.bfloat16), ffn_grads_packed)
    )
    normed_grad_two = col_sum(normed_low_two)
    resid_norm_grad, ffn_gain_grad = norm_back(resid, inv_two, ffn_gain, normed_grad_two)
    ffn_grads_local = lax.psum_scatter(ffn_grads_packed, "row", scatter_dimension=0, tiled=True)
    resid_grad = full_grads.astype(jnp.float32) + resid_norm_grad
    attn_grad_low = resid_grad.astype(jnp.bfloat16)
    mixed_grad = matmul(attn_grad_low, output_w).astype(jnp.bfloat16)
    mixed_grad_heads = mixed_grad.reshape(row_count, query_heads_count, HD).transpose(1, 0, 2)
    query_grads, key_grads, value_grads = attention_backward(
        query_rot, key_rot, value_heads, mixed_grad_heads, log_totals, allowed, scale_factor
    )
    query_grad = (
        rotate_back(query_grads.transpose(1, 0, 2), cosine, sine)
        .reshape(row_count, query_heads_count * HD)
        .astype(jnp.bfloat16)
    )
    key_sum = key_grads.transpose(1, 0, 2)
    key_grad = (
        rotate_back(key_sum, cosine, sine).reshape(row_count, kv_count * HD).astype(jnp.bfloat16)
    )
    value_sum = value_grads.transpose(1, 0, 2)
    value_grad = value_sum.reshape(row_count, kv_count * HD).astype(jnp.bfloat16)
    normed_terms_one = (
        matmul(query_grad, query_w.T) + matmul(key_grad, key_w.T) + matmul(value_grad, value_w.T)
    )
    output_share = (resid_part + ffn_share_low.astype(jnp.float32)).astype(jnp.bfloat16)
    back_rows = lax.all_to_all(
        output_share[arrived_slots], "row", split_axis=0, concat_axis=0, tiled=True
    )
    attn_grads_packed, ffn_grads_local, back_rows, normed_low_one = lax.optimization_barrier(
        (
            packed_weight_grads(
                [normed_one, attn_grad_low],
                [(0, query_grad), (0, key_grad), (0, value_grad), (1, mixed)],
            ),
            ffn_grads_local,
            back_rows,
            normed_terms_one.astype(jnp.bfloat16),
        )
    )
    attn_grads_local = lax.psum_scatter(attn_grads_packed, "row", scatter_dimension=0, tiled=True)
    normed_grad_block = col_scatter(normed_low_one)
    normed_block = lax.dynamic_slice_in_dim(rows_wide, col_start, quarter, 1) * inv_one
    scaled_block = normed_grad_block * lax.dynamic_slice_in_dim(attn_gain, col_start, quarter, 0)
    token_part = jnp.sum(scaled_block * normed_block, axis=-1)
    gain_part = jnp.sum(normed_grad_block * normed_block, axis=0)
    exchanged = col_gather(jnp.concatenate([token_part, gain_part])).reshape(
        -1, token_part.shape[0] + gain_part.shape[0]
    )
    row_mean = jnp.sum(exchanged[:, : token_part.shape[0]], axis=0) / rows_wide.shape[-1]
    attn_gain_grad = exchanged[:, token_part.shape[0] :].reshape(-1)
    input_block = lax.dynamic_slice_in_dim(resid_grad, col_start, quarter, 1) + inv_one * (
        scaled_block - normed_block * row_mean[:, None]
    )
    input_share = input_block.astype(jnp.bfloat16)
    query_result, key_result, value_result, output_result = split_columns(
        attn_grads_local.astype(jnp.float32), attn_widths
    )
    gate_result, up_result, down_result = split_columns(
        ffn_grads_local.astype(jnp.float32), ffn_widths
    )
    row_devices = lax.axis_size("row")
    gains = jnp.stack([attn_gain_grad, ffn_gain_grad])
    gain_blocks = jnp.moveaxis(gains.reshape(2, row_devices, -1), 1, 0).reshape(row_devices, -1)
    gain_width = gain_blocks.shape[1]
    assert gain_width <= quarter
    gain_rows = jnp.pad(gain_blocks, ((0, 0), (0, quarter - gain_width)))[:, None, :]
    token_rows = input_share[arrived_slots].reshape(row_devices, -1, quarter)
    received = lax.all_to_all(
        jnp.concatenate([token_rows, gain_rows.astype(jnp.bfloat16)], axis=1),
        "row",
        split_axis=0,
        concat_axis=0,
        tiled=True,
    )
    back_grads = received[:, :-1].reshape(row_count, quarter)
    gain_sums = jnp.sum(received[:, -1, :gain_width].astype(jnp.float32), axis=0).reshape(2, -1)
    attn_gain_result, ffn_gain_result = gain_sums[0], gain_sums[1]
    restore = jnp.argsort(send_order)
    return (
        back_rows[restore],
        back_grads[restore],
        attn_gain_result,
        query_result,
        key_result,
        value_result,
        output_result,
        ffn_gain_result,
        gate_result,
        up_result,
        down_result,
    )

def solution(mesh):
    placed = (
        P("row", "col"),
        P("row", "col"),
        P("row"),
        P("row"),
        P(),
        P("row", "col"),
        P("row", "col"),
        P("row", "col"),
        P("row", "col"),
        P(),
        P("row", "col"),
        P("row", "col"),
        P("row", "col"),
    )
    return jax.shard_map(
        body,
        mesh=mesh,
        in_specs=placed,
        out_specs=(
            P("row", "col"),
            P("row", "col"),
            P("row"),
            P("row", "col"),
            P("row", "col"),
            P("row", "col"),
            P("row", "col"),
            P("row"),
            P("row", "col"),
            P("row", "col"),
            P("row", "col"),
        ),
        check_vma=False,
    )
```
